32 devices in a mesh: seq: 8 (over z, core), wide: 4 (over y, x).
Axes of the slice: x: 2, y: 2, z: 4, core: 2. Of those that a mesh axis runs over, the one named last changes fastest.
Arguments:
- inputs: bfloat16 [16, 1024, 768], P('wide', 'seq'), may hold values from -6 to 6
- routes: int32 [16, 1024, 1], P('wide', 'seq'), may hold values from 0 to 7
- bucket_ids: int32 [2047], replicated, may hold values from 0 to 31
- gain_attn: bfloat16 [768], replicated, may hold values from 0.5 to 1.5
- w_query: bfloat16 [768, 768], replicated, may hold values from -0.02734375 to 0.02734375
- w_key: bfloat16 [768, 768], replicated, may hold values from -0.21875 to 0.21875
- w_value: bfloat16 [768, 768], replicated, may hold values from -0.21875 to 0.21875
- w_output: bfloat16 [768, 768], replicated, may hold values from -3.5 to 3.5
- rel_table: bfloat16 [32, 12], replicated, may hold values from -6 to 6
- gain_ffn: bfloat16 [768], replicated, may hold values from 0.5 to 1.5
- w_router: bfloat16 [768, 8], replicated, may hold values from -0.109375 to 0.109375
- w_in: bfloat16 [8, 768, 3072], P('wide'), may hold values from -0.21875 to 0.21875
- w_out: bfloat16 [8, 3072, 768], P('wide'), may hold values from -1.5 to 1.5
- cotangent: bfloat16 [16, 1024, 768], P('wide', 'seq'), may hold values from -6 to 6
Outputs:
- output: bfloat16 [16, 1024, 768], P('wide', 'seq')
- grad_inputs: float32 [16, 1024, 768], P('wide', 'seq')
- grad_gain_attn: float32 [768], P('seq')
- grad_w_query: float32 [768, 768], P('seq')
- grad_w_key: float32 [768, 768], P('seq')
- grad_w_value: float32 [768, 768], P('seq')
- grad_w_output: float32 [768, 768], P('seq')
- grad_rel_table: float32 [32, 12], P('seq')
- grad_gain_ffn: float32 [768], P('seq')
- grad_w_router: float32 [768, 8], P('seq')
- grad_w_in: float32 [8, 768, 3072], P('wide', None, 'seq')
- grad_w_out: float32 [8, 3072, 768], P('wide', 'seq')
The draws below stay inside these ranges and needn't reach their ends.
Inputs may be any that keep to these rules, and one draw needn't show every extreme that they name: `routes`: each token names one expert.
All inputs are finite; a program needn't handle non-finite values.
Results may differ from the reference program's by a relative error of at most 0.025.
Values may be sent and summed in bfloat16 or wider, within the bound.
A program may use at most 320 MiB of HBM per device.

```python
import jax
import jax.numpy as jnp
from jax import lax

D = 768
HEADS = 12
HEAD_DIM = 64
FF = 3072
BUCKETS = 32
S_DEV = 4
SEQ_DEV = 128
EXPERTS = 8
LEN = 1024
SEQS = 16
CAPACITY = 80
N_SEQ = 8
N_WIDE = 4


def touch_ends(array, rng, smallest, high):
    longest = array.shape.index(max(array.shape))
    spots = []
    for shift in (0, 1):
        where = [jax.random.randint(jax.random.fold_in(rng, axis), (), 0, length) for axis, length in enumerate(array.shape)]
        where[longest] = (where[longest] + shift) % array.shape[longest]
        spots.append(tuple(where))
    return array.at[spots[0]].set(smallest).at[spots[1]].set(high)


def steps_of(key, shape, shards, low, high):
    level, own = 1.0, jax.random.fold_in(key, 6)
    for dim, blocks in shards:
        steps = jnp.exp(jax.random.uniform(jax.random.fold_in(own, dim), (blocks,), jnp.float32, low / len(shards), high / len(shards)))
        level = level * jnp.repeat(steps, shape[dim] // blocks).reshape([-1 if axis == dim else 1 for axis in range(len(shape))])
    return level


def distinct(rng, rows, number_of, top, lift):
    order = jax.random.permutation(jax.random.fold_in(rng, 1), number_of)
    favour = order
    for power in range(3):
        favour = favour * favour // number_of
    favour = favour * lift // number_of
    lots = jax.random.randint(jax.random.fold_in(rng, 2), (rows, number_of), 0, 4096) + favour
    holders = jax.random.permutation(jax.random.fold_in(rng, 3), rows)[jnp.arange(number_of) % rows]
    lots = jnp.where(jnp.arange(rows)[:, None] == holders[None, :], 1 << 14, lots)
    merit = lots * number_of + jnp.arange(number_of)
    return lax.top_k(merit.astype(jnp.int32), top)[1].astype(jnp.int32)


def normal_values(key, shape, width, most, cuts=(), kind=jnp.bfloat16):
    array = jax.random.normal(key, shape, jnp.float32) * width
    if len(cuts) > 0:
        array = steps_of(key, shape, cuts, -0.22, 0.18) * array
    return jnp.clip(array, min=-most, max=most).astype(kind)


def setup_inputs(seed: int = 0) -> dict:
    splits = jax.random.split(jax.random.key(seed), 15)
    return {
        "inputs": normal_values(splits[0], (SEQS, LEN, D), 1.0, 6.0, ((0, 4), (1, 8))),
        "routes": distinct(splits[1], SEQS * LEN, EXPERTS, 1, 1024).reshape((SEQS, LEN, 1)),
        "bucket_ids": touch_ends(jax.random.randint(splits[2], (2 * LEN - 1,), 0, BUCKETS), jax.random.fold_in(splits[2], 1), 0, BUCKETS - 1).astype(jnp.int32),
        "gain_attn": jnp.clip(1.0 + 0.1 * jax.random.normal(splits[3], (D,), jnp.float32), 0.5, 1.5).astype(jnp.bfloat16),
        "w_query": normal_values(splits[4], (D, D), (D * HEAD_DIM) ** -0.5, 0.02734375),
        "w_key": normal_values(splits[5], (D, D), D ** -0.5, 0.21875),
        "w_value": normal_values(splits[6], (D, D), D ** -0.5, 0.21875),
        "w_output": normal_values(splits[7], (D, D), (max(D // 256, 1)) ** -0.5, 3.5),
        "rel_table": normal_values(splits[8], (BUCKETS, HEADS), 1.0, 6.0),
        "gain_ffn": jnp.clip(1.0 + 0.1 * jax.random.normal(splits[9], (D,), jnp.float32), 0.5, 1.5).astype(jnp.bfloat16),
        "w_router": normal_values(splits[10], (D, EXPERTS), (4 * D) ** -0.5, 0.109375),
        "w_in": normal_values(splits[11], (EXPERTS, D, FF), D ** -0.5, 0.21875, ((0, 4),)),
        "w_out": normal_values(splits[12], (EXPERTS, FF, D), (max(FF // (3 * EXPERTS * EXPERTS), 1)) ** -0.5, 1.5, ((0, 4),)),
        "cotangent": normal_values(splits[13], (SEQS, LEN, D), 1.0, 6.0, ((0, 4), (1, 8))),
    }


@jax.custom_vjp
def low(v):
    return lax.optimization_barrier(v.astype(jnp.bfloat16)).astype(jnp.float32)

@jax.custom_vjp
def low_back(v):
    return v

def low_keep(v):
    return (low(v), None)

def low_pass(kept, grad):
    return (grad,)

def back_keep(v):
    return (v, None)

def back_low(kept, grad):
    return (low(grad),)
low.defvjp(low_keep, low_pass)
low_back.defvjp(back_keep, back_low)
EPSILON = 1e-06

def rms_scaled(source, gain_vec):
    return source * lax.rsqrt(lax.optimization_barrier(jnp.mean(source * source, axis=-1, keepdims=True)) + EPSILON) * gain_vec

def to_groups(tensor):
    trailing = tensor.shape[2:]
    shaped = tensor.reshape((N_WIDE, S_DEV, N_SEQ, SEQ_DEV) + trailing)
    axis_order = (0, 2, 1, 3) + tuple(range(4, 4 + len(trailing)))
    return shaped.transpose(axis_order).reshape((N_WIDE * N_SEQ, S_DEV * SEQ_DEV) + trailing)

def from_groups(tensor):
    trailing = tensor.shape[2:]
    shaped = tensor.reshape((N_WIDE, N_SEQ, S_DEV, SEQ_DEV) + trailing)
    axis_order = (0, 2, 1, 3) + tuple(range(4, 4 + len(trailing)))
    return shaped.transpose(axis_order).reshape((N_WIDE * S_DEV, N_SEQ * SEQ_DEV) + trailing)

def reference(inputs, routes, bucket_ids, gain_attn, w_query, w_key, w_value, w_output, rel_table, gain_ffn, w_router, w_in, w_out, cotangent):
    highest_precision = lax.Precision.HIGHEST
    group_count = N_WIDE * N_SEQ
    slot_count = EXPERTS * CAPACITY
    positions = jnp.arange(LEN, dtype=jnp.int32)
    offsets = (positions[None, :] - positions[:, None] + LEN - 1).astype(jnp.int32)
    bucket_map = jnp.take(bucket_ids, offsets)
    chosen = to_groups(routes)[:, :, 0].astype(jnp.int32)
    picked = (chosen[:, :, None] == jnp.arange(EXPERTS, dtype=jnp.int32)[None, None, :]).astype(jnp.int32)
    earlier = (jnp.cumsum(picked, axis=1) - picked).astype(jnp.int32)
    rank_in = lax.optimization_barrier(jnp.sum(earlier * picked, axis=2)).astype(jnp.int32)
    slot_of = jnp.where(rank_in < CAPACITY, chosen * CAPACITY + rank_in, slot_count).astype(jnp.int32)
    group_ids = jnp.arange(group_count, dtype=jnp.int32)[:, None]
    route_hot = (routes[:, :, 0][:, :, None] == jnp.arange(EXPERTS, dtype=jnp.int32)[None, None, :]).astype(jnp.float32)

    def attend(blocks, rel_bias):
        projected_query_rows, projected_key_rows, projected_value_rows = blocks
        q_heads = projected_query_rows.reshape(LEN, HEADS, HEAD_DIM)
        k_heads = projected_key_rows.reshape(LEN, HEADS, HEAD_DIM)
        v_heads = projected_value_rows.reshape(LEN, HEADS, HEAD_DIM)
        scores = jnp.einsum('ahd,jhd->haj', q_heads, k_heads, precision=highest_precision) + rel_bias
        scores = low_back(scores)
        attn_probs = jax.nn.softmax(scores, axis=-1)
        mixed_heads = jnp.einsum('haj,jhd->ahd', low(attn_probs), v_heads, precision=highest_precision)
        return mixed_heads.reshape(LEN, D)

    def expert(blocks):
        rows_in, weight_in, weight_out = blocks
        pre_act = low_back(jnp.dot(rows_in, weight_in, precision=highest_precision))
        hidden = low(low_back(jax.nn.gelu(pre_act, approximate=True)))
        return low(low_back(jnp.dot(hidden, weight_out, precision=highest_precision)))

    def forward(act_in, gain_one, query_projection_weight, key_projection_weight, value_projection_weight, output_projection_weight, rel_tab, gain_two, router_gate_weight, weight_in, weight_out):
        first_normed_input = low(rms_scaled(act_in, gain_one))
        projected_query_rows = low_back(low(jnp.einsum('hbu,uc->hbc', first_normed_input, query_projection_weight, precision=highest_precision)))
        projected_key_rows = low_back(low(jnp.einsum('hbu,uc->hbc', first_normed_input, key_projection_weight, precision=highest_precision)))
        projected_value_rows = low_back(low(jnp.einsum('hbu,uc->hbc', first_normed_input, value_projection_weight, precision=highest_precision)))
        rel_bias = jnp.take(rel_tab.T, bucket_map, axis=1)
        mixed_all = lax.map(jax.checkpoint(lambda blocks: attend(blocks, rel_bias)), (projected_query_rows, projected_key_rows, projected_value_rows))
        attention_output = low(low_back(mixed_all))
        residual_branch = low_back(jnp.einsum('hbu,uc->hbc', attention_output, output_projection_weight, precision=highest_precision))
        middle = act_in + residual_branch
        second_normed_input = low(rms_scaled(middle, gain_two))
        router_logits = low_back(jnp.einsum('hbu,uc->hbc', second_normed_input, router_gate_weight, precision=highest_precision))
        router_probs = jax.nn.softmax(router_logits, axis=-1)
        gate_prob = lax.optimization_barrier(jnp.sum(router_probs * route_hot, axis=-1))
        packed = jnp.zeros((group_count, slot_count + 1, D), jnp.float32).at[group_ids, slot_of].set(to_groups(second_normed_input))
        packed = packed[:, :slot_count].reshape(group_count, EXPERTS, CAPACITY, D).transpose(1, 0, 2, 3)
        packed = low_back(packed.reshape(EXPERTS, group_count * CAPACITY, D))
        expert_out = lax.map(jax.checkpoint(expert), (packed, weight_in, weight_out))
        expert_out = expert_out.reshape(EXPERTS, group_count, CAPACITY, D).transpose(1, 0, 2, 3).reshape(group_count, slot_count, D)
        expert_out = jnp.concatenate([expert_out, jnp.zeros((group_count, 1, D), jnp.float32)], axis=1)
        selected = from_groups(expert_out[group_ids, slot_of])
        return middle + gate_prob[:, :, None] * selected
    primals = (inputs.astype(jnp.float32), gain_attn.astype(jnp.float32), w_query.astype(jnp.float32), w_key.astype(jnp.float32), w_value.astype(jnp.float32), w_output.astype(jnp.float32), rel_table.astype(jnp.float32), gain_ffn.astype(jnp.float32), w_router.astype(jnp.float32), w_in.astype(jnp.float32), w_out.astype(jnp.float32))
    result, pullback = jax.vjp(forward, *primals)
    gradients = pullback(cotangent.astype(jnp.float32))
    return (result.astype(jnp.bfloat16), gradients[0], gradients[1], gradients[2], gradients[3], gradients[4], gradients[5], gradients[6], gradients[7], gradients[8], gradients[9], gradients[10])
```

```python
import functools

import jax
import jax.numpy as jnp
from jax import lax
from jax.experimental import pallas as pl
from jax.experimental.pallas import tpu as pltpu
from jax.sharding import PartitionSpec as P

EPSILON = 1e-06
F32 = jnp.float32
BF16 = jnp.bfloat16
LANES = 128


def contract(a, b, da, db):
    return lax.dot_general(a, b, (((da,), (db,)), ((), ())), preferred_element_type=F32)


def inverse_rms(source):
    return lax.rsqrt(jnp.mean(source * source, axis=-1, keepdims=True) + EPSILON)


def norm_backward(source, inv_rms, gain_vec, upstream):
    scaled = upstream * gain_vec
    gain_grad = jnp.sum(upstream * source * inv_rms, axis=0)
    mean_inner = jnp.mean(source * scaled, axis=-1, keepdims=True)
    return (inv_rms * scaled - source * (inv_rms * inv_rms * inv_rms) * mean_inner, gain_grad)


def smooth_act(values):
    return jax.nn.gelu(values, approximate=True)


def attend_kernel(length, width, q_ref, k_ref, v_ref, bias_ref, out_ref, exp_ref, inv_ref, strip, keys, scores):
    block = pl.program_id(1)
    rows = 2 * length - LANES

    @pl.when(block == 0)
    def _():
        keys[...] = k_ref[...].T
        for b in range(rows // LANES):
            start = 2 * length - 2 * LANES - LANES * b
            base = jnp.broadcast_to(bias_ref[0, :, start : start + 2 * LANES], (LANES, 2 * LANES))
            rolled = pltpu.roll(base, 0, 1, stride=1, stride_axis=0)
            strip[LANES * b : LANES * (b + 1), :] = rolled[:, LANES:]

    chunk = 256
    subs = width // LANES
    tops = [jnp.full((1, LANES), -jnp.inf, F32)] * subs
    for c in range(length // chunk):
        part = contract(keys[c * chunk : (c + 1) * chunk, :], q_ref[...], 1, 0)
        for s in range(subs):
            row = pl.multiple_of(length - LANES - (block * width + s * LANES) + c * chunk, LANES)
            piece = part[:, s * LANES : (s + 1) * LANES] + strip[pl.ds(row, chunk), :]
            scores[c * chunk : (c + 1) * chunk, s * LANES : (s + 1) * LANES] = piece
            tops[s] = jnp.maximum(tops[s], jnp.max(piece, axis=0, keepdims=True))
    sums = [jnp.zeros((1, LANES), F32)] * subs
    for c in range(length // chunk):
        for s in range(subs):
            piece = scores[c * chunk : (c + 1) * chunk, s * LANES : (s + 1) * LANES]
            grown = jnp.exp(piece - tops[s])
            sums[s] = sums[s] + jnp.sum(grown, axis=0, keepdims=True)
            exp_ref[0, c * chunk : (c + 1) * chunk, s * LANES : (s + 1) * LANES] = grown.astype(BF16)
    mixed = contract(v_ref[...], exp_ref[0], 1, 0)
    for s in range(subs):
        inverse = 1.0 / sums[s]
        inv_ref[0, :, s * LANES : (s + 1) * LANES] = inverse
        out_ref[s] = (mixed[:, s * LANES : (s + 1) * LANES] * inverse).astype(BF16)


def attend_back_kernel(
    length, width, exp_ref, inv_ref, grad_ref, out_ref, q_ref, k_ref, v_ref, dq_ref, dk_ref, dv_ref, diag_ref, strip, values, dk_sum, dv_sum, scores
):
    block = pl.program_id(1)
    rows = 2 * length - LANES
    subs = width // LANES

    @pl.when(block == 0)
    def _():
        values[...] = v_ref[...].T
        strip[...] = jnp.zeros_like(strip)
        dk_sum[...] = jnp.zeros_like(dk_sum)
        dv_sum[...] = jnp.zeros_like(dv_sum)

    grads, inner = [], []
    for s in range(subs):
        inverse = inv_ref[0, :, s * LANES : (s + 1) * LANES]
        scaled = grad_ref[s].astype(F32) * inverse
        inner.append(jnp.sum(scaled * out_ref[s].astype(F32), axis=0, keepdims=True))
        grads.append(scaled.astype(BF16))
    grad = jnp.concatenate(grads, axis=1) if subs > 1 else grads[0]
    chunk = 256
    for c in range(length // chunk):
        part = contract(values[c * chunk : (c + 1) * chunk, :], grad, 1, 0)
        for s in range(subs):
            grown = exp_ref[0, c * chunk : (c + 1) * chunk, s * LANES : (s + 1) * LANES].astype(F32)
            slope = grown * (part[:, s * LANES : (s + 1) * LANES] - inner[s])
            row = pl.multiple_of(length - LANES - (block * width + s * LANES) + c * chunk, LANES)
            strip[pl.ds(row, chunk), :] += slope
            scores[c * chunk : (c + 1) * chunk, s * LANES : (s + 1) * LANES] = slope.astype(BF16)
    dq_ref[...] = contract(k_ref[...], scores[...], 1, 0).astype(BF16)
    dk_sum[...] += contract(scores[...], q_ref[...].T, 1, 0)
    dv_sum[...] += contract(exp_ref[0], grad.T, 1, 0)

    @pl.when(block == pl.num_programs(1) - 1)
    def _():
        dk_ref[...] = dk_sum[...].T.astype(BF16)
        dv_ref[...] = dv_sum[...].T.astype(BF16)
        diag_ref[...] = jnp.zeros_like(diag_ref)
        down = lax.broadcasted_iota(jnp.int32, (LANES, LANES), 0)
        over = lax.broadcasted_iota(jnp.int32, (LANES, LANES), 1)
        mirror = (down + over == LANES - 1).astype(F32)
        for b in range(rows // LANES):
            held = lax.dot_general(
                strip[LANES * b : LANES * (b + 1), :],
                mirror,
                (((1,), (0,)), ((), ())),
                precision=lax.Precision.HIGHEST,
                preferred_element_type=F32,
            )
            spread = jnp.concatenate([held, jnp.zeros_like(held)], axis=1)
            rolled = pltpu.roll(spread, 0, 1, stride=1, stride_axis=0)
            diag_ref[0, :, LANES * b : LANES * (b + 2)] += jnp.sum(rolled, axis=0, keepdims=True)


def attention_specs(heads, size, length, width):
    subs = width // LANES
    return dict(
        query=pl.BlockSpec((size, width), lambda h, b: (h, b)),
        key=pl.BlockSpec((size, length), lambda h, b: (heads + h, 0)),
        value=pl.BlockSpec((size, length), lambda h, b: (2 * heads + h, 0)),
        whole=pl.BlockSpec((size, length), lambda h, b: (h, 0)),
        line=pl.BlockSpec((1, 1, 2 * length), lambda h, b: (h, 0, 0)),
        exps=pl.BlockSpec((1, length, width), lambda h, b: (h, 0, b)),
        inv=pl.BlockSpec((1, 1, width), lambda h, b: (h, 0, b)),
        tokens=pl.BlockSpec((subs, size, LANES), lambda h, b: (b, h, 0)),
    )


def attend(qkv, bias_line, heads, size, length, width):
    spec = attention_specs(heads, size, length, width)
    return pl.pallas_call(
        functools.partial(attend_kernel, length, width),
        grid=(heads, length // width),
        in_specs=[spec["query"], spec["key"], spec["value"], spec["line"]],
        out_specs=[spec["tokens"], spec["exps"], spec["inv"]],
        out_shape=[
            jax.ShapeDtypeStruct((length // LANES, heads * size, LANES), BF16),
            jax.ShapeDtypeStruct((heads, length, length), BF16),
            jax.ShapeDtypeStruct((heads, 1, length), F32),
        ],
        scratch_shapes=[
            pltpu.VMEM((2 * length - LANES, LANES), F32),
            pltpu.VMEM((length, size), BF16),
            pltpu.VMEM((length, width), F32),
        ],
        compiler_params=pltpu.CompilerParams(vmem_limit_bytes=40 << 20),
        cost_estimate=pl.CostEstimate(
            flops=4 * heads * length * length * size, bytes_accessed=2 * heads * length * length, transcendentals=heads * length * length
        ),
        name="attend",
    )(qkv, qkv, qkv, bias_line)


def attend_back(exps, inverse, grads, outs, qkv, heads, size, length, width):
    spec = attention_specs(heads, size, length, width)
    return pl.pallas_call(
        functools.partial(attend_back_kernel, length, width),
        grid=(heads, length // width),
        in_specs=[spec["exps"], spec["inv"], spec["tokens"], spec["tokens"], spec["query"], spec["key"], spec["value"]],
        out_specs=[spec["query"], spec["whole"], spec["whole"], spec["line"]],
        out_shape=[
            jax.ShapeDtypeStruct((heads * size, length), BF16),
            jax.ShapeDtypeStruct((heads * size, length), BF16),
            jax.ShapeDtypeStruct((heads * size, length), BF16),
            jax.ShapeDtypeStruct((heads, 1, 2 * length), F32),
        ],
        scratch_shapes=[
            pltpu.VMEM((2 * length - LANES, LANES), F32),
            pltpu.VMEM((length, size), BF16),
            pltpu.VMEM((length, size), F32),
            pltpu.VMEM((length, size), F32),
            pltpu.VMEM((length, width), BF16),
        ],
        compiler_params=pltpu.CompilerParams(vmem_limit_bytes=40 << 20),
        cost_estimate=pl.CostEstimate(
            flops=8 * heads * length * length * size, bytes_accessed=2 * heads * length * length, transcendentals=0
        ),
        name="attend_back",
    )(exps, inverse, grads, outs, qkv, qkv, qkv)


def ring_pairs(total, parts, shift):
    return [(i, i - i % parts + (i % parts + shift) % parts) for i in range(total)]


def pick(pieces, index):
    out = pieces[0]
    for k in range(1, len(pieces)):
        out = jnp.where(index == k, pieces[k], out)
    return out


def gather_parts(block, part, parts, total):
    near = [block] + [lax.ppermute(block, "seq", ring_pairs(total, parts, k)) for k in range(1, parts)]
    return [pick(near, (part - j) % parts) for j in range(parts)]


def swap_parts(pieces, part, parts, total):
    near = [pick(pieces, part)]
    for k in range(1, parts):
        near.append(lax.ppermute(pick(pieces, (part + k) % parts), "seq", ring_pairs(total, parts, k)))
    return [pick(near, (part - j) % parts) for j in range(parts)]


def sum_replicated(own, seqs):
    total, parts = lax.axis_size("seq"), lax.axis_size("seq") // seqs
    across = lax.axis_size("wide")
    _, rows, columns = own.shape
    split = own.reshape(seqs, across, rows // across, columns).transpose(1, 0, 2, 3)
    got = lax.all_to_all(split, "wide", 0, 0, tiled=True)
    mine = jnp.sum(got.astype(F32), axis=0).astype(BF16)
    groups = [[s * parts + p for s in range(seqs)] for p in range(parts)]
    got = lax.all_to_all(mine, "seq", 0, 0, tiled=True, axis_index_groups=groups)
    mine = jnp.sum(got.astype(F32), axis=0)
    return lax.all_gather(mine.astype(BF16), "wide", axis=0, tiled=True).astype(F32)


def per_device(
    inputs,
    routes,
    bucket_ids,
    gain_attn,
    w_query,
    w_key,
    w_value,
    w_output,
    rel_table,
    gain_ffn,
    w_router,
    w_in,
    w_out,
    cotangent,
):
    seqs, local_len, width = inputs.shape
    buckets, head_count = rel_table.shape
    size = width // head_count
    total = lax.axis_size("seq")
    across = lax.axis_size("wide")
    length = local_len * total
    parts = total // seqs
    heads = head_count // parts
    cols = heads * size
    me = lax.axis_index("seq")
    part = me % parts
    experts = w_router.shape[1]
    own_experts = w_in.shape[0]
    tokens = seqs * local_len
    capacity = (5 * tokens + 4 * experts - 1) // (4 * experts)
    slots = experts * capacity
    gain_one = gain_attn.astype(F32)
    gain_two = gain_ffn.astype(F32)

    got = lax.all_to_all(inputs.reshape(total, local_len // parts, width), "seq", 0, 0, tiled=True)
    seq_in = jnp.stack(gather_parts(got, part, parts, total), axis=1).reshape(length, width).astype(F32)
    inv_one = inverse_rms(seq_in)
    normed_one = (seq_in * inv_one * gain_one).astype(BF16)
    own_weights = jnp.concatenate(
        [lax.dynamic_slice(w, (0, part * cols), (width, cols)) for w in (w_query, w_key, w_value)], axis=1
    )
    qkv = contract(own_weights, normed_one, 0, 1).astype(BF16)
    own_table = lax.dynamic_slice(rel_table, (0, part * heads), (buckets, heads))
    ids = jnp.concatenate([bucket_ids, jnp.full((1,), buckets, jnp.int32)])
    bucket_hot = (ids[None, :] == jnp.arange(buckets, dtype=jnp.int32)[:, None]).astype(BF16)
    reverse_hot = (ids[::-1][None, :] == jnp.arange(buckets, dtype=jnp.int32)[:, None]).astype(BF16)
    bias_line = contract(own_table, reverse_hot, 0, 0).reshape(heads, 1, 2 * length)
    block = 256
    outs, exps, inverse = attend(qkv, bias_line, heads, size, length, block)

    attended = lax.all_to_all(outs, "seq", 0, 0, tiled=True).reshape(seqs, width, local_len)
    flat_in = inputs.reshape(tokens, width).astype(F32)
    middle = flat_in + jnp.einsum("sft,fe->ste", attended, w_output, preferred_element_type=F32).reshape(tokens, width)
    inv_two = inverse_rms(middle)
    normed_two = (middle * inv_two * gain_two).astype(BF16)
    router_probs = jax.nn.softmax(jnp.dot(normed_two, w_router, preferred_element_type=F32), axis=-1)
    chosen = routes.reshape(tokens)
    picked = chosen[:, None] == jnp.arange(experts, dtype=jnp.int32)[None, :]
    order = jnp.arange(tokens, dtype=jnp.int32)
    before = (order[None, :] < order[:, None]).astype(BF16)
    earlier = jnp.dot(before, picked.astype(BF16), preferred_element_type=F32)
    picked = picked.astype(F32)
    rank_in = jnp.sum(earlier * picked, axis=1).astype(jnp.int32)
    place = (chosen % own_experts) * (across * capacity) + (chosen // own_experts) * capacity + rank_in
    slot_of = jnp.where(rank_in < capacity, place, slots)
    slot_hot = (slot_of[:, None] == jnp.arange(slots, dtype=jnp.int32)[None, :]).astype(BF16)
    gate_prob = jnp.sum(router_probs * picked, axis=1)
    upstream = cotangent.reshape(tokens, width).astype(F32)
    weighted = (gate_prob[:, None] * upstream).astype(BF16)
    both = jnp.concatenate([normed_two, weighted], axis=1)
    packed = contract(slot_hot, both, 0, 0).astype(BF16).reshape(own_experts, across, capacity, 2 * width)
    returned, gathered = [], []
    for e in range(own_experts):
        received = lax.all_to_all(packed[e], "wide", 0, 0, tiled=True).reshape(across * capacity, 2 * width)
        gathered.append(lax.all_gather(received, "seq", axis=0, tiled=True))
        rows_in, rows_grad = received[:, :width], received[:, width:]
        pre_act = jnp.dot(rows_in, w_in[e], preferred_element_type=F32)
        act, pullback = jax.vjp(smooth_act, pre_act)
        expert_out = jnp.dot(act.astype(BF16), w_out[e], preferred_element_type=F32).astype(BF16)
        grad_hidden = contract(rows_grad, w_out[e], 1, 1).astype(BF16)
        grad_pre = pullback(grad_hidden.astype(F32))[0].astype(BF16)
        grad_rows = contract(grad_pre, w_in[e], 1, 1).astype(BF16)
        pair = jnp.concatenate([expert_out, grad_rows], axis=1).reshape(across, capacity, 2 * width)
        returned.append(lax.all_to_all(pair, "wide", 0, 0, tiled=True).reshape(across * capacity, 2 * width))
    token_rows = jnp.dot(slot_hot, jnp.concatenate(returned, axis=0), preferred_element_type=F32)
    selected, grad_token = token_rows[:, :width], token_rows[:, width:]
    output = (middle + gate_prob[:, None] * selected).astype(BF16).reshape(inputs.shape)
    grad_gate = jnp.sum(upstream * selected, axis=1)
    grad_logits = (grad_gate[:, None] * router_probs * (picked - gate_prob[:, None])).astype(BF16)
    grad_router = contract(normed_two, grad_logits, 0, 0)
    grad_normed_two = grad_token + contract(grad_logits, w_router, 1, 1)
    grad_mid_norm, grad_gain_two = norm_backward(middle, inv_two, gain_two, grad_normed_two)
    grad_middle = upstream + grad_mid_norm
    grad_branch = grad_middle.astype(BF16)
    grad_att = jnp.einsum(
        "ste,fe->sft", grad_branch.reshape(seqs, local_len, width), w_output, preferred_element_type=F32
    ).astype(BF16)
    grad_outs = lax.all_to_all(grad_att.reshape(total, cols, local_len), "seq", 0, 0, tiled=True)
    grad_w_output = jnp.einsum(
        "sft,ste->fe", attended, grad_branch.reshape(seqs, local_len, width), preferred_element_type=F32
    )

    dq, dk, dv, diagonal = attend_back(exps, inverse, grad_outs, outs, qkv, heads, size, length, block)
    grads = jnp.concatenate([dq, dk, dv], axis=0)
    grad_table = jnp.einsum(
        "bo,ho->bh", bucket_hot.astype(F32), diagonal[:, 0, :], precision=lax.Precision.HIGHEST
    )
    grad_normed_one = contract(grads, own_weights, 0, 1)
    grad_in_norm, grad_gain_one = norm_backward(seq_in, inv_one, gain_one, grad_normed_one)
    pieces = grad_in_norm.astype(BF16).reshape(total, parts, local_len // parts, width)
    swapped = swap_parts([pieces[:, p] for p in range(parts)], part, parts, total)
    home = sum(p.astype(F32) for p in swapped).astype(BF16)
    home = lax.all_to_all(home, "seq", 0, 0, tiled=True).reshape(tokens, width).astype(F32)
    grad_inputs = (grad_middle + home).reshape(inputs.shape)
    grad_w_qkv = contract(normed_one, grads, 0, 1).astype(BF16)

    share = width // total
    small = jnp.zeros((width, LANES), F32)
    table_full = lax.dynamic_update_slice(jnp.zeros((buckets, head_count), F32), grad_table, (0, part * heads))
    table_rows = jnp.pad(table_full.reshape(total, -1), ((0, 0), (0, share - buckets * head_count // total)))
    small = jnp.concatenate(
        [
            grad_gain_one[:, None],
            table_rows.reshape(width, 1),
            grad_gain_two[:, None],
            grad_router,
            jnp.zeros((width, LANES - 3 - experts), F32),
        ],
        axis=1,
    )
    summed = jnp.concatenate([grad_w_output, small], axis=1).astype(BF16)
    summed = summed.reshape(seqs, parts, share, width + LANES)
    summed = swap_parts([summed[:, p] for p in range(parts)], part, parts, total)
    summed = sum(p.astype(F32) for p in summed).astype(BF16)
    joined = grad_w_qkv.reshape(seqs, parts, share, 3, cols)
    joined = swap_parts([joined[:, p] for p in range(parts)], part, parts, total)
    joined = jnp.stack(joined, axis=3).reshape(seqs, share, 3 * width)
    result = sum_replicated(jnp.concatenate([joined, summed], axis=2), seqs)
    total_query, total_key, total_value, total_output, rest = jnp.split(
        result, [width, 2 * width, 3 * width, 4 * width], axis=1
    )
    total_table = rest[: buckets * head_count // total, 1].reshape(buckets // total, head_count)

    hidden_share = w_in.shape[2] // total
    part_in, part_out = [], []
    for e in range(own_experts):
        rows_in, rows_grad = gathered[e][:, :width], gathered[e][:, width:]
        in_share = lax.dynamic_slice(w_in[e], (0, me * hidden_share), (width, hidden_share))
        out_share = lax.dynamic_slice(w_out[e], (me * hidden_share, 0), (hidden_share, width))
        act, pullback = jax.vjp(smooth_act, jnp.dot(rows_in, in_share, preferred_element_type=F32))
        grad_hidden = contract(rows_grad, out_share, 1, 1).astype(BF16)
        grad_pre = pullback(grad_hidden.astype(F32))[0].astype(BF16)
        part_in.append(contract(rows_in, grad_pre, 0, 0))
        part_out.append(contract(act.astype(BF16), rows_grad, 0, 0))
    return (
        output,
        grad_inputs,
        rest[:, 0],
        total_query,
        total_key,
        total_value,
        total_output,
        total_table,
        rest[:, 2],
        rest[:, 3 : 3 + experts],
        jnp.stack(part_in),
        jnp.stack(part_out),
    )


def solution(mesh):
    in_specs = (
        P("wide", "seq", None),
        P("wide", "seq", None),
        P(),
        P(),
        P(),
        P(),
        P(),
        P(),
        P(),
        P(),
        P(),
        P("wide", None, None),
        P("wide", None, None),
        P("wide", "seq", None),
    )
    out_specs = (
        P("wide", "seq", None),
        P("wide", "seq", None),
        P("seq"),
        P("seq", None),
        P("seq", None),
        P("seq", None),
        P("seq", None),
        P("seq", None),
        P("seq"),
        P("seq", None),
        P("wide", None, "seq"),
        P("wide", "seq", None),
    )
    return jax.shard_map(
        per_device, mesh=mesh, in_specs=in_specs, out_specs=out_specs, check_vma=False
    )
```

```python
import functools

import jax
import jax.numpy as jnp
from jax import lax
from jax.experimental import pallas as pl
from jax.experimental.pallas import tpu as pltpu
from jax.sharding import PartitionSpec as P

EPSILON = 1e-06
F32 = jnp.float32
BF16 = jnp.bfloat16
LANES = 128


def contract(a, b, da, db):
    return lax.dot_general(a, b, (((da,), (db,)), ((), ())), preferred_element_type=F32)


def inverse_rms(source):
    return lax.rsqrt(jnp.mean(source * source, axis=-1, keepdims=True) + EPSILON)


def norm_backward(source, inv_rms, gain_vec, upstream):
    scaled = upstream * gain_vec
    gain_grad = jnp.sum(upstream * source * inv_rms, axis=0)
    mean_inner = jnp.mean(source * scaled, axis=-1, keepdims=True)
    return (inv_rms * scaled - source * (inv_rms * inv_rms * inv_rms) * mean_inner, gain_grad)


def smooth_act(values):
    return jax.nn.gelu(values, approximate=True)


def attend_kernel(length, width, q_ref, k_ref, v_ref, bias_ref, out_ref, exp_ref, inv_ref, strip, keys, scores):
    block = pl.program_id(1)
    rows = 2 * length - LANES

    @pl.when(block == 0)
    def _():
        keys[...] = k_ref[...].T
        for b in range(rows // LANES):
            start = 2 * length - 2 * LANES - LANES * b
            base = jnp.broadcast_to(bias_ref[0, :, start : start + 2 * LANES], (LANES, 2 * LANES))
            rolled = pltpu.roll(base, 0, 1, stride=1, stride_axis=0)
            strip[LANES * b : LANES * (b + 1), :] = rolled[:, LANES:]

    chunk = 256
    subs = width // LANES
    tops = [jnp.full((1, LANES), -jnp.inf, F32)] * subs
    for c in range(length // chunk):
        part = contract(keys[c * chunk : (c + 1) * chunk, :], q_ref[...], 1, 0)
        for s in range(subs):
            row = pl.multiple_of(length - LANES - (block * width + s * LANES) + c * chunk, LANES)
            piece = part[:, s * LANES : (s + 1) * LANES] + strip[pl.ds(row, chunk), :]
            scores[c * chunk : (c + 1) * chunk, s * LANES : (s + 1) * LANES] = piece
            tops[s] = jnp.maximum(tops[s], jnp.max(piece, axis=0, keepdims=True))
    sums = [jnp.zeros((1, LANES), F32)] * subs
    for c in range(length // chunk):
        for s in range(subs):
            piece = scores[c * chunk : (c + 1) * chunk, s * LANES : (s + 1) * LANES]
            grown = jnp.exp(piece - tops[s])
            sums[s] = sums[s] + jnp.sum(grown, axis=0, keepdims=True)
            exp_ref[0, c * chunk : (c + 1) * chunk, s * LANES : (s + 1) * LANES] = grown.astype(BF16)
    mixed = contract(v_ref[...], exp_ref[0], 1, 0)
    for s in range(subs):
        inverse = 1.0 / sums[s]
        inv_ref[0, :, s * LANES : (s + 1) * LANES] = inverse
        out_ref[s] = (mixed[:, s * LANES : (s + 1) * LANES] * inverse).astype(BF16)


def attend_back_kernel(
    length, width, exp_ref, inv_ref, grad_ref, out_ref, q_ref, k_ref, v_ref, three_ref, diag_ref, strip, values, dk_sum, dv_sum, scores
):
    block = pl.program_id(1)
    rows = 2 * length - LANES
    subs = width // LANES

    @pl.when(block == 0)
    def _():
        values[...] = v_ref[...].T
        strip[...] = jnp.zeros_like(strip)
        dk_sum[...] = jnp.zeros_like(dk_sum)
        dv_sum[...] = jnp.zeros_like(dv_sum)

    grads, inner = [], []
    for s in range(subs):
        inverse = inv_ref[0, :, s * LANES : (s + 1) * LANES]
        scaled = grad_ref[s].astype(F32) * inverse
        inner.append(jnp.sum(scaled * out_ref[s].astype(F32), axis=0, keepdims=True))
        grads.append(scaled.astype(BF16))
    grad = jnp.concatenate(grads, axis=1) if subs > 1 else grads[0]
    chunk = 256
    for c in range(length // chunk):
        part = contract(values[c * chunk : (c + 1) * chunk, :], grad, 1, 0)
        for s in range(subs):
            grown = exp_ref[0, c * chunk : (c + 1) * chunk, s * LANES : (s + 1) * LANES].astype(F32)
            slope = grown * (part[:, s * LANES : (s + 1) * LANES] - inner[s])
            row = pl.multiple_of(length - LANES - (block * width + s * LANES) + c * chunk, LANES)
            strip[pl.ds(row, chunk), :] += slope
            scores[c * chunk : (c + 1) * chunk, s * LANES : (s + 1) * LANES] = slope.astype(BF16)
    here = pl.ds(pl.multiple_of(block * width, LANES), width)
    three_ref[0, :, here] = contract(k_ref[...], scores[...], 1, 0).astype(BF16)
    dk_sum[...] += contract(scores[...], q_ref[...].T, 1, 0)
    dv_sum[...] += contract(exp_ref[0], grad.T, 1, 0)

    @pl.when(block == pl.num_programs(1) - 1)
    def _():
        three_ref[1] = dk_sum[...].T.astype(BF16)
        three_ref[2] = dv_sum[...].T.astype(BF16)
        diag_ref[...] = jnp.zeros_like(diag_ref)
        down = lax.broadcasted_iota(jnp.int32, (LANES, LANES), 0)
        over = lax.broadcasted_iota(jnp.int32, (LANES, LANES), 1)
        mirror = (down + over == LANES - 1).astype(F32)
        for b in range(rows // LANES):
            held = lax.dot_general(
                strip[LANES * b : LANES * (b + 1), :],
                mirror,
                (((1,), (0,)), ((), ())),
                precision=lax.Precision.HIGHEST,
                preferred_element_type=F32,
            )
            spread = jnp.concatenate([held, jnp.zeros_like(held)], axis=1)
            rolled = pltpu.roll(spread, 0, 1, stride=1, stride_axis=0)
            diag_ref[0, :, LANES * b : LANES * (b + 2)] += jnp.sum(rolled, axis=0, keepdims=True)


def attention_specs(heads, first, size, length, width):
    subs = width // LANES
    return dict(
        query=pl.BlockSpec((size, width), lambda h, b: (first + h, b)),
        key=pl.BlockSpec((size, length), lambda h, b: (heads + first + h, 0)),
        value=pl.BlockSpec((size, length), lambda h, b: (2 * heads + first + h, 0)),
        three=pl.BlockSpec((3, size, length), lambda h, b: (0, h, 0)),
        bias=pl.BlockSpec((1, 1, 2 * length), lambda h, b: (first + h, 0, 0)),
        line=pl.BlockSpec((1, 1, 2 * length), lambda h, b: (h, 0, 0)),
        exps=pl.BlockSpec((1, length, width), lambda h, b: (h, 0, b)),
        inv=pl.BlockSpec((1, 1, width), lambda h, b: (h, 0, b)),
        tokens=pl.BlockSpec((subs, size, LANES), lambda h, b: (b, h, 0)),
    )


def attend(qkv, bias_line, heads, first, count, size, length, width):
    spec = attention_specs(heads, first, size, length, width)
    return pl.pallas_call(
        functools.partial(attend_kernel, length, width),
        grid=(count, length // width),
        in_specs=[spec["query"], spec["key"], spec["value"], spec["bias"]],
        out_specs=[spec["tokens"], spec["exps"], spec["inv"]],
        out_shape=[
            jax.ShapeDtypeStruct((length // LANES, count * size, LANES), BF16),
            jax.ShapeDtypeStruct((count, length, length), BF16),
            jax.ShapeDtypeStruct((count, 1, length), F32),
        ],
        scratch_shapes=[
            pltpu.VMEM((2 * length - LANES, LANES), F32),
            pltpu.VMEM((length, size), BF16),
            pltpu.VMEM((length, width), F32),
        ],
        compiler_params=pltpu.CompilerParams(vmem_limit_bytes=62 << 20),
        cost_estimate=pl.CostEstimate(
            flops=4 * count * length * length * size, bytes_accessed=2 * count * length * length, transcendentals=count * length * length
        ),
        name="attend",
    )(qkv, qkv, qkv, bias_line)


def attend_back(exps, inverse, grads, outs, qkv, heads, first, count, size, length, width):
    spec = attention_specs(heads, first, size, length, width)
    return pl.pallas_call(
        functools.partial(attend_back_kernel, length, width),
        grid=(count, length // width),
        in_specs=[spec["exps"], spec["inv"], spec["tokens"], spec["tokens"], spec["query"], spec["key"], spec["value"]],
        out_specs=[spec["three"], spec["line"]],
        out_shape=[
            jax.ShapeDtypeStruct((3, count * size, length), BF16),
            jax.ShapeDtypeStruct((count, 1, 2 * length), F32),
        ],
        scratch_shapes=[
            pltpu.VMEM((2 * length - LANES, LANES), F32),
            pltpu.VMEM((length, size), BF16),
            pltpu.VMEM((length, size), F32),
            pltpu.VMEM((length, size), F32),
            pltpu.VMEM((length, width), BF16),
        ],
        compiler_params=pltpu.CompilerParams(vmem_limit_bytes=62 << 20),
        cost_estimate=pl.CostEstimate(
            flops=8 * count * length * length * size, bytes_accessed=2 * count * length * length, transcendentals=0
        ),
        name="attend_back",
    )(exps, inverse, grads, outs, qkv, qkv, qkv)


def activation(v):
    square = v * v
    bent = jnp.tanh(0.7978845608 * v * (1.0 + 0.044715 * square))
    half = 0.5 * (1.0 + bent)
    slope = half + 0.5 * v * (1.0 - bent * bent) * (0.7978845608 * (1.0 + 3.0 * 0.044715 * square))
    return v * half, slope


def expert_kernel(rows_ref, in_ref, out_ref, both_ref, forward, backward):
    step = pl.program_id(0)
    width = rows_ref.shape[1] // 2

    @pl.when(step == 0)
    def _():
        forward[...] = jnp.zeros_like(forward)
        backward[...] = jnp.zeros_like(backward)

    hidden, slope = activation(contract(rows_ref[:, :width], in_ref[0], 1, 0))
    grad_hidden = contract(rows_ref[:, width:], out_ref[0], 1, 1).astype(BF16).astype(F32)
    forward[...] += contract(hidden.astype(BF16), out_ref[0], 1, 0)
    backward[...] += contract((grad_hidden * slope).astype(BF16), in_ref[0], 1, 1)

    @pl.when(step == pl.num_programs(0) - 1)
    def _():
        both_ref[:, :width] = forward[...].astype(BF16)
        both_ref[:, width:] = backward[...].astype(BF16)


def run_expert(rows, w_in, w_out, expert, block):
    count, double = rows.shape
    width = double // 2
    units = w_in.shape[2]
    return pl.pallas_call(
        expert_kernel,
        grid=(units // block,),
        in_specs=[
            pl.BlockSpec((count, double), lambda f: (0, 0)),
            pl.BlockSpec((1, width, block), lambda f: (expert, 0, f)),
            pl.BlockSpec((1, block, width), lambda f: (expert, f, 0)),
        ],
        out_specs=pl.BlockSpec((count, double), lambda f: (0, 0)),
        out_shape=jax.ShapeDtypeStruct((count, double), BF16),
        scratch_shapes=[pltpu.VMEM((count, width), F32), pltpu.VMEM((count, width), F32)],
        compiler_params=pltpu.CompilerParams(vmem_limit_bytes=62 << 20),
        cost_estimate=pl.CostEstimate(
            flops=8 * count * width * units, bytes_accessed=4 * width * units, transcendentals=count * units
        ),
        name="expert",
    )(rows, w_in, w_out)


def share_kernel(share_ref, rows_ref, in_ref, out_ref, *refs):
    grad_in_ref, grad_out_ref, flipped, total_in = refs[-4:]
    step = pl.program_id(0)
    width = rows_ref.shape[1] // 2

    @pl.when(step == 0)
    def _():
        flipped[...] = in_ref[0].T
        total_in[...] = jnp.zeros_like(total_in)
        grad_out_ref[...] = jnp.zeros_like(grad_out_ref)

    rows, grads = rows_ref[:, :width], rows_ref[:, width:]
    hidden, slope = activation(contract(flipped[...], rows, 1, 1))
    grad_hidden = contract(out_ref[0], grads, 1, 1).astype(BF16).astype(F32)
    grad_out_ref[0] += contract(hidden.astype(BF16), grads, 1, 0)
    total_in[...] += contract((grad_hidden * slope).astype(BF16), rows, 1, 0)

    @pl.when(step == pl.num_programs(0) - 1)
    def _():
        grad_in_ref[0] = total_in[...].T


def run_share(me, rows, w_in, w_out, expert, total, held, block):
    count, double = rows.shape
    width = double // 2
    own = w_in.shape[0]
    share = w_in.shape[2] // total
    if share % LANES == 0:
        where = jnp.full((1,), me, jnp.int32)
        in_spec = pl.BlockSpec((1, width, share), lambda r, at: (expert, 0, at[0]))
        out_spec = pl.BlockSpec((1, share, width), lambda r, at: (expert, at[0], 0))
    else:
        where = jnp.zeros((1,), jnp.int32)
        w_in = lax.dynamic_slice(w_in, (0, 0, me * share), (own, width, share))
        w_out = lax.dynamic_slice(w_out, (0, me * share, 0), (own, share, width))
        in_spec = pl.BlockSpec((1, width, share), lambda r, at: (expert, 0, 0))
        out_spec = pl.BlockSpec((1, share, width), lambda r, at: (expert, 0, 0))
    held_specs = [pl.BlockSpec(memory_space=pl.ANY)] * len(held)
    return pl.pallas_call(
        share_kernel,
        grid_spec=pltpu.PrefetchScalarGridSpec(
            num_scalar_prefetch=1,
            grid=(count // block,),
            in_specs=[pl.BlockSpec((block, double), lambda r, at: (r, 0)), in_spec, out_spec, *held_specs],
            out_specs=[
                pl.BlockSpec((1, width, share), lambda r, at: (expert, 0, 0)),
                pl.BlockSpec((1, share, width), lambda r, at: (expert, 0, 0)),
            ],
            scratch_shapes=[pltpu.VMEM((share, width), BF16), pltpu.VMEM((share, width), F32)],
        ),
        out_shape=[
            jax.ShapeDtypeStruct((own, width, share), F32),
            jax.ShapeDtypeStruct((own, share, width), F32),
        ],
        input_output_aliases={4 + i: i for i in range(len(held))},
        compiler_params=pltpu.CompilerParams(vmem_limit_bytes=62 << 20),
        cost_estimate=pl.CostEstimate(
            flops=8 * count * width * share, bytes_accessed=2 * count * double, transcendentals=count * share
        ),
        name="share",
    )(where, rows, w_in, w_out, *held)


MESH = pl.DeviceIdType.MESH


def remote(src, dst, send, recv, where):
    copy = pltpu.make_async_remote_copy(src, dst, send, recv, device_id=where, device_id_type=MESH)
    copy.start()
    return copy


def meet(peers):
    barrier = pltpu.get_barrier_semaphore()
    for where in peers:
        pl.semaphore_signal(barrier, inc=1, device_id=where, device_id_type=MESH)
    pl.semaphore_wait(barrier, len(peers))


def far_first(total):
    return sorted(range(1, total), key=lambda k: -min(k, total - k))


def spread_kernel(parts, in_ref, out_ref, send, recv, pass_send, pass_recv, local):
    total = lax.axis_size("seq")
    me = lax.axis_index("seq")
    part = lax.rem(me, parts)
    meet([{"seq": lax.rem(me + k, total)} for k in range(1, total)])
    copies = []
    for k in far_first(total):
        to = lax.rem(me + k, total)
        copies.append(remote(in_ref.at[to], out_ref.at[me, lax.rem(to, parts)], send.at[k - 1], recv.at[k - 1], {"seq": to}))
    own = pltpu.make_async_copy(in_ref.at[me], out_ref.at[me, part], local)
    own.start()
    own.wait()
    passed = []

    def forward(source, k):
        for j in range(1, parts):
            to = me - part + lax.rem(part + j, parts)
            at = (j - 1) * total + k
            block = out_ref.at[source, part]
            passed.append(remote(block, block, pass_send.at[at], pass_recv.at[at], {"seq": to}))

    forward(me, 0)
    for k in far_first(total)[::-1]:
        source = lax.rem(me - k + total, total)
        block = out_ref.at[source, part]
        pltpu.make_async_remote_copy(
            block, block, send.at[k - 1], recv.at[k - 1], device_id={"seq": source}, device_id_type=MESH
        ).wait_recv()
        forward(source, k)
    for copy in copies:
        copy.wait_send()
    for copy in passed:
        copy.wait()


def spread(blocks, parts):
    total, rows, width = blocks.shape
    passes = (parts - 1) * total
    return pl.pallas_call(
        functools.partial(spread_kernel, parts),
        in_specs=[pl.BlockSpec(memory_space=pl.ANY)],
        out_specs=pl.BlockSpec(memory_space=pl.ANY),
        out_shape=jax.ShapeDtypeStruct((total, parts, rows, width), blocks.dtype),
        scratch_shapes=[
            pltpu.SemaphoreType.DMA((total - 1,)),
            pltpu.SemaphoreType.DMA((total - 1,)),
            pltpu.SemaphoreType.DMA((passes,)),
            pltpu.SemaphoreType.DMA((passes,)),
            pltpu.SemaphoreType.DMA,
        ],
        compiler_params=pltpu.CompilerParams(collective_id=0, has_side_effects=True),
        name="spread",
    )(blocks)


def finish_kernel(
    seqs,
    grad_ref,
    late_ref,
    early_ref,
    home_ref,
    late_out,
    early_out,
    near,
    summed,
    wide_got,
    wide_sum,
    far_got,
    early_got,
    mine,
    early_mine,
    near_sems,
    home_sems,
    wide_sems,
    far_sems,
    early_sems,
    last_sems,
    last_early_sems,
    local,
):
    total, across = lax.axis_size("seq"), lax.axis_size("wide")
    parts = total // seqs
    me, row = lax.axis_index("seq"), lax.axis_index("wide")
    part, seq = lax.rem(me, parts), me // parts
    base = me - part

    def part_at(k):
        return base + lax.rem(part + k, parts)

    def seq_at(k):
        return lax.rem(seq + k, seqs) * parts + part

    def row_at(k):
        return lax.rem(row + k, across)

    peers = [{"seq": lax.rem(me + k, total)} for k in range(1, total)]
    peers += [{"wide": row_at(k)} for k in range(1, across)]
    pairs = [(a, b) for a in range(across) for b in range(parts) if a or b]
    peers += [{"wide": row_at(a), "seq": part_at(b)} for a, b in pairs if a and b]
    meet(peers)

    near_copies = [
        remote(
            grad_ref.at[lax.rem(part + k, parts)],
            near.at[k - 1],
            near_sems.at[0, k - 1],
            near_sems.at[1, k - 1],
            {"seq": part_at(k)},
        )
        for k in range(1, parts)
    ]
    wide_copies = [
        remote(late_ref.at[row_at(k)], wide_got.at[k - 1], wide_sems.at[0, k - 1], wide_sems.at[1, k - 1], {"wide": row_at(k)})
        for k in range(1, across)
    ]
    for copy in near_copies:
        copy.wait_recv()
    home_copies = []
    for k in far_first(total) + [0]:
        to = lax.rem(me + k, total)
        value = grad_ref[part, to].astype(F32)
        for j in range(parts - 1):
            value = value + near[j, to].astype(F32)
        summed[to] = value.astype(BF16)
        if k:
            home_copies.append(
                remote(summed.at[to], home_ref.at[me], home_sems.at[0, k - 1], home_sems.at[1, k - 1], {"seq": to})
            )
    own = pltpu.make_async_copy(summed.at[me], home_ref.at[me], local.at[0])
    own.start()
    for copy in wide_copies:
        copy.wait_recv()
    far_copies = []
    for k in list(range(1, seqs)) + [0]:
        at = lax.rem(seq + k, seqs)
        for p in range(parts):
            value = late_ref[row, at, p].astype(F32)
            for j in range(across - 1):
                value = value + wide_got[j, at, p].astype(F32)
            wide_sum[at, p] = value.astype(BF16)
        if k:
            where = {"seq": seq_at(k)}
            far_copies.append(
                remote(wide_sum.at[at], far_got.at[k - 1], far_sems.at[0, k - 1], far_sems.at[1, k - 1], where)
            )
            far_copies.append(
                remote(early_ref.at[at], early_got.at[k - 1], early_sems.at[0, k - 1], early_sems.at[1, k - 1], where)
            )
    for copy in far_copies:
        copy.wait_recv()
    for p in range(parts):
        value = wide_sum[seq, p].astype(F32)
        for j in range(seqs - 1):
            value = value + far_got[j, p].astype(F32)
        mine[p] = value.astype(BF16)
    value = early_ref[seq].astype(F32)
    for j in range(seqs - 1):
        value = value + early_got[j].astype(F32)
    early_mine[...] = value.astype(BF16)
    last = []
    for a, b in pairs:
        at = a * parts + b - 1
        last.append(
            remote(
                mine.at[lax.rem(part + b, parts)],
                late_out.at[row, part],
                last_sems.at[0, at],
                last_sems.at[1, at],
                {"wide": row_at(a), "seq": part_at(b)},
            )
        )
    for k in range(1, across):
        last.append(
            remote(early_mine, early_out.at[row], last_early_sems.at[0, k - 1], last_early_sems.at[1, k - 1], {"wide": row_at(k)})
        )
    own_late = pltpu.make_async_copy(mine.at[part], late_out.at[row, part], local.at[1])
    own_late.start()
    own_early = pltpu.make_async_copy(early_mine, early_out.at[row], local.at[2])
    own_early.start()
    for copy in near_copies + wide_copies + far_copies:
        copy.wait_send()
    for copy in home_copies + last:
        copy.wait()
    own.wait()
    own_late.wait()
    own_early.wait()


def finish(grads, late, early):
    parts, total, rows, width = grads.shape
    across, seqs, _, slim, columns = late.shape
    early_columns = early.shape[2]
    pair = pltpu.SemaphoreType.DMA
    vmem = pl.BlockSpec(memory_space=pltpu.VMEM)
    return pl.pallas_call(
        functools.partial(finish_kernel, seqs),
        in_specs=[vmem, vmem, vmem],
        out_specs=[vmem, vmem, vmem],
        out_shape=[
            jax.ShapeDtypeStruct((total, rows, width), BF16),
            jax.ShapeDtypeStruct((across, parts, slim, columns), BF16),
            jax.ShapeDtypeStruct((across, slim, early_columns), BF16),
        ],
        scratch_shapes=[
            pltpu.VMEM((parts - 1, total, rows, width), BF16),
            pltpu.VMEM((total, rows, width), BF16),
            pltpu.VMEM((across - 1, seqs, parts, slim, columns), BF16),
            pltpu.VMEM((seqs, parts, slim, columns), BF16),
            pltpu.VMEM((seqs - 1, parts, slim, columns), BF16),
            pltpu.VMEM((seqs - 1, slim, early_columns), BF16),
            pltpu.VMEM((parts, slim, columns), BF16),
            pltpu.VMEM((slim, early_columns), BF16),
            pair((2, parts - 1)),
            pair((2, total - 1)),
            pair((2, across - 1)),
            pair((2, seqs - 1)),
            pair((2, seqs - 1)),
            pair((2, across * parts - 1)),
            pair((2, across - 1)),
            pair((3,)),
        ],
        compiler_params=pltpu.CompilerParams(collective_id=1, has_side_effects=True, vmem_limit_bytes=40 << 20),
        cost_estimate=pl.CostEstimate(flops=0, bytes_accessed=100 << 20, transcendentals=0),
        name="finish",
    )(grads, late, early)


def ring_pairs(total, parts, shift):
    return [(i, i - i % parts + (i % parts + shift) % parts) for i in range(total)]


def pick(pieces, index):
    out = pieces[0]
    for k in range(1, len(pieces)):
        out = jnp.where(index == k, pieces[k], out)
    return out


def swap_parts(pieces, part, parts, total):
    near = [pick(pieces, part)]
    for k in range(1, parts):
        near.append(lax.ppermute(pick(pieces, (part + k) % parts), "seq", ring_pairs(total, parts, k)))
    return [pick(near, (part - j) % parts) for j in range(parts)]


def head_groups(heads):
    return [(0, heads - 2), (heads - 2, 2)] if heads % 2 == 0 and heads > 2 else [(0, heads)]


def per_device(
    inputs,
    routes,
    bucket_ids,
    gain_attn,
    w_query,
    w_key,
    w_value,
    w_output,
    rel_table,
    gain_ffn,
    w_router,
    w_in,
    w_out,
    cotangent,
):
    seqs, local_len, width = inputs.shape
    buckets, head_count = rel_table.shape
    size = width // head_count
    total = lax.axis_size("seq")
    across = lax.axis_size("wide")
    length = local_len * total
    parts = total // seqs
    heads = head_count // parts
    cols = heads * size
    me = lax.axis_index("seq")
    part = me % parts
    experts = w_router.shape[1]
    own_experts = w_in.shape[0]
    tokens = seqs * local_len
    capacity = (5 * tokens + 4 * experts - 1) // (4 * experts)
    slots = experts * capacity
    gain_one = gain_attn.astype(F32)
    gain_two = gain_ffn.astype(F32)

    seq_in = spread(inputs.reshape(total, local_len // parts, width), parts).reshape(length, width).astype(F32)
    inv_one = inverse_rms(seq_in)
    normed_one = (seq_in * inv_one * gain_one).astype(BF16)
    own_weights = jnp.concatenate(
        [lax.dynamic_slice(w, (0, part * cols), (width, cols)) for w in (w_query, w_key, w_value)], axis=1
    )
    qkv = contract(own_weights, normed_one, 0, 1).astype(BF16)
    own_table = lax.dynamic_slice(rel_table, (0, part * heads), (buckets, heads))
    ids = jnp.concatenate([bucket_ids, jnp.full((1,), buckets, jnp.int32)])
    bucket_hot = (ids[None, :] == jnp.arange(buckets, dtype=jnp.int32)[:, None]).astype(BF16)
    reverse_hot = (ids[::-1][None, :] == jnp.arange(buckets, dtype=jnp.int32)[:, None]).astype(BF16)
    bias_line = contract(own_table, reverse_hot, 0, 0).reshape(heads, 1, 2 * length)
    block = 256
    groups = head_groups(heads)
    kept, attended = {}, {}
    for first, count in groups[::-1]:
        kept[first] = attend(qkv, bias_line, heads, first, count, size, length, block)
        back = lax.all_to_all(kept[first][0], "seq", 0, 0, tiled=True)
        attended[first] = back.reshape(seqs, parts, count * size, local_len)
    attended = jnp.concatenate([attended[first] for first, _ in groups], axis=2).reshape(seqs, width, local_len)

    flat_in = inputs.reshape(tokens, width).astype(F32)
    middle = flat_in + jnp.einsum("sft,fe->ste", attended, w_output, preferred_element_type=F32).reshape(tokens, width)
    inv_two = inverse_rms(middle)
    normed_two = (middle * inv_two * gain_two).astype(BF16)
    router_probs = jax.nn.softmax(jnp.dot(normed_two, w_router, preferred_element_type=F32), axis=-1)
    chosen = routes.reshape(tokens)
    picked = chosen[:, None] == jnp.arange(experts, dtype=jnp.int32)[None, :]
    order = jnp.arange(tokens, dtype=jnp.int32)
    before = (order[None, :] < order[:, None]).astype(BF16)
    earlier = jnp.dot(before, picked.astype(BF16), preferred_element_type=F32)
    picked = picked.astype(F32)
    rank_in = jnp.sum(earlier * picked, axis=1).astype(jnp.int32)
    place = (chosen % own_experts) * (across * capacity) + (chosen // own_experts) * capacity + rank_in
    slot_of = jnp.where(rank_in < capacity, place, slots)
    slot_hot = (slot_of[:, None] == jnp.arange(slots, dtype=jnp.int32)[None, :]).astype(BF16)
    gate_prob = jnp.sum(router_probs * picked, axis=1)
    upstream = cotangent.reshape(tokens, width).astype(F32)
    weighted = (gate_prob[:, None] * upstream).astype(BF16)
    both = jnp.concatenate([normed_two, weighted], axis=1)
    packed = contract(slot_hot, both, 0, 0).astype(BF16).reshape(own_experts, across, capacity, 2 * width)
    returned, gathered = [], []
    for e in range(own_experts):
        received = lax.all_to_all(packed[e], "wide", 0, 0, tiled=True).reshape(across * capacity, 2 * width)
        gathered.append(lax.all_gather(received, "seq", axis=0, tiled=True))
        pair = run_expert(received, w_in, w_out, e, 512).reshape(across, capacity, 2 * width)
        returned.append(lax.all_to_all(pair, "wide", 0, 0, tiled=True).reshape(across * capacity, 2 * width))
    token_rows = jnp.dot(slot_hot, jnp.concatenate(returned, axis=0), preferred_element_type=F32)
    selected, grad_token = token_rows[:, :width], token_rows[:, width:]
    output = (middle + gate_prob[:, None] * selected).astype(BF16).reshape(inputs.shape)
    grad_gate = jnp.sum(upstream * selected, axis=1)
    grad_logits = (grad_gate[:, None] * router_probs * (picked - gate_prob[:, None])).astype(BF16)
    grad_router = contract(normed_two, grad_logits, 0, 0)
    grad_normed_two = grad_token + contract(grad_logits, w_router, 1, 1)
    grad_mid_norm, grad_gain_two = norm_backward(middle, inv_two, gain_two, grad_normed_two)
    grad_middle = upstream + grad_mid_norm
    grad_branch = grad_middle.astype(BF16).reshape(seqs, local_len, width)
    split_output = w_output.reshape(parts, cols, width)
    grad_outs = {}
    for first, count in groups:
        own = split_output[:, first * size : (first + count) * size]
        grad_att = jnp.einsum("ste,pfe->spft", grad_branch, own, preferred_element_type=F32).astype(BF16)
        grad_outs[first] = lax.all_to_all(grad_att.reshape(total, count * size, local_len), "seq", 0, 0, tiled=True)

    share = width // total
    slim = share // across
    grad_w_output = jnp.einsum("sft,ste->fe", attended, grad_branch, preferred_element_type=F32)
    early = jnp.concatenate(
        [grad_w_output, grad_gain_two[:, None], grad_router, jnp.zeros((width, LANES - 1 - experts), F32)], axis=1
    )
    early = early.astype(BF16).reshape(seqs, parts, share, width + LANES)
    early = swap_parts([early[:, p] for p in range(parts)], part, parts, total)
    early = sum(p.astype(F32) for p in early).astype(BF16)
    early = jnp.swapaxes(early.reshape(seqs, across, slim, width + LANES), 0, 1)
    early = lax.all_to_all(early, "wide", 0, 0, tiled=True)
    early = jnp.sum(early.astype(F32), axis=0).astype(BF16)

    grad_normed_one = 0.0
    own_weights = own_weights.reshape(width, 3, cols)
    late, diagonals = [], []
    for first, count in groups:
        outs, exps, inverse = kept[first]
        three, diagonal = attend_back(
            exps, inverse, grad_outs[first], outs, qkv, heads, first, count, size, length, block
        )
        three = three.reshape(3 * count * size, length)
        diagonals.append(diagonal[:, 0, :])
        own = own_weights[:, :, first * size : (first + count) * size].reshape(width, 3 * count * size)
        grad_normed_one = grad_normed_one + contract(three, own, 0, 1)
        late.append(contract(normed_one, three, 0, 1))
    grad_in_norm, grad_gain_one = norm_backward(seq_in, inv_one, gain_one, grad_normed_one)
    pieces = grad_in_norm.astype(BF16).reshape(total, parts, local_len // parts, width)
    grad_table = jnp.einsum(
        "bo,ho->bh", bucket_hot.astype(F32), jnp.concatenate(diagonals, axis=0), precision=lax.Precision.HIGHEST
    )
    table_full = lax.dynamic_update_slice(jnp.zeros((buckets, head_count), F32), grad_table, (0, part * heads))
    table_rows = jnp.pad(table_full.reshape(total, -1), ((0, 0), (0, share - buckets * head_count // total)))
    small = [grad_gain_one[:, None], table_rows.reshape(width, 1), jnp.zeros((width, LANES - 2), F32)]
    late = jnp.concatenate([*late, *small], axis=1).astype(BF16)
    late = late.reshape(seqs, parts, across, slim, late.shape[1]).transpose(2, 0, 1, 3, 4)
    home, rows, early = finish(jnp.swapaxes(pieces, 0, 1), late, early)
    grad_inputs = (grad_middle + home.reshape(tokens, width).astype(F32)).reshape(inputs.shape)
    rows = [rows[:, p].reshape(share, rows.shape[3]) for p in range(parts)]
    early = early.reshape(share, width + LANES).astype(F32)
    tables, at = [[], [], []], 0
    for _, count in groups:
        for k in range(3):
            tables[k].append((at, at + count * size))
            at += count * size
    total_query, total_key, total_value = (
        jnp.concatenate([r[:, a:b] for r in rows for a, b in tables[k]], axis=1).astype(F32) for k in range(3)
    )
    small = sum(r[:, at : at + LANES].astype(F32) for r in rows)
    total_table = small[: buckets * head_count // total, 1].reshape(buckets // total, head_count)
    total_output, early = early[:, :width], early[:, width:]

    held = []
    for e in range(own_experts):
        held = run_share(me, gathered[e], w_in, w_out, e, total, held, 512)
    return (
        output,
        grad_inputs,
        small[:, 0],
        total_query,
        total_key,
        total_value,
        total_output,
        total_table,
        early[:, 0],
        early[:, 1 : 1 + experts],
        *held,
    )


def solution(mesh):
    in_specs = (
        P("wide", "seq", None),
        P("wide", "seq", None),
        P(),
        P(),
        P(),
        P(),
        P(),
        P(),
        P(),
        P(),
        P(),
        P("wide", None, None),
        P("wide", None, None),
        P("wide", "seq", None),
    )
    out_specs = (
        P("wide", "seq", None),
        P("wide", "seq", None),
        P("seq"),
        P("seq", None),
        P("seq", None),
        P("seq", None),
        P("seq", None),
        P("seq", None),
        P("seq"),
        P("seq", None),
        P("wide", None, "seq"),
        P("wide", "seq", None),
    )
    return jax.shard_map(
        per_device, mesh=mesh, in_specs=in_specs, out_specs=out_specs, check_vma=False
    )
```

```python
import functools

import jax
import jax.numpy as jnp
from jax import lax
from jax.experimental import pallas as pl
from jax.experimental.pallas import tpu as pltpu
from jax.sharding import PartitionSpec as P

EPSILON = 1e-06
F32 = jnp.float32
BF16 = jnp.bfloat16
LANES = 128


def contract(a, b, da, db):
    return lax.dot_general(a, b, (((da,), (db,)), ((), ())), preferred_element_type=F32)


def inverse_rms(source):
    return lax.rsqrt(jnp.mean(source * source, axis=-1, keepdims=True) + EPSILON)


def norm_backward(source, inv_rms, gain_vec, upstream):
    scaled = upstream * gain_vec
    gain_grad = jnp.sum(upstream * source * inv_rms, axis=0)
    mean_inner = jnp.mean(source * scaled, axis=-1, keepdims=True)
    return (inv_rms * scaled - source * (inv_rms * inv_rms * inv_rms) * mean_inner, gain_grad)


def smooth_act(values):
    return jax.nn.gelu(values, approximate=True)


MESH = pl.DeviceIdType.MESH


def remote(src, dst, send, recv, where):
    copy = pltpu.make_async_remote_copy(src, dst, send, recv, device_id=where, device_id_type=MESH)
    copy.start()
    return copy


def meet(peers):
    barrier = pltpu.get_barrier_semaphore()
    for where in peers:
        pl.semaphore_signal(barrier, inc=1, device_id=where, device_id_type=MESH)
    pl.semaphore_wait(barrier, len(peers))


def far_first(total):
    return sorted(range(1, total), key=lambda k: -min(k, total - k))


def twist(a, b, total):
    out, bit = 0, 1
    while bit < total:
        out = out + lax.rem(lax.div(a, bit) + lax.div(b, bit), 2) * bit
        bit *= 2
    return out


def attend_kernel(
    qkv_ref, bias_ref, out_ref, home_ref, exp_ref, inv_ref, strip, keys, scores, held, send, recv, local, exp_sems
):
    _, heads, size, length = qkv_ref.shape
    total = lax.axis_size("seq")
    me = lax.axis_index("seq")
    tokens = out_ref.shape[3]
    width = 2 * tokens
    pairs = total // 2
    rows = 2 * length - tokens
    chunk = 256
    meet([{"seq": lax.rem(me + k, total)} for k in range(1, total)])

    def prepare(h, carry):
        keys[h] = qkv_ref[1, h].T
        for b in range(rows // tokens):
            start = 2 * length - 2 * tokens - tokens * b
            base = jnp.broadcast_to(bias_ref[h, :, start : start + 2 * tokens], (tokens, 2 * tokens))
            rolled = pltpu.roll(base, 0, 1, stride=1, stride_axis=0)
            strip[h, tokens * b : tokens * (b + 1), :] = rolled[:, tokens:]
        return carry

    lax.fori_loop(0, heads, prepare, 0)

    def store(slot, pair, h):
        return pltpu.make_async_copy(held.at[slot], exp_ref.at[pair, h], exp_sems.at[slot])

    def step(t, carry):
        pair = twist(lax.div(me, 2), pairs - 1 - t, pairs)
        at = pl.ds(pl.multiple_of(pair * width, tokens), width)

        def head(h, carry):
            count = t * heads + h
            slot = lax.rem(count, 2)

            @pl.when(count >= 2)
            def _():
                store(slot, pair, h).wait()

            query = qkv_ref[0, h, :, at]
            tops = [jnp.full((1, tokens), -jnp.inf, F32)] * 2
            for c in range(length // chunk):
                part = contract(keys[h, c * chunk : (c + 1) * chunk, :], query, 1, 0)
                for s in range(2):
                    row = pl.multiple_of(length - tokens - (pair * width + s * tokens) + c * chunk, tokens)
                    piece = part[:, s * tokens : (s + 1) * tokens] + strip[h, pl.ds(row, chunk), :]
                    scores[c * chunk : (c + 1) * chunk, s * tokens : (s + 1) * tokens] = piece
                    tops[s] = jnp.maximum(tops[s], jnp.max(piece, axis=0, keepdims=True))
            sums = [jnp.zeros((1, tokens), F32)] * 2
            for c in range(length // chunk):
                for s in range(2):
                    piece = scores[c * chunk : (c + 1) * chunk, s * tokens : (s + 1) * tokens]
                    grown = jnp.exp(piece - tops[s])
                    sums[s] = sums[s] + jnp.sum(grown, axis=0, keepdims=True)
                    held[slot, c * chunk : (c + 1) * chunk, s * tokens : (s + 1) * tokens] = grown.astype(BF16)
            store(slot, pair, h).start()
            mixed = contract(qkv_ref[2, h], held[slot], 1, 0)
            for s in range(2):
                inverse = 1.0 / sums[s]
                inv_ref[pair, h, :, s * tokens : (s + 1) * tokens] = inverse
                out_ref[2 * pair + s, h] = (mixed[:, s * tokens : (s + 1) * tokens] * inverse).astype(BF16)
            return carry

        lax.fori_loop(0, heads, head, 0)
        for s in range(2):
            to = 2 * pair + s
            k = twist(me, to, total)

            @pl.when(to != me)
            def _():
                pltpu.make_async_remote_copy(
                    out_ref.at[to], home_ref.at[me], send.at[k], recv.at[k], device_id={"seq": to}, device_id_type=MESH
                ).start()

        return carry

    lax.fori_loop(0, pairs, step, 0)
    own = pltpu.make_async_copy(out_ref.at[me], home_ref.at[me], local)
    own.start()
    for slot in range(2):
        store(slot, 0, 0).wait()

    def settle(k, carry):
        source = twist(me, k, total)
        pltpu.make_async_remote_copy(
            out_ref.at[source], home_ref.at[source], send.at[k], recv.at[k], device_id={"seq": source}, device_id_type=MESH
        ).wait()
        return carry

    lax.fori_loop(1, total, settle, 0)
    own.wait()


def attend(qkv, bias_line, total):
    _, heads, size, length = qkv.shape
    tokens = length // total
    vmem = pl.BlockSpec(memory_space=pltpu.VMEM)
    return pl.pallas_call(
        attend_kernel,
        in_specs=[vmem, vmem],
        out_specs=[vmem, vmem, pl.BlockSpec(memory_space=pl.ANY), vmem],
        out_shape=[
            jax.ShapeDtypeStruct((total, heads, size, tokens), BF16),
            jax.ShapeDtypeStruct((total, heads, size, tokens), BF16),
            jax.ShapeDtypeStruct((total // 2, heads, length, 2 * tokens), BF16),
            jax.ShapeDtypeStruct((total // 2, heads, 1, 2 * tokens), F32),
        ],
        scratch_shapes=[
            pltpu.VMEM((heads, 2 * length - tokens, tokens), F32),
            pltpu.VMEM((heads, length, size), BF16),
            pltpu.VMEM((length, 2 * tokens), F32),
            pltpu.VMEM((2, length, 2 * tokens), BF16),
            pltpu.SemaphoreType.DMA((total,)),
            pltpu.SemaphoreType.DMA((total,)),
            pltpu.SemaphoreType.DMA,
            pltpu.SemaphoreType.DMA((2,)),
        ],
        compiler_params=pltpu.CompilerParams(collective_id=2, has_side_effects=True, vmem_limit_bytes=62 << 20),
        cost_estimate=pl.CostEstimate(
            flops=4 * heads * length * length * size, bytes_accessed=2 * heads * length * length, transcendentals=heads * length * length
        ),
        name="attend",
    )(qkv, bias_line)


def attend_back_kernel(early, *refs):
    refs = list(refs)
    exp_ref, inv_ref, branch_ref, weight_ref, out_ref, qkv_ref, hot_ref = refs[:7]
    early_ref = refs.pop(7) if early else None
    three_ref, table_ref = refs[7:9]
    early_out = refs.pop(9) if early else None
    leaving, got, strip, values, dq_all, dk_sum, dv_sum, scores, held, diagonal, send, recv, exp_sems = refs[9:22]
    _, heads, size, length = qkv_ref.shape
    total = lax.axis_size("seq")
    me = lax.axis_index("seq")
    tokens = out_ref.shape[3]
    parts = weight_ref.shape[0]
    part = lax.rem(me, parts)
    width = 2 * tokens
    pairs = total // 2
    rows = 2 * length - tokens
    chunk = 256

    def pair_at(t):
        return twist(lax.div(me, 2), t, pairs)

    def load(count):
        slot = lax.rem(count, 2)
        at = exp_ref.at[pair_at(lax.div(count, heads)), lax.rem(count, heads)]
        return pltpu.make_async_copy(at, held.at[slot], exp_sems.at[slot])

    load(0).start()
    peers = [{"seq": lax.rem(me + k, total)} for k in range(1, total)]
    if early:
        across, row = lax.axis_size("wide"), lax.axis_index("wide")
        other = twist(me, 1, total)
        peers += [{"wide": lax.rem(row + k, across)} for k in range(1, across)]
    meet(peers)
    if early:
        near, near_sum, wide_got, near_sems, wide_sems = refs[22:]
        seqs = early_ref.shape[0]

        def near_copy():
            return pltpu.make_async_remote_copy(
                early_ref.at[:, lax.rem(part + 1, parts)],
                near,
                near_sems.at[0],
                near_sems.at[1],
                device_id={"seq": other},
                device_id_type=MESH,
            )

        def wide_copy(k):
            to = lax.rem(row + k, across)
            return pltpu.make_async_remote_copy(
                near_sum.at[to],
                wide_got.at[k - 1],
                wide_sems.at[0, k - 1],
                wide_sems.at[1, k - 1],
                device_id={"wide": to},
                device_id_type=MESH,
            )

        near_copy().start()

    def product(to):
        value = contract(weight_ref[lax.rem(to, parts)], branch_ref[lax.div(to, parts)], 1, 1)
        return value.astype(BF16).reshape(heads, size, tokens)

    def leave(k, carry):
        to = twist(me, k, total)
        leaving[to] = product(to)
        pltpu.make_async_remote_copy(
            leaving.at[to], got.at[me], send.at[k], recv.at[k], device_id={"seq": to}, device_id_type=MESH
        ).start()
        return carry

    lax.fori_loop(1, total, leave, 0)
    got[me] = product(me)

    def prepare(h, carry):
        values[h] = qkv_ref[2, h].T
        strip[h] = jnp.zeros(strip.shape[1:], F32)
        dk_sum[h] = jnp.zeros(dk_sum.shape[1:], F32)
        dv_sum[h] = jnp.zeros(dv_sum.shape[1:], F32)
        return carry

    lax.fori_loop(0, heads, prepare, 0)

    def arrive(k):
        source = twist(me, k, total)
        pltpu.make_async_remote_copy(
            leaving.at[source], got.at[source], send.at[k], recv.at[k], device_id={"seq": source}, device_id_type=MESH
        ).wait()

    def step(t, carry):
        pair = pair_at(t)
        at = pl.ds(pl.multiple_of(pair * width, tokens), width)

        @pl.when(t > 0)
        def _():
            arrive(2 * t)

        arrive(2 * t + 1)
        if early:

            @pl.when(t == 1)
            def _():
                near_copy().wait()
                for n in range(seqs):
                    for a in range(across):
                        value = early_ref[n, part, a].astype(F32) + near[n, a].astype(F32)
                        near_sum[a, n] = value.astype(BF16)
                for k in range(1, across):
                    wide_copy(k).start()

            @pl.when(t == pairs - 1)
            def _():
                for k in range(1, across):
                    wide_copy(k).wait()
                for n in range(seqs):
                    value = near_sum[row, n].astype(F32)
                    for k in range(1, across):
                        value = value + wide_got[k - 1, n].astype(F32)
                    early_out[n] = value.astype(BF16)

        def head(h, carry):
            count = t * heads + h
            slot = lax.rem(count, 2)

            @pl.when(count + 1 < pairs * heads)
            def _():
                load(count + 1).start()

            grads, inner = [], []
            for s in range(2):
                inverse = inv_ref[pair, h, :, s * tokens : (s + 1) * tokens]
                scaled = got[2 * pair + s, h].astype(F32) * inverse
                inner.append(jnp.sum(scaled * out_ref[2 * pair + s, h].astype(F32), axis=0, keepdims=True))
                grads.append(scaled.astype(BF16))
            grad = jnp.concatenate(grads, axis=1)
            load(count).wait()
            for c in range(length // chunk):
                part_grad = contract(values[h, c * chunk : (c + 1) * chunk, :], grad, 1, 0)
                for s in range(2):
                    grown = held[slot, c * chunk : (c + 1) * chunk, s * tokens : (s + 1) * tokens].astype(F32)
                    slope = grown * (part_grad[:, s * tokens : (s + 1) * tokens] - inner[s])
                    line = pl.multiple_of(length - tokens - (pair * width + s * tokens) + c * chunk, tokens)
                    strip[h, pl.ds(line, chunk), :] += slope
                    scores[c * chunk : (c + 1) * chunk, s * tokens : (s + 1) * tokens] = slope.astype(BF16)
            dq_all[h, at, :] = contract(qkv_ref[1, h], scores[...], 1, 0).T.astype(BF16)
            dk_sum[h] += contract(scores[...], qkv_ref[0, h, :, at].T, 1, 0)
            dv_sum[h] += contract(held[slot], grad.T, 1, 0)
            return carry

        lax.fori_loop(0, heads, head, 0)
        return carry

    lax.fori_loop(0, pairs, step, 0)
    down = lax.broadcasted_iota(jnp.int32, (tokens, tokens), 0)
    over = lax.broadcasted_iota(jnp.int32, (tokens, tokens), 1)
    mirror = (down + over == tokens - 1).astype(F32)
    cols = heads * size
    for c in range(length // chunk):
        here = slice(c * chunk, (c + 1) * chunk)
        for n, ref in enumerate((dq_all, dk_sum, dv_sum)):
            joined = jnp.concatenate([ref[h, here, :].astype(F32) for h in range(heads)], axis=1)
            three_ref[here, n * cols : (n + 1) * cols] = joined.astype(BF16)

    def close(h, carry):
        diagonal[h] = jnp.zeros(diagonal.shape[1:], F32)
        for b in range(rows // tokens):
            flipped = lax.dot_general(
                strip[h, tokens * b : tokens * (b + 1), :],
                mirror,
                (((1,), (0,)), ((), ())),
                precision=lax.Precision.HIGHEST,
                preferred_element_type=F32,
            )
            spread_out = jnp.concatenate([flipped, jnp.zeros_like(flipped)], axis=1)
            rolled = pltpu.roll(spread_out, 0, 1, stride=1, stride_axis=0)
            diagonal[h, :, tokens * b : tokens * (b + 2)] += jnp.sum(rolled, axis=0, keepdims=True)
        return carry

    lax.fori_loop(0, heads, close, 0)
    sums = jnp.concatenate([diagonal[h] for h in range(heads)], axis=0)
    table = lax.dot_general(
        hot_ref[...].astype(F32),
        sums,
        (((1,), (1,)), ((), ())),
        precision=lax.Precision.HIGHEST,
        preferred_element_type=F32,
    )
    column = lax.broadcasted_iota(jnp.int32, (heads, LANES), 1)
    first = lax.broadcasted_iota(jnp.int32, (heads, LANES), 0) + part * heads
    table_ref[...] = lax.dot_general(
        table,
        (column == first).astype(F32),
        (((1,), (0,)), ((), ())),
        precision=lax.Precision.HIGHEST,
        preferred_element_type=F32,
    )


def attend_back(exps, inverse, branch, weight, outs, qkv, hot, early):
    _, heads, size, length = qkv.shape
    total, tokens = outs.shape[0], outs.shape[3]
    vmem = pl.BlockSpec(memory_space=pltpu.VMEM)
    sems = pltpu.SemaphoreType.DMA
    out_shape = [
        jax.ShapeDtypeStruct((length, 3 * heads * size), BF16),
        jax.ShapeDtypeStruct((hot.shape[0], LANES), F32),
    ]
    more, given = [], []
    if early is not None:
        seqs, _, across, slim, columns = early.shape
        given = [early]
        out_shape.append(jax.ShapeDtypeStruct((seqs, slim, columns), BF16))
        more = [
            pltpu.VMEM((seqs, across, slim, columns), BF16),
            pltpu.VMEM((across, seqs, slim, columns), BF16),
            pltpu.VMEM((across - 1, seqs, slim, columns), BF16),
            sems((2,)),
            sems((2, across - 1)),
        ]
    return pl.pallas_call(
        functools.partial(attend_back_kernel, early is not None),
        in_specs=[pl.BlockSpec(memory_space=pl.ANY)] + [vmem] * (6 + len(given)),
        out_specs=[vmem] * len(out_shape),
        out_shape=out_shape,
        scratch_shapes=[
            pltpu.VMEM((total, heads, size, tokens), BF16),
            pltpu.VMEM((total, heads, size, tokens), BF16),
            pltpu.VMEM((heads, 2 * length - tokens, tokens), F32),
            pltpu.VMEM((heads, length, size), BF16),
            pltpu.VMEM((heads, length, size), BF16),
            pltpu.VMEM((heads, length, size), F32),
            pltpu.VMEM((heads, length, size), F32),
            pltpu.VMEM((length, 2 * tokens), BF16),
            pltpu.VMEM((2, length, 2 * tokens), BF16),
            pltpu.VMEM((heads, 1, 2 * length), F32),
            sems((total,)),
            sems((total,)),
            sems((2,)),
            *more,
        ],
        compiler_params=pltpu.CompilerParams(collective_id=3, has_side_effects=True, vmem_limit_bytes=62 << 20),
        cost_estimate=pl.CostEstimate(
            flops=8 * heads * length * length * size, bytes_accessed=2 * heads * length * length, transcendentals=0
        ),
        name="attend_back",
    )(exps, inverse, branch, weight, outs, qkv, hot, *given)


def activation(v):
    square = v * v
    bent = jnp.tanh(0.7978845608 * v * (1.0 + 0.044715 * square))
    half = 0.5 * (1.0 + bent)
    slope = half + 0.5 * v * (1.0 - bent * bent) * (0.7978845608 * (1.0 + 3.0 * 0.044715 * square))
    return v * half, slope


def gated(rows, cots):
    width = cots.shape[1]
    gate = rows[:, width : width + 1].astype(F32) + rows[:, width + 1 : width + 2].astype(F32)
    return rows[:, :width], (gate * cots.astype(F32)).astype(BF16)


def expert_kernel(rows_ref, cot_ref, in_ref, out_ref, both_ref, forward, backward):
    step = pl.program_id(0)
    width = cot_ref.shape[1]

    @pl.when(step == 0)
    def _():
        forward[...] = jnp.zeros_like(forward)
        backward[...] = jnp.zeros_like(backward)

    rows, grads = gated(rows_ref[...], cot_ref[...])
    hidden, slope = activation(contract(rows, in_ref[0], 1, 0))
    grad_hidden = contract(grads, out_ref[0], 1, 1).astype(BF16).astype(F32)
    forward[...] += contract(hidden.astype(BF16), out_ref[0], 1, 0)
    backward[...] += contract((grad_hidden * slope).astype(BF16), in_ref[0], 1, 1)

    @pl.when(step == pl.num_programs(0) - 1)
    def _():
        both_ref[:, :width] = forward[...].astype(BF16)
        both_ref[:, width:] = backward[...].astype(BF16)


def run_expert(rows, cots, w_in, w_out, expert, block):
    count, width = cots.shape
    units = w_in.shape[2]
    return pl.pallas_call(
        expert_kernel,
        grid=(units // block,),
        in_specs=[
            pl.BlockSpec(rows.shape, lambda f: (0, 0)),
            pl.BlockSpec(cots.shape, lambda f: (0, 0)),
            pl.BlockSpec((1, width, block), lambda f: (expert, 0, f)),
            pl.BlockSpec((1, block, width), lambda f: (expert, f, 0)),
        ],
        out_specs=pl.BlockSpec((count, 2 * width), lambda f: (0, 0)),
        out_shape=jax.ShapeDtypeStruct((count, 2 * width), BF16),
        scratch_shapes=[pltpu.VMEM((count, width), F32), pltpu.VMEM((count, width), F32)],
        compiler_params=pltpu.CompilerParams(vmem_limit_bytes=40 << 20),
        name="expert",
    )(rows, cots, w_in, w_out)


def exchange_kernel(axis, in_ref, out_ref, send, recv, local):
    total = lax.axis_size(axis)
    me = lax.axis_index(axis)
    own = in_ref.shape[0]
    count = in_ref.shape[1] // total
    meet([{axis: lax.rem(me + k, total)} for k in range(1, total)])
    copies = []
    mine = pl.ds(me * count, count)
    for n in range(own):
        for k in range(1, total):
            to = lax.rem(me + k, total)
            copies.append(
                remote(
                    in_ref.at[n, pl.ds(to * count, count)],
                    out_ref.at[n, mine],
                    send.at[n, k - 1],
                    recv.at[n, k - 1],
                    {axis: to},
                )
            )
    kept = [pltpu.make_async_copy(in_ref.at[n, mine], out_ref.at[n, mine], local.at[n]) for n in range(own)]
    for copy in kept:
        copy.start()
    for copy in kept + copies:
        copy.wait()


def exchange(rows, axis):
    total = lax.axis_size(axis)
    own = rows.shape[0]
    vmem = pl.BlockSpec(memory_space=pltpu.VMEM)
    return pl.pallas_call(
        functools.partial(exchange_kernel, axis),
        in_specs=[vmem],
        out_specs=pl.BlockSpec(memory_space=pl.ANY),
        out_shape=jax.ShapeDtypeStruct(rows.shape, rows.dtype),
        scratch_shapes=[
            pltpu.SemaphoreType.DMA((own, total - 1)),
            pltpu.SemaphoreType.DMA((own, total - 1)),
            pltpu.SemaphoreType.DMA((own,)),
        ],
        compiler_params=pltpu.CompilerParams(collective_id=4, has_side_effects=True, vmem_limit_bytes=62 << 20),
        name="exchange",
    )(rows)


def experts_kernel(
    block,
    rows_ref,
    cot_ref,
    in_ref,
    out_ref,
    back_ref,
    done,
    grads,
    forward,
    backward,
    in_held,
    out_held,
    back_send,
    back_recv,
    local,
    held_sems,
):
    own, rows, double = back_ref.shape
    width = double // 2
    across = lax.axis_size("wide")
    me = lax.axis_index("wide")
    count = rows // across
    steps = in_ref.shape[2] // block

    def load(at):
        slot = lax.rem(at, 2)
        expert, place = lax.div(at, steps), pl.multiple_of(lax.rem(at, steps) * block, block)
        return (
            pltpu.make_async_copy(in_ref.at[expert, :, pl.ds(place, block)], in_held.at[slot], held_sems.at[0, slot]),
            pltpu.make_async_copy(out_ref.at[expert, pl.ds(place, block), :], out_held.at[slot], held_sems.at[1, slot]),
        )

    for copy in load(0):
        copy.start()
    meet([{"wide": lax.rem(me + k, across)} for k in range(1, across)])
    coming = []
    mine = pl.ds(me * count, count)
    for e in range(own):
        grads[...] = gated(rows_ref[e], cot_ref[e])[1]
        forward[...] = jnp.zeros_like(forward)
        backward[...] = jnp.zeros_like(backward)

        def step(f, carry):
            at = e * steps + f
            slot = lax.rem(at, 2)

            @pl.when(at + 1 < own * steps)
            def _():
                for copy in load(at + 1):
                    copy.start()

            for copy in load(at):
                copy.wait()
            hidden, slope = activation(contract(rows_ref[e, :, :width], in_held[slot], 1, 0))
            grad_hidden = contract(grads[...], out_held[slot], 1, 1).astype(BF16).astype(F32)
            forward[...] += contract(hidden.astype(BF16), out_held[slot], 1, 0)
            backward[...] += contract((grad_hidden * slope).astype(BF16), in_held[slot], 1, 1)
            return carry

        lax.fori_loop(0, steps, step, 0)
        done[e, :, :width] = forward[...].astype(BF16)
        done[e, :, width:] = backward[...].astype(BF16)
        for k in range(1, across):
            to = lax.rem(me + k, across)
            coming.append(
                remote(
                    done.at[e, pl.ds(to * count, count)],
                    back_ref.at[e, mine],
                    back_send.at[e, k - 1],
                    back_recv.at[e, k - 1],
                    {"wide": to},
                )
            )
        kept = pltpu.make_async_copy(done.at[e, mine], back_ref.at[e, mine], local.at[e])
        kept.start()
        kept.wait()
    for copy in coming:
        copy.wait()


def run_experts(rows, cots, w_in, w_out, block):
    own, count, width = cots.shape
    units = w_in.shape[2]
    across = lax.axis_size("wide")
    vmem, hbm = pl.BlockSpec(memory_space=pltpu.VMEM), pl.BlockSpec(memory_space=pl.ANY)
    sems = pltpu.SemaphoreType.DMA
    return pl.pallas_call(
        functools.partial(experts_kernel, block),
        in_specs=[vmem, vmem, hbm, hbm],
        out_specs=vmem,
        out_shape=jax.ShapeDtypeStruct((own, count, 2 * width), BF16),
        scratch_shapes=[
            pltpu.VMEM((own, count, 2 * width), BF16),
            pltpu.VMEM((count, width), BF16),
            pltpu.VMEM((count, width), F32),
            pltpu.VMEM((count, width), F32),
            pltpu.VMEM((2, width, block), BF16),
            pltpu.VMEM((2, block, width), BF16),
            sems((own, across - 1)),
            sems((own, across - 1)),
            sems((own,)),
            sems((2, 2)),
        ],
        compiler_params=pltpu.CompilerParams(collective_id=5, has_side_effects=True, vmem_limit_bytes=62 << 20),
        cost_estimate=pl.CostEstimate(
            flops=8 * own * count * width * units, bytes_accessed=4 * own * width * units, transcendentals=own * count * units
        ),
        name="experts",
    )(rows, cots, w_in, w_out)


def share_kernel(share_ref, rows_ref, cot_ref, in_ref, out_ref, *refs):
    grad_in_ref, grad_out_ref, flipped, total_in = refs[-4:]
    step = pl.program_id(0)

    @pl.when(step == 0)
    def _():
        flipped[...] = in_ref[0].T
        total_in[...] = jnp.zeros_like(total_in)
        grad_out_ref[...] = jnp.zeros_like(grad_out_ref)

    rows, grads = gated(rows_ref[0], cot_ref[0])
    hidden, slope = activation(contract(flipped[...], rows, 1, 1))
    grad_hidden = contract(out_ref[0], grads, 1, 1).astype(BF16).astype(F32)
    grad_out_ref[0] += contract(hidden.astype(BF16), grads, 1, 0)
    total_in[...] += contract((grad_hidden * slope).astype(BF16), rows, 1, 0)

    @pl.when(step == pl.num_programs(0) - 1)
    def _():
        grad_in_ref[0] = total_in[...].T


def run_share(me, rows, cots, w_in, w_out, expert, held):
    own, width, units = w_in.shape
    sources, count = rows.shape[0] // own, rows.shape[1]
    share = units // sources
    if share % LANES == 0:
        where = jnp.full((1,), me, jnp.int32)
        in_spec = pl.BlockSpec((1, width, share), lambda r, at: (expert, 0, at[0]))
        out_spec = pl.BlockSpec((1, share, width), lambda r, at: (expert, at[0], 0))
    else:
        where = jnp.zeros((1,), jnp.int32)
        w_in = lax.dynamic_slice(w_in, (0, 0, me * share), (own, width, share))
        w_out = lax.dynamic_slice(w_out, (0, me * share, 0), (own, share, width))
        in_spec = pl.BlockSpec((1, width, share), lambda r, at: (expert, 0, 0))
        out_spec = pl.BlockSpec((1, share, width), lambda r, at: (expert, 0, 0))
    held_specs = [pl.BlockSpec(memory_space=pl.ANY)] * len(held)
    return pl.pallas_call(
        share_kernel,
        grid_spec=pltpu.PrefetchScalarGridSpec(
            num_scalar_prefetch=1,
            grid=(sources,),
            in_specs=[
                pl.BlockSpec((1, count, rows.shape[2]), lambda r, at: (own * r + expert, 0, 0)),
                pl.BlockSpec((1, count, width), lambda r, at: (own * r + expert, 0, 0)),
                in_spec,
                out_spec,
                *held_specs,
            ],
            out_specs=[
                pl.BlockSpec((1, width, share), lambda r, at: (expert, 0, 0)),
                pl.BlockSpec((1, share, width), lambda r, at: (expert, 0, 0)),
            ],
            scratch_shapes=[pltpu.VMEM((share, width), BF16), pltpu.VMEM((share, width), F32)],
        ),
        out_shape=[
            jax.ShapeDtypeStruct((own, width, share), F32),
            jax.ShapeDtypeStruct((own, share, width), F32),
        ],
        input_output_aliases={5 + i: i for i in range(len(held))},
        compiler_params=pltpu.CompilerParams(vmem_limit_bytes=62 << 20),
        cost_estimate=pl.CostEstimate(
            flops=8 * sources * count * width * share, bytes_accessed=4 * sources * count * width, transcendentals=0
        ),
        name="share",
    )(where, rows, cots, w_in, w_out, *held)


def spread_kernel(parts, in_ref, out_ref, send, recv, pass_send, pass_recv, local):
    total = lax.axis_size("seq")
    me = lax.axis_index("seq")
    part = lax.rem(me, parts)
    meet([{"seq": lax.rem(me + k, total)} for k in range(1, total)])
    copies = []
    for k in far_first(total):
        to = lax.rem(me + k, total)
        copies.append(remote(in_ref.at[to], out_ref.at[me, lax.rem(to, parts)], send.at[k - 1], recv.at[k - 1], {"seq": to}))
    own = pltpu.make_async_copy(in_ref.at[me], out_ref.at[me, part], local)
    own.start()
    own.wait()
    passed = []

    def forward(source, k):
        for j in range(1, parts):
            to = me - part + lax.rem(part + j, parts)
            at = (j - 1) * total + k
            block = out_ref.at[source, part]
            passed.append(remote(block, block, pass_send.at[at], pass_recv.at[at], {"seq": to}))

    forward(me, 0)
    for k in far_first(total)[::-1]:
        source = lax.rem(me - k + total, total)
        block = out_ref.at[source, part]
        pltpu.make_async_remote_copy(
            block, block, send.at[k - 1], recv.at[k - 1], device_id={"seq": source}, device_id_type=MESH
        ).wait_recv()
        forward(source, k)
    for copy in copies:
        copy.wait_send()
    for copy in passed:
        copy.wait()


def spread(blocks, parts):
    total, rows, width = blocks.shape
    passes = (parts - 1) * total
    return pl.pallas_call(
        functools.partial(spread_kernel, parts),
        in_specs=[pl.BlockSpec(memory_space=pl.ANY)],
        out_specs=pl.BlockSpec(memory_space=pl.ANY),
        out_shape=jax.ShapeDtypeStruct((total, parts, rows, width), blocks.dtype),
        scratch_shapes=[
            pltpu.SemaphoreType.DMA((total - 1,)),
            pltpu.SemaphoreType.DMA((total - 1,)),
            pltpu.SemaphoreType.DMA((passes,)),
            pltpu.SemaphoreType.DMA((passes,)),
            pltpu.SemaphoreType.DMA,
        ],
        compiler_params=pltpu.CompilerParams(collective_id=0, has_side_effects=True),
        name="spread",
    )(blocks)


def begin_kernel(
    capacity,
    in_ref,
    query_ref,
    key_ref,
    value_ref,
    gain_ref,
    routes_ref,
    base_ref,
    cot_ref,
    all_ref,
    qkv_ref,
    flip_ref,
    hot_ref,
    rows_ref,
    weights,
    packed,
    send,
    recv,
    pass_send,
    pass_recv,
    wide_send,
    wide_recv,
    local,
):
    total, parts, rows, width = all_ref.shape
    _, heads, size, _ = qkv_ref.shape
    own = rows_ref.shape[0]
    cols = heads * size
    across = lax.axis_size("wide")
    me, row = lax.axis_index("seq"), lax.axis_index("wide")
    part = lax.rem(me, parts)
    other = twist(me, 1, total)
    pairs = total // 2
    peers = [{"seq": lax.rem(me + k, total)} for k in range(1, total)]
    peers += [{"wide": lax.rem(row + k, across)} for k in range(1, across)]
    meet(peers)
    sent = []
    for k in range(total - 1, 0, -1):
        to = twist(me, k, total)
        sent.append(remote(in_ref.at[to], all_ref.at[me, lax.rem(to, parts)], send.at[to], recv.at[me], {"seq": to}))
    kept = pltpu.make_async_copy(in_ref.at[me], all_ref.at[me, part], local.at[0])
    kept.start()
    kept.wait()
    passed = []

    def forward(source):
        block = all_ref.at[source, part]
        passed.append(remote(block, block, pass_send.at[source], pass_recv.at[source], {"seq": other}))

    def await_recv(block, sem):
        pltpu.make_async_remote_copy(
            block, block, local.at[1], sem, device_id={"seq": other}, device_id_type=MESH
        ).wait_recv()

    forward(me)

    tokens, slots = hot_ref.shape
    picked = (routes_ref[...] == lax.broadcasted_iota(jnp.int32, (tokens, LANES), 1)).astype(F32)
    down = lax.broadcasted_iota(jnp.int32, (tokens, tokens), 0)
    over = lax.broadcasted_iota(jnp.int32, (tokens, tokens), 1)
    earlier = contract((over < down).astype(F32).astype(BF16), picked.astype(BF16), 1, 0)
    rank = jnp.sum(earlier * picked, axis=1, keepdims=True)
    place = jnp.sum(base_ref[...] * picked, axis=1, keepdims=True) + rank
    place = jnp.where(rank < capacity, place, float(slots)).astype(jnp.int32)
    hot = (place == lax.broadcasted_iota(jnp.int32, (tokens, slots), 1)).astype(F32).astype(BF16)
    hot_ref[...] = hot
    packed[...] = contract(hot, cot_ref[...], 0, 0).astype(BF16).reshape(packed.shape)
    wide = []
    mine = pl.ds(row * capacity, capacity)
    for e in range(own):
        for k in range(1, across):
            to = lax.rem(row + k, across)
            wide.append(
                remote(
                    packed.at[e, pl.ds(to * capacity, capacity)],
                    rows_ref.at[e, mine],
                    wide_send.at[e, k - 1],
                    wide_recv.at[e, k - 1],
                    {"wide": to},
                )
            )
    stay = [pltpu.make_async_copy(packed.at[e, mine], rows_ref.at[e, mine], local.at[2 + e]) for e in range(own)]
    for copy in stay:
        copy.start()
    at = pl.ds(pl.multiple_of(part * cols, LANES), cols)
    for n, ref in enumerate((query_ref, key_ref, value_ref)):
        weights[n * cols : (n + 1) * cols, :] = ref[:, at].T

    for t in range(pairs):
        pair = twist(lax.div(me, 2), t, pairs)
        for b in range(2):
            if 2 * t + b:
                source = twist(me, 2 * t + b, total)
                await_recv(all_ref.at[source, part], recv.at[source])
                forward(source)
        for b in range(2):
            source = 2 * pair + b
            await_recv(all_ref.at[source, lax.rem(part + 1, parts)], pass_recv.at[source])
        block = all_ref[pl.ds(2 * pair, 2)].reshape(2 * parts * rows, width).astype(F32)
        normed = (block * inverse_rms(block) * gain_ref[...]).astype(BF16)
        here = pl.ds(pl.multiple_of(pair * (2 * parts * rows), LANES), 2 * parts * rows)
        flip_ref[:, here] = normed.T
        projected = contract(weights[...], normed, 1, 1).astype(BF16)
        qkv_ref[:, :, :, here] = projected.reshape(3, heads, size, 2 * parts * rows)
    for copy in sent + passed:
        copy.wait_send()
    for copy in wide + stay:
        copy.wait()


def begin(blocks, w_query, w_key, w_value, gain, routes, base, cot, heads, size, own, capacity):
    total, rows, width = blocks.shape
    tokens = cot.shape[0]
    across = lax.axis_size("wide")
    slots = own * across * capacity
    length = total * 2 * rows
    vmem = pl.BlockSpec(memory_space=pltpu.VMEM)
    sems = pltpu.SemaphoreType.DMA
    return pl.pallas_call(
        functools.partial(begin_kernel, capacity),
        in_specs=[vmem] * 8,
        out_specs=[vmem] * 5,
        out_shape=[
            jax.ShapeDtypeStruct((total, 2, rows, width), BF16),
            jax.ShapeDtypeStruct((3, heads, size, length), BF16),
            jax.ShapeDtypeStruct((width, length), BF16),
            jax.ShapeDtypeStruct((tokens, slots), BF16),
            jax.ShapeDtypeStruct((own, across * capacity, width), BF16),
        ],
        scratch_shapes=[
            pltpu.VMEM((3 * heads * size, width), BF16),
            pltpu.VMEM((own, across * capacity, width), BF16),
            sems((total,)),
            sems((total,)),
            sems((total,)),
            sems((total,)),
            sems((own, across - 1)),
            sems((own, across - 1)),
            sems((2 + own,)),
        ],
        compiler_params=pltpu.CompilerParams(collective_id=6, has_side_effects=True, vmem_limit_bytes=62 << 20),
        cost_estimate=pl.CostEstimate(flops=4 << 30, bytes_accessed=80 << 20, transcendentals=0),
        name="begin",
    )(blocks, w_query, w_key, w_value, gain, routes, base, cot)


def finish_kernel(
    seqs,
    three_ref,
    flip_ref,
    weight_ref,
    x_ref,
    gain_ref,
    early_ref,
    tiny_ref,
    table_ref,
    rows_ref,
    cots_ref,
    in_ref,
    out_ref,
    home_ref,
    query_out,
    key_out,
    value_out,
    output_out,
    tiny_out,
    table_out,
    grad_in_ref,
    grad_out_ref,
    grads,
    near,
    summed,
    gw,
    wide_got,
    wide_sum,
    far_got,
    early_got,
    mine,
    early_mine,
    late_all,
    early_all,
    tiny,
    tiny_got,
    table,
    table_got,
    rows_held,
    cots_held,
    in_held,
    out_held,
    sums,
    total_in,
    leaving,
    share_got,
    share_sems,
    near_sems,
    home_sems,
    wide_sems,
    far_sems,
    early_sems,
    last_sems,
    last_early_sems,
    tiny_sems,
    table_sems,
    held_sems,
    local,
):
    total, across = lax.axis_size("seq"), lax.axis_size("wide")
    parts = total // seqs
    me, row = lax.axis_index("seq"), lax.axis_index("wide")
    part, seq = lax.rem(me, parts), lax.div(me, parts)
    other = twist(me, 1, total)
    width = gain_ref.shape[1]
    slim = gw.shape[2]
    own = in_ref.shape[0]
    share = in_ref.shape[2] // total
    cols = three_ref.shape[1] // 3
    half = three_ref.shape[0] // 2

    def seq_at(k):
        return lax.rem(seq + k, seqs) * parts + part

    def row_at(k):
        return lax.rem(row + k, across)

    def part_at(k):
        return me - part + lax.rem(part + k, parts)

    at = pl.ds(pl.multiple_of(lax.div(me, 2) * (2 * share), LANES), 2 * share)
    weights = [
        pltpu.make_async_copy(in_ref.at[:, :, at], in_held, local.at[0]),
        pltpu.make_async_copy(out_ref.at[:, at, :], out_held, local.at[1]),
    ]
    for copy in weights:
        copy.start()

    def load(e):
        return (
            pltpu.make_async_copy(rows_ref.at[:, e], rows_held.at[e], held_sems.at[0, e]),
            pltpu.make_async_copy(cots_ref.at[:, e], cots_held.at[e], held_sems.at[1, e]),
        )

    for e in range(own):
        for copy in load(e):
            copy.start()

    pairs = [(a, b) for a in range(across) for b in range(parts) if a or b]
    peers = [{"seq": lax.rem(me + k, total)} for k in range(1, total)]
    peers += [{"wide": row_at(k)} for k in range(1, across)]
    peers += [{"wide": row_at(a), "seq": part_at(b)} for a, b in pairs if a and b]
    meet(peers)

    late = contract(flip_ref[...], three_ref[...], 1, 0).astype(BF16)
    gw[...] = late.reshape(gw.shape)
    wide_copies = [
        remote(gw.at[:, row_at(k)], wide_got.at[k - 1], wide_sems.at[0, k - 1], wide_sems.at[1, k - 1], {"wide": row_at(k)})
        for k in range(1, across)
    ]

    gain = gain_ref[...]
    gain_grad = jnp.zeros((1, width), F32)
    near_copies = []
    for n in range(2):
        scaled = contract(three_ref[n * half : (n + 1) * half, :], weight_ref[...], 1, 1)
        x = x_ref[n * total // 2 : (n + 1) * total // 2].reshape(half, width).astype(F32)
        inverse = inverse_rms(x)
        gain_grad = gain_grad + jnp.sum(scaled * x * inverse, axis=0, keepdims=True)
        scaled = scaled * gain
        mean_inner = jnp.mean(x * scaled, axis=-1, keepdims=True)
        value = inverse * scaled - x * (inverse * inverse * inverse) * mean_inner
        here = pl.ds(n * total // 2, total // 2)
        grads[here] = value.astype(BF16).reshape(total // 2, *grads.shape[1:])
        near_copies.append(
            remote(
                grads.at[here, lax.rem(part + 1, parts)],
                near.at[here],
                near_sems.at[0, n],
                near_sems.at[1, n],
                {"seq": other},
            )
        )
    first = lax.broadcasted_iota(jnp.int32, tiny_ref.shape, 0) == 0
    tiny[...] = jnp.where(first, gain_grad, tiny_ref[...]).astype(BF16)
    table[...] = table_ref[...].astype(BF16)

    def pass_tiny(stage, wheres):
        copies = []
        for n, where in enumerate(wheres):
            for src, dst, sem in ((tiny, tiny_got, tiny_sems), (table, table_got, table_sems)):
                copies.append(remote(src, dst.at[stage, n], sem.at[0, stage, n], sem.at[1, stage, n], where))
        return copies

    def take_tiny(stage, copies):
        for copy in copies:
            copy.wait()
        for src, dst in ((tiny, tiny_got), (table, table_got)):
            value = src[...].astype(F32)
            for n in range(len(copies) // 2):
                value = value + dst[stage, n].astype(F32)
            src[...] = value.astype(BF16)

    tiny_copies = pass_tiny(0, [{"wide": row_at(k)} for k in range(1, across)])
    for copy in near_copies:
        copy.wait()
    home_copies = []
    for k in range(total - 1, -1, -1):
        to = twist(me, k, total)
        summed[to] = (grads[to, part].astype(F32) + near[to].astype(F32)).astype(BF16)
        if k:
            home_copies.append(
                remote(summed.at[to], home_ref.at[me], home_sems.at[0, k - 1], home_sems.at[1, k - 1], {"seq": to})
            )
    kept = pltpu.make_async_copy(summed.at[me], home_ref.at[me], local.at[2])
    kept.start()
    for copy in weights:
        copy.wait()

    mine_rows = pl.ds(pl.multiple_of(part * share, LANES), share)
    other_rows = pl.ds(pl.multiple_of((1 - part) * share, LANES), share)

    def share_turn(e, n):
        if n == 0:
            for copy in load(e):
                copy.wait()
        some = rows_held.shape[1] // 2
        count = some * rows_held.shape[2]
        here = slice(n * some, (n + 1) * some)
        rows, cots = gated(rows_held[e, here].reshape(count, -1), cots_held[e, here].reshape(count, width))
        hidden, slope = activation(contract(in_held[e].T, rows, 1, 1))
        grad_hidden = contract(out_held[e], cots, 1, 1).astype(BF16).astype(F32)
        part_out = contract(hidden.astype(BF16), cots, 1, 0)
        part_in = contract((grad_hidden * slope).astype(BF16), rows, 1, 0)
        if n == 0:
            sums[0] = part_out
            sums[1] = part_in
            return []
        sums[0] += part_out
        sums[1] += part_in
        grad_out_ref[e] = sums[0, mine_rows, :]
        total_in[e] = sums[1, mine_rows, :]
        copies = []
        for k in range(2):
            leaving[e, k] = sums[k, other_rows, :].astype(BF16)
            copies.append(
                remote(leaving.at[e, k], share_got.at[e, k], share_sems.at[0, e, k], share_sems.at[1, e, k], {"seq": other})
            )
        return copies

    def share_end(e, copies):
        for copy in copies:
            copy.wait()
        grad_out_ref[e] += share_got[e, 0].astype(F32)
        grad_in_ref[e] = (total_in[e] + share_got[e, 1].astype(F32)).T

    share_turn(0, 0)
    first_share = share_turn(0, 1)
    take_tiny(0, tiny_copies)
    for copy in wide_copies:
        copy.wait_recv()
    far_copies = []
    for k in list(range(1, seqs)) + [0]:
        place = lax.rem(seq + k, seqs)
        for p in range(parts):
            block = place * parts + p
            value = gw[block, row].astype(F32)
            for j in range(across - 1):
                value = value + wide_got[j, block].astype(F32)
            wide_sum[place, p] = value.astype(BF16)
        if k:
            where = {"seq": seq_at(k)}
            far_copies.append(
                remote(wide_sum.at[place], far_got.at[k - 1], far_sems.at[0, k - 1], far_sems.at[1, k - 1], where)
            )
            far_copies.append(
                remote(early_ref.at[place], early_got.at[k - 1], early_sems.at[0, k - 1], early_sems.at[1, k - 1], where)
            )
    tiny_copies = pass_tiny(1, [{"seq": seq_at(k)} for k in range(1, seqs)])
    share_turn(1, 0)
    share_end(0, first_share)
    take_tiny(1, tiny_copies)
    for copy in far_copies:
        copy.wait_recv()
    for p in range(parts):
        value = wide_sum[seq, p].astype(F32)
        for j in range(seqs - 1):
            value = value + far_got[j, p].astype(F32)
        mine[p] = value.astype(BF16)
    value = early_ref[seq].astype(F32)
    for j in range(seqs - 1):
        value = value + early_got[j].astype(F32)
    early_mine[...] = value.astype(BF16)
    last = pass_tiny(2, [{"seq": part_at(k)} for k in range(1, parts)])
    count = len(last)
    for a, b in pairs:
        n = a * parts + b - 1
        last.append(
            remote(
                mine.at[lax.rem(part + b, parts)],
                late_all.at[row, part],
                last_sems.at[0, n],
                last_sems.at[1, n],
                {"wide": row_at(a), "seq": part_at(b)},
            )
        )
    for k in range(1, across):
        last.append(
            remote(
                early_mine, early_all.at[row], last_early_sems.at[0, k - 1], last_early_sems.at[1, k - 1], {"wide": row_at(k)}
            )
        )
    stay = [
        pltpu.make_async_copy(mine.at[part], late_all.at[row, part], local.at[3]),
        pltpu.make_async_copy(early_mine, early_all.at[row], local.at[4]),
    ]
    for copy in stay:
        copy.start()
    second_share = share_turn(1, 1)
    take_tiny(2, last[:count])
    share_end(1, second_share)
    for copy in last[count:] + stay + home_copies + [kept]:
        copy.wait()
    for copy in wide_copies + far_copies:
        copy.wait_send()
    for a in range(across):
        here = slice(a * slim, (a + 1) * slim)
        for p in range(parts):
            for n, ref in enumerate((query_out, key_out, value_out)):
                ref[here, p * cols : (p + 1) * cols] = late_all[a, p, :, n * cols : (n + 1) * cols].astype(F32)
        output_out[here, :] = early_all[a].astype(F32)
    piece = tiny_out.shape[1]
    chosen = lax.broadcasted_iota(jnp.int32, (width, piece), 0) == (
        lax.broadcasted_iota(jnp.int32, (width, piece), 1) + me * piece
    )
    tiny_out[...] = contract(tiny[...], chosen.astype(F32).astype(BF16), 1, 0)
    lines = table_out.shape[0]
    chosen = lax.broadcasted_iota(jnp.int32, (lines, table.shape[0]), 1) == (
        lax.broadcasted_iota(jnp.int32, (lines, table.shape[0]), 0) + me * lines
    )
    table_out[...] = contract(chosen.astype(F32).astype(BF16), table[...], 1, 0)


def finish(three, flipped, weights, x, gain, early, tiny, table, rows, cots, w_in, w_out):
    length, columns = three.shape
    total, parts, piece, width = x.shape
    seqs, slim, _ = early.shape
    across = lax.axis_size("wide")
    own, _, units = w_in.shape
    share, part = units // total, width // total
    vmem, hbm = pl.BlockSpec(memory_space=pltpu.VMEM), pl.BlockSpec(memory_space=pl.ANY)
    sems = pltpu.SemaphoreType.DMA
    most = max(across, seqs, parts) - 1
    return pl.pallas_call(
        functools.partial(finish_kernel, seqs),
        in_specs=[vmem] * 8 + [hbm] * 4,
        out_specs=[vmem] * 9,
        out_shape=[
            jax.ShapeDtypeStruct((total, piece, width), BF16),
            *[jax.ShapeDtypeStruct((part, width), F32)] * 4,
            jax.ShapeDtypeStruct((tiny.shape[0], part), F32),
            jax.ShapeDtypeStruct((table.shape[0] // total, LANES), F32),
            jax.ShapeDtypeStruct((own, width, share), F32),
            jax.ShapeDtypeStruct((own, share, width), F32),
        ],
        scratch_shapes=[
            pltpu.VMEM((total, parts, piece, width), BF16),
            pltpu.VMEM((total, piece, width), BF16),
            pltpu.VMEM((total, piece, width), BF16),
            pltpu.VMEM((total, across, slim, columns), BF16),
            pltpu.VMEM((across - 1, total, slim, columns), BF16),
            pltpu.VMEM((seqs, parts, slim, columns), BF16),
            pltpu.VMEM((seqs - 1, parts, slim, columns), BF16),
            pltpu.VMEM((seqs - 1, slim, width), BF16),
            pltpu.VMEM((parts, slim, columns), BF16),
            pltpu.VMEM((slim, width), BF16),
            pltpu.VMEM((across, parts, slim, columns), BF16),
            pltpu.VMEM((across, slim, width), BF16),
            pltpu.VMEM(tiny.shape, BF16),
            pltpu.VMEM((3, most, *tiny.shape), BF16),
            pltpu.VMEM(table.shape, BF16),
            pltpu.VMEM((3, most, *table.shape), BF16),
            pltpu.VMEM((own, seqs, *rows.shape[2:]), BF16),
            pltpu.VMEM((own, seqs, *cots.shape[2:]), BF16),
            pltpu.VMEM((own, width, 2 * share), BF16),
            pltpu.VMEM((own, 2 * share, width), BF16),
            pltpu.VMEM((2, 2 * share, width), F32),
            pltpu.VMEM((own, share, width), F32),
            pltpu.VMEM((own, 2, share, width), BF16),
            pltpu.VMEM((own, 2, share, width), BF16),
            sems((2, own, 2)),
            sems((2, 2)),
            sems((2, total - 1)),
            sems((2, across - 1)),
            sems((2, seqs - 1)),
            sems((2, seqs - 1)),
            sems((2, across * parts - 1)),
            sems((2, across - 1)),
            sems((2, 3, most)),
            sems((2, 3, most)),
            sems((2, own)),
            sems((5,)),
        ],
        compiler_params=pltpu.CompilerParams(collective_id=1, has_side_effects=True, vmem_limit_bytes=62 << 20),
        cost_estimate=pl.CostEstimate(flops=16 << 30, bytes_accessed=60 << 20, transcendentals=0),
        name="finish",
    )(three, flipped, weights, x, gain, early, tiny, table, rows, cots, w_in, w_out)


def ring_pairs(total, parts, shift):
    return [(i, i - i % parts + (i % parts + shift) % parts) for i in range(total)]


def pick(pieces, index):
    out = pieces[0]
    for k in range(1, len(pieces)):
        out = jnp.where(index == k, pieces[k], out)
    return out


def swap_parts(pieces, part, parts, total):
    near = [pick(pieces, part)]
    for k in range(1, parts):
        near.append(lax.ppermute(pick(pieces, (part + k) % parts), "seq", ring_pairs(total, parts, k)))
    return [pick(near, (part - j) % parts) for j in range(parts)]


def per_device(
    inputs,
    routes,
    bucket_ids,
    gain_attn,
    w_query,
    w_key,
    w_value,
    w_output,
    rel_table,
    gain_ffn,
    w_router,
    w_in,
    w_out,
    cotangent,
):
    seqs, local_len, width = inputs.shape
    buckets, head_count = rel_table.shape
    size = width // head_count
    total = lax.axis_size("seq")
    across = lax.axis_size("wide")
    length = local_len * total
    parts = total // seqs
    heads = head_count // parts
    cols = heads * size
    me = lax.axis_index("seq")
    part = me % parts
    experts = w_router.shape[1]
    own_experts = w_in.shape[0]
    tokens = seqs * local_len
    capacity = (5 * tokens + 4 * experts - 1) // (4 * experts)
    slots = experts * capacity
    gain_one = gain_attn.astype(F32)
    gain_two = gain_ffn.astype(F32)

    fast = parts == 2 and capacity % 16 == 0 and own_experts == 2 and seqs % 2 == 0 and cols % LANES == 0 and local_len == LANES
    flat_cot = cotangent.reshape(tokens, width)
    chosen = routes.reshape(tokens)
    blocks = inputs.reshape(total, local_len // parts, width)
    own_weights = jnp.concatenate(
        [lax.dynamic_slice(w, (0, part * cols), (width, cols)) for w in (w_query, w_key, w_value)], axis=1
    )

    if fast:
        first_slot = [(e % own_experts) * (across * capacity) + (e // own_experts) * capacity for e in range(experts)]
        base = jnp.array(first_slot + [0] * (LANES - experts), F32)[None]
        seq_in, qkv, flipped, slot_hot, cot_rows = begin(
            blocks,
            w_query,
            w_key,
            w_value,
            gain_one[None],
            chosen[:, None],
            base,
            flat_cot,
            heads,
            size,
            own_experts,
            capacity,
        )
    else:
        seq_in = spread(blocks, parts).reshape(length, width).astype(F32)
        inv_one = inverse_rms(seq_in)
        normed_one = (seq_in * inv_one * gain_one).astype(BF16)
        flipped = normed_one.T
        qkv = contract(own_weights, normed_one, 0, 1).astype(BF16).reshape(3, heads, size, length)
        picked = (chosen[:, None] == jnp.arange(experts, dtype=jnp.int32)[None, :]).astype(F32)
        order = jnp.arange(tokens, dtype=jnp.int32)
        before = (order[None, :] < order[:, None]).astype(BF16)
        earlier = jnp.dot(before, picked.astype(BF16), preferred_element_type=F32)
        rank_in = jnp.sum(earlier * picked, axis=1).astype(jnp.int32)
        place = (chosen % own_experts) * (across * capacity) + (chosen // own_experts) * capacity + rank_in
        slot_of = jnp.where(rank_in < capacity, place, slots)
        slot_hot = (slot_of[:, None] == jnp.arange(slots, dtype=jnp.int32)[None, :]).astype(BF16)
        packed = contract(slot_hot, flat_cot, 0, 0).astype(BF16).reshape(own_experts, across, capacity, width)
        cot_rows = jnp.stack([lax.all_to_all(packed[e], "wide", 0, 0, tiled=True) for e in range(own_experts)])
        cot_rows = cot_rows.reshape(own_experts, across * capacity, width)
    rings = [[n * parts + p for n in range(seqs)] for p in range(parts)] if fast else None
    all_cots = lax.all_gather(cot_rows, "seq", axis=0, axis_index_groups=rings)
    own_table = lax.dynamic_slice(rel_table, (0, part * heads), (buckets, heads))
    ids = jnp.concatenate([bucket_ids, jnp.full((1,), buckets, jnp.int32)])
    bucket_hot = (ids[None, :] == jnp.arange(buckets, dtype=jnp.int32)[:, None]).astype(BF16)
    reverse_hot = (ids[::-1][None, :] == jnp.arange(buckets, dtype=jnp.int32)[:, None]).astype(BF16)
    bias_line = contract(own_table, reverse_hot, 0, 0).reshape(heads, 1, 2 * length)
    outs, attended, exps, inverse = attend(qkv, bias_line, total)
    attended = attended.reshape(seqs, width, local_len)

    flat_in = inputs.reshape(tokens, width).astype(F32)
    middle = flat_in + jnp.einsum("sft,fe->ste", attended, w_output, preferred_element_type=F32).reshape(tokens, width)
    inv_two = inverse_rms(middle)
    normed_two = (middle * inv_two * gain_two).astype(BF16)
    router_probs = jax.nn.softmax(jnp.dot(normed_two, w_router, preferred_element_type=F32), axis=-1)
    picked = (chosen[:, None] == jnp.arange(experts, dtype=jnp.int32)[None, :]).astype(F32)
    gate_prob = jnp.sum(router_probs * picked, axis=1)
    upstream = flat_cot.astype(F32)
    gate_high = gate_prob.astype(BF16)
    gate_low = (gate_prob - gate_high.astype(F32)).astype(BF16)
    pad = jnp.zeros((tokens, LANES - 2), BF16)
    both = jnp.concatenate([normed_two, gate_high[:, None], gate_low[:, None], pad], axis=1)
    packed = contract(slot_hot, both, 0, 0).astype(BF16)
    if fast:
        received = exchange(packed.reshape(own_experts, across * capacity, width + LANES), "wide")
        returned = run_experts(received, cot_rows, w_in, w_out, 512).reshape(slots, 2 * width)
    else:
        packed = packed.reshape(own_experts, across, capacity, width + LANES)
        received, returned = [], []
        for e in range(own_experts):
            got = lax.all_to_all(packed[e], "wide", 0, 0, tiled=True).reshape(across * capacity, width + LANES)
            received.append(got)
            pair = run_expert(got, cot_rows[e], w_in, w_out, e, 512).reshape(across, capacity, 2 * width)
            returned.append(lax.all_to_all(pair, "wide", 0, 0, tiled=True).reshape(across * capacity, 2 * width))
        received, returned = jnp.stack(received), jnp.concatenate(returned, axis=0)
    all_rows = lax.all_gather(received, "seq", axis=0, axis_index_groups=rings)
    token_rows = jnp.dot(slot_hot, returned, preferred_element_type=F32)
    selected, grad_token = token_rows[:, :width], token_rows[:, width:]
    output = (middle + gate_prob[:, None] * selected).astype(BF16).reshape(inputs.shape)
    grad_gate = jnp.sum(upstream * selected, axis=1)
    grad_logits = (grad_gate[:, None] * router_probs * (picked - gate_prob[:, None])).astype(BF16)
    grad_router = contract(grad_logits, normed_two, 0, 0)
    grad_normed_two = grad_token + contract(grad_logits, w_router, 1, 1)
    grad_mid_norm, grad_gain_two = norm_backward(middle, inv_two, gain_two, grad_normed_two)
    grad_middle = upstream + grad_mid_norm
    grad_branch = grad_middle.astype(BF16).reshape(seqs, local_len, width)
    grad_w_output = jnp.einsum("sft,ste->fe", attended, grad_branch, preferred_element_type=F32)
    share = width // total
    slim = share // across
    back = (exps, inverse, grad_branch, w_output.reshape(parts, cols, width), outs, qkv, bucket_hot)
    if fast:
        early = grad_w_output.astype(BF16).reshape(seqs, parts, across, slim, width)
        three, table, early = attend_back(*back, early)
        tiny = jnp.concatenate(
            [jnp.zeros((1, width), F32), grad_gain_two[None], grad_router, jnp.zeros((14 - experts, width), F32)], axis=0
        )
        home, total_query, total_key, total_value, total_output, tiny, table, grad_w_in, grad_w_out = finish(
            three,
            flipped,
            own_weights,
            seq_in,
            gain_one[None],
            early,
            tiny,
            table,
            all_rows,
            all_cots,
            w_in,
            w_out,
        )
        return (
            output,
            (grad_middle + home.reshape(tokens, width).astype(F32)).reshape(inputs.shape),
            tiny[0],
            total_query,
            total_key,
            total_value,
            total_output,
            table[:, :head_count],
            tiny[1],
            tiny[2 : 2 + experts].T,
            grad_w_in,
            grad_w_out,
        )

    three, table = attend_back(*back, None)
    grad_normed_one = contract(three, own_weights, 1, 1)
    grad_in_norm, grad_gain_one = norm_backward(seq_in, inv_one, gain_one, grad_normed_one)
    pieces = grad_in_norm.astype(BF16).reshape(total, parts, local_len // parts, width)
    swapped = swap_parts([pieces[:, p] for p in range(parts)], part, parts, total)
    home = sum(p.astype(F32) for p in swapped).astype(BF16)
    home = lax.all_to_all(home, "seq", 0, 0, tiled=True).reshape(tokens, width).astype(F32)
    grad_projections = lax.dynamic_update_slice(
        jnp.zeros((width, 3, width), F32), contract(flipped, three, 1, 0).reshape(width, 3, cols), (0, 0, part * cols)
    )
    rows = [grad_projections[:, k] for k in range(3)]
    rows += [grad_w_output, grad_gain_one[:, None], grad_gain_two[:, None], grad_router.T]
    rows, table = lax.psum((jnp.concatenate(rows, axis=1).astype(BF16), table.astype(BF16)), "wide")
    rows = lax.psum_scatter(rows, "seq", scatter_dimension=0, tiled=True).astype(F32)
    table = lax.psum_scatter(table, "seq", scatter_dimension=0, tiled=True).astype(F32)
    held = []
    for e in range(own_experts):
        held = run_share(
            me,
            all_rows.reshape(total * own_experts, *received.shape[1:]),
            all_cots.reshape(total * own_experts, *cot_rows.shape[1:]),
            w_in,
            w_out,
            e,
            held,
        )
    last = rows[:, 4 * width :]
    return (
        output,
        (grad_middle + home).reshape(inputs.shape),
        last[:, 0],
        *[rows[:, k * width : (k + 1) * width] for k in range(4)],
        table[:, :head_count],
        last[:, 1],
        last[:, 2 : 2 + experts],
        *held,
    )


def solution(mesh):
    in_specs = (
        P("wide", "seq", None),
        P("wide", "seq", None),
        P(),
        P(),
        P(),
        P(),
        P(),
        P(),
        P(),
        P(),
        P(),
        P("wide", None, None),
        P("wide", None, None),
        P("wide", "seq", None),
    )
    out_specs = (
        P("wide", "seq", None),
        P("wide", "seq", None),
        P("seq"),
        P("seq", None),
        P("seq", None),
        P("seq", None),
        P("seq", None),
        P("seq", None),
        P("seq"),
        P("seq", None),
        P("wide", None, "seq"),
        P("wide", "seq", None),
    )
    return jax.shard_map(
        per_device, mesh=mesh, in_specs=in_specs, out_specs=out_specs, check_vma=False
    )
```

```python
import functools

import jax
import jax.numpy as jnp
from jax import lax
from jax.experimental import pallas as pl
from jax.experimental.pallas import tpu as pltpu
from jax.sharding import PartitionSpec as P

EPSILON = 1e-06
F32 = jnp.float32
BF16 = jnp.bfloat16
LANES = 128


def contract(a, b, da, db):
    return lax.dot_general(a, b, (((da,), (db,)), ((), ())), preferred_element_type=F32)


def inverse_rms(source):
    return lax.rsqrt(jnp.mean(source * source, axis=-1, keepdims=True) + EPSILON)


def norm_backward(source, inv_rms, gain_vec, upstream):
    scaled = upstream * gain_vec
    gain_grad = jnp.sum(upstream * source * inv_rms, axis=0)
    mean_inner = jnp.mean(source * scaled, axis=-1, keepdims=True)
    return (inv_rms * scaled - source * (inv_rms * inv_rms * inv_rms) * mean_inner, gain_grad)


def smooth_act(values):
    return jax.nn.gelu(values, approximate=True)


MESH = pl.DeviceIdType.MESH


def remote(src, dst, send, recv, where):
    copy = pltpu.make_async_remote_copy(src, dst, send, recv, device_id=where, device_id_type=MESH)
    copy.start()
    return copy


def meet(peers):
    barrier = pltpu.get_barrier_semaphore()
    for where in peers:
        pl.semaphore_signal(barrier, inc=1, device_id=where, device_id_type=MESH)
    pl.semaphore_wait(barrier, len(peers))


def far_first(total):
    return sorted(range(1, total), key=lambda k: -min(k, total - k))


def twist(a, b, total):
    out, bit = 0, 1
    while bit < total:
        out = out + lax.rem(lax.div(a, bit) + lax.div(b, bit), 2) * bit
        bit *= 2
    return out


def attend_kernel(
    qkv_ref, bias_ref, out_ref, home_ref, exp_ref, inv_ref, strip, keys, scores, held, send, recv, local, exp_sems
):
    _, heads, size, length = qkv_ref.shape
    total = lax.axis_size("seq")
    me = lax.axis_index("seq")
    tokens = out_ref.shape[3]
    width = 2 * tokens
    pairs = total // 2
    rows = 2 * length - tokens
    chunk = 256
    meet([{"seq": lax.rem(me + k, total)} for k in range(1, total)])

    def prepare(h, carry):
        keys[h] = qkv_ref[1, h].T
        for b in range(rows // tokens):
            start = 2 * length - 2 * tokens - tokens * b
            base = jnp.broadcast_to(bias_ref[h, :, start : start + 2 * tokens], (tokens, 2 * tokens))
            rolled = pltpu.roll(base, 0, 1, stride=1, stride_axis=0)
            strip[h, tokens * b : tokens * (b + 1), :] = rolled[:, tokens:]
        return carry

    lax.fori_loop(0, heads, prepare, 0)

    def store(slot, pair, h):
        return pltpu.make_async_copy(held.at[slot], exp_ref.at[pair, h], exp_sems.at[slot])

    def step(t, carry):
        pair = twist(lax.div(me, 2), pairs - 1 - t, pairs)
        at = pl.ds(pl.multiple_of(pair * width, tokens), width)

        def head(h, carry):
            count = t * heads + h
            slot = lax.rem(count, 2)

            @pl.when(count >= 2)
            def _():
                store(slot, pair, h).wait()

            query = qkv_ref[0, h, :, at]
            tops = [jnp.full((1, tokens), -jnp.inf, F32)] * 2
            for c in range(length // chunk):
                part = contract(keys[h, c * chunk : (c + 1) * chunk, :], query, 1, 0)
                for s in range(2):
                    row = pl.multiple_of(length - tokens - (pair * width + s * tokens) + c * chunk, tokens)
                    piece = part[:, s * tokens : (s + 1) * tokens] + strip[h, pl.ds(row, chunk), :]
                    scores[c * chunk : (c + 1) * chunk, s * tokens : (s + 1) * tokens] = piece
                    tops[s] = jnp.maximum(tops[s], jnp.max(piece, axis=0, keepdims=True))
            sums = [jnp.zeros((1, tokens), F32)] * 2
            for c in range(length // chunk):
                for s in range(2):
                    piece = scores[c * chunk : (c + 1) * chunk, s * tokens : (s + 1) * tokens]
                    grown = jnp.exp(piece - tops[s])
                    sums[s] = sums[s] + jnp.sum(grown, axis=0, keepdims=True)
                    held[slot, c * chunk : (c + 1) * chunk, s * tokens : (s + 1) * tokens] = grown.astype(BF16)
            store(slot, pair, h).start()
            mixed = contract(qkv_ref[2, h], held[slot], 1, 0)
            for s in range(2):
                inverse = 1.0 / sums[s]
                inv_ref[pair, h, :, s * tokens : (s + 1) * tokens] = inverse
                out_ref[2 * pair + s, h] = (mixed[:, s * tokens : (s + 1) * tokens] * inverse).astype(BF16)
            return carry

        lax.fori_loop(0, heads, head, 0)
        for s in range(2):
            to = 2 * pair + s
            k = twist(me, to, total)

            @pl.when(to != me)
            def _():
                pltpu.make_async_remote_copy(
                    out_ref.at[to], home_ref.at[me], send.at[k], recv.at[k], device_id={"seq": to}, device_id_type=MESH
                ).start()

        return carry

    lax.fori_loop(0, pairs, step, 0)
    own = pltpu.make_async_copy(out_ref.at[me], home_ref.at[me], local)
    own.start()
    for slot in range(2):
        store(slot, 0, 0).wait()

    def settle(k, carry):
        source = twist(me, k, total)
        pltpu.make_async_remote_copy(
            out_ref.at[source], home_ref.at[source], send.at[k], recv.at[k], device_id={"seq": source}, device_id_type=MESH
        ).wait()
        return carry

    lax.fori_loop(1, total, settle, 0)
    own.wait()


def attend(qkv, bias_line, total):
    _, heads, size, length = qkv.shape
    tokens = length // total
    vmem = pl.BlockSpec(memory_space=pltpu.VMEM)
    return pl.pallas_call(
        attend_kernel,
        in_specs=[vmem, vmem],
        out_specs=[vmem, vmem, pl.BlockSpec(memory_space=pl.ANY), vmem],
        out_shape=[
            jax.ShapeDtypeStruct((total, heads, size, tokens), BF16),
            jax.ShapeDtypeStruct((total, heads, size, tokens), BF16),
            jax.ShapeDtypeStruct((total // 2, heads, length, 2 * tokens), BF16),
            jax.ShapeDtypeStruct((total // 2, heads, 1, 2 * tokens), F32),
        ],
        scratch_shapes=[
            pltpu.VMEM((heads, 2 * length - tokens, tokens), F32),
            pltpu.VMEM((heads, length, size), BF16),
            pltpu.VMEM((length, 2 * tokens), F32),
            pltpu.VMEM((2, length, 2 * tokens), BF16),
            pltpu.SemaphoreType.DMA((total,)),
            pltpu.SemaphoreType.DMA((total,)),
            pltpu.SemaphoreType.DMA,
            pltpu.SemaphoreType.DMA((2,)),
        ],
        compiler_params=pltpu.CompilerParams(collective_id=2, has_side_effects=True, vmem_limit_bytes=62 << 20),
        cost_estimate=pl.CostEstimate(
            flops=4 * heads * length * length * size, bytes_accessed=2 * heads * length * length, transcendentals=heads * length * length
        ),
        name="attend",
    )(qkv, bias_line)


def attend_back_kernel(early, *refs):
    refs = list(refs)
    exp_ref, inv_ref, branch_ref, weight_ref, out_ref, qkv_ref, hot_ref = refs[:7]
    early_ref, *line_refs = [refs.pop(7) for _ in range(3)] if early else [None]
    three_ref, table_ref = refs[7:9]
    early_out, *line_outs = [refs.pop(9) for _ in range(3)] if early else [None]
    leaving, got, strip, values, dq_all, dk_sum, dv_sum, scores, held, diagonal, send, recv, exp_sems = refs[9:22]
    _, heads, size, length = qkv_ref.shape
    total = lax.axis_size("seq")
    me = lax.axis_index("seq")
    tokens = out_ref.shape[3]
    parts = weight_ref.shape[0]
    part = lax.rem(me, parts)
    width = 2 * tokens
    pairs = total // 2
    rows = 2 * length - tokens
    chunk = 256

    def pair_at(t):
        return twist(lax.div(me, 2), t, pairs)

    def load(count):
        slot = lax.rem(count, 2)
        at = exp_ref.at[pair_at(lax.div(count, heads)), lax.rem(count, heads)]
        return pltpu.make_async_copy(at, held.at[slot], exp_sems.at[slot])

    load(0).start()
    peers = [{"seq": lax.rem(me + k, total)} for k in range(1, total)]
    if early:
        across, row = lax.axis_size("wide"), lax.axis_index("wide")
        other = twist(me, 1, total)
        peers += [{"wide": lax.rem(row + k, across)} for k in range(1, across)]
    meet(peers)
    if early:
        near, near_sum, wide_got, near_sems, wide_sems, line_sems = refs[22:]
        seqs = early_ref.shape[0]

        def near_copy():
            return pltpu.make_async_remote_copy(
                early_ref.at[:, lax.rem(part + 1, parts)],
                near,
                near_sems.at[0],
                near_sems.at[1],
                device_id={"seq": other},
                device_id_type=MESH,
            )

        def wide_copy(k):
            to = lax.rem(row + k, across)
            return pltpu.make_async_remote_copy(
                near_sum.at[to],
                wide_got.at[k - 1],
                wide_sems.at[0, k - 1],
                wide_sems.at[1, k - 1],
                device_id={"wide": to},
                device_id_type=MESH,
            )

        near_copy().start()

    def product(to):
        value = contract(weight_ref[lax.rem(to, parts)], branch_ref[lax.div(to, parts)], 1, 1)
        return value.astype(BF16).reshape(heads, size, tokens)

    def leave(k, carry):
        to = twist(me, k, total)
        leaving[to] = product(to)
        pltpu.make_async_remote_copy(
            leaving.at[to], got.at[me], send.at[k], recv.at[k], device_id={"seq": to}, device_id_type=MESH
        ).start()
        return carry

    lax.fori_loop(1, total, leave, 0)
    line_ends = []
    if early:
        for e in range(line_refs[0].shape[0]):
            up, down = ((1, seqs - 2, line_refs[n].at[e], line_outs[n].at[e]) for n in range(2))
            line_ends.append(pass_on(parts, up, down, line_sems.at[e]))
    got[me] = product(me)

    def prepare(h, carry):
        values[h] = qkv_ref[2, h].T
        strip[h] = jnp.zeros(strip.shape[1:], F32)
        dk_sum[h] = jnp.zeros(dk_sum.shape[1:], F32)
        dv_sum[h] = jnp.zeros(dv_sum.shape[1:], F32)
        return carry

    lax.fori_loop(0, heads, prepare, 0)

    def arrive(k):
        source = twist(me, k, total)
        pltpu.make_async_remote_copy(
            leaving.at[source], got.at[source], send.at[k], recv.at[k], device_id={"seq": source}, device_id_type=MESH
        ).wait()

    def step(t, carry):
        pair = pair_at(t)
        at = pl.ds(pl.multiple_of(pair * width, tokens), width)

        @pl.when(t > 0)
        def _():
            arrive(2 * t)

        arrive(2 * t + 1)
        if early:

            @pl.when(t == 1)
            def _():
                near_copy().wait()
                for n in range(seqs):
                    for a in range(across):
                        value = early_ref[n, part, a].astype(F32) + near[n, a].astype(F32)
                        near_sum[a, n] = value.astype(BF16)
                for k in range(1, across):
                    wide_copy(k).start()

            @pl.when(t == pairs - 1)
            def _():
                for k in range(1, across):
                    wide_copy(k).wait()
                for n in range(seqs):
                    value = near_sum[row, n].astype(F32)
                    for k in range(1, across):
                        value = value + wide_got[k - 1, n].astype(F32)
                    early_out[n] = value.astype(BF16)

        def head(h, carry):
            count = t * heads + h
            slot = lax.rem(count, 2)

            @pl.when(count + 1 < pairs * heads)
            def _():
                load(count + 1).start()

            grads, inner = [], []
            for s in range(2):
                inverse = inv_ref[pair, h, :, s * tokens : (s + 1) * tokens]
                scaled = got[2 * pair + s, h].astype(F32) * inverse
                inner.append(jnp.sum(scaled * out_ref[2 * pair + s, h].astype(F32), axis=0, keepdims=True))
                grads.append(scaled.astype(BF16))
            grad = jnp.concatenate(grads, axis=1)
            load(count).wait()
            for c in range(length // chunk):
                part_grad = contract(values[h, c * chunk : (c + 1) * chunk, :], grad, 1, 0)
                for s in range(2):
                    grown = held[slot, c * chunk : (c + 1) * chunk, s * tokens : (s + 1) * tokens].astype(F32)
                    slope = grown * (part_grad[:, s * tokens : (s + 1) * tokens] - inner[s])
                    line = pl.multiple_of(length - tokens - (pair * width + s * tokens) + c * chunk, tokens)
                    strip[h, pl.ds(line, chunk), :] += slope
                    scores[c * chunk : (c + 1) * chunk, s * tokens : (s + 1) * tokens] = slope.astype(BF16)
            dq_all[h, at, :] = contract(qkv_ref[1, h], scores[...], 1, 0).T.astype(BF16)
            dk_sum[h] += contract(scores[...], qkv_ref[0, h, :, at].T, 1, 0)
            dv_sum[h] += contract(held[slot], grad.T, 1, 0)
            return carry

        lax.fori_loop(0, heads, head, 0)
        return carry

    lax.fori_loop(0, pairs, step, 0)
    down = lax.broadcasted_iota(jnp.int32, (tokens, tokens), 0)
    over = lax.broadcasted_iota(jnp.int32, (tokens, tokens), 1)
    mirror = (down + over == tokens - 1).astype(F32)
    cols = heads * size
    for c in range(length // chunk):
        here = slice(c * chunk, (c + 1) * chunk)
        for n, ref in enumerate((dq_all, dk_sum, dv_sum)):
            joined = jnp.concatenate([ref[h, here, :].astype(F32) for h in range(heads)], axis=1)
            three_ref[here, n * cols : (n + 1) * cols] = joined.astype(BF16)

    def close(h, carry):
        diagonal[h] = jnp.zeros(diagonal.shape[1:], F32)
        for b in range(rows // tokens):
            flipped = lax.dot_general(
                strip[h, tokens * b : tokens * (b + 1), :],
                mirror,
                (((1,), (0,)), ((), ())),
                precision=lax.Precision.HIGHEST,
                preferred_element_type=F32,
            )
            spread_out = jnp.concatenate([flipped, jnp.zeros_like(flipped)], axis=1)
            rolled = pltpu.roll(spread_out, 0, 1, stride=1, stride_axis=0)
            diagonal[h, :, tokens * b : tokens * (b + 2)] += jnp.sum(rolled, axis=0, keepdims=True)
        return carry

    lax.fori_loop(0, heads, close, 0)
    sums = jnp.concatenate([diagonal[h] for h in range(heads)], axis=0)
    table = lax.dot_general(
        sums,
        hot_ref[...].astype(F32),
        (((1,), (1,)), ((), ())),
        precision=lax.Precision.HIGHEST,
        preferred_element_type=F32,
    )
    line = lax.broadcasted_iota(jnp.int32, (table_ref.shape[0], heads), 0)
    head_line = lax.broadcasted_iota(jnp.int32, (table_ref.shape[0], heads), 1) + part * heads
    table_ref[...] = lax.dot_general(
        (line == head_line).astype(F32),
        table,
        (((1,), (0,)), ((), ())),
        precision=lax.Precision.HIGHEST,
        preferred_element_type=F32,
    )
    for end in line_ends:
        end()


def attend_back(exps, inverse, branch, weight, outs, qkv, hot, early, line):
    _, heads, size, length = qkv.shape
    total, tokens = outs.shape[0], outs.shape[3]
    vmem = pl.BlockSpec(memory_space=pltpu.VMEM)
    sems = pltpu.SemaphoreType.DMA
    out_shape = [
        jax.ShapeDtypeStruct((length, 3 * heads * size), BF16),
        jax.ShapeDtypeStruct((16, hot.shape[0]), F32),
    ]
    more, given = [], []
    if early is not None:
        seqs, _, across, slim, columns = early.shape
        given = [early, *line]
        out_shape.append(jax.ShapeDtypeStruct((seqs, slim, columns), BF16))
        out_shape += [jax.ShapeDtypeStruct(rows.shape, BF16) for rows in line]
        more = [
            pltpu.VMEM((seqs, across, slim, columns), BF16),
            pltpu.VMEM((across, seqs, slim, columns), BF16),
            pltpu.VMEM((across - 1, seqs, slim, columns), BF16),
            sems((2,)),
            sems((2, across - 1)),
            sems((line[0].shape[0], 2, 2)),
        ]
    hbm = pl.BlockSpec(memory_space=pl.ANY)
    return pl.pallas_call(
        functools.partial(attend_back_kernel, early is not None),
        in_specs=[hbm] + [vmem] * (6 + len(given[:1])) + [hbm] * len(line),
        out_specs=[vmem] * (len(out_shape) - len(line)) + [hbm] * len(line),
        out_shape=out_shape,
        scratch_shapes=[
            pltpu.VMEM((total, heads, size, tokens), BF16),
            pltpu.VMEM((total, heads, size, tokens), BF16),
            pltpu.VMEM((heads, 2 * length - tokens, tokens), F32),
            pltpu.VMEM((heads, length, size), BF16),
            pltpu.VMEM((heads, length, size), BF16),
            pltpu.VMEM((heads, length, size), F32),
            pltpu.VMEM((heads, length, size), F32),
            pltpu.VMEM((length, 2 * tokens), BF16),
            pltpu.VMEM((2, length, 2 * tokens), BF16),
            pltpu.VMEM((heads, 1, 2 * length), F32),
            sems((total,)),
            sems((total,)),
            sems((2,)),
            *more,
        ],
        compiler_params=pltpu.CompilerParams(collective_id=3, has_side_effects=True, vmem_limit_bytes=62 << 20),
        cost_estimate=pl.CostEstimate(
            flops=8 * heads * length * length * size, bytes_accessed=2 * heads * length * length, transcendentals=0
        ),
        name="attend_back",
    )(exps, inverse, branch, weight, outs, qkv, hot, *given)


def activation(v):
    square = v * v
    bent = jnp.tanh(0.7978845608 * v * (1.0 + 0.044715 * square))
    half = 0.5 * (1.0 + bent)
    slope = half + 0.5 * v * (1.0 - bent * bent) * (0.7978845608 * (1.0 + 3.0 * 0.044715 * square))
    return v * half, slope


def gated(rows, cots, router, expert):
    logits = contract(rows, router, 1, 0)
    grown = jnp.exp(logits - jnp.max(logits, axis=1, keepdims=True))
    named = lax.broadcasted_iota(jnp.int32, grown.shape, 1) == expert
    gate = jnp.sum(jnp.where(named, grown, 0.0), axis=1, keepdims=True) / jnp.sum(grown, axis=1, keepdims=True)
    return (gate * cots.astype(F32)).astype(BF16)


def expert_kernel(expert, rows_ref, cot_ref, router_ref, in_ref, out_ref, both_ref, forward, backward):
    step = pl.program_id(0)
    width = cot_ref.shape[1]

    @pl.when(step == 0)
    def _():
        forward[...] = jnp.zeros_like(forward)
        backward[...] = jnp.zeros_like(backward)

    rows = rows_ref[...]
    own = router_ref.shape[1] // lax.axis_size("wide")
    grads = gated(rows, cot_ref[...], router_ref[...], lax.axis_index("wide") * own + expert)
    hidden, slope = activation(contract(rows, in_ref[0], 1, 0))
    grad_hidden = contract(grads, out_ref[0], 1, 1).astype(BF16).astype(F32)
    forward[...] += contract(hidden.astype(BF16), out_ref[0], 1, 0)
    backward[...] += contract((grad_hidden * slope).astype(BF16), in_ref[0], 1, 1)

    @pl.when(step == pl.num_programs(0) - 1)
    def _():
        both_ref[:, :width] = forward[...].astype(BF16)
        both_ref[:, width:] = backward[...].astype(BF16)


def run_expert(rows, cots, router, w_in, w_out, expert, block):
    count, width = cots.shape
    units = w_in.shape[2]
    return pl.pallas_call(
        functools.partial(expert_kernel, expert),
        grid=(units // block,),
        in_specs=[
            pl.BlockSpec(rows.shape, lambda f: (0, 0)),
            pl.BlockSpec(cots.shape, lambda f: (0, 0)),
            pl.BlockSpec(router.shape, lambda f: (0, 0)),
            pl.BlockSpec((1, width, block), lambda f: (expert, 0, f)),
            pl.BlockSpec((1, block, width), lambda f: (expert, f, 0)),
        ],
        out_specs=pl.BlockSpec((count, 2 * width), lambda f: (0, 0)),
        out_shape=jax.ShapeDtypeStruct((count, 2 * width), BF16),
        scratch_shapes=[pltpu.VMEM((count, width), F32), pltpu.VMEM((count, width), F32)],
        compiler_params=pltpu.CompilerParams(vmem_limit_bytes=40 << 20),
        name="expert",
    )(rows, cots, router, w_in, w_out)


def line_peers(parts):
    total, me = lax.axis_size("seq"), lax.axis_index("seq")
    return [{"seq": lax.rem(me + parts, total)}, {"seq": lax.rem(me - parts + total, total)}]


def pass_on(parts, up, down, sems):
    me = lax.axis_index("seq")
    z = lax.div(me, parts)

    def copy(n, src, dst, step):
        return pltpu.make_async_remote_copy(
            src, dst, sems.at[0, n], sems.at[1, n], device_id={"seq": me + step}, device_id_type=MESH
        )

    legs = [(0, *up, parts), (1, *down, -parts)]
    for n, low, high, src, dst, step in legs:

        @pl.when(jnp.logical_and(z >= low, z <= high))
        def _():
            copy(n, src, dst, step).start()

    def end():
        for n, low, high, src, dst, step in legs:
            move = 1 if step > 0 else -1

            @pl.when(jnp.logical_and(z >= low, z <= high))
            def _():
                copy(n, src, dst, step).wait_send()

            @pl.when(jnp.logical_and(z >= low + move, z <= high + move))
            def _():
                copy(n, src, dst, -step).wait_recv()

    return end


def exchange_kernel(
    seqs, in_ref, before_ref, after_ref, out_ref, before_out, after_out, send, recv, local, line_sems
):
    across = lax.axis_size("wide")
    parts = lax.axis_size("seq") // seqs
    me = lax.axis_index("wide")
    own = in_ref.shape[0]
    count = in_ref.shape[1] // across
    meet([{"wide": lax.rem(me + k, across)} for k in range(1, across)] + line_peers(parts))
    line_end = pass_on(
        parts, (1, seqs - 2, before_ref.at[0], before_out), (1, seqs - 2, after_ref.at[0], after_out), line_sems
    )
    copies = []
    mine = pl.ds(me * count, count)
    for n in range(own):
        for k in range(1, across):
            to = lax.rem(me + k, across)
            copies.append(
                remote(
                    in_ref.at[n, pl.ds(to * count, count)],
                    out_ref.at[n, mine],
                    send.at[n, k - 1],
                    recv.at[n, k - 1],
                    {"wide": to},
                )
            )
    kept = [pltpu.make_async_copy(in_ref.at[n, mine], out_ref.at[n, mine], local.at[n]) for n in range(own)]
    for copy in kept:
        copy.start()
    for copy in kept + copies:
        copy.wait()
    line_end()


def exchange(rows, before, after, seqs):
    across = lax.axis_size("wide")
    own = rows.shape[0]
    vmem, hbm = pl.BlockSpec(memory_space=pltpu.VMEM), pl.BlockSpec(memory_space=pl.ANY)
    one = jax.ShapeDtypeStruct(before.shape[1:], before.dtype)
    return pl.pallas_call(
        functools.partial(exchange_kernel, seqs),
        in_specs=[vmem, hbm, hbm],
        out_specs=[hbm, hbm, hbm],
        out_shape=[jax.ShapeDtypeStruct(rows.shape, rows.dtype), one, one],
        scratch_shapes=[
            pltpu.SemaphoreType.DMA((own, across - 1)),
            pltpu.SemaphoreType.DMA((own, across - 1)),
            pltpu.SemaphoreType.DMA((own,)),
            pltpu.SemaphoreType.DMA((2, 2)),
        ],
        compiler_params=pltpu.CompilerParams(collective_id=4, has_side_effects=True, vmem_limit_bytes=62 << 20),
        name="exchange",
    )(rows, before, after)


def experts_kernel(
    block,
    seqs,
    rows_ref,
    cot_ref,
    router_ref,
    in_ref,
    out_ref,
    line_ref,
    before_ref,
    after_ref,
    back_ref,
    before_out,
    after_out,
    line_before,
    line_after,
    done,
    grads,
    forward,
    backward,
    in_held,
    out_held,
    back_send,
    back_recv,
    local,
    held_sems,
    line_sems,
):
    own, rows, double = back_ref.shape
    width = double // 2
    across = lax.axis_size("wide")
    me = lax.axis_index("wide")
    count = rows // across
    steps = in_ref.shape[2] // block

    def load(at):
        slot = lax.rem(at, 2)
        expert, place = lax.div(at, steps), pl.multiple_of(lax.rem(at, steps) * block, block)
        return (
            pltpu.make_async_copy(in_ref.at[expert, :, pl.ds(place, block)], in_held.at[slot], held_sems.at[0, slot]),
            pltpu.make_async_copy(out_ref.at[expert, pl.ds(place, block), :], out_held.at[slot], held_sems.at[1, slot]),
        )

    for copy in load(0):
        copy.start()
    parts = lax.axis_size("seq") // seqs
    meet([{"wide": lax.rem(me + k, across)} for k in range(1, across)] + line_peers(parts))
    line_ends = [
        pass_on(
            parts,
            (1, seqs - 2, before_ref.at[1], before_out),
            (1, seqs - 2, after_ref.at[1], after_out),
            line_sems.at[0],
        ),
        pass_on(parts, (0, seqs - 2, line_ref, line_before), (1, seqs - 1, line_ref, line_after), line_sems.at[1]),
    ]
    coming = []
    mine = pl.ds(me * count, count)
    for e in range(own):
        grads[...] = gated(rows_ref[e], cot_ref[e], router_ref[...], me * own + e)
        forward[...] = jnp.zeros_like(forward)
        backward[...] = jnp.zeros_like(backward)

        def step(f, carry):
            at = e * steps + f
            slot = lax.rem(at, 2)

            @pl.when(at + 1 < own * steps)
            def _():
                for copy in load(at + 1):
                    copy.start()

            for copy in load(at):
                copy.wait()
            hidden, slope = activation(contract(rows_ref[e], in_held[slot], 1, 0))
            grad_hidden = contract(grads[...], out_held[slot], 1, 1).astype(BF16).astype(F32)
            forward[...] += contract(hidden.astype(BF16), out_held[slot], 1, 0)
            backward[...] += contract((grad_hidden * slope).astype(BF16), in_held[slot], 1, 1)
            return carry

        lax.fori_loop(0, steps, step, 0)
        done[e, :, :width] = forward[...].astype(BF16)
        done[e, :, width:] = backward[...].astype(BF16)
        for k in range(1, across):
            to = lax.rem(me + k, across)
            coming.append(
                remote(
                    done.at[e, pl.ds(to * count, count)],
                    back_ref.at[e, mine],
                    back_send.at[e, k - 1],
                    back_recv.at[e, k - 1],
                    {"wide": to},
                )
            )
        kept = pltpu.make_async_copy(done.at[e, mine], back_ref.at[e, mine], local.at[e])
        kept.start()
        kept.wait()
    for copy in coming:
        copy.wait()
    for end in line_ends:
        end()


def run_experts(rows, cots, router, w_in, w_out, before, after, seqs, block):
    own, count, width = cots.shape
    units = w_in.shape[2]
    across = lax.axis_size("wide")
    vmem, hbm = pl.BlockSpec(memory_space=pltpu.VMEM), pl.BlockSpec(memory_space=pl.ANY)
    sems = pltpu.SemaphoreType.DMA
    return pl.pallas_call(
        functools.partial(experts_kernel, block, seqs),
        in_specs=[vmem, vmem, vmem, hbm, hbm, hbm, hbm, hbm],
        out_specs=[vmem, hbm, hbm, hbm, hbm],
        out_shape=[
            jax.ShapeDtypeStruct((own, count, 2 * width), BF16),
            *[jax.ShapeDtypeStruct(before.shape[1:], BF16)] * 2,
            *[jax.ShapeDtypeStruct(rows.shape, BF16)] * 2,
        ],
        scratch_shapes=[
            pltpu.VMEM((own, count, 2 * width), BF16),
            pltpu.VMEM((count, width), BF16),
            pltpu.VMEM((count, width), F32),
            pltpu.VMEM((count, width), F32),
            pltpu.VMEM((2, width, block), BF16),
            pltpu.VMEM((2, block, width), BF16),
            sems((own, across - 1)),
            sems((own, across - 1)),
            sems((own,)),
            sems((2, 2)),
            sems((2, 2, 2)),
        ],
        compiler_params=pltpu.CompilerParams(collective_id=5, has_side_effects=True, vmem_limit_bytes=62 << 20),
        cost_estimate=pl.CostEstimate(
            flops=8 * own * count * width * units, bytes_accessed=4 * own * width * units, transcendentals=own * count * units
        ),
        name="experts",
    )(rows, cots, router, w_in, w_out, rows, before, after)


def share_kernel(expert, share_ref, rows_ref, cot_ref, router_ref, in_ref, out_ref, *refs):
    grad_in_ref, grad_out_ref, flipped, total_in = refs[-4:]
    step = pl.program_id(0)

    @pl.when(step == 0)
    def _():
        flipped[...] = in_ref[0].T
        total_in[...] = jnp.zeros_like(total_in)
        grad_out_ref[...] = jnp.zeros_like(grad_out_ref)

    rows = rows_ref[0]
    own = router_ref.shape[1] // lax.axis_size("wide")
    grads = gated(rows, cot_ref[0], router_ref[...], lax.axis_index("wide") * own + expert)
    hidden, slope = activation(contract(flipped[...], rows, 1, 1))
    grad_hidden = contract(out_ref[0], grads, 1, 1).astype(BF16).astype(F32)
    grad_out_ref[0] += contract(hidden.astype(BF16), grads, 1, 0)
    total_in[...] += contract((grad_hidden * slope).astype(BF16), rows, 1, 0)

    @pl.when(step == pl.num_programs(0) - 1)
    def _():
        grad_in_ref[0] = total_in[...].T


def run_share(me, rows, cots, router, w_in, w_out, expert, held):
    own, width, units = w_in.shape
    sources, count = rows.shape[0] // own, rows.shape[1]
    share = units // sources
    if share % LANES == 0:
        where = jnp.full((1,), me, jnp.int32)
        in_spec = pl.BlockSpec((1, width, share), lambda r, at: (expert, 0, at[0]))
        out_spec = pl.BlockSpec((1, share, width), lambda r, at: (expert, at[0], 0))
    else:
        where = jnp.zeros((1,), jnp.int32)
        w_in = lax.dynamic_slice(w_in, (0, 0, me * share), (own, width, share))
        w_out = lax.dynamic_slice(w_out, (0, me * share, 0), (own, share, width))
        in_spec = pl.BlockSpec((1, width, share), lambda r, at: (expert, 0, 0))
        out_spec = pl.BlockSpec((1, share, width), lambda r, at: (expert, 0, 0))
    held_specs = [pl.BlockSpec(memory_space=pl.ANY)] * len(held)
    return pl.pallas_call(
        functools.partial(share_kernel, expert),
        grid_spec=pltpu.PrefetchScalarGridSpec(
            num_scalar_prefetch=1,
            grid=(sources,),
            in_specs=[
                pl.BlockSpec((1, count, rows.shape[2]), lambda r, at: (own * r + expert, 0, 0)),
                pl.BlockSpec((1, count, width), lambda r, at: (own * r + expert, 0, 0)),
                pl.BlockSpec(router.shape, lambda r, at: (0, 0)),
                in_spec,
                out_spec,
                *held_specs,
            ],
            out_specs=[
                pl.BlockSpec((1, width, share), lambda r, at: (expert, 0, 0)),
                pl.BlockSpec((1, share, width), lambda r, at: (expert, 0, 0)),
            ],
            scratch_shapes=[pltpu.VMEM((share, width), BF16), pltpu.VMEM((share, width), F32)],
        ),
        out_shape=[
            jax.ShapeDtypeStruct((own, width, share), F32),
            jax.ShapeDtypeStruct((own, share, width), F32),
        ],
        input_output_aliases={6 + i: i for i in range(len(held))},
        compiler_params=pltpu.CompilerParams(vmem_limit_bytes=62 << 20),
        cost_estimate=pl.CostEstimate(
            flops=8 * sources * count * width * share, bytes_accessed=4 * sources * count * width, transcendentals=0
        ),
        name="share",
    )(where, rows, cots, router, w_in, w_out, *held)


def spread_kernel(parts, in_ref, out_ref, send, recv, pass_send, pass_recv, local):
    total = lax.axis_size("seq")
    me = lax.axis_index("seq")
    part = lax.rem(me, parts)
    meet([{"seq": lax.rem(me + k, total)} for k in range(1, total)])
    copies = []
    for k in far_first(total):
        to = lax.rem(me + k, total)
        copies.append(remote(in_ref.at[to], out_ref.at[me, lax.rem(to, parts)], send.at[k - 1], recv.at[k - 1], {"seq": to}))
    own = pltpu.make_async_copy(in_ref.at[me], out_ref.at[me, part], local)
    own.start()
    own.wait()
    passed = []

    def forward(source, k):
        for j in range(1, parts):
            to = me - part + lax.rem(part + j, parts)
            at = (j - 1) * total + k
            block = out_ref.at[source, part]
            passed.append(remote(block, block, pass_send.at[at], pass_recv.at[at], {"seq": to}))

    forward(me, 0)
    for k in far_first(total)[::-1]:
        source = lax.rem(me - k + total, total)
        block = out_ref.at[source, part]
        pltpu.make_async_remote_copy(
            block, block, send.at[k - 1], recv.at[k - 1], device_id={"seq": source}, device_id_type=MESH
        ).wait_recv()
        forward(source, k)
    for copy in copies:
        copy.wait_send()
    for copy in passed:
        copy.wait()


def spread(blocks, parts):
    total, rows, width = blocks.shape
    passes = (parts - 1) * total
    return pl.pallas_call(
        functools.partial(spread_kernel, parts),
        in_specs=[pl.BlockSpec(memory_space=pl.ANY)],
        out_specs=pl.BlockSpec(memory_space=pl.ANY),
        out_shape=jax.ShapeDtypeStruct((total, parts, rows, width), blocks.dtype),
        scratch_shapes=[
            pltpu.SemaphoreType.DMA((total - 1,)),
            pltpu.SemaphoreType.DMA((total - 1,)),
            pltpu.SemaphoreType.DMA((passes,)),
            pltpu.SemaphoreType.DMA((passes,)),
            pltpu.SemaphoreType.DMA,
        ],
        compiler_params=pltpu.CompilerParams(collective_id=0, has_side_effects=True),
        name="spread",
    )(blocks)


def begin_kernel(
    capacity,
    in_ref,
    query_ref,
    key_ref,
    value_ref,
    gain_ref,
    routes_ref,
    base_ref,
    cot_ref,
    all_ref,
    qkv_ref,
    flip_ref,
    hot_ref,
    rows_ref,
    weights,
    packed,
    send,
    recv,
    pass_send,
    pass_recv,
    wide_send,
    wide_recv,
    local,
):
    total, parts, rows, width = all_ref.shape
    _, heads, size, _ = qkv_ref.shape
    own = rows_ref.shape[0]
    cols = heads * size
    across = lax.axis_size("wide")
    me, row = lax.axis_index("seq"), lax.axis_index("wide")
    part = lax.rem(me, parts)
    other = twist(me, 1, total)
    pairs = total // 2
    peers = [{"seq": lax.rem(me + k, total)} for k in range(1, total)]
    peers += [{"wide": lax.rem(row + k, across)} for k in range(1, across)]
    meet(peers)
    sent = []
    for k in range(1, total):
        to = twist(me, k, total)
        sent.append(remote(in_ref.at[to], all_ref.at[me, lax.rem(to, parts)], send.at[to], recv.at[me], {"seq": to}))
    kept = pltpu.make_async_copy(in_ref.at[me], all_ref.at[me, part], local.at[0])
    kept.start()
    kept.wait()
    passed = []

    def forward(source):
        block = all_ref.at[source, part]
        passed.append(remote(block, block, pass_send.at[source], pass_recv.at[source], {"seq": other}))

    def await_recv(block, sem):
        pltpu.make_async_remote_copy(
            block, block, local.at[1], sem, device_id={"seq": other}, device_id_type=MESH
        ).wait_recv()

    forward(me)

    tokens, slots = hot_ref.shape
    picked = (routes_ref[...] == lax.broadcasted_iota(jnp.int32, (tokens, LANES), 1)).astype(F32)
    down = lax.broadcasted_iota(jnp.int32, (tokens, tokens), 0)
    over = lax.broadcasted_iota(jnp.int32, (tokens, tokens), 1)
    earlier = contract((over < down).astype(F32).astype(BF16), picked.astype(BF16), 1, 0)
    rank = jnp.sum(earlier * picked, axis=1, keepdims=True)
    place = jnp.sum(base_ref[...] * picked, axis=1, keepdims=True) + rank
    place = jnp.where(rank < capacity, place, float(slots)).astype(jnp.int32)
    hot = (place == lax.broadcasted_iota(jnp.int32, (tokens, slots), 1)).astype(F32).astype(BF16)
    hot_ref[...] = hot
    packed[...] = contract(hot, cot_ref[...], 0, 0).astype(BF16).reshape(packed.shape)
    wide = []
    mine = pl.ds(row * capacity, capacity)
    for e in range(own):
        for k in range(1, across):
            to = lax.rem(row + k, across)
            wide.append(
                remote(
                    packed.at[e, pl.ds(to * capacity, capacity)],
                    rows_ref.at[e, mine],
                    wide_send.at[e, k - 1],
                    wide_recv.at[e, k - 1],
                    {"wide": to},
                )
            )
    stay = [pltpu.make_async_copy(packed.at[e, mine], rows_ref.at[e, mine], local.at[2 + e]) for e in range(own)]
    for copy in stay:
        copy.start()
    at = pl.ds(pl.multiple_of(part * cols, LANES), cols)
    for n, ref in enumerate((query_ref, key_ref, value_ref)):
        weights[n * cols : (n + 1) * cols, :] = ref[:, at].T

    for t in range(pairs):
        pair = twist(lax.div(me, 2), t, pairs)
        for b in range(2):
            if 2 * t + b:
                source = twist(me, 2 * t + b, total)
                await_recv(all_ref.at[source, part], recv.at[source])
                forward(source)
        for b in range(2):
            source = 2 * pair + b
            await_recv(all_ref.at[source, lax.rem(part + 1, parts)], pass_recv.at[source])
        block = all_ref[pl.ds(2 * pair, 2)].reshape(2 * parts * rows, width).astype(F32)
        normed = (block * inverse_rms(block) * gain_ref[...]).astype(BF16)
        here = pl.ds(pl.multiple_of(pair * (2 * parts * rows), LANES), 2 * parts * rows)
        flip_ref[:, here] = normed.T
        projected = contract(weights[...], normed, 1, 1).astype(BF16)
        qkv_ref[:, :, :, here] = projected.reshape(3, heads, size, 2 * parts * rows)
    for copy in sent + passed:
        copy.wait_send()
    for copy in wide + stay:
        copy.wait()


def begin(blocks, w_query, w_key, w_value, gain, routes, base, cot, heads, size, own, capacity):
    total, rows, width = blocks.shape
    tokens = cot.shape[0]
    across = lax.axis_size("wide")
    slots = own * across * capacity
    length = total * 2 * rows
    vmem = pl.BlockSpec(memory_space=pltpu.VMEM)
    sems = pltpu.SemaphoreType.DMA
    return pl.pallas_call(
        functools.partial(begin_kernel, capacity),
        in_specs=[vmem] * 8,
        out_specs=[vmem] * 6,
        out_shape=[
            jax.ShapeDtypeStruct((total, 2, rows, width), BF16),
            jax.ShapeDtypeStruct((3, heads, size, length), BF16),
            jax.ShapeDtypeStruct((width, length), BF16),
            jax.ShapeDtypeStruct((tokens, slots), BF16),
            jax.ShapeDtypeStruct((own, across * capacity, width), BF16),
            jax.ShapeDtypeStruct((3 * heads * size, width), BF16),
        ],
        scratch_shapes=[
            pltpu.VMEM((own, across * capacity, width), BF16),
            sems((total,)),
            sems((total,)),
            sems((total,)),
            sems((total,)),
            sems((own, across - 1)),
            sems((own, across - 1)),
            sems((2 + own,)),
        ],
        compiler_params=pltpu.CompilerParams(collective_id=6, has_side_effects=True, vmem_limit_bytes=62 << 20),
        cost_estimate=pl.CostEstimate(flops=4 << 30, bytes_accessed=80 << 20, transcendentals=0),
        name="begin",
    )(blocks, w_query, w_key, w_value, gain, routes, base, cot)


def finish_kernel(
    seqs,
    three_ref,
    flip_ref,
    weight_ref,
    x_ref,
    gain_ref,
    early_ref,
    tiny_ref,
    table_ref,
    router_ref,
    *refs,
):
    own, steps = 2, 2 * seqs - 1
    rows_refs = refs[: steps - 2]
    cots_refs = refs[steps - 2 : steps - 2 + 3 + own * (steps - 3)]
    finish_rest(
        seqs,
        rows_refs,
        cots_refs,
        three_ref,
        flip_ref,
        weight_ref,
        x_ref,
        gain_ref,
        early_ref,
        tiny_ref,
        table_ref,
        router_ref,
        *refs[len(rows_refs) + len(cots_refs) :],
    )


def finish_rest(
    seqs,
    rows_refs,
    cots_refs,
    three_ref,
    flip_ref,
    weight_ref,
    x_ref,
    gain_ref,
    early_ref,
    tiny_ref,
    table_ref,
    router_ref,
    in_ref,
    out_ref,
    home_ref,
    late_all,
    early_all,
    tiny,
    grad_in_ref,
    grad_out_ref,
    grads,
    near,
    summed,
    gw,
    wide_got,
    wide_sum,
    far_got,
    early_got,
    mine,
    early_mine,
    tiny_got,
    rows_held,
    cots_held,
    in_held,
    out_held,
    sums,
    total_in,
    leaving,
    share_got,
    share_sems,
    near_sems,
    home_sems,
    wide_sems,
    far_sems,
    early_sems,
    last_sems,
    last_early_sems,
    tiny_sems,
    held_sems,
    line_sems,
    local,
):
    total, across = lax.axis_size("seq"), lax.axis_size("wide")
    parts = total // seqs
    me, row = lax.axis_index("seq"), lax.axis_index("wide")
    part, seq = lax.rem(me, parts), lax.div(me, parts)
    other = twist(me, 1, total)
    width = gain_ref.shape[1]
    slim = gw.shape[2]
    own = in_ref.shape[0]
    share = in_ref.shape[2] // total
    cols = three_ref.shape[1] // 3
    half = three_ref.shape[0] // 2

    def seq_at(k):
        return lax.rem(seq + k, seqs) * parts + part

    def row_at(k):
        return lax.rem(row + k, across)

    def part_at(k):
        return me - part + lax.rem(part + k, parts)

    at = pl.ds(pl.multiple_of(lax.div(me, 2) * (2 * share), LANES), 2 * share)
    weights = [
        pltpu.make_async_copy(in_ref.at[:, :, at], in_held, local.at[0]),
        pltpu.make_async_copy(out_ref.at[:, at, :], out_held, local.at[1]),
    ]
    for copy in weights:
        copy.start()

    def load_rows(e, n, k):
        return pltpu.make_async_copy(rows_refs[k].at[e], rows_held.at[e, n], held_sems.at[0, e, n])

    def load_cots(e, n, k):
        src = cots_refs[k].at[e] if k < 3 else cots_refs[3 + own * (k - 3) + e]
        return pltpu.make_async_copy(src, cots_held.at[e, n], held_sems.at[1, e, n])

    last_place = seqs - 1
    far_end = jnp.logical_or(seq == 0, seq == last_place)
    for e in range(own):
        load_rows(e, 0, 0).start()
        load_cots(e, 0, 0).start()
        for here in range(seqs):

            @pl.when(seq == here)
            def _():
                sources = [2 * k - 1 for k in range(1, here + 1)] + [2 * k for k in range(1, seqs - here)]
                for n, k in enumerate(sources):
                    load_cots(e, n + 1, k).start()
                    if k < len(rows_refs):
                        load_rows(e, n + 1, k).start()

    pairs = [(a, b) for a in range(across) for b in range(parts) if a or b]
    peers = [{"seq": lax.rem(me + k, total)} for k in range(1, total)]
    peers += [{"wide": row_at(k)} for k in range(1, across)]
    peers += [{"wide": row_at(a), "seq": part_at(b)} for a, b in pairs if a and b]
    meet(peers)

    def far_rows(e, up):
        src = rows_refs[3 if up else 4].at[e]
        to = lax.rem(me + (parts if up else total - parts), total)
        return pltpu.make_async_remote_copy(
            src, rows_held.at[e, last_place], line_sems.at[0, e], line_sems.at[1, e], device_id={"seq": to}, device_id_type=MESH
        )

    for e in range(own):

        @pl.when(seq == last_place - 1)
        def _():
            far_rows(e, True).start()

        @pl.when(seq == 1)
        def _():
            far_rows(e, False).start()

    late = contract(flip_ref[...], three_ref[...], 1, 0).astype(BF16)
    gw[...] = late.reshape(gw.shape)
    wide_copies = [
        remote(gw.at[:, row_at(k)], wide_got.at[k - 1], wide_sems.at[0, k - 1], wide_sems.at[1, k - 1], {"wide": row_at(k)})
        for k in range(1, across)
    ]

    gain = gain_ref[...]
    gain_grad = jnp.zeros((1, width), F32)
    near_copies = []
    for n in range(2):
        scaled = contract(three_ref[n * half : (n + 1) * half, :], weight_ref[...], 1, 0)
        x = x_ref[n * total // 2 : (n + 1) * total // 2].reshape(half, width).astype(F32)
        inverse = inverse_rms(x)
        gain_grad = gain_grad + jnp.sum(scaled * x * inverse, axis=0, keepdims=True)
        scaled = scaled * gain
        mean_inner = jnp.mean(x * scaled, axis=-1, keepdims=True)
        value = inverse * scaled - x * (inverse * inverse * inverse) * mean_inner
        here = pl.ds(n * total // 2, total // 2)
        grads[here] = value.astype(BF16).reshape(total // 2, *grads.shape[1:])
        near_copies.append(
            remote(
                grads.at[here, lax.rem(part + 1, parts)],
                near.at[here],
                near_sems.at[0, n],
                near_sems.at[1, n],
                {"seq": other},
            )
        )
    lines = tiny_ref.shape[0]
    first = lax.broadcasted_iota(jnp.int32, tiny_ref.shape, 0) == 0
    tiny[:lines, :] = jnp.where(first, gain_grad, tiny_ref[...]).astype(BF16)
    table = table_ref[...]
    tiny[lines:, :] = jnp.concatenate([table, jnp.zeros((table.shape[0], width - table.shape[1]), F32)], axis=1).astype(BF16)

    def pass_tiny(stage, wheres):
        return [
            remote(tiny, tiny_got.at[stage, n], tiny_sems.at[0, stage, n], tiny_sems.at[1, stage, n], where)
            for n, where in enumerate(wheres)
        ]

    def take_tiny(stage, copies):
        for copy in copies:
            copy.wait()
        value = tiny[...].astype(F32)
        for n in range(len(copies)):
            value = value + tiny_got[stage, n].astype(F32)
        tiny[...] = value.astype(BF16)

    tiny_copies = pass_tiny(0, [{"wide": row_at(k)} for k in range(1, across)])
    for copy in near_copies:
        copy.wait()
    home_copies = []
    for k in range(total - 1, -1, -1):
        to = twist(me, k, total)
        summed[to] = (grads[to, part].astype(F32) + near[to].astype(F32)).astype(BF16)
        if k:
            home_copies.append(
                remote(summed.at[to], home_ref.at[me], home_sems.at[0, k - 1], home_sems.at[1, k - 1], {"seq": to})
            )
    kept = pltpu.make_async_copy(summed.at[me], home_ref.at[me], local.at[2])
    kept.start()
    for copy in weights:
        copy.wait()

    mine_rows = pl.ds(pl.multiple_of(part * share, LANES), share)
    other_rows = pl.ds(pl.multiple_of((1 - part) * share, LANES), share)

    def share_turn(e, n):
        some = rows_held.shape[1] // 2
        for m in range(n * some, (n + 1) * some):
            load_cots(e, m, 0).wait()
            if m < last_place:
                load_rows(e, m, 0).wait()
            else:

                @pl.when(far_end)
                def _():
                    far_rows(e, True).wait_recv()

                @pl.when(jnp.logical_not(far_end))
                def _():
                    load_rows(e, m, 0).wait()

        count = some * rows_held.shape[2]
        here = slice(n * some, (n + 1) * some)
        rows = rows_held[e, here].reshape(count, width)
        cots = gated(rows, cots_held[e, here].reshape(count, width), router_ref[...], row * own + e)
        hidden, slope = activation(contract(in_held[e].T, rows, 1, 1))
        grad_hidden = contract(out_held[e], cots, 1, 1).astype(BF16).astype(F32)
        part_out = contract(hidden.astype(BF16), cots, 1, 0)
        part_in = contract((grad_hidden * slope).astype(BF16), rows, 1, 0)
        if n == 0:
            sums[e, 0] = part_out
            sums[e, 1] = part_in
            return []
        sums[e, 0] += part_out
        sums[e, 1] += part_in
        grad_out_ref[e] = sums[e, 0, mine_rows, :]
        total_in[e] = sums[e, 1, mine_rows, :]
        copies = []
        for k in range(2):
            leaving[e, k] = sums[e, k, other_rows, :].astype(BF16)
            copies.append(
                remote(leaving.at[e, k], share_got.at[e, k], share_sems.at[0, e, k], share_sems.at[1, e, k], {"seq": other})
            )
        return copies

    def share_end(e, copies):
        for copy in copies:
            copy.wait()
        grad_out_ref[e] += share_got[e, 0].astype(F32)
        grad_in_ref[e] = (total_in[e] + share_got[e, 1].astype(F32)).T

    share_turn(0, 0)
    share_turn(1, 0)
    take_tiny(0, tiny_copies)
    for copy in wide_copies:
        copy.wait_recv()
    far_copies = []
    for k in list(range(1, seqs)) + [0]:
        place = lax.rem(seq + k, seqs)
        for p in range(parts):
            block = place * parts + p
            value = gw[block, row].astype(F32)
            for j in range(across - 1):
                value = value + wide_got[j, block].astype(F32)
            wide_sum[place, p] = value.astype(BF16)
        if k:
            where = {"seq": seq_at(k)}
            far_copies.append(
                remote(wide_sum.at[place], far_got.at[k - 1], far_sems.at[0, k - 1], far_sems.at[1, k - 1], where)
            )
            far_copies.append(
                remote(early_ref.at[place], early_got.at[k - 1], early_sems.at[0, k - 1], early_sems.at[1, k - 1], where)
            )
    tiny_copies = pass_tiny(1, [{"seq": seq_at(k)} for k in range(1, seqs)])
    first_share = share_turn(0, 1)
    take_tiny(1, tiny_copies)
    for copy in far_copies:
        copy.wait_recv()
    for p in range(parts):
        value = wide_sum[seq, p].astype(F32)
        for j in range(seqs - 1):
            value = value + far_got[j, p].astype(F32)
        mine[p] = value.astype(BF16)
    value = early_ref[seq].astype(F32)
    for j in range(seqs - 1):
        value = value + early_got[j].astype(F32)
    early_mine[...] = value.astype(BF16)
    last = pass_tiny(2, [{"seq": part_at(k)} for k in range(1, parts)])
    count = len(last)
    for a, b in pairs:
        n = a * parts + b - 1
        last.append(
            remote(
                mine.at[lax.rem(part + b, parts)],
                late_all.at[row, part],
                last_sems.at[0, n],
                last_sems.at[1, n],
                {"wide": row_at(a), "seq": part_at(b)},
            )
        )
    for k in range(1, across):
        last.append(
            remote(
                early_mine, early_all.at[row], last_early_sems.at[0, k - 1], last_early_sems.at[1, k - 1], {"wide": row_at(k)}
            )
        )
    stay = [
        pltpu.make_async_copy(mine.at[part], late_all.at[row, part], local.at[3]),
        pltpu.make_async_copy(early_mine, early_all.at[row], local.at[4]),
    ]
    for copy in stay:
        copy.start()
    second_share = share_turn(1, 1)
    share_end(0, first_share)
    take_tiny(2, last[:count])
    share_end(1, second_share)
    for e in range(own):

        @pl.when(jnp.logical_or(seq == 1, seq == last_place - 1))
        def _():
            far_rows(e, True).wait_send()

    for copy in last[count:] + stay + home_copies + [kept]:
        copy.wait()
    for copy in wide_copies + far_copies:
        copy.wait_send()


def finish(three, flipped, weights, x, gain, early, tiny, table, router, rows, cots, w_in, w_out):
    columns = three.shape[1]
    total, parts, piece, width = x.shape
    seqs, slim, _ = early.shape
    across = lax.axis_size("wide")
    own, _, units = w_in.shape
    share = units // total
    vmem, hbm = pl.BlockSpec(memory_space=pltpu.VMEM), pl.BlockSpec(memory_space=pl.ANY)
    sems = pltpu.SemaphoreType.DMA
    most = max(across, seqs, parts) - 1
    lines = tiny.shape[0] + table.shape[0]
    return pl.pallas_call(
        functools.partial(finish_kernel, seqs),
        in_specs=[vmem] * 9 + [hbm] * (len(rows) + len(cots) + 2),
        out_specs=[vmem] * 6,
        out_shape=[
            jax.ShapeDtypeStruct((total, piece, width), BF16),
            jax.ShapeDtypeStruct((across, parts, slim, columns), BF16),
            jax.ShapeDtypeStruct((across, slim, width), BF16),
            jax.ShapeDtypeStruct((lines, width), BF16),
            jax.ShapeDtypeStruct((own, width, share), F32),
            jax.ShapeDtypeStruct((own, share, width), F32),
        ],
        scratch_shapes=[
            pltpu.VMEM((total, parts, piece, width), BF16),
            pltpu.VMEM((total, piece, width), BF16),
            pltpu.VMEM((total, piece, width), BF16),
            pltpu.VMEM((total, across, slim, columns), BF16),
            pltpu.VMEM((across - 1, total, slim, columns), BF16),
            pltpu.VMEM((seqs, parts, slim, columns), BF16),
            pltpu.VMEM((seqs - 1, parts, slim, columns), BF16),
            pltpu.VMEM((seqs - 1, slim, width), BF16),
            pltpu.VMEM((parts, slim, columns), BF16),
            pltpu.VMEM((slim, width), BF16),
            pltpu.VMEM((3, most, lines, width), BF16),
            pltpu.VMEM((own, seqs, *rows[0].shape[1:]), BF16),
            pltpu.VMEM((own, seqs, *cots[0].shape[1:]), BF16),
            pltpu.VMEM((own, width, 2 * share), BF16),
            pltpu.VMEM((own, 2 * share, width), BF16),
            pltpu.VMEM((own, 2, 2 * share, width), F32),
            pltpu.VMEM((own, share, width), F32),
            pltpu.VMEM((own, 2, share, width), BF16),
            pltpu.VMEM((own, 2, share, width), BF16),
            sems((2, own, 2)),
            sems((2, 2)),
            sems((2, total - 1)),
            sems((2, across - 1)),
            sems((2, seqs - 1)),
            sems((2, seqs - 1)),
            sems((2, across * parts - 1)),
            sems((2, across - 1)),
            sems((2, 3, most)),
            sems((2, own, seqs)),
            sems((2, own)),
            sems((5,)),
        ],
        compiler_params=pltpu.CompilerParams(collective_id=1, has_side_effects=True, vmem_limit_bytes=62 << 20),
        cost_estimate=pl.CostEstimate(flops=16 << 30, bytes_accessed=60 << 20, transcendentals=0),
        name="finish",
    )(three, flipped, weights, x, gain, early, tiny, table, router, *rows, *cots, w_in, w_out)


def close_kernel(
    heads,
    home_ref,
    middle_ref,
    late_ref,
    early_ref,
    tiny_ref,
    in_ref,
    out_ref,
    inputs_ref,
    query_ref,
    key_ref,
    value_ref,
    output_ref,
    gain_one_ref,
    gain_two_ref,
    router_ref,
    table_ref,
    grad_in_ref,
    grad_out_ref,
    sems,
):
    copies = [
        pltpu.make_async_copy(in_ref, grad_in_ref, sems.at[0]),
        pltpu.make_async_copy(out_ref, grad_out_ref, sems.at[1]),
    ]
    for copy in copies:
        copy.start()
    me = lax.axis_index("seq")
    across, parts, slim, columns = late_ref.shape
    cols = columns // 3
    inputs_ref[...] = middle_ref[...] + home_ref[...].reshape(middle_ref.shape).astype(F32)
    for a in range(across):
        here = slice(a * slim, (a + 1) * slim)
        for p in range(parts):
            for n, ref in enumerate((query_ref, key_ref, value_ref)):
                ref[here, p * cols : (p + 1) * cols] = late_ref[a, p, :, n * cols : (n + 1) * cols].astype(F32)
        output_ref[here, :] = early_ref[a].astype(F32)
    width, piece = tiny_ref.shape[1], gain_one_ref.shape[1]
    chosen = lax.broadcasted_iota(jnp.int32, (width, piece), 0) == (
        lax.broadcasted_iota(jnp.int32, (width, piece), 1) + me * piece
    )
    picked = contract(tiny_ref[...], chosen.astype(F32).astype(BF16), 1, 0)
    gain_one_ref[...] = picked[0:1]
    gain_two_ref[...] = picked[1:2]
    router_ref[...] = picked[2 : 2 + router_ref.shape[0]]
    lines = table_ref.shape[0]
    chosen = lax.broadcasted_iota(jnp.int32, (lines, LANES), 1) == (
        lax.broadcasted_iota(jnp.int32, (lines, LANES), 0) + me * lines
    )
    table_ref[...] = contract(chosen.astype(F32).astype(BF16), tiny_ref[16:, :LANES], 1, 1)[:, :heads]
    for copy in copies:
        copy.wait()


def close(home, middle, late, early, tiny, grad_in, grad_out, heads, buckets, experts):
    across, parts, slim, columns = late.shape
    width = early.shape[2]
    total = home.shape[0]
    rows = across * slim
    vmem, hbm = pl.BlockSpec(memory_space=pltpu.VMEM), pl.BlockSpec(memory_space=pl.ANY)
    shapes = [
        middle.shape,
        *[(rows, width)] * 4,
        (1, width // total),
        (1, width // total),
        (experts, width // total),
        (buckets // total, heads),
        grad_in.shape,
        grad_out.shape,
    ]
    return pl.pallas_call(
        functools.partial(close_kernel, heads),
        in_specs=[vmem] * 5 + [hbm] * 2,
        out_specs=[vmem] * 9 + [hbm] * 2,
        out_shape=[jax.ShapeDtypeStruct(shape, F32) for shape in shapes],
        scratch_shapes=[pltpu.SemaphoreType.DMA((2,))],
        compiler_params=pltpu.CompilerParams(vmem_limit_bytes=62 << 20),
        name="close",
    )(home, middle, late, early, tiny, grad_in, grad_out)


def ring_pairs(total, parts, shift):
    return [(i, i - i % parts + (i % parts + shift) % parts) for i in range(total)]


def pick(pieces, index):
    out = pieces[0]
    for k in range(1, len(pieces)):
        out = jnp.where(index == k, pieces[k], out)
    return out


def swap_parts(pieces, part, parts, total):
    near = [pick(pieces, part)]
    for k in range(1, parts):
        near.append(lax.ppermute(pick(pieces, (part + k) % parts), "seq", ring_pairs(total, parts, k)))
    return [pick(near, (part - j) % parts) for j in range(parts)]


def line_step(before, after, seqs, step):
    total = lax.axis_size("seq")
    parts = total // seqs
    up = [(i, i + parts) for i in range(total - parts) if i // parts >= step - 1]
    down = [(i, i - parts) for i in range(parts, total) if i // parts <= seqs - step]
    return [lax.ppermute(before, "seq", up), lax.ppermute(after, "seq", down)]


def per_device(
    inputs,
    routes,
    bucket_ids,
    gain_attn,
    w_query,
    w_key,
    w_value,
    w_output,
    rel_table,
    gain_ffn,
    w_router,
    w_in,
    w_out,
    cotangent,
):
    seqs, local_len, width = inputs.shape
    buckets, head_count = rel_table.shape
    size = width // head_count
    total = lax.axis_size("seq")
    across = lax.axis_size("wide")
    length = local_len * total
    parts = total // seqs
    heads = head_count // parts
    cols = heads * size
    me = lax.axis_index("seq")
    part = me % parts
    experts = w_router.shape[1]
    own_experts = w_in.shape[0]
    tokens = seqs * local_len
    capacity = (5 * tokens + 4 * experts - 1) // (4 * experts)
    slots = experts * capacity
    gain_one = gain_attn.astype(F32)
    gain_two = gain_ffn.astype(F32)

    fast = parts == 2 and capacity % 16 == 0 and own_experts == 2 and seqs == 4 and cols % LANES == 0 and local_len == LANES
    flat_cot = cotangent.reshape(tokens, width)
    chosen = routes.reshape(tokens)
    blocks = inputs.reshape(total, local_len // parts, width)

    if fast:
        first_slot = [(e % own_experts) * (across * capacity) + (e // own_experts) * capacity for e in range(experts)]
        base = jnp.array(first_slot + [0] * (LANES - experts), F32)[None]
        seq_in, qkv, flipped, slot_hot, cot_rows, own_weights = begin(
            blocks,
            w_query,
            w_key,
            w_value,
            gain_one[None],
            chosen[:, None],
            base,
            flat_cot,
            heads,
            size,
            own_experts,
            capacity,
        )
    else:
        own_weights = jnp.concatenate(
            [lax.dynamic_slice(w, (0, part * cols), (width, cols)) for w in (w_query, w_key, w_value)], axis=1
        )
        seq_in = spread(blocks, parts).reshape(length, width).astype(F32)
        inv_one = inverse_rms(seq_in)
        normed_one = (seq_in * inv_one * gain_one).astype(BF16)
        flipped = normed_one.T
        qkv = contract(own_weights, normed_one, 0, 1).astype(BF16).reshape(3, heads, size, length)
        picked = (chosen[:, None] == jnp.arange(experts, dtype=jnp.int32)[None, :]).astype(F32)
        order = jnp.arange(tokens, dtype=jnp.int32)
        before = (order[None, :] < order[:, None]).astype(BF16)
        earlier = jnp.dot(before, picked.astype(BF16), preferred_element_type=F32)
        rank_in = jnp.sum(earlier * picked, axis=1).astype(jnp.int32)
        place = (chosen % own_experts) * (across * capacity) + (chosen // own_experts) * capacity + rank_in
        slot_of = jnp.where(rank_in < capacity, place, slots)
        slot_hot = (slot_of[:, None] == jnp.arange(slots, dtype=jnp.int32)[None, :]).astype(BF16)
        packed = contract(slot_hot, flat_cot, 0, 0).astype(BF16).reshape(own_experts, across, capacity, width)
        cot_rows = jnp.stack([lax.all_to_all(packed[e], "wide", 0, 0, tiled=True) for e in range(own_experts)])
        cot_rows = cot_rows.reshape(own_experts, across * capacity, width)
    own_table = lax.dynamic_slice(rel_table, (0, part * heads), (buckets, heads))
    ids = jnp.concatenate([bucket_ids, jnp.full((1,), LANES, jnp.int32)])
    bucket_hot = (ids[None, :] == jnp.arange(LANES, dtype=jnp.int32)[:, None]).astype(BF16)
    reverse_hot = (ids[::-1][None, :] == jnp.arange(buckets, dtype=jnp.int32)[:, None]).astype(BF16)
    bias_line = contract(own_table, reverse_hot, 0, 0).reshape(heads, 1, 2 * length)
    outs, attended, exps, inverse = attend(qkv, bias_line, total)
    attended = attended.reshape(seqs, width, local_len)

    flat_in = inputs.reshape(tokens, width).astype(F32)
    middle = flat_in + jnp.einsum("sft,fe->ste", attended, w_output, preferred_element_type=F32).reshape(tokens, width)
    inv_two = inverse_rms(middle)
    normed_two = (middle * inv_two * gain_two).astype(BF16)
    router_probs = jax.nn.softmax(jnp.dot(normed_two, w_router, preferred_element_type=F32), axis=-1)
    picked = (chosen[:, None] == jnp.arange(experts, dtype=jnp.int32)[None, :]).astype(F32)
    gate_prob = jnp.sum(router_probs * picked, axis=1)
    upstream = flat_cot.astype(F32)
    packed = contract(slot_hot, normed_two, 0, 0).astype(BF16)
    if fast:
        near_cots = line_step(cot_rows, cot_rows, seqs, 1)
        received, *second = exchange(
            packed.reshape(own_experts, across * capacity, width), *near_cots, seqs
        )
        returned, *more = run_experts(received, cot_rows, w_router, w_in, w_out, *near_cots, seqs, 512)
        second = [second[0], more[0], second[1], more[1]]
        near_rows = more[2:]
        third = [line_step(second[e], second[2 + e], seqs, 3) for e in range(own_experts)]
        all_cots = [cot_rows, *near_cots, *second, third[0][0], third[1][0], third[0][1], third[1][1]]
        returned = returned.reshape(slots, 2 * width)
    else:
        packed = packed.reshape(own_experts, across, capacity, width)
        received, returned = [], []
        for e in range(own_experts):
            got = lax.all_to_all(packed[e], "wide", 0, 0, tiled=True).reshape(across * capacity, width)
            received.append(got)
            pair = run_expert(got, cot_rows[e], w_router, w_in, w_out, e, 512).reshape(across, capacity, 2 * width)
            returned.append(lax.all_to_all(pair, "wide", 0, 0, tiled=True).reshape(across * capacity, 2 * width))
        received, returned = jnp.stack(received), jnp.concatenate(returned, axis=0)
    token_rows = jnp.dot(slot_hot, returned, preferred_element_type=F32)
    selected, grad_token = token_rows[:, :width], token_rows[:, width:]
    output = (middle + gate_prob[:, None] * selected).astype(BF16).reshape(inputs.shape)
    grad_gate = jnp.sum(upstream * selected, axis=1)
    grad_logits = (grad_gate[:, None] * router_probs * (picked - gate_prob[:, None])).astype(BF16)
    grad_router = contract(grad_logits, normed_two, 0, 0)
    grad_normed_two = grad_token + contract(grad_logits, w_router, 1, 1)
    grad_mid_norm, grad_gain_two = norm_backward(middle, inv_two, gain_two, grad_normed_two)
    grad_middle = upstream + grad_mid_norm
    grad_branch = grad_middle.astype(BF16).reshape(seqs, local_len, width)
    grad_w_output = jnp.einsum("sft,ste->fe", attended, grad_branch, preferred_element_type=F32)
    share = width // total
    slim = share // across
    back = (exps, inverse, grad_branch, w_output.reshape(parts, cols, width), outs, qkv, bucket_hot)
    if fast:
        early = grad_w_output.astype(BF16).reshape(seqs, parts, across, slim, width)
        three, table, early, *far_rows = attend_back(*back, early, near_rows)
        all_rows = [received, *near_rows, *far_rows]
        tiny = jnp.concatenate(
            [jnp.zeros((1, width), F32), grad_gain_two[None], grad_router, jnp.zeros((14 - experts, width), F32)], axis=0
        )
        home, *found = finish(
            three,
            flipped,
            own_weights,
            seq_in,
            gain_one[None],
            early,
            tiny,
            table,
            w_router,
            all_rows,
            all_cots,
            w_in,
            w_out,
        )
        grad_inputs, *grads_qkvo, grad_gain_one, grad_gain_two, grad_router, grad_table, grad_in, grad_out = close(
            home, grad_middle, *found, head_count, buckets, experts
        )
        return (
            output,
            grad_inputs.reshape(inputs.shape),
            grad_gain_one[0],
            *grads_qkvo,
            grad_table,
            grad_gain_two[0],
            grad_router.T,
            grad_in,
            grad_out,
        )

    all_cots = lax.all_gather(cot_rows, "seq", axis=0)
    all_rows = lax.all_gather(received, "seq", axis=0)
    three, table = attend_back(*back, None, [])
    grad_normed_one = contract(three, own_weights, 1, 1)
    grad_in_norm, grad_gain_one = norm_backward(seq_in, inv_one, gain_one, grad_normed_one)
    pieces = grad_in_norm.astype(BF16).reshape(total, parts, local_len // parts, width)
    swapped = swap_parts([pieces[:, p] for p in range(parts)], part, parts, total)
    home = sum(p.astype(F32) for p in swapped).astype(BF16)
    home = lax.all_to_all(home, "seq", 0, 0, tiled=True).reshape(tokens, width).astype(F32)
    grad_projections = lax.dynamic_update_slice(
        jnp.zeros((width, 3, width), F32), contract(flipped, three, 1, 0).reshape(width, 3, cols), (0, 0, part * cols)
    )
    rows = [grad_projections[:, k] for k in range(3)]
    rows += [grad_w_output, grad_gain_one[:, None], grad_gain_two[:, None], grad_router.T]
    table = table.T[:buckets]
    rows, table = lax.psum((jnp.concatenate(rows, axis=1).astype(BF16), table.astype(BF16)), "wide")
    rows = lax.psum_scatter(rows, "seq", scatter_dimension=0, tiled=True).astype(F32)
    table = lax.psum_scatter(table, "seq", scatter_dimension=0, tiled=True).astype(F32)
    held = []
    for e in range(own_experts):
        held = run_share(
            me,
            all_rows.reshape(total * own_experts, *received.shape[1:]),
            all_cots.reshape(total * own_experts, *cot_rows.shape[1:]),
            w_router,
            w_in,
            w_out,
            e,
            held,
        )
    last = rows[:, 4 * width :]
    return (
        output,
        (grad_middle + home).reshape(inputs.shape),
        last[:, 0],
        *[rows[:, k * width : (k + 1) * width] for k in range(4)],
        table[:, :head_count],
        last[:, 1],
        last[:, 2 : 2 + experts],
        *held,
    )


def solution(mesh):
    in_specs = (
        P("wide", "seq", None),
        P("wide", "seq", None),
        P(),
        P(),
        P(),
        P(),
        P(),
        P(),
        P(),
        P(),
        P(),
        P("wide", None, None),
        P("wide", None, None),
        P("wide", "seq", None),
    )
    out_specs = (
        P("wide", "seq", None),
        P("wide", "seq", None),
        P("seq"),
        P("seq", None),
        P("seq", None),
        P("seq", None),
        P("seq", None),
        P("seq", None),
        P("seq"),
        P("seq", None),
        P("wide", None, "seq"),
        P("wide", "seq", None),
    )
    return jax.shard_map(
        per_device, mesh=mesh, in_specs=in_specs, out_specs=out_specs, check_vma=False
    )
```

```python
import functools

import jax
import jax.numpy as jnp
from jax import lax
from jax.experimental import pallas as pl
from jax.experimental.pallas import tpu as pltpu
from jax.sharding import PartitionSpec as P

EPSILON = 1e-06
F32 = jnp.float32
BF16 = jnp.bfloat16
LANES = 128


def contract(a, b, da, db):
    return lax.dot_general(a, b, (((da,), (db,)), ((), ())), preferred_element_type=F32)


def inverse_rms(source):
    return lax.rsqrt(jnp.mean(source * source, axis=-1, keepdims=True) + EPSILON)


def norm_backward(source, inv_rms, gain_vec, upstream):
    scaled = upstream * gain_vec
    gain_grad = jnp.sum(upstream * source * inv_rms, axis=0)
    mean_inner = jnp.mean(source * scaled, axis=-1, keepdims=True)
    return (inv_rms * scaled - source * (inv_rms * inv_rms * inv_rms) * mean_inner, gain_grad)


def smooth_act(values):
    return jax.nn.gelu(values, approximate=True)


MESH = pl.DeviceIdType.MESH


def remote(src, dst, send, recv, where):
    copy = pltpu.make_async_remote_copy(src, dst, send, recv, device_id=where, device_id_type=MESH)
    copy.start()
    return copy


def meet(peers):
    barrier = pltpu.get_barrier_semaphore()
    for where in peers:
        pl.semaphore_signal(barrier, inc=1, device_id=where, device_id_type=MESH)
    pl.semaphore_wait(barrier, len(peers))


def line_peers(parts):
    total, me = lax.axis_size("seq"), lax.axis_index("seq")
    return [{"seq": lax.rem(me + parts, total)}, {"seq": lax.rem(me - parts + total, total)}]


def pass_on(parts, up, down, sems):
    me = lax.axis_index("seq")
    z = lax.div(me, parts)

    def copy(n, src, dst, step):
        return pltpu.make_async_remote_copy(
            src, dst, sems.at[0, n], sems.at[1, n], device_id={"seq": me + step}, device_id_type=MESH
        )

    legs = [(0, *up, parts), (1, *down, -parts)]
    for n, low, high, src, dst, step in legs:

        @pl.when(jnp.logical_and(z >= low, z <= high))
        def _():
            copy(n, src, dst, step).start()

    def end():
        for n, low, high, src, dst, step in legs:
            move = 1 if step > 0 else -1

            @pl.when(jnp.logical_and(z >= low, z <= high))
            def _():
                copy(n, src, dst, step).wait_send()

            @pl.when(jnp.logical_and(z >= low + move, z <= high + move))
            def _():
                copy(n, src, dst, -step).wait_recv()

    return end


def far_first(total):
    return sorted(range(1, total), key=lambda k: -min(k, total - k))


def twist(a, b, total):
    out, bit = 0, 1
    while bit < total:
        out = out + lax.rem(lax.div(a, bit) + lax.div(b, bit), 2) * bit
        bit *= 2
    return out


def attend_kernel(seqs, *refs):
    refs = list(refs)
    qkv_ref, bias_ref = refs[:2]
    line_ref = refs.pop(2) if seqs else None
    out_ref, home_ref, exp_ref, inv_ref = refs[2:6]
    line_outs = [refs.pop(6) for _ in range(2)] if seqs else []
    strip, keys, scores, held, send, recv, local, exp_sems, *line_sems = refs[6:]
    _, heads, size, length = qkv_ref.shape
    total = lax.axis_size("seq")
    me = lax.axis_index("seq")
    tokens = out_ref.shape[3]
    width = 2 * tokens
    pairs = total // 2
    rows = 2 * length - tokens
    chunk = 256
    meet([{"seq": lax.rem(me + k, total)} for k in range(1, total)])
    if seqs:
        before, after = line_outs
        line_end = pass_on(
            total // seqs, (0, seqs - 2, line_ref.at[0], before), (1, seqs - 1, line_ref.at[0], after), line_sems[0]
        )

    def prepare(h, carry):
        keys[h] = qkv_ref[1, h].T
        for b in range(rows // tokens):
            start = 2 * length - 2 * tokens - tokens * b
            base = jnp.broadcast_to(bias_ref[h, :, start : start + 2 * tokens], (tokens, 2 * tokens))
            rolled = pltpu.roll(base, 0, 1, stride=1, stride_axis=0)
            strip[h, tokens * b : tokens * (b + 1), :] = rolled[:, tokens:]
        return carry

    lax.fori_loop(0, heads, prepare, 0)

    def store(slot, pair, h):
        return pltpu.make_async_copy(held.at[slot], exp_ref.at[pair, h], exp_sems.at[slot])

    def step(t, carry):
        pair = twist(lax.div(me, 2), pairs - 1 - t, pairs)
        at = pl.ds(pl.multiple_of(pair * width, tokens), width)

        def head(h, carry):
            count = t * heads + h
            slot = lax.rem(count, 2)

            @pl.when(count >= 2)
            def _():
                store(slot, pair, h).wait()

            query = qkv_ref[0, h, :, at]
            tops = [jnp.full((1, tokens), -jnp.inf, F32)] * 2
            for c in range(length // chunk):
                part = contract(keys[h, c * chunk : (c + 1) * chunk, :], query, 1, 0)
                for s in range(2):
                    row = pl.multiple_of(length - tokens - (pair * width + s * tokens) + c * chunk, tokens)
                    piece = part[:, s * tokens : (s + 1) * tokens] + strip[h, pl.ds(row, chunk), :]
                    scores[c * chunk : (c + 1) * chunk, s * tokens : (s + 1) * tokens] = piece
                    tops[s] = jnp.maximum(tops[s], jnp.max(piece, axis=0, keepdims=True))
            sums = [jnp.zeros((1, tokens), F32)] * 2
            for c in range(length // chunk):
                for s in range(2):
                    piece = scores[c * chunk : (c + 1) * chunk, s * tokens : (s + 1) * tokens]
                    grown = jnp.exp(piece - tops[s])
                    sums[s] = sums[s] + jnp.sum(grown, axis=0, keepdims=True)
                    held[slot, c * chunk : (c + 1) * chunk, s * tokens : (s + 1) * tokens] = grown.astype(BF16)
            store(slot, pair, h).start()
            mixed = contract(qkv_ref[2, h], held[slot], 1, 0)
            for s in range(2):
                inverse = 1.0 / sums[s]
                inv_ref[pair, h, :, s * tokens : (s + 1) * tokens] = inverse
                out_ref[2 * pair + s, h] = (mixed[:, s * tokens : (s + 1) * tokens] * inverse).astype(BF16)
            return carry

        lax.fori_loop(0, heads, head, 0)
        for s in range(2):
            to = 2 * pair + s
            k = twist(me, to, total)

            @pl.when(to != me)
            def _():
                pltpu.make_async_remote_copy(
                    out_ref.at[to], home_ref.at[me], send.at[k], recv.at[k], device_id={"seq": to}, device_id_type=MESH
                ).start()

        return carry

    lax.fori_loop(0, pairs, step, 0)
    own = pltpu.make_async_copy(out_ref.at[me], home_ref.at[me], local)
    own.start()
    for slot in range(2):
        store(slot, 0, 0).wait()

    def settle(k, carry):
        source = twist(me, k, total)
        pltpu.make_async_remote_copy(
            out_ref.at[source], home_ref.at[source], send.at[k], recv.at[k], device_id={"seq": source}, device_id_type=MESH
        ).wait()
        return carry

    lax.fori_loop(1, total, settle, 0)
    own.wait()
    if seqs:
        line_end()


def attend(qkv, bias_line, total, line, seqs):
    _, heads, size, length = qkv.shape
    tokens = length // total
    vmem, hbm = pl.BlockSpec(memory_space=pltpu.VMEM), pl.BlockSpec(memory_space=pl.ANY)
    return pl.pallas_call(
        functools.partial(attend_kernel, seqs if line else 0),
        in_specs=[vmem, vmem] + [hbm] * len(line),
        out_specs=[vmem, vmem, hbm, vmem] + [hbm] * (2 * len(line)),
        out_shape=[
            jax.ShapeDtypeStruct((total, heads, size, tokens), BF16),
            jax.ShapeDtypeStruct((total, heads, size, tokens), BF16),
            jax.ShapeDtypeStruct((total // 2, heads, length, 2 * tokens), BF16),
            jax.ShapeDtypeStruct((total // 2, heads, 1, 2 * tokens), F32),
            *[jax.ShapeDtypeStruct(rows.shape[1:], BF16) for rows in line for _ in range(2)],
        ],
        scratch_shapes=[
            pltpu.VMEM((heads, 2 * length - tokens, tokens), F32),
            pltpu.VMEM((heads, length, size), BF16),
            pltpu.VMEM((length, 2 * tokens), F32),
            pltpu.VMEM((2, length, 2 * tokens), BF16),
            pltpu.SemaphoreType.DMA((total,)),
            pltpu.SemaphoreType.DMA((total,)),
            pltpu.SemaphoreType.DMA,
            pltpu.SemaphoreType.DMA((2,)),
            *[pltpu.SemaphoreType.DMA((2, 2)) for _ in line],
        ],
        compiler_params=pltpu.CompilerParams(collective_id=2, has_side_effects=True, vmem_limit_bytes=62 << 20),
        cost_estimate=pl.CostEstimate(
            flops=4 * heads * length * length * size, bytes_accessed=2 * heads * length * length, transcendentals=heads * length * length
        ),
        name="attend",
    )(qkv, bias_line, *line)


def attend_back_kernel(fast, *refs):
    refs = list(refs)
    exp_ref, inv_ref, weight_ref, out_ref, qkv_ref, hot_ref = refs[:6]
    if fast:
        back_ref, slot_ref, middle_ref, normed_ref, router_ref, routes_ref, cot_ref, gain_ref, att_ref = refs[6:15]
        line_refs, far_refs = refs[15:17], refs[17:21]
        refs = refs[21:]
    else:
        branch_ref = refs[6]
        refs = refs[7:]
    three_ref, table_ref = refs[:2]
    if fast:
        early_out, output_ref, grad_middle_ref, tiny_ref = refs[2:6]
        line_outs, far_outs = refs[6:8], refs[8:12]
        refs = refs[12:]
    else:
        refs = refs[2:]
    leaving, got, strip, values, dq_all, dk_sum, dv_sum, scores, held, diagonal, send, recv, exp_sems = refs[:13]
    _, heads, size, length = qkv_ref.shape
    total = lax.axis_size("seq")
    me = lax.axis_index("seq")
    tokens = out_ref.shape[3]
    parts = weight_ref.shape[0]
    part = lax.rem(me, parts)
    width = 2 * tokens
    pairs = total // 2
    rows = 2 * length - tokens
    chunk = 256

    def pair_at(t):
        return twist(lax.div(me, 2), t, pairs)

    def load(count):
        slot = lax.rem(count, 2)
        at = exp_ref.at[pair_at(lax.div(count, heads)), lax.rem(count, heads)]
        return pltpu.make_async_copy(at, held.at[slot], exp_sems.at[slot])

    load(0).start()
    peers = [{"seq": lax.rem(me + k, total)} for k in range(1, total)]
    if fast:
        across, row = lax.axis_size("wide"), lax.axis_index("wide")
        other = twist(me, 1, total)
        peers += [{"wide": lax.rem(row + k, across)} for k in range(1, across)]
    meet(peers)
    if fast:
        branch_ref, early_ref, near, near_sum, wide_got, near_sems, wide_sems, line_sems, far_sems = refs[13:]
        seqs = early_ref.shape[0]

        def far_step(e):
            up, down = far_refs[e], far_refs[2 + e]
            return pass_on(
                parts, (seqs - 2, seqs - 2, up, far_outs[e]), (1, 1, down, far_outs[2 + e]), far_sems.at[e]
            )

        line_ends = [far_step(0)]

        def near_copy():
            return pltpu.make_async_remote_copy(
                early_ref.at[:, lax.rem(part + 1, parts)],
                near,
                near_sems.at[0],
                near_sems.at[1],
                device_id={"seq": other},
                device_id_type=MESH,
            )

        def wide_copy(k):
            to = lax.rem(row + k, across)
            return pltpu.make_async_remote_copy(
                near_sum.at[to],
                wide_got.at[k - 1],
                wide_sems.at[0, k - 1],
                wide_sems.at[1, k - 1],
                device_id={"wide": to},
                device_id_type=MESH,
            )

        features = middle_ref.shape[1]
        found = contract(slot_ref[...], back_ref[...].reshape(slot_ref.shape[1], 2 * features), 1, 0)
        selected = found[:, :features]
        logits = contract(normed_ref[...], router_ref[...], 1, 0)
        grown = jnp.exp(logits - jnp.max(logits, axis=1, keepdims=True))
        probs = grown / jnp.sum(grown, axis=1, keepdims=True)
        picked = (routes_ref[...] == lax.broadcasted_iota(jnp.int32, probs.shape, 1)).astype(F32)
        gate = jnp.sum(probs * picked, axis=1, keepdims=True)
        upstream = cot_ref[...].astype(F32)
        middle = middle_ref[...]
        output_ref[...] = (middle + gate * selected).astype(BF16)
        grad_gate = jnp.sum(upstream * selected, axis=1, keepdims=True)
        grad_logits = (grad_gate * probs * (picked - gate)).astype(BF16)
        grad_normed = found[:, features:] + contract(grad_logits, router_ref[...], 1, 1)
        inverse = inverse_rms(middle)
        gain_grad = jnp.sum(grad_normed * middle * inverse, axis=0, keepdims=True)
        grad_normed = grad_normed * gain_ref[...]
        mean_inner = jnp.mean(middle * grad_normed, axis=-1, keepdims=True)
        grad_middle = upstream + inverse * grad_normed - middle * (inverse * inverse * inverse) * mean_inner
        grad_middle_ref[...] = grad_middle
        branch = grad_middle.astype(BF16)
        branch_ref[...] = branch.reshape(branch_ref.shape)

    def product(to):
        value = contract(weight_ref[lax.rem(to, parts)], branch_ref[lax.div(to, parts)], 1, 1)
        return value.astype(BF16).reshape(heads, size, tokens)

    def leave(k, carry):
        to = twist(me, k, total)
        leaving[to] = product(to)
        pltpu.make_async_remote_copy(
            leaving.at[to], got.at[me], send.at[k], recv.at[k], device_id={"seq": to}, device_id_type=MESH
        ).start()
        return carry

    lax.fori_loop(1, total, leave, 0)
    if fast:
        for e in range(line_refs[0].shape[0]):
            up, down = ((1, seqs - 2, line_refs[n].at[e], line_outs[n].at[e]) for n in range(2))
            line_ends.append(pass_on(parts, up, down, line_sems.at[e]))
        line_ends.append(far_step(1))
        attended = jnp.concatenate([att_ref[s] for s in range(seqs)], axis=1)
        early_ref[...] = contract(attended, branch, 1, 0).astype(BF16).reshape(early_ref.shape)
        near_copy().start()
        grad_router = contract(grad_logits, normed_ref[...], 0, 0)
        spare = tiny_ref.shape[0] - 2 - grad_router.shape[0]
        tiny_ref[...] = jnp.concatenate(
            [jnp.zeros((1, features), F32), gain_grad, grad_router, jnp.zeros((spare, features), F32)], axis=0
        )
    got[me] = product(me)

    def prepare(h, carry):
        values[h] = qkv_ref[2, h].T
        strip[h] = jnp.zeros(strip.shape[1:], F32)
        dk_sum[h] = jnp.zeros(dk_sum.shape[1:], F32)
        dv_sum[h] = jnp.zeros(dv_sum.shape[1:], F32)
        return carry

    lax.fori_loop(0, heads, prepare, 0)

    def arrive(k):
        source = twist(me, k, total)
        pltpu.make_async_remote_copy(
            leaving.at[source], got.at[source], send.at[k], recv.at[k], device_id={"seq": source}, device_id_type=MESH
        ).wait()

    def step(t, carry):
        pair = pair_at(t)
        at = pl.ds(pl.multiple_of(pair * width, tokens), width)

        @pl.when(t > 0)
        def _():
            arrive(2 * t)

        arrive(2 * t + 1)
        if fast:

            @pl.when(t == 1)
            def _():
                near_copy().wait()
                for n in range(seqs):
                    for a in range(across):
                        value = early_ref[n, part, a].astype(F32) + near[n, a].astype(F32)
                        near_sum[a, n] = value.astype(BF16)
                for k in range(1, across):
                    wide_copy(k).start()

            @pl.when(t == pairs - 1)
            def _():
                for k in range(1, across):
                    wide_copy(k).wait()
                for n in range(seqs):
                    value = near_sum[row, n].astype(F32)
                    for k in range(1, across):
                        value = value + wide_got[k - 1, n].astype(F32)
                    early_out[n] = value.astype(BF16)

        def head(h, carry):
            count = t * heads + h
            slot = lax.rem(count, 2)

            @pl.when(count + 1 < pairs * heads)
            def _():
                load(count + 1).start()

            grads, inner = [], []
            for s in range(2):
                inverse = inv_ref[pair, h, :, s * tokens : (s + 1) * tokens]
                scaled = got[2 * pair + s, h].astype(F32) * inverse
                inner.append(jnp.sum(scaled * out_ref[2 * pair + s, h].astype(F32), axis=0, keepdims=True))
                grads.append(scaled.astype(BF16))
            grad = jnp.concatenate(grads, axis=1)
            load(count).wait()
            for c in range(length // chunk):
                part_grad = contract(values[h, c * chunk : (c + 1) * chunk, :], grad, 1, 0)
                for s in range(2):
                    grown = held[slot, c * chunk : (c + 1) * chunk, s * tokens : (s + 1) * tokens].astype(F32)
                    slope = grown * (part_grad[:, s * tokens : (s + 1) * tokens] - inner[s])
                    line = pl.multiple_of(length - tokens - (pair * width + s * tokens) + c * chunk, tokens)
                    strip[h, pl.ds(line, chunk), :] += slope
                    scores[c * chunk : (c + 1) * chunk, s * tokens : (s + 1) * tokens] = slope.astype(BF16)
            dq_all[h, at, :] = contract(qkv_ref[1, h], scores[...], 1, 0).T.astype(BF16)
            dk_sum[h] += contract(scores[...], qkv_ref[0, h, :, at].T, 1, 0)
            dv_sum[h] += contract(held[slot], grad.T, 1, 0)
            return carry

        lax.fori_loop(0, heads, head, 0)
        return carry

    lax.fori_loop(0, pairs, step, 0)
    down = lax.broadcasted_iota(jnp.int32, (tokens, tokens), 0)
    over = lax.broadcasted_iota(jnp.int32, (tokens, tokens), 1)
    mirror = (down + over == tokens - 1).astype(F32)
    cols = heads * size
    for c in range(length // chunk):
        here = slice(c * chunk, (c + 1) * chunk)
        for n, ref in enumerate((dq_all, dk_sum, dv_sum)):
            joined = jnp.concatenate([ref[h, here, :].astype(F32) for h in range(heads)], axis=1)
            three_ref[here, n * cols : (n + 1) * cols] = joined.astype(BF16)

    def close(h, carry):
        diagonal[h] = jnp.zeros(diagonal.shape[1:], F32)
        for b in range(rows // tokens):
            flipped = lax.dot_general(
                strip[h, tokens * b : tokens * (b + 1), :],
                mirror,
                (((1,), (0,)), ((), ())),
                precision=lax.Precision.HIGHEST,
                preferred_element_type=F32,
            )
            spread_out = jnp.concatenate([flipped, jnp.zeros_like(flipped)], axis=1)
            rolled = pltpu.roll(spread_out, 0, 1, stride=1, stride_axis=0)
            diagonal[h, :, tokens * b : tokens * (b + 2)] += jnp.sum(rolled, axis=0, keepdims=True)
        return carry

    lax.fori_loop(0, heads, close, 0)
    sums = jnp.concatenate([diagonal[h] for h in range(heads)], axis=0)
    table = lax.dot_general(
        sums,
        hot_ref[...].astype(F32),
        (((1,), (1,)), ((), ())),
        precision=lax.Precision.HIGHEST,
        preferred_element_type=F32,
    )
    line = lax.broadcasted_iota(jnp.int32, (table_ref.shape[0], heads), 0)
    head_line = lax.broadcasted_iota(jnp.int32, (table_ref.shape[0], heads), 1) + part * heads
    table_ref[...] = lax.dot_general(
        (line == head_line).astype(F32),
        table,
        (((1,), (0,)), ((), ())),
        precision=lax.Precision.HIGHEST,
        preferred_element_type=F32,
    )
    if fast:
        for end in line_ends:
            end()


def attend_back(exps, inverse, weight, outs, qkv, hot, branch, more, line, far):
    _, heads, size, length = qkv.shape
    total, tokens = outs.shape[0], outs.shape[3]
    parts, cols, width = weight.shape
    vmem, hbm = pl.BlockSpec(memory_space=pltpu.VMEM), pl.BlockSpec(memory_space=pl.ANY)
    sems = pltpu.SemaphoreType.DMA
    out_shape = [
        jax.ShapeDtypeStruct((length, 3 * heads * size), BF16),
        jax.ShapeDtypeStruct((16, hot.shape[0]), F32),
    ]
    given, scratch = [branch], []
    if branch is None:
        given = more
        across = lax.axis_size("wide")
        slim = width // total // across
        seqs = total // parts
        count = seqs * tokens
        out_shape += [
            jax.ShapeDtypeStruct((seqs, slim, width), BF16),
            jax.ShapeDtypeStruct((count, width), BF16),
            jax.ShapeDtypeStruct((count, width), F32),
            jax.ShapeDtypeStruct((16, width), F32),
        ]
        scratch = [
            pltpu.VMEM((seqs, tokens, width), BF16),
            pltpu.VMEM((seqs, parts, across, slim, width), BF16),
            pltpu.VMEM((seqs, across, slim, width), BF16),
            pltpu.VMEM((across, seqs, slim, width), BF16),
            pltpu.VMEM((across - 1, seqs, slim, width), BF16),
            sems((2,)),
            sems((2, across - 1)),
            sems((line[0].shape[0], 2, 2)),
            sems((len(far) // 2, 2, 2)),
        ]
    passed = [*line, *far]
    in_place = len(out_shape)
    out_shape += [jax.ShapeDtypeStruct(rows.shape, BF16) for rows in passed]
    return pl.pallas_call(
        functools.partial(attend_back_kernel, branch is None),
        in_specs=[hbm] + [vmem] * (5 + len(given)) + [hbm] * len(passed),
        out_specs=[vmem] * in_place + [hbm] * len(passed),
        out_shape=out_shape,
        scratch_shapes=[
            pltpu.VMEM((total, heads, size, tokens), BF16),
            pltpu.VMEM((total, heads, size, tokens), BF16),
            pltpu.VMEM((heads, 2 * length - tokens, tokens), F32),
            pltpu.VMEM((heads, length, size), BF16),
            pltpu.VMEM((heads, length, size), BF16),
            pltpu.VMEM((heads, length, size), F32),
            pltpu.VMEM((heads, length, size), F32),
            pltpu.VMEM((length, 2 * tokens), BF16),
            pltpu.VMEM((2, length, 2 * tokens), BF16),
            pltpu.VMEM((heads, 1, 2 * length), F32),
            sems((total,)),
            sems((total,)),
            sems((2,)),
            *scratch,
        ],
        compiler_params=pltpu.CompilerParams(collective_id=3, has_side_effects=True, vmem_limit_bytes=62 << 20),
        cost_estimate=pl.CostEstimate(
            flops=8 * heads * length * length * size, bytes_accessed=2 * heads * length * length, transcendentals=0
        ),
        name="attend_back",
    )(exps, inverse, weight, outs, qkv, hot, *given, *passed)


def activation(v):
    square = v * v
    bent = jnp.tanh(0.7978845608 * v * (1.0 + 0.044715 * square))
    half = 0.5 * (1.0 + bent)
    slope = half + 0.5 * v * (1.0 - bent * bent) * (0.7978845608 * (1.0 + 3.0 * 0.044715 * square))
    return v * half, slope


def gated(rows, cots, router, expert):
    logits = contract(rows, router, 1, 0)
    grown = jnp.exp(logits - jnp.max(logits, axis=1, keepdims=True))
    named = lax.broadcasted_iota(jnp.int32, grown.shape, 1) == expert
    gate = jnp.sum(jnp.where(named, grown, 0.0), axis=1, keepdims=True) / jnp.sum(grown, axis=1, keepdims=True)
    return (gate * cots.astype(F32)).astype(BF16)


def expert_kernel(expert, rows_ref, cot_ref, router_ref, in_ref, out_ref, both_ref, forward, backward):
    step = pl.program_id(0)
    width = cot_ref.shape[1]

    @pl.when(step == 0)
    def _():
        forward[...] = jnp.zeros_like(forward)
        backward[...] = jnp.zeros_like(backward)

    rows = rows_ref[...]
    own = router_ref.shape[1] // lax.axis_size("wide")
    grads = gated(rows, cot_ref[...], router_ref[...], lax.axis_index("wide") * own + expert)
    hidden, slope = activation(contract(rows, in_ref[0], 1, 0))
    grad_hidden = contract(grads, out_ref[0], 1, 1).astype(BF16).astype(F32)
    forward[...] += contract(hidden.astype(BF16), out_ref[0], 1, 0)
    backward[...] += contract((grad_hidden * slope).astype(BF16), in_ref[0], 1, 1)

    @pl.when(step == pl.num_programs(0) - 1)
    def _():
        both_ref[:, :width] = forward[...].astype(BF16)
        both_ref[:, width:] = backward[...].astype(BF16)


def run_expert(rows, cots, router, w_in, w_out, expert, block):
    count, width = cots.shape
    units = w_in.shape[2]
    return pl.pallas_call(
        functools.partial(expert_kernel, expert),
        grid=(units // block,),
        in_specs=[
            pl.BlockSpec(rows.shape, lambda f: (0, 0)),
            pl.BlockSpec(cots.shape, lambda f: (0, 0)),
            pl.BlockSpec(router.shape, lambda f: (0, 0)),
            pl.BlockSpec((1, width, block), lambda f: (expert, 0, f)),
            pl.BlockSpec((1, block, width), lambda f: (expert, f, 0)),
        ],
        out_specs=pl.BlockSpec((count, 2 * width), lambda f: (0, 0)),
        out_shape=jax.ShapeDtypeStruct((count, 2 * width), BF16),
        scratch_shapes=[pltpu.VMEM((count, width), F32), pltpu.VMEM((count, width), F32)],
        compiler_params=pltpu.CompilerParams(vmem_limit_bytes=40 << 20),
        name="expert",
    )(rows, cots, router, w_in, w_out)


def route_kernel(
    capacity,
    own,
    att_ref,
    weight_ref,
    in_ref,
    gain_ref,
    hot_ref,
    cot_ref,
    before_ref,
    after_ref,
    middle_ref,
    normed_ref,
    out_ref,
    second_before,
    second_after,
    next_before,
    next_after,
    packed,
    send,
    recv,
    local,
    line_sems,
):
    seqs = att_ref.shape[0]
    across = lax.axis_size("wide")
    parts = lax.axis_size("seq") // seqs
    me = lax.axis_index("wide")
    meet([{"wide": lax.rem(me + k, across)} for k in range(1, across)] + line_peers(parts))
    line_ends = [
        pass_on(parts, (0, seqs - 2, cot_ref.at[1], next_before), (1, seqs - 1, cot_ref.at[1], next_after), line_sems.at[0]),
        pass_on(parts, (1, seqs - 2, before_ref, second_before), (1, seqs - 2, after_ref, second_after), line_sems.at[1]),
    ]
    attended = jnp.concatenate([att_ref[s] for s in range(seqs)], axis=1)
    middle = in_ref[...].astype(F32) + contract(attended, weight_ref[...], 0, 0)
    middle_ref[...] = middle
    normed = (middle * inverse_rms(middle) * gain_ref[...]).astype(BF16)
    normed_ref[...] = normed
    packed[...] = contract(hot_ref[...], normed, 0, 0).astype(BF16).reshape(packed.shape)
    copies = []
    mine = pl.ds(me * capacity, capacity)
    for n in range(own):
        for k in range(1, across):
            to = lax.rem(me + k, across)
            copies.append(
                remote(
                    packed.at[n, pl.ds(to * capacity, capacity)],
                    out_ref.at[n, mine],
                    send.at[n, k - 1],
                    recv.at[n, k - 1],
                    {"wide": to},
                )
            )
    kept = [pltpu.make_async_copy(packed.at[n, mine], out_ref.at[n, mine], local.at[n]) for n in range(own)]
    for copy in kept:
        copy.start()
    for copy in kept + copies:
        copy.wait()
    for end in line_ends:
        end()


def route(attended, weight, tokens_in, gain, hot, cots, before, after, capacity):
    across = lax.axis_size("wide")
    own = cots.shape[0]
    tokens, width = tokens_in.shape
    vmem, hbm = pl.BlockSpec(memory_space=pltpu.VMEM), pl.BlockSpec(memory_space=pl.ANY)
    one = jax.ShapeDtypeStruct(before.shape, before.dtype)
    sems = pltpu.SemaphoreType.DMA
    return pl.pallas_call(
        functools.partial(route_kernel, capacity, own),
        in_specs=[vmem] * 5 + [hbm] * 3,
        out_specs=[vmem, vmem] + [hbm] * 5,
        out_shape=[
            jax.ShapeDtypeStruct((tokens, width), F32),
            jax.ShapeDtypeStruct((tokens, width), BF16),
            jax.ShapeDtypeStruct(cots.shape, BF16),
            *[one] * 4,
        ],
        scratch_shapes=[
            pltpu.VMEM(cots.shape, BF16),
            sems((own, across - 1)),
            sems((own, across - 1)),
            sems((own,)),
            sems((2, 2, 2)),
        ],
        compiler_params=pltpu.CompilerParams(collective_id=4, has_side_effects=True, vmem_limit_bytes=62 << 20),
        name="route",
    )(attended, weight, tokens_in, gain, hot, cots, before, after)


def experts_kernel(
    block,
    seqs,
    rows_ref,
    cot_ref,
    router_ref,
    in_ref,
    out_ref,
    line_ref,
    before_ref,
    after_ref,
    back_ref,
    before_out,
    after_out,
    line_before,
    line_after,
    done,
    grads,
    forward,
    backward,
    in_held,
    out_held,
    back_send,
    back_recv,
    local,
    held_sems,
    line_sems,
):
    own, rows, double = back_ref.shape
    width = double // 2
    across = lax.axis_size("wide")
    me = lax.axis_index("wide")
    count = rows // across
    steps = in_ref.shape[2] // block

    def load(at):
        slot = lax.rem(at, 2)
        expert, place = lax.div(at, steps), pl.multiple_of(lax.rem(at, steps) * block, block)
        return (
            pltpu.make_async_copy(in_ref.at[expert, :, pl.ds(place, block)], in_held.at[slot], held_sems.at[0, slot]),
            pltpu.make_async_copy(out_ref.at[expert, pl.ds(place, block), :], out_held.at[slot], held_sems.at[1, slot]),
        )

    for copy in load(0):
        copy.start()
    parts = lax.axis_size("seq") // seqs
    meet([{"wide": lax.rem(me + k, across)} for k in range(1, across)] + line_peers(parts))
    line_ends = [
        pass_on(
            parts,
            (1, seqs - 2, before_ref, before_out),
            (1, seqs - 2, after_ref, after_out),
            line_sems.at[0],
        ),
        pass_on(parts, (0, seqs - 2, line_ref, line_before), (1, seqs - 1, line_ref, line_after), line_sems.at[1]),
    ]
    coming = []
    mine = pl.ds(me * count, count)
    for e in range(own):
        grads[...] = gated(rows_ref[e], cot_ref[e], router_ref[...], me * own + e)
        forward[...] = jnp.zeros_like(forward)
        backward[...] = jnp.zeros_like(backward)

        def step(f, carry):
            at = e * steps + f
            slot = lax.rem(at, 2)

            @pl.when(at + 1 < own * steps)
            def _():
                for copy in load(at + 1):
                    copy.start()

            for copy in load(at):
                copy.wait()
            hidden, slope = activation(contract(rows_ref[e], in_held[slot], 1, 0))
            grad_hidden = contract(grads[...], out_held[slot], 1, 1).astype(BF16).astype(F32)
            forward[...] += contract(hidden.astype(BF16), out_held[slot], 1, 0)
            backward[...] += contract((grad_hidden * slope).astype(BF16), in_held[slot], 1, 1)
            return carry

        lax.fori_loop(0, steps, step, 0)
        done[e, :, :width] = forward[...].astype(BF16)
        done[e, :, width:] = backward[...].astype(BF16)
        for k in range(1, across):
            to = lax.rem(me + k, across)
            coming.append(
                remote(
                    done.at[e, pl.ds(to * count, count)],
                    back_ref.at[e, mine],
                    back_send.at[e, k - 1],
                    back_recv.at[e, k - 1],
                    {"wide": to},
                )
            )
        kept = pltpu.make_async_copy(done.at[e, mine], back_ref.at[e, mine], local.at[e])
        kept.start()
        kept.wait()
    for copy in coming:
        copy.wait()
    for end in line_ends:
        end()


def run_experts(rows, cots, router, w_in, w_out, before, after, seqs, block):
    own, count, width = cots.shape
    units = w_in.shape[2]
    across = lax.axis_size("wide")
    vmem, hbm = pl.BlockSpec(memory_space=pltpu.VMEM), pl.BlockSpec(memory_space=pl.ANY)
    sems = pltpu.SemaphoreType.DMA
    return pl.pallas_call(
        functools.partial(experts_kernel, block, seqs),
        in_specs=[vmem, vmem, vmem, hbm, hbm, hbm, hbm, hbm],
        out_specs=[vmem, hbm, hbm, hbm, hbm],
        out_shape=[
            jax.ShapeDtypeStruct((own, count, 2 * width), BF16),
            *[jax.ShapeDtypeStruct(before.shape, BF16)] * 2,
            *[jax.ShapeDtypeStruct(rows.shape, BF16)] * 2,
        ],
        scratch_shapes=[
            pltpu.VMEM((own, count, 2 * width), BF16),
            pltpu.VMEM((count, width), BF16),
            pltpu.VMEM((count, width), F32),
            pltpu.VMEM((count, width), F32),
            pltpu.VMEM((2, width, block), BF16),
            pltpu.VMEM((2, block, width), BF16),
            sems((own, across - 1)),
            sems((own, across - 1)),
            sems((own,)),
            sems((2, 2)),
            sems((2, 2, 2)),
        ],
        compiler_params=pltpu.CompilerParams(collective_id=5, has_side_effects=True, vmem_limit_bytes=62 << 20),
        cost_estimate=pl.CostEstimate(
            flops=8 * own * count * width * units, bytes_accessed=4 * own * width * units, transcendentals=own * count * units
        ),
        name="experts",
    )(rows, cots, router, w_in, w_out, rows, before, after)


def share_kernel(expert, share_ref, rows_ref, cot_ref, router_ref, in_ref, out_ref, *refs):
    grad_in_ref, grad_out_ref, flipped, total_in = refs[-4:]
    step = pl.program_id(0)

    @pl.when(step == 0)
    def _():
        flipped[...] = in_ref[0].T
        total_in[...] = jnp.zeros_like(total_in)
        grad_out_ref[...] = jnp.zeros_like(grad_out_ref)

    rows = rows_ref[0]
    own = router_ref.shape[1] // lax.axis_size("wide")
    grads = gated(rows, cot_ref[0], router_ref[...], lax.axis_index("wide") * own + expert)
    hidden, slope = activation(contract(flipped[...], rows, 1, 1))
    grad_hidden = contract(out_ref[0], grads, 1, 1).astype(BF16).astype(F32)
    grad_out_ref[0] += contract(hidden.astype(BF16), grads, 1, 0)
    total_in[...] += contract((grad_hidden * slope).astype(BF16), rows, 1, 0)

    @pl.when(step == pl.num_programs(0) - 1)
    def _():
        grad_in_ref[0] = total_in[...].T


def run_share(me, rows, cots, router, w_in, w_out, expert, held):
    own, width, units = w_in.shape
    sources, count = rows.shape[0] // own, rows.shape[1]
    share = units // sources
    if share % LANES == 0:
        where = jnp.full((1,), me, jnp.int32)
        in_spec = pl.BlockSpec((1, width, share), lambda r, at: (expert, 0, at[0]))
        out_spec = pl.BlockSpec((1, share, width), lambda r, at: (expert, at[0], 0))
    else:
        where = jnp.zeros((1,), jnp.int32)
        w_in = lax.dynamic_slice(w_in, (0, 0, me * share), (own, width, share))
        w_out = lax.dynamic_slice(w_out, (0, me * share, 0), (own, share, width))
        in_spec = pl.BlockSpec((1, width, share), lambda r, at: (expert, 0, 0))
        out_spec = pl.BlockSpec((1, share, width), lambda r, at: (expert, 0, 0))
    held_specs = [pl.BlockSpec(memory_space=pl.ANY)] * len(held)
    return pl.pallas_call(
        functools.partial(share_kernel, expert),
        grid_spec=pltpu.PrefetchScalarGridSpec(
            num_scalar_prefetch=1,
            grid=(sources,),
            in_specs=[
                pl.BlockSpec((1, count, rows.shape[2]), lambda r, at: (own * r + expert, 0, 0)),
                pl.BlockSpec((1, count, width), lambda r, at: (own * r + expert, 0, 0)),
                pl.BlockSpec(router.shape, lambda r, at: (0, 0)),
                in_spec,
                out_spec,
                *held_specs,
            ],
            out_specs=[
                pl.BlockSpec((1, width, share), lambda r, at: (expert, 0, 0)),
                pl.BlockSpec((1, share, width), lambda r, at: (expert, 0, 0)),
            ],
            scratch_shapes=[pltpu.VMEM((share, width), BF16), pltpu.VMEM((share, width), F32)],
        ),
        out_shape=[
            jax.ShapeDtypeStruct((own, width, share), F32),
            jax.ShapeDtypeStruct((own, share, width), F32),
        ],
        input_output_aliases={6 + i: i for i in range(len(held))},
        compiler_params=pltpu.CompilerParams(vmem_limit_bytes=62 << 20),
        cost_estimate=pl.CostEstimate(
            flops=8 * sources * count * width * share, bytes_accessed=4 * sources * count * width, transcendentals=0
        ),
        name="share",
    )(where, rows, cots, router, w_in, w_out, *held)


def spread_kernel(parts, in_ref, out_ref, send, recv, pass_send, pass_recv, local):
    total = lax.axis_size("seq")
    me = lax.axis_index("seq")
    part = lax.rem(me, parts)
    meet([{"seq": lax.rem(me + k, total)} for k in range(1, total)])
    copies = []
    for k in far_first(total):
        to = lax.rem(me + k, total)
        copies.append(remote(in_ref.at[to], out_ref.at[me, lax.rem(to, parts)], send.at[k - 1], recv.at[k - 1], {"seq": to}))
    own = pltpu.make_async_copy(in_ref.at[me], out_ref.at[me, part], local)
    own.start()
    own.wait()
    passed = []

    def forward(source, k):
        for j in range(1, parts):
            to = me - part + lax.rem(part + j, parts)
            at = (j - 1) * total + k
            block = out_ref.at[source, part]
            passed.append(remote(block, block, pass_send.at[at], pass_recv.at[at], {"seq": to}))

    forward(me, 0)
    for k in far_first(total)[::-1]:
        source = lax.rem(me - k + total, total)
        block = out_ref.at[source, part]
        pltpu.make_async_remote_copy(
            block, block, send.at[k - 1], recv.at[k - 1], device_id={"seq": source}, device_id_type=MESH
        ).wait_recv()
        forward(source, k)
    for copy in copies:
        copy.wait_send()
    for copy in passed:
        copy.wait()


def spread(blocks, parts):
    total, rows, width = blocks.shape
    passes = (parts - 1) * total
    return pl.pallas_call(
        functools.partial(spread_kernel, parts),
        in_specs=[pl.BlockSpec(memory_space=pl.ANY)],
        out_specs=pl.BlockSpec(memory_space=pl.ANY),
        out_shape=jax.ShapeDtypeStruct((total, parts, rows, width), blocks.dtype),
        scratch_shapes=[
            pltpu.SemaphoreType.DMA((total - 1,)),
            pltpu.SemaphoreType.DMA((total - 1,)),
            pltpu.SemaphoreType.DMA((passes,)),
            pltpu.SemaphoreType.DMA((passes,)),
            pltpu.SemaphoreType.DMA,
        ],
        compiler_params=pltpu.CompilerParams(collective_id=0, has_side_effects=True),
        name="spread",
    )(blocks)


def begin_kernel(
    capacity,
    in_ref,
    query_ref,
    key_ref,
    value_ref,
    gain_ref,
    routes_ref,
    base_ref,
    cot_ref,
    all_ref,
    qkv_ref,
    flip_ref,
    hot_ref,
    rows_ref,
    weights,
    packed,
    send,
    recv,
    pass_send,
    pass_recv,
    wide_send,
    wide_recv,
    local,
):
    total, parts, rows, width = all_ref.shape
    _, heads, size, _ = qkv_ref.shape
    own = rows_ref.shape[0]
    cols = heads * size
    across = lax.axis_size("wide")
    me, row = lax.axis_index("seq"), lax.axis_index("wide")
    part = lax.rem(me, parts)
    other = twist(me, 1, total)
    pairs = total // 2
    peers = [{"seq": lax.rem(me + k, total)} for k in range(1, total)]
    peers += [{"wide": lax.rem(row + k, across)} for k in range(1, across)]
    meet(peers)
    sent = []
    for k in range(1, total):
        to = twist(me, k, total)
        sent.append(remote(in_ref.at[to], all_ref.at[me, lax.rem(to, parts)], send.at[to], recv.at[me], {"seq": to}))
    kept = pltpu.make_async_copy(in_ref.at[me], all_ref.at[me, part], local.at[0])
    kept.start()
    kept.wait()
    passed = []

    def forward(source):
        block = all_ref.at[source, part]
        passed.append(remote(block, block, pass_send.at[source], pass_recv.at[source], {"seq": other}))

    def await_recv(block, sem):
        pltpu.make_async_remote_copy(
            block, block, local.at[1], sem, device_id={"seq": other}, device_id_type=MESH
        ).wait_recv()

    forward(me)

    tokens, slots = hot_ref.shape
    picked = (routes_ref[...] == lax.broadcasted_iota(jnp.int32, (tokens, LANES), 1)).astype(F32)
    down = lax.broadcasted_iota(jnp.int32, (tokens, tokens), 0)
    over = lax.broadcasted_iota(jnp.int32, (tokens, tokens), 1)
    earlier = contract((over < down).astype(F32).astype(BF16), picked.astype(BF16), 1, 0)
    rank = jnp.sum(earlier * picked, axis=1, keepdims=True)
    place = jnp.sum(base_ref[...] * picked, axis=1, keepdims=True) + rank
    place = jnp.where(rank < capacity, place, float(slots)).astype(jnp.int32)
    hot = (place == lax.broadcasted_iota(jnp.int32, (tokens, slots), 1)).astype(F32).astype(BF16)
    hot_ref[...] = hot
    packed[...] = contract(hot, cot_ref[...], 0, 0).astype(BF16).reshape(packed.shape)
    wide = []
    mine = pl.ds(row * capacity, capacity)
    for e in range(own):
        for k in range(1, across):
            to = lax.rem(row + k, across)
            wide.append(
                remote(
                    packed.at[e, pl.ds(to * capacity, capacity)],
                    rows_ref.at[e, mine],
                    wide_send.at[e, k - 1],
                    wide_recv.at[e, k - 1],
                    {"wide": to},
                )
            )
    stay = [pltpu.make_async_copy(packed.at[e, mine], rows_ref.at[e, mine], local.at[2 + e]) for e in range(own)]
    for copy in stay:
        copy.start()
    at = pl.ds(pl.multiple_of(part * cols, LANES), cols)
    for n, ref in enumerate((query_ref, key_ref, value_ref)):
        weights[n * cols : (n + 1) * cols, :] = ref[:, at].T

    for t in range(pairs):
        pair = twist(lax.div(me, 2), t, pairs)
        for b in range(2):
            if 2 * t + b:
                source = twist(me, 2 * t + b, total)
                await_recv(all_ref.at[source, part], recv.at[source])
                forward(source)
        for b in range(2):
            source = 2 * pair + b
            await_recv(all_ref.at[source, lax.rem(part + 1, parts)], pass_recv.at[source])
        block = all_ref[pl.ds(2 * pair, 2)].reshape(2 * parts * rows, width).astype(F32)
        normed = (block * inverse_rms(block) * gain_ref[...]).astype(BF16)
        here = pl.ds(pl.multiple_of(pair * (2 * parts * rows), LANES), 2 * parts * rows)
        flip_ref[:, here] = normed.T
        projected = contract(weights[...], normed, 1, 1).astype(BF16)
        qkv_ref[:, :, :, here] = projected.reshape(3, heads, size, 2 * parts * rows)
    for copy in sent + passed:
        copy.wait_send()
    for copy in wide + stay:
        copy.wait()


def begin(blocks, w_query, w_key, w_value, gain, routes, base, cot, heads, size, own, capacity):
    total, rows, width = blocks.shape
    tokens = cot.shape[0]
    across = lax.axis_size("wide")
    slots = own * across * capacity
    length = total * 2 * rows
    vmem = pl.BlockSpec(memory_space=pltpu.VMEM)
    sems = pltpu.SemaphoreType.DMA
    return pl.pallas_call(
        functools.partial(begin_kernel, capacity),
        in_specs=[vmem] * 8,
        out_specs=[vmem] * 6,
        out_shape=[
            jax.ShapeDtypeStruct((total, 2, rows, width), BF16),
            jax.ShapeDtypeStruct((3, heads, size, length), BF16),
            jax.ShapeDtypeStruct((width, length), BF16),
            jax.ShapeDtypeStruct((tokens, slots), BF16),
            jax.ShapeDtypeStruct((own, across * capacity, width), BF16),
            jax.ShapeDtypeStruct((3 * heads * size, width), BF16),
        ],
        scratch_shapes=[
            pltpu.VMEM((own, across * capacity, width), BF16),
            sems((total,)),
            sems((total,)),
            sems((total,)),
            sems((total,)),
            sems((own, across - 1)),
            sems((own, across - 1)),
            sems((2 + own,)),
        ],
        compiler_params=pltpu.CompilerParams(collective_id=6, has_side_effects=True, vmem_limit_bytes=62 << 20),
        cost_estimate=pl.CostEstimate(flops=4 << 30, bytes_accessed=80 << 20, transcendentals=0),
        name="begin",
    )(blocks, w_query, w_key, w_value, gain, routes, base, cot)


def finish_kernel(
    seqs,
    three_ref,
    flip_ref,
    weight_ref,
    x_ref,
    gain_ref,
    early_ref,
    tiny_ref,
    table_ref,
    router_ref,
    *refs,
):
    own, steps = 2, 2 * seqs - 1
    rows_refs = refs[: steps - 2]
    cots_refs = refs[steps - 2 : steps - 2 + 1 + own * (steps - 1)]
    finish_rest(
        seqs,
        rows_refs,
        cots_refs,
        three_ref,
        flip_ref,
        weight_ref,
        x_ref,
        gain_ref,
        early_ref,
        tiny_ref,
        table_ref,
        router_ref,
        *refs[len(rows_refs) + len(cots_refs) :],
    )


def finish_rest(
    seqs,
    rows_refs,
    cots_refs,
    three_ref,
    flip_ref,
    weight_ref,
    x_ref,
    gain_ref,
    early_ref,
    tiny_ref,
    table_ref,
    router_ref,
    in_ref,
    out_ref,
    home_ref,
    late_all,
    early_all,
    tiny,
    grad_in_ref,
    grad_out_ref,
    grads,
    near,
    summed,
    gw,
    wide_got,
    wide_sum,
    far_got,
    early_got,
    mine,
    early_mine,
    tiny_got,
    rows_held,
    cots_held,
    in_held,
    out_held,
    sums,
    total_in,
    leaving,
    share_got,
    share_sems,
    near_sems,
    home_sems,
    wide_sems,
    far_sems,
    early_sems,
    last_sems,
    last_early_sems,
    tiny_sems,
    held_sems,
    line_sems,
    local,
):
    total, across = lax.axis_size("seq"), lax.axis_size("wide")
    parts = total // seqs
    me, row = lax.axis_index("seq"), lax.axis_index("wide")
    part, seq = lax.rem(me, parts), lax.div(me, parts)
    other = twist(me, 1, total)
    width = gain_ref.shape[1]
    slim = gw.shape[2]
    own = in_ref.shape[0]
    share = in_ref.shape[2] // total
    cols = three_ref.shape[1] // 3
    half = three_ref.shape[0] // 2

    def seq_at(k):
        return lax.rem(seq + k, seqs) * parts + part

    def row_at(k):
        return lax.rem(row + k, across)

    def part_at(k):
        return me - part + lax.rem(part + k, parts)

    at = pl.ds(pl.multiple_of(lax.div(me, 2) * (2 * share), LANES), 2 * share)
    weights = [
        pltpu.make_async_copy(in_ref.at[:, :, at], in_held, local.at[0]),
        pltpu.make_async_copy(out_ref.at[:, at, :], out_held, local.at[1]),
    ]
    for copy in weights:
        copy.start()

    def load_rows(e, n, k):
        return pltpu.make_async_copy(rows_refs[k].at[e], rows_held.at[e, n], held_sems.at[0, e, n])

    def load_cots(e, n, k):
        src = cots_refs[1 + own * (k - 1) + e] if k else cots_refs[0].at[e]
        return pltpu.make_async_copy(src, cots_held.at[e, n], held_sems.at[1, e, n])

    last_place = seqs - 1
    far_end = jnp.logical_or(seq == 0, seq == last_place)
    for e in range(own):
        load_rows(e, 0, 0).start()
        load_cots(e, 0, 0).start()
        for here in range(seqs):

            @pl.when(seq == here)
            def _():
                sources = [2 * k - 1 for k in range(1, here + 1)] + [2 * k for k in range(1, seqs - here)]
                for n, k in enumerate(sources):
                    load_cots(e, n + 1, k).start()
                    if k < len(rows_refs):
                        load_rows(e, n + 1, k).start()

    pairs = [(a, b) for a in range(across) for b in range(parts) if a or b]
    peers = [{"seq": lax.rem(me + k, total)} for k in range(1, total)]
    peers += [{"wide": row_at(k)} for k in range(1, across)]
    peers += [{"wide": row_at(a), "seq": part_at(b)} for a, b in pairs if a and b]
    meet(peers)

    def far_rows(e, up):
        src = rows_refs[3 if up else 4].at[e]
        to = lax.rem(me + (parts if up else total - parts), total)
        return pltpu.make_async_remote_copy(
            src, rows_held.at[e, last_place], line_sems.at[0, e], line_sems.at[1, e], device_id={"seq": to}, device_id_type=MESH
        )

    for e in range(own):

        @pl.when(seq == last_place - 1)
        def _():
            far_rows(e, True).start()

        @pl.when(seq == 1)
        def _():
            far_rows(e, False).start()

    late = contract(flip_ref[...], three_ref[...], 1, 0).astype(BF16)
    gw[...] = late.reshape(gw.shape)
    wide_copies = [
        remote(gw.at[:, row_at(k)], wide_got.at[k - 1], wide_sems.at[0, k - 1], wide_sems.at[1, k - 1], {"wide": row_at(k)})
        for k in range(1, across)
    ]

    gain = gain_ref[...]
    gain_grad = jnp.zeros((1, width), F32)
    near_copies = []
    for n in range(2):
        scaled = contract(three_ref[n * half : (n + 1) * half, :], weight_ref[...], 1, 0)
        x = x_ref[n * total // 2 : (n + 1) * total // 2].reshape(half, width).astype(F32)
        inverse = inverse_rms(x)
        gain_grad = gain_grad + jnp.sum(scaled * x * inverse, axis=0, keepdims=True)
        scaled = scaled * gain
        mean_inner = jnp.mean(x * scaled, axis=-1, keepdims=True)
        value = inverse * scaled - x * (inverse * inverse * inverse) * mean_inner
        here = pl.ds(n * total // 2, total // 2)
        grads[here] = value.astype(BF16).reshape(total // 2, *grads.shape[1:])
        near_copies.append(
            remote(
                grads.at[here, lax.rem(part + 1, parts)],
                near.at[here],
                near_sems.at[0, n],
                near_sems.at[1, n],
                {"seq": other},
            )
        )
    lines = tiny_ref.shape[0]
    first = lax.broadcasted_iota(jnp.int32, tiny_ref.shape, 0) == 0
    tiny[:lines, :] = jnp.where(first, gain_grad, tiny_ref[...]).astype(BF16)
    table = table_ref[...]
    tiny[lines:, :] = jnp.concatenate([table, jnp.zeros((table.shape[0], width - table.shape[1]), F32)], axis=1).astype(BF16)

    def pass_tiny(stage, wheres):
        return [
            remote(tiny, tiny_got.at[stage, n], tiny_sems.at[0, stage, n], tiny_sems.at[1, stage, n], where)
            for n, where in enumerate(wheres)
        ]

    def take_tiny(stage, copies):
        for copy in copies:
            copy.wait()
        value = tiny[...].astype(F32)
        for n in range(len(copies)):
            value = value + tiny_got[stage, n].astype(F32)
        tiny[...] = value.astype(BF16)

    tiny_copies = pass_tiny(0, [{"wide": row_at(k)} for k in range(1, across)])
    for copy in near_copies:
        copy.wait()
    home_copies = []
    for k in range(total - 1, -1, -1):
        to = twist(me, k, total)
        summed[to] = (grads[to, part].astype(F32) + near[to].astype(F32)).astype(BF16)
        if k:
            home_copies.append(
                remote(summed.at[to], home_ref.at[me], home_sems.at[0, k - 1], home_sems.at[1, k - 1], {"seq": to})
            )
    kept = pltpu.make_async_copy(summed.at[me], home_ref.at[me], local.at[2])
    kept.start()
    for copy in weights:
        copy.wait()

    mine_rows = pl.ds(pl.multiple_of(part * share, LANES), share)
    other_rows = pl.ds(pl.multiple_of((1 - part) * share, LANES), share)

    def share_turn(e, n):
        some = rows_held.shape[1] // 2
        for m in range(n * some, (n + 1) * some):
            load_cots(e, m, 0).wait()
            if m < last_place:
                load_rows(e, m, 0).wait()
            else:

                @pl.when(far_end)
                def _():
                    far_rows(e, True).wait_recv()

                @pl.when(jnp.logical_not(far_end))
                def _():
                    load_rows(e, m, 0).wait()

        count = some * rows_held.shape[2]
        here = slice(n * some, (n + 1) * some)
        rows = rows_held[e, here].reshape(count, width)
        cots = gated(rows, cots_held[e, here].reshape(count, width), router_ref[...], row * own + e)
        hidden, slope = activation(contract(in_held[e].T, rows, 1, 1))
        grad_hidden = contract(out_held[e], cots, 1, 1).astype(BF16).astype(F32)
        part_out = contract(hidden.astype(BF16), cots, 1, 0)
        part_in = contract((grad_hidden * slope).astype(BF16), rows, 1, 0)
        if n == 0:
            sums[e, 0] = part_out
            sums[e, 1] = part_in
            return []
        sums[e, 0] += part_out
        sums[e, 1] += part_in
        grad_out_ref[e] = sums[e, 0, mine_rows, :]
        total_in[e] = sums[e, 1, mine_rows, :]
        copies = []
        for k in range(2):
            leaving[e, k] = sums[e, k, other_rows, :].astype(BF16)
            copies.append(
                remote(leaving.at[e, k], share_got.at[e, k], share_sems.at[0, e, k], share_sems.at[1, e, k], {"seq": other})
            )
        return copies

    def share_end(e, copies):
        for copy in copies:
            copy.wait()
        grad_out_ref[e] += share_got[e, 0].astype(F32)
        grad_in_ref[e] = (total_in[e] + share_got[e, 1].astype(F32)).T

    share_turn(0, 0)
    share_turn(1, 0)
    take_tiny(0, tiny_copies)
    for copy in wide_copies:
        copy.wait_recv()
    far_copies = []
    for k in list(range(1, seqs)) + [0]:
        place = lax.rem(seq + k, seqs)
        for p in range(parts):
            block = place * parts + p
            value = gw[block, row].astype(F32)
            for j in range(across - 1):
                value = value + wide_got[j, block].astype(F32)
            wide_sum[place, p] = value.astype(BF16)
        if k:
            where = {"seq": seq_at(k)}
            far_copies.append(
                remote(wide_sum.at[place], far_got.at[k - 1], far_sems.at[0, k - 1], far_sems.at[1, k - 1], where)
            )
            far_copies.append(
                remote(early_ref.at[place], early_got.at[k - 1], early_sems.at[0, k - 1], early_sems.at[1, k - 1], where)
            )
    tiny_copies = pass_tiny(1, [{"seq": seq_at(k)} for k in range(1, seqs)])
    first_share = share_turn(0, 1)
    take_tiny(1, tiny_copies)
    for copy in far_copies:
        copy.wait_recv()
    for p in range(parts):
        value = wide_sum[seq, p].astype(F32)
        for j in range(seqs - 1):
            value = value + far_got[j, p].astype(F32)
        mine[p] = value.astype(BF16)
    value = early_ref[seq].astype(F32)
    for j in range(seqs - 1):
        value = value + early_got[j].astype(F32)
    early_mine[...] = value.astype(BF16)
    last = pass_tiny(2, [{"seq": part_at(k)} for k in range(1, parts)])
    count = len(last)
    for a, b in pairs:
        n = a * parts + b - 1
        last.append(
            remote(
                mine.at[lax.rem(part + b, parts)],
                late_all.at[row, part],
                last_sems.at[0, n],
                last_sems.at[1, n],
                {"wide": row_at(a), "seq": part_at(b)},
            )
        )
    for k in range(1, across):
        last.append(
            remote(
                early_mine, early_all.at[row], last_early_sems.at[0, k - 1], last_early_sems.at[1, k - 1], {"wide": row_at(k)}
            )
        )
    stay = [
        pltpu.make_async_copy(mine.at[part], late_all.at[row, part], local.at[3]),
        pltpu.make_async_copy(early_mine, early_all.at[row], local.at[4]),
    ]
    for copy in stay:
        copy.start()
    second_share = share_turn(1, 1)
    share_end(0, first_share)
    take_tiny(2, last[:count])
    share_end(1, second_share)
    for e in range(own):

        @pl.when(jnp.logical_or(seq == 1, seq == last_place - 1))
        def _():
            far_rows(e, True).wait_send()

    for copy in last[count:] + stay + home_copies + [kept]:
        copy.wait()
    for copy in wide_copies + far_copies:
        copy.wait_send()


def finish(three, flipped, weights, x, gain, early, tiny, table, router, rows, cots, w_in, w_out):
    columns = three.shape[1]
    total, parts, piece, width = x.shape
    seqs, slim, _ = early.shape
    across = lax.axis_size("wide")
    own, _, units = w_in.shape
    share = units // total
    vmem, hbm = pl.BlockSpec(memory_space=pltpu.VMEM), pl.BlockSpec(memory_space=pl.ANY)
    sems = pltpu.SemaphoreType.DMA
    most = max(across, seqs, parts) - 1
    lines = tiny.shape[0] + table.shape[0]
    return pl.pallas_call(
        functools.partial(finish_kernel, seqs),
        in_specs=[vmem] * 9 + [hbm] * (len(rows) + len(cots) + 2),
        out_specs=[vmem] * 6,
        out_shape=[
            jax.ShapeDtypeStruct((total, piece, width), BF16),
            jax.ShapeDtypeStruct((across, parts, slim, columns), BF16),
            jax.ShapeDtypeStruct((across, slim, width), BF16),
            jax.ShapeDtypeStruct((lines, width), BF16),
            jax.ShapeDtypeStruct((own, width, share), F32),
            jax.ShapeDtypeStruct((own, share, width), F32),
        ],
        scratch_shapes=[
            pltpu.VMEM((total, parts, piece, width), BF16),
            pltpu.VMEM((total, piece, width), BF16),
            pltpu.VMEM((total, piece, width), BF16),
            pltpu.VMEM((total, across, slim, columns), BF16),
            pltpu.VMEM((across - 1, total, slim, columns), BF16),
            pltpu.VMEM((seqs, parts, slim, columns), BF16),
            pltpu.VMEM((seqs - 1, parts, slim, columns), BF16),
            pltpu.VMEM((seqs - 1, slim, width), BF16),
            pltpu.VMEM((parts, slim, columns), BF16),
            pltpu.VMEM((slim, width), BF16),
            pltpu.VMEM((3, most, lines, width), BF16),
            pltpu.VMEM((own, seqs, *rows[0].shape[1:]), BF16),
            pltpu.VMEM((own, seqs, *cots[0].shape[1:]), BF16),
            pltpu.VMEM((own, width, 2 * share), BF16),
            pltpu.VMEM((own, 2 * share, width), BF16),
            pltpu.VMEM((own, 2, 2 * share, width), F32),
            pltpu.VMEM((own, share, width), F32),
            pltpu.VMEM((own, 2, share, width), BF16),
            pltpu.VMEM((own, 2, share, width), BF16),
            sems((2, own, 2)),
            sems((2, 2)),
            sems((2, total - 1)),
            sems((2, across - 1)),
            sems((2, seqs - 1)),
            sems((2, seqs - 1)),
            sems((2, across * parts - 1)),
            sems((2, across - 1)),
            sems((2, 3, most)),
            sems((2, own, seqs)),
            sems((2, own)),
            sems((5,)),
        ],
        compiler_params=pltpu.CompilerParams(collective_id=1, has_side_effects=True, vmem_limit_bytes=62 << 20),
        cost_estimate=pl.CostEstimate(flops=16 << 30, bytes_accessed=60 << 20, transcendentals=0),
        name="finish",
    )(three, flipped, weights, x, gain, early, tiny, table, router, *rows, *cots, w_in, w_out)


def close_kernel(
    heads,
    home_ref,
    middle_ref,
    late_ref,
    early_ref,
    tiny_ref,
    in_ref,
    out_ref,
    inputs_ref,
    query_ref,
    key_ref,
    value_ref,
    output_ref,
    gain_one_ref,
    gain_two_ref,
    router_ref,
    table_ref,
    grad_in_ref,
    grad_out_ref,
):
    grad_in_ref[...] = in_ref[...]
    grad_out_ref[...] = out_ref[...]
    me = lax.axis_index("seq")
    across, parts, slim, columns = late_ref.shape
    cols = columns // 3
    inputs_ref[...] = middle_ref[...] + home_ref[...].reshape(middle_ref.shape).astype(F32)
    for a in range(across):
        here = slice(a * slim, (a + 1) * slim)
        for p in range(parts):
            for n, ref in enumerate((query_ref, key_ref, value_ref)):
                ref[here, p * cols : (p + 1) * cols] = late_ref[a, p, :, n * cols : (n + 1) * cols].astype(F32)
        output_ref[here, :] = early_ref[a].astype(F32)
    width, piece = tiny_ref.shape[1], gain_one_ref.shape[1]
    chosen = lax.broadcasted_iota(jnp.int32, (width, piece), 0) == (
        lax.broadcasted_iota(jnp.int32, (width, piece), 1) + me * piece
    )
    picked = contract(tiny_ref[...], chosen.astype(F32).astype(BF16), 1, 0)
    gain_one_ref[...] = picked[0:1]
    gain_two_ref[...] = picked[1:2]
    router_ref[...] = picked[2 : 2 + router_ref.shape[0]]
    lines = table_ref.shape[0]
    chosen = lax.broadcasted_iota(jnp.int32, (lines, LANES), 1) == (
        lax.broadcasted_iota(jnp.int32, (lines, LANES), 0) + me * lines
    )
    table_ref[...] = contract(chosen.astype(F32).astype(BF16), tiny_ref[16:, :LANES], 1, 1)[:, :heads]


def close(home, middle, late, early, tiny, grad_in, grad_out, heads, buckets, experts):
    across, parts, slim, columns = late.shape
    width = early.shape[2]
    total = home.shape[0]
    rows = across * slim
    vmem = pl.BlockSpec(memory_space=pltpu.VMEM)
    shapes = [
        middle.shape,
        *[(rows, width)] * 4,
        (1, width // total),
        (1, width // total),
        (experts, width // total),
        (buckets // total, heads),
        grad_in.shape,
        grad_out.shape,
    ]
    return pl.pallas_call(
        functools.partial(close_kernel, heads),
        in_specs=[vmem] * 7,
        out_specs=[vmem] * 11,
        out_shape=[jax.ShapeDtypeStruct(shape, F32) for shape in shapes],
        compiler_params=pltpu.CompilerParams(vmem_limit_bytes=62 << 20),
        name="close",
    )(home, middle, late, early, tiny, grad_in, grad_out)


def ring_pairs(total, parts, shift):
    return [(i, i - i % parts + (i % parts + shift) % parts) for i in range(total)]


def pick(pieces, index):
    out = pieces[0]
    for k in range(1, len(pieces)):
        out = jnp.where(index == k, pieces[k], out)
    return out


def swap_parts(pieces, part, parts, total):
    near = [pick(pieces, part)]
    for k in range(1, parts):
        near.append(lax.ppermute(pick(pieces, (part + k) % parts), "seq", ring_pairs(total, parts, k)))
    return [pick(near, (part - j) % parts) for j in range(parts)]


def per_device(
    inputs,
    routes,
    bucket_ids,
    gain_attn,
    w_query,
    w_key,
    w_value,
    w_output,
    rel_table,
    gain_ffn,
    w_router,
    w_in,
    w_out,
    cotangent,
):
    seqs, local_len, width = inputs.shape
    buckets, head_count = rel_table.shape
    size = width // head_count
    total = lax.axis_size("seq")
    across = lax.axis_size("wide")
    length = local_len * total
    parts = total // seqs
    heads = head_count // parts
    cols = heads * size
    me = lax.axis_index("seq")
    part = me % parts
    experts = w_router.shape[1]
    own_experts = w_in.shape[0]
    tokens = seqs * local_len
    capacity = (5 * tokens + 4 * experts - 1) // (4 * experts)
    slots = experts * capacity
    gain_one = gain_attn.astype(F32)
    gain_two = gain_ffn.astype(F32)

    fast = parts == 2 and capacity % 16 == 0 and own_experts == 2 and seqs == 4 and cols % LANES == 0 and local_len == LANES
    flat_cot = cotangent.reshape(tokens, width)
    chosen = routes.reshape(tokens)
    blocks = inputs.reshape(total, local_len // parts, width)

    if fast:
        first_slot = [(e % own_experts) * (across * capacity) + (e // own_experts) * capacity for e in range(experts)]
        base = jnp.array(first_slot + [0] * (LANES - experts), F32)[None]
        seq_in, qkv, flipped, slot_hot, cot_rows, own_weights = begin(
            blocks,
            w_query,
            w_key,
            w_value,
            gain_one[None],
            chosen[:, None],
            base,
            flat_cot,
            heads,
            size,
            own_experts,
            capacity,
        )
    else:
        own_weights = jnp.concatenate(
            [lax.dynamic_slice(w, (0, part * cols), (width, cols)) for w in (w_query, w_key, w_value)], axis=1
        )
        seq_in = spread(blocks, parts).reshape(length, width).astype(F32)
        inv_one = inverse_rms(seq_in)
        normed_one = (seq_in * inv_one * gain_one).astype(BF16)
        flipped = normed_one.T
        qkv = contract(own_weights, normed_one, 0, 1).astype(BF16).reshape(3, heads, size, length)
        picked = (chosen[:, None] == jnp.arange(experts, dtype=jnp.int32)[None, :]).astype(F32)
        order = jnp.arange(tokens, dtype=jnp.int32)
        before = (order[None, :] < order[:, None]).astype(BF16)
        earlier = jnp.dot(before, picked.astype(BF16), preferred_element_type=F32)
        rank_in = jnp.sum(earlier * picked, axis=1).astype(jnp.int32)
        place = (chosen % own_experts) * (across * capacity) + (chosen // own_experts) * capacity + rank_in
        slot_of = jnp.where(rank_in < capacity, place, slots)
        slot_hot = (slot_of[:, None] == jnp.arange(slots, dtype=jnp.int32)[None, :]).astype(BF16)
        packed = contract(slot_hot, flat_cot, 0, 0).astype(BF16).reshape(own_experts, across, capacity, width)
        cot_rows = jnp.stack([lax.all_to_all(packed[e], "wide", 0, 0, tiled=True) for e in range(own_experts)])
        cot_rows = cot_rows.reshape(own_experts, across * capacity, width)
    own_table = lax.dynamic_slice(rel_table, (0, part * heads), (buckets, heads))
    ids = jnp.concatenate([bucket_ids, jnp.full((1,), LANES, jnp.int32)])
    bucket_hot = (ids[None, :] == jnp.arange(LANES, dtype=jnp.int32)[:, None]).astype(BF16)
    reverse_hot = (ids[::-1][None, :] == jnp.arange(buckets, dtype=jnp.int32)[:, None]).astype(BF16)
    bias_line = contract(own_table, reverse_hot, 0, 0).reshape(heads, 1, 2 * length)
    outs, attended, exps, inverse, *first = attend(qkv, bias_line, total, [cot_rows] if fast else [], seqs)
    attended = attended.reshape(seqs, width, local_len)
    share = width // total
    flat_in = inputs.reshape(tokens, width)
    back = (exps, inverse, w_output.reshape(parts, cols, width), outs, qkv, bucket_hot)
    if fast:
        middle, normed_two, received, *second = route(
            attended, w_output, flat_in, gain_two[None], slot_hot, cot_rows, *first, capacity
        )
        next_cots = second[2:]
        returned, *passed = run_experts(received, cot_rows, w_router, w_in, w_out, *next_cots, seqs, 512)
        second = [second[0], passed[0], second[1], passed[1]]
        near_rows = passed[2:]
        more = [
            returned,
            slot_hot,
            middle,
            normed_two,
            w_router,
            chosen[:, None],
            flat_cot,
            gain_two[None],
            attended,
        ]
        three, table, early, output, grad_middle, tiny, *passed = attend_back(*back, None, more, near_rows, second)
        all_rows = [received, *near_rows, *passed[:2]]
        all_cots = [cot_rows, first[0], next_cots[0], first[1], next_cots[1], *second, *passed[2:]]
        home, *found = finish(
            three,
            flipped,
            own_weights,
            seq_in,
            gain_one[None],
            early,
            tiny,
            table,
            w_router,
            all_rows,
            all_cots,
            w_in,
            w_out,
        )
        grad_inputs, *grads_qkvo, grad_gain_one, grad_gain_two, grad_router, grad_table, grad_in, grad_out = close(
            home, grad_middle, *found, head_count, buckets, experts
        )
        return (
            output.reshape(inputs.shape),
            grad_inputs.reshape(inputs.shape),
            grad_gain_one[0],
            *grads_qkvo,
            grad_table,
            grad_gain_two[0],
            grad_router.T,
            grad_in,
            grad_out,
        )

    flat_in = flat_in.astype(F32)
    middle = flat_in + jnp.einsum("sft,fe->ste", attended, w_output, preferred_element_type=F32).reshape(tokens, width)
    inv_two = inverse_rms(middle)
    normed_two = (middle * inv_two * gain_two).astype(BF16)
    router_probs = jax.nn.softmax(jnp.dot(normed_two, w_router, preferred_element_type=F32), axis=-1)
    picked = (chosen[:, None] == jnp.arange(experts, dtype=jnp.int32)[None, :]).astype(F32)
    gate_prob = jnp.sum(router_probs * picked, axis=1)
    upstream = flat_cot.astype(F32)
    packed = contract(slot_hot, normed_two, 0, 0).astype(BF16).reshape(own_experts, across, capacity, width)
    received, returned = [], []
    for e in range(own_experts):
        got = lax.all_to_all(packed[e], "wide", 0, 0, tiled=True).reshape(across * capacity, width)
        received.append(got)
        pair = run_expert(got, cot_rows[e], w_router, w_in, w_out, e, 512).reshape(across, capacity, 2 * width)
        returned.append(lax.all_to_all(pair, "wide", 0, 0, tiled=True).reshape(across * capacity, 2 * width))
    received, returned = jnp.stack(received), jnp.concatenate(returned, axis=0)
    token_rows = jnp.dot(slot_hot, returned, preferred_element_type=F32)
    selected, grad_token = token_rows[:, :width], token_rows[:, width:]
    output = (middle + gate_prob[:, None] * selected).astype(BF16).reshape(inputs.shape)
    grad_gate = jnp.sum(upstream * selected, axis=1)
    grad_logits = (grad_gate[:, None] * router_probs * (picked - gate_prob[:, None])).astype(BF16)
    grad_router = contract(grad_logits, normed_two, 0, 0)
    grad_normed_two = grad_token + contract(grad_logits, w_router, 1, 1)
    grad_mid_norm, grad_gain_two = norm_backward(middle, inv_two, gain_two, grad_normed_two)
    grad_middle = upstream + grad_mid_norm
    grad_branch = grad_middle.astype(BF16).reshape(seqs, local_len, width)
    grad_w_output = jnp.einsum("sft,ste->fe", attended, grad_branch, preferred_element_type=F32)
    all_cots = lax.all_gather(cot_rows, "seq", axis=0)
    all_rows = lax.all_gather(received, "seq", axis=0)
    three, table = attend_back(*back, grad_branch, [], [], [])
    grad_normed_one = contract(three, own_weights, 1, 1)
    grad_in_norm, grad_gain_one = norm_backward(seq_in, inv_one, gain_one, grad_normed_one)
    pieces = grad_in_norm.astype(BF16).reshape(total, parts, local_len // parts, width)
    swapped = swap_parts([pieces[:, p] for p in range(parts)], part, parts, total)
    home = sum(p.astype(F32) for p in swapped).astype(BF16)
    home = lax.all_to_all(home, "seq", 0, 0, tiled=True).reshape(tokens, width).astype(F32)
    grad_projections = lax.dynamic_update_slice(
        jnp.zeros((width, 3, width), F32), contract(flipped, three, 1, 0).reshape(width, 3, cols), (0, 0, part * cols)
    )
    rows = [grad_projections[:, k] for k in range(3)]
    rows += [grad_w_output, grad_gain_one[:, None], grad_gain_two[:, None], grad_router.T]
    table = table.T[:buckets]
    rows, table = lax.psum((jnp.concatenate(rows, axis=1).astype(BF16), table.astype(BF16)), "wide")
    rows = lax.psum_scatter(rows, "seq", scatter_dimension=0, tiled=True).astype(F32)
    table = lax.psum_scatter(table, "seq", scatter_dimension=0, tiled=True).astype(F32)
    held = []
    for e in range(own_experts):
        held = run_share(
            me,
            all_rows.reshape(total * own_experts, *received.shape[1:]),
            all_cots.reshape(total * own_experts, *cot_rows.shape[1:]),
            w_router,
            w_in,
            w_out,
            e,
            held,
        )
    last = rows[:, 4 * width :]
    return (
        output,
        (grad_middle + home).reshape(inputs.shape),
        last[:, 0],
        *[rows[:, k * width : (k + 1) * width] for k in range(4)],
        table[:, :head_count],
        last[:, 1],
        last[:, 2 : 2 + experts],
        *held,
    )


def solution(mesh):
    in_specs = (
        P("wide", "seq", None),
        P("wide", "seq", None),
        P(),
        P(),
        P(),
        P(),
        P(),
        P(),
        P(),
        P(),
        P(),
        P("wide", None, None),
        P("wide", None, None),
        P("wide", "seq", None),
    )
    out_specs = (
        P("wide", "seq", None),
        P("wide", "seq", None),
        P("seq"),
        P("seq", None),
        P("seq", None),
        P("seq", None),
        P("seq", None),
        P("seq", None),
        P("seq"),
        P("seq", None),
        P("wide", None, "seq"),
        P("wide", "seq", None),
    )
    return jax.shard_map(
        per_device, mesh=mesh, in_specs=in_specs, out_specs=out_specs, check_vma=False
    )
```

```python
import functools

import jax
import jax.numpy as jnp
from jax import lax
from jax.experimental import pallas as pl
from jax.experimental.pallas import tpu as pltpu
from jax.sharding import PartitionSpec as P

EPSILON = 1e-06
F32 = jnp.float32
BF16 = jnp.bfloat16
LANES = 128


def contract(a, b, da, db):
    return lax.dot_general(a, b, (((da,), (db,)), ((), ())), preferred_element_type=F32)


def inverse_rms(source):
    return lax.rsqrt(jnp.mean(source * source, axis=-1, keepdims=True) + EPSILON)


def norm_backward(source, inv_rms, gain_vec, upstream):
    scaled = upstream * gain_vec
    gain_grad = jnp.sum(upstream * source * inv_rms, axis=0)
    mean_inner = jnp.mean(source * scaled, axis=-1, keepdims=True)
    return (inv_rms * scaled - source * (inv_rms * inv_rms * inv_rms) * mean_inner, gain_grad)


def smooth_act(values):
    return jax.nn.gelu(values, approximate=True)


MESH = pl.DeviceIdType.MESH


def remote(src, dst, send, recv, where):
    copy = pltpu.make_async_remote_copy(src, dst, send, recv, device_id=where, device_id_type=MESH)
    copy.start()
    return copy


def router_of(table, experts):
    return table[2 : 2 + experts, :].astype(BF16)


def routes_of(table, experts, tokens):
    lines = table[2 + experts : 2 + experts + tokens // LANES, :LANES]
    lines = jnp.concatenate([lines, jnp.zeros((LANES - lines.shape[0], LANES), F32)], axis=0).T
    return jnp.concatenate([lines[:, n : n + 1] for n in range(tokens // LANES)], axis=0)


def fetch(sources, targets, sems):
    copies = [pltpu.make_async_copy(a, b, sems.at[n]) for n, (a, b) in enumerate(zip(sources, targets, strict=True))]
    for copy in copies:
        copy.start()
    return copies


def meet(peers):
    barrier = pltpu.get_barrier_semaphore()
    for where in peers:
        pl.semaphore_signal(barrier, inc=1, device_id=where, device_id_type=MESH)
    pl.semaphore_wait(barrier, len(peers))


def line_peers(parts):
    total, me = lax.axis_size("seq"), lax.axis_index("seq")
    return [{"seq": lax.rem(me + parts, total)}, {"seq": lax.rem(me - parts + total, total)}]


def pass_on(parts, up, down, sems):
    me = lax.axis_index("seq")
    z = lax.div(me, parts)

    def copy(n, src, dst, step):
        return pltpu.make_async_remote_copy(
            src, dst, sems.at[0, n], sems.at[1, n], device_id={"seq": me + step}, device_id_type=MESH
        )

    legs = [(0, *up, parts), (1, *down, -parts)]
    for n, low, high, src, dst, step in legs:

        @pl.when(jnp.logical_and(z >= low, z <= high))
        def _():
            copy(n, src, dst, step).start()

    def end():
        for n, low, high, src, dst, step in legs:
            move = 1 if step > 0 else -1

            @pl.when(jnp.logical_and(z >= low, z <= high))
            def _():
                copy(n, src, dst, step).wait_send()

            @pl.when(jnp.logical_and(z >= low + move, z <= high + move))
            def _():
                copy(n, src, dst, -step).wait_recv()

    return end


def far_first(total):
    return sorted(range(1, total), key=lambda k: -min(k, total - k))


def twist(a, b, total):
    out, bit = 0, 1
    while bit < total:
        out = out + lax.rem(lax.div(a, bit) + lax.div(b, bit), 2) * bit
        bit *= 2
    return out


def attend_kernel(seqs, *refs):
    refs = list(refs)
    qkv_ref, bias_ref = refs[:2]
    line_ref = refs.pop(2) if seqs else None
    out_ref, home_ref, exp_ref, inv_ref = refs[2:6]
    line_outs = [refs.pop(6) for _ in range(2)] if seqs else []
    strip, keys, scores, held, send, recv, local, exp_sems, *line_sems = refs[6:]
    _, heads, size, length = qkv_ref.shape
    total = lax.axis_size("seq")
    me = lax.axis_index("seq")
    tokens = out_ref.shape[3]
    width = 2 * tokens
    pairs = total // 2
    rows = 2 * length - tokens
    chunk = 256
    meet([{"seq": lax.rem(me + k, total)} for k in range(1, total)])
    if seqs:
        before, after = line_outs
        line_end = pass_on(
            total // seqs, (0, seqs - 2, line_ref.at[0], before), (1, seqs - 1, line_ref.at[0], after), line_sems[0]
        )

    def prepare(h, carry):
        keys[h] = qkv_ref[1, h].T
        for b in range(rows // tokens):
            start = 2 * length - 2 * tokens - tokens * b
            base = jnp.broadcast_to(bias_ref[h, :, start : start + 2 * tokens], (tokens, 2 * tokens))
            rolled = pltpu.roll(base, 0, 1, stride=1, stride_axis=0)
            strip[h, tokens * b : tokens * (b + 1), :] = rolled[:, tokens:]
        return carry

    lax.fori_loop(0, heads, prepare, 0)

    def store(slot, pair, h):
        return pltpu.make_async_copy(held.at[slot], exp_ref.at[pair, h], exp_sems.at[slot])

    def step(t, carry):
        pair = twist(lax.div(me, 2), pairs - 1 - t, pairs)
        at = pl.ds(pl.multiple_of(pair * width, tokens), width)

        def head(h, carry):
            count = t * heads + h
            slot = lax.rem(count, 2)

            @pl.when(count >= 2)
            def _():
                store(slot, pair, h).wait()

            query = qkv_ref[0, h, :, at]
            tops = [jnp.full((1, tokens), -jnp.inf, F32)] * 2
            for c in range(length // chunk):
                part = contract(keys[h, c * chunk : (c + 1) * chunk, :], query, 1, 0)
                for s in range(2):
                    row = pl.multiple_of(length - tokens - (pair * width + s * tokens) + c * chunk, tokens)
                    piece = part[:, s * tokens : (s + 1) * tokens] + strip[h, pl.ds(row, chunk), :]
                    scores[c * chunk : (c + 1) * chunk, s * tokens : (s + 1) * tokens] = piece
                    tops[s] = jnp.maximum(tops[s], jnp.max(piece, axis=0, keepdims=True))
            sums = [jnp.zeros((1, tokens), F32)] * 2
            for c in range(length // chunk):
                for s in range(2):
                    piece = scores[c * chunk : (c + 1) * chunk, s * tokens : (s + 1) * tokens]
                    grown = jnp.exp(piece - tops[s])
                    sums[s] = sums[s] + jnp.sum(grown, axis=0, keepdims=True)
                    held[slot, c * chunk : (c + 1) * chunk, s * tokens : (s + 1) * tokens] = grown.astype(BF16)
            store(slot, pair, h).start()
            mixed = contract(qkv_ref[2, h], held[slot], 1, 0)
            for s in range(2):
                inverse = 1.0 / sums[s]
                inv_ref[pair, h, :, s * tokens : (s + 1) * tokens] = inverse
                out_ref[2 * pair + s, h] = (mixed[:, s * tokens : (s + 1) * tokens] * inverse).astype(BF16)
            return carry

        lax.fori_loop(0, heads, head, 0)
        for s in range(2):
            to = 2 * pair + s
            k = twist(me, to, total)

            @pl.when(to != me)
            def _():
                pltpu.make_async_remote_copy(
                    out_ref.at[to], home_ref.at[me], send.at[k], recv.at[k], device_id={"seq": to}, device_id_type=MESH
                ).start()

        return carry

    lax.fori_loop(0, pairs, step, 0)
    own = pltpu.make_async_copy(out_ref.at[me], home_ref.at[me], local)
    own.start()
    for slot in range(2):
        store(slot, 0, 0).wait()

    def settle(k, carry):
        source = twist(me, k, total)
        pltpu.make_async_remote_copy(
            out_ref.at[source], home_ref.at[source], send.at[k], recv.at[k], device_id={"seq": source}, device_id_type=MESH
        ).wait()
        return carry

    lax.fori_loop(1, total, settle, 0)
    own.wait()
    if seqs:
        line_end()


def attend(qkv, bias_line, total, line, seqs):
    _, heads, size, length = qkv.shape
    tokens = length // total
    vmem, hbm = pl.BlockSpec(memory_space=pltpu.VMEM), pl.BlockSpec(memory_space=pl.ANY)
    return pl.pallas_call(
        functools.partial(attend_kernel, seqs if line else 0),
        in_specs=[vmem, vmem] + [hbm] * len(line),
        out_specs=[vmem, vmem, hbm, vmem] + [hbm] * (2 * len(line)),
        out_shape=[
            jax.ShapeDtypeStruct((total, heads, size, tokens), BF16),
            jax.ShapeDtypeStruct((total, heads, size, tokens), BF16),
            jax.ShapeDtypeStruct((total // 2, heads, length, 2 * tokens), BF16),
            jax.ShapeDtypeStruct((total // 2, heads, 1, 2 * tokens), F32),
            *[jax.ShapeDtypeStruct(rows.shape[1:], BF16) for rows in line for _ in range(2)],
        ],
        scratch_shapes=[
            pltpu.VMEM((heads, 2 * length - tokens, tokens), F32),
            pltpu.VMEM((heads, length, size), BF16),
            pltpu.VMEM((length, 2 * tokens), F32),
            pltpu.VMEM((2, length, 2 * tokens), BF16),
            pltpu.SemaphoreType.DMA((total,)),
            pltpu.SemaphoreType.DMA((total,)),
            pltpu.SemaphoreType.DMA,
            pltpu.SemaphoreType.DMA((2,)),
            *[pltpu.SemaphoreType.DMA((2, 2)) for _ in line],
        ],
        compiler_params=pltpu.CompilerParams(collective_id=2, has_side_effects=True, vmem_limit_bytes=62 << 20),
        cost_estimate=pl.CostEstimate(
            flops=4 * heads * length * length * size, bytes_accessed=2 * heads * length * length, transcendentals=heads * length * length
        ),
        name="attend",
    )(qkv, bias_line, *line)


def attend_back_kernel(fast, *refs):
    refs = list(refs)
    exp_ref, inv_ref, weight_in, out_in, qkv_in, hot_ref = refs[:6]
    weight_ref, out_ref, qkv_ref, *late_sems = refs[-4:]
    refs = refs[:-4]
    late = fetch((weight_in, out_in, qkv_in), (weight_ref, out_ref, qkv_ref), late_sems[0])
    if fast:
        *soon, params_ref = refs[6:13]
        line_refs, far_refs = refs[13:15], refs[15:19]
        *held_refs, soon_sems = refs[-7:]
        soon = fetch(soon, held_refs, soon_sems)
        back_ref, slot_ref, middle_ref, normed_ref, cot_ref, att_ref = held_refs
        refs = refs[19:-7]
    else:
        branch_ref = refs[6]
        refs = refs[7:]
    three_ref, table_ref = refs[:2]
    if fast:
        early_out, output_ref, grad_middle_ref, tiny_ref = refs[2:6]
        line_outs, far_outs = refs[6:8], refs[8:12]
        refs = refs[12:]
    else:
        refs = refs[2:]
    leaving, got, strip, values, dq_all, dk_sum, dv_sum, scores, held, diagonal, send, recv, exp_sems = refs[:13]
    _, heads, size, length = qkv_ref.shape
    total = lax.axis_size("seq")
    me = lax.axis_index("seq")
    tokens = out_ref.shape[3]
    parts = weight_ref.shape[0]
    part = lax.rem(me, parts)
    width = 2 * tokens
    pairs = total // 2
    rows = 2 * length - tokens
    chunk = 256

    def pair_at(t):
        return twist(lax.div(me, 2), t, pairs)

    def load(count):
        slot = lax.rem(count, 2)
        at = exp_ref.at[pair_at(lax.div(count, heads)), lax.rem(count, heads)]
        return pltpu.make_async_copy(at, held.at[slot], exp_sems.at[slot])

    load(0).start()
    peers = [{"seq": lax.rem(me + k, total)} for k in range(1, total)]
    if fast:
        across, row = lax.axis_size("wide"), lax.axis_index("wide")
        other = twist(me, 1, total)
        peers += [{"wide": lax.rem(row + k, across)} for k in range(1, across)]
    meet(peers)
    if fast:
        branch_ref, early_ref, near, near_sum, wide_got, near_sems, wide_sems, line_sems, far_sems = refs[13:]
        seqs = early_ref.shape[0]

        def far_step(e):
            up, down = far_refs[e], far_refs[2 + e]
            return pass_on(
                parts, (seqs - 2, seqs - 2, up, far_outs[e]), (1, 1, down, far_outs[2 + e]), far_sems.at[e]
            )

        line_ends = [far_step(0)]

        def near_copy():
            return pltpu.make_async_remote_copy(
                early_ref.at[:, lax.rem(part + 1, parts)],
                near,
                near_sems.at[0],
                near_sems.at[1],
                device_id={"seq": other},
                device_id_type=MESH,
            )

        def wide_copy(k):
            to = lax.rem(row + k, across)
            return pltpu.make_async_remote_copy(
                near_sum.at[to],
                wide_got.at[k - 1],
                wide_sems.at[0, k - 1],
                wide_sems.at[1, k - 1],
                device_id={"wide": to},
                device_id_type=MESH,
            )

        for copy in soon:
            copy.wait()
        features = middle_ref.shape[1]
        found = contract(slot_ref[...], back_ref[...].reshape(slot_ref.shape[1], 2 * features), 1, 0)
        selected = found[:, :features]
        router = router_of(params_ref, 2 * across)
        logits = contract(normed_ref[...], router, 1, 1)
        grown = jnp.exp(logits - jnp.max(logits, axis=1, keepdims=True))
        probs = grown / jnp.sum(grown, axis=1, keepdims=True)
        routes = routes_of(params_ref, router.shape[0], probs.shape[0])
        picked = (routes == lax.broadcasted_iota(jnp.int32, probs.shape, 1).astype(F32)).astype(F32)
        gate = jnp.sum(probs * picked, axis=1, keepdims=True)
        upstream = cot_ref[...].astype(F32)
        middle = middle_ref[...]
        output_ref[...] = (middle + gate * selected).astype(BF16)
        grad_gate = jnp.sum(upstream * selected, axis=1, keepdims=True)
        grad_logits = (grad_gate * probs * (picked - gate)).astype(BF16)
        grad_normed = found[:, features:] + contract(grad_logits, router, 1, 0)
        inverse = inverse_rms(middle)
        gain_grad = jnp.sum(grad_normed * middle * inverse, axis=0, keepdims=True)
        grad_normed = grad_normed * params_ref[1:2, :]
        mean_inner = jnp.mean(middle * grad_normed, axis=-1, keepdims=True)
        grad_middle = upstream + inverse * grad_normed - middle * (inverse * inverse * inverse) * mean_inner
        grad_middle_ref[...] = grad_middle
        branch = grad_middle.astype(BF16)
        branch_ref[...] = branch.reshape(branch_ref.shape)

    for copy in late:
        copy.wait()

    def product(to):
        value = contract(weight_ref[lax.rem(to, parts)], branch_ref[lax.div(to, parts)], 1, 1)
        return value.astype(BF16).reshape(heads, size, tokens)

    def leave(k, carry):
        to = twist(me, k, total)
        leaving[to] = product(to)
        pltpu.make_async_remote_copy(
            leaving.at[to], got.at[me], send.at[k], recv.at[k], device_id={"seq": to}, device_id_type=MESH
        ).start()
        return carry

    lax.fori_loop(1, total, leave, 0)
    if fast:
        for e in range(line_refs[0].shape[0]):
            up, down = ((1, seqs - 2, line_refs[n].at[e], line_outs[n].at[e]) for n in range(2))
            line_ends.append(pass_on(parts, up, down, line_sems.at[e]))
        line_ends.append(far_step(1))
        attended = jnp.concatenate([att_ref[s] for s in range(seqs)], axis=1)
        early_ref[...] = contract(attended, branch, 1, 0).astype(BF16).reshape(early_ref.shape)
        near_copy().start()
        grad_router = contract(grad_logits, normed_ref[...], 0, 0)
        spare = tiny_ref.shape[0] - 2 - grad_router.shape[0]
        tiny_ref[...] = jnp.concatenate(
            [jnp.zeros((1, features), F32), gain_grad, grad_router, jnp.zeros((spare, features), F32)], axis=0
        )
    got[me] = product(me)

    def prepare(h, carry):
        values[h] = qkv_ref[2, h].T
        strip[h] = jnp.zeros(strip.shape[1:], F32)
        dk_sum[h] = jnp.zeros(dk_sum.shape[1:], F32)
        dv_sum[h] = jnp.zeros(dv_sum.shape[1:], F32)
        return carry

    lax.fori_loop(0, heads, prepare, 0)

    def arrive(k):
        source = twist(me, k, total)
        pltpu.make_async_remote_copy(
            leaving.at[source], got.at[source], send.at[k], recv.at[k], device_id={"seq": source}, device_id_type=MESH
        ).wait()

    def step(t, carry):
        pair = pair_at(t)
        at = pl.ds(pl.multiple_of(pair * width, tokens), width)

        @pl.when(t > 0)
        def _():
            arrive(2 * t)

        arrive(2 * t + 1)
        if fast:

            @pl.when(t == 1)
            def _():
                near_copy().wait()
                for n in range(seqs):
                    for a in range(across):
                        value = early_ref[n, part, a].astype(F32) + near[n, a].astype(F32)
                        near_sum[a, n] = value.astype(BF16)
                for k in range(1, across):
                    wide_copy(k).start()

            @pl.when(t == pairs - 1)
            def _():
                for k in range(1, across):
                    wide_copy(k).wait()
                for n in range(seqs):
                    value = near_sum[row, n].astype(F32)
                    for k in range(1, across):
                        value = value + wide_got[k - 1, n].astype(F32)
                    early_out[n] = value.astype(BF16)

        def head(h, carry):
            count = t * heads + h
            slot = lax.rem(count, 2)

            @pl.when(count + 1 < pairs * heads)
            def _():
                load(count + 1).start()

            grads, inner = [], []
            for s in range(2):
                inverse = inv_ref[pair, h, :, s * tokens : (s + 1) * tokens]
                scaled = got[2 * pair + s, h].astype(F32) * inverse
                inner.append(jnp.sum(scaled * out_ref[2 * pair + s, h].astype(F32), axis=0, keepdims=True))
                grads.append(scaled.astype(BF16))
            grad = jnp.concatenate(grads, axis=1)
            load(count).wait()
            for c in range(length // chunk):
                part_grad = contract(values[h, c * chunk : (c + 1) * chunk, :], grad, 1, 0)
                for s in range(2):
                    grown = held[slot, c * chunk : (c + 1) * chunk, s * tokens : (s + 1) * tokens].astype(F32)
                    slope = grown * (part_grad[:, s * tokens : (s + 1) * tokens] - inner[s])
                    line = pl.multiple_of(length - tokens - (pair * width + s * tokens) + c * chunk, tokens)
                    strip[h, pl.ds(line, chunk), :] += slope
                    scores[c * chunk : (c + 1) * chunk, s * tokens : (s + 1) * tokens] = slope.astype(BF16)
            dq_all[h, at, :] = contract(qkv_ref[1, h], scores[...], 1, 0).T.astype(BF16)
            dk_sum[h] += contract(scores[...], qkv_ref[0, h, :, at].T, 1, 0)
            dv_sum[h] += contract(held[slot], grad.T, 1, 0)
            return carry

        lax.fori_loop(0, heads, head, 0)
        return carry

    lax.fori_loop(0, pairs, step, 0)
    down = lax.broadcasted_iota(jnp.int32, (tokens, tokens), 0)
    over = lax.broadcasted_iota(jnp.int32, (tokens, tokens), 1)
    mirror = (down + over == tokens - 1).astype(F32)
    cols = heads * size
    for c in range(length // chunk):
        here = slice(c * chunk, (c + 1) * chunk)
        for n, ref in enumerate((dq_all, dk_sum, dv_sum)):
            joined = jnp.concatenate([ref[h, here, :].astype(F32) for h in range(heads)], axis=1)
            three_ref[here, n * cols : (n + 1) * cols] = joined.astype(BF16)

    def close(h, carry):
        diagonal[h] = jnp.zeros(diagonal.shape[1:], F32)
        for b in range(rows // tokens):
            flipped = lax.dot_general(
                strip[h, tokens * b : tokens * (b + 1), :],
                mirror,
                (((1,), (0,)), ((), ())),
                precision=lax.Precision.HIGHEST,
                preferred_element_type=F32,
            )
            spread_out = jnp.concatenate([flipped, jnp.zeros_like(flipped)], axis=1)
            rolled = pltpu.roll(spread_out, 0, 1, stride=1, stride_axis=0)
            diagonal[h, :, tokens * b : tokens * (b + 2)] += jnp.sum(rolled, axis=0, keepdims=True)
        return carry

    lax.fori_loop(0, heads, close, 0)
    sums = jnp.concatenate([diagonal[h] for h in range(heads)], axis=0)
    table = lax.dot_general(
        sums,
        hot_ref[...].astype(F32),
        (((1,), (1,)), ((), ())),
        precision=lax.Precision.HIGHEST,
        preferred_element_type=F32,
    )
    line = lax.broadcasted_iota(jnp.int32, (table_ref.shape[0], heads), 0)
    head_line = lax.broadcasted_iota(jnp.int32, (table_ref.shape[0], heads), 1) + part * heads
    table_ref[...] = lax.dot_general(
        (line == head_line).astype(F32),
        table,
        (((1,), (0,)), ((), ())),
        precision=lax.Precision.HIGHEST,
        preferred_element_type=F32,
    )
    if fast:
        for end in line_ends:
            end()


def attend_back(exps, inverse, weight, outs, qkv, hot, branch, more, line, far):
    _, heads, size, length = qkv.shape
    total, tokens = outs.shape[0], outs.shape[3]
    parts, cols, width = weight.shape
    vmem, hbm = pl.BlockSpec(memory_space=pltpu.VMEM), pl.BlockSpec(memory_space=pl.ANY)
    sems = pltpu.SemaphoreType.DMA
    out_shape = [
        jax.ShapeDtypeStruct((length, 3 * heads * size), BF16),
        jax.ShapeDtypeStruct((16, hot.shape[0]), F32),
    ]
    given, scratch = [branch], []
    if branch is None:
        given = more
        across = lax.axis_size("wide")
        slim = width // total // across
        seqs = total // parts
        count = seqs * tokens
        out_shape += [
            jax.ShapeDtypeStruct((seqs, slim, width), BF16),
            jax.ShapeDtypeStruct((count, width), BF16),
            jax.ShapeDtypeStruct((count, width), F32),
            jax.ShapeDtypeStruct((16, width), F32),
        ]
        scratch = [
            pltpu.VMEM((seqs, tokens, width), BF16),
            pltpu.VMEM((seqs, parts, across, slim, width), BF16),
            pltpu.VMEM((seqs, across, slim, width), BF16),
            pltpu.VMEM((across, seqs, slim, width), BF16),
            pltpu.VMEM((across - 1, seqs, slim, width), BF16),
            sems((2,)),
            sems((2, across - 1)),
            sems((line[0].shape[0], 2, 2)),
            sems((len(far) // 2, 2, 2)),
        ]
    passed = [*line, *far]
    held = [pltpu.VMEM(a.shape, a.dtype) for a in more[:6]] + [sems((6,))] if branch is None else []
    spaces = [hbm] * 6 + [vmem] if branch is None else [vmem]
    in_place = len(out_shape)
    out_shape += [jax.ShapeDtypeStruct(rows.shape, BF16) for rows in passed]
    return pl.pallas_call(
        functools.partial(attend_back_kernel, branch is None),
        in_specs=[hbm, vmem, hbm, hbm, hbm, vmem] + spaces + [hbm] * len(passed),
        out_specs=[vmem] * in_place + [hbm] * len(passed),
        out_shape=out_shape,
        scratch_shapes=[
            pltpu.VMEM((total, heads, size, tokens), BF16),
            pltpu.VMEM((total, heads, size, tokens), BF16),
            pltpu.VMEM((heads, 2 * length - tokens, tokens), F32),
            pltpu.VMEM((heads, length, size), BF16),
            pltpu.VMEM((heads, length, size), BF16),
            pltpu.VMEM((heads, length, size), F32),
            pltpu.VMEM((heads, length, size), F32),
            pltpu.VMEM((length, 2 * tokens), BF16),
            pltpu.VMEM((2, length, 2 * tokens), BF16),
            pltpu.VMEM((heads, 1, 2 * length), F32),
            sems((total,)),
            sems((total,)),
            sems((2,)),
            *scratch,
            *held,
            *[pltpu.VMEM(a.shape, a.dtype) for a in (weight, outs, qkv)],
            sems((3,)),
        ],
        compiler_params=pltpu.CompilerParams(collective_id=3, has_side_effects=True, vmem_limit_bytes=62 << 20),
        cost_estimate=pl.CostEstimate(
            flops=8 * heads * length * length * size, bytes_accessed=2 * heads * length * length, transcendentals=0
        ),
        name="attend_back",
    )(exps, inverse, weight, outs, qkv, hot, *given, *passed)


def activation(v):
    square = v * v
    bent = jnp.tanh(0.7978845608 * v * (1.0 + 0.044715 * square))
    half = 0.5 * (1.0 + bent)
    slope = half + 0.5 * v * (1.0 - bent * bent) * (0.7978845608 * (1.0 + 3.0 * 0.044715 * square))
    return v * half, slope


def gated(rows, cots, router, expert):
    logits = contract(rows, router, 1, 1)
    grown = jnp.exp(logits - jnp.max(logits, axis=1, keepdims=True))
    named = lax.broadcasted_iota(jnp.int32, grown.shape, 1) == expert
    gate = jnp.sum(jnp.where(named, grown, 0.0), axis=1, keepdims=True) / jnp.sum(grown, axis=1, keepdims=True)
    return (gate * cots.astype(F32)).astype(BF16)


def expert_kernel(expert, rows_ref, cot_ref, router_ref, in_ref, out_ref, both_ref, forward, backward):
    step = pl.program_id(0)
    width = cot_ref.shape[1]

    @pl.when(step == 0)
    def _():
        forward[...] = jnp.zeros_like(forward)
        backward[...] = jnp.zeros_like(backward)

    rows = rows_ref[...]
    own = router_ref.shape[0] // lax.axis_size("wide")
    grads = gated(rows, cot_ref[...], router_ref[...], lax.axis_index("wide") * own + expert)
    hidden, slope = activation(contract(rows, in_ref[0], 1, 0))
    grad_hidden = contract(grads, out_ref[0], 1, 1).astype(BF16).astype(F32)
    forward[...] += contract(hidden.astype(BF16), out_ref[0], 1, 0)
    backward[...] += contract((grad_hidden * slope).astype(BF16), in_ref[0], 1, 1)

    @pl.when(step == pl.num_programs(0) - 1)
    def _():
        both_ref[:, :width] = forward[...].astype(BF16)
        both_ref[:, width:] = backward[...].astype(BF16)


def run_expert(rows, cots, router, w_in, w_out, expert, block):
    count, width = cots.shape
    units = w_in.shape[2]
    return pl.pallas_call(
        functools.partial(expert_kernel, expert),
        grid=(units // block,),
        in_specs=[
            pl.BlockSpec(rows.shape, lambda f: (0, 0)),
            pl.BlockSpec(cots.shape, lambda f: (0, 0)),
            pl.BlockSpec(router.shape, lambda f: (0, 0)),
            pl.BlockSpec((1, width, block), lambda f: (expert, 0, f)),
            pl.BlockSpec((1, block, width), lambda f: (expert, f, 0)),
        ],
        out_specs=pl.BlockSpec((count, 2 * width), lambda f: (0, 0)),
        out_shape=jax.ShapeDtypeStruct((count, 2 * width), BF16),
        scratch_shapes=[pltpu.VMEM((count, width), F32), pltpu.VMEM((count, width), F32)],
        compiler_params=pltpu.CompilerParams(vmem_limit_bytes=40 << 20),
        name="expert",
    )(rows, cots, router, w_in, w_out)


def route_kernel(
    capacity,
    own,
    att_in,
    weight_in,
    tokens_in,
    hot_in,
    table_ref,
    cot_ref,
    before_ref,
    after_ref,
    middle_ref,
    normed_ref,
    out_ref,
    second_before,
    second_after,
    next_before,
    next_after,
    att_ref,
    weight_ref,
    in_ref,
    hot_ref,
    fetch_sems,
    packed,
    send,
    recv,
    local,
    line_sems,
):
    seqs = att_ref.shape[0]
    across = lax.axis_size("wide")
    parts = lax.axis_size("seq") // seqs
    me = lax.axis_index("wide")
    held = fetch((att_in, weight_in, tokens_in, hot_in), (att_ref, weight_ref, in_ref, hot_ref), fetch_sems)
    meet([{"wide": lax.rem(me + k, across)} for k in range(1, across)] + line_peers(parts))
    line_ends = [
        pass_on(parts, (0, seqs - 2, cot_ref.at[1], next_before), (1, seqs - 1, cot_ref.at[1], next_after), line_sems.at[0]),
        pass_on(parts, (1, seqs - 2, before_ref, second_before), (1, seqs - 2, after_ref, second_after), line_sems.at[1]),
    ]
    for copy in held:
        copy.wait()
    attended = jnp.concatenate([att_ref[s] for s in range(seqs)], axis=1)
    middle = in_ref[...].astype(F32) + contract(attended, weight_ref[...], 0, 0)
    middle_ref[...] = middle
    normed = (middle * inverse_rms(middle) * table_ref[1:2, :]).astype(BF16)
    normed_ref[...] = normed
    packed[...] = contract(hot_ref[...], normed, 0, 0).astype(BF16).reshape(packed.shape)
    copies = []
    mine = pl.ds(me * capacity, capacity)
    for n in range(own):
        for k in range(1, across):
            to = lax.rem(me + k, across)
            copies.append(
                remote(
                    packed.at[n, pl.ds(to * capacity, capacity)],
                    out_ref.at[n, mine],
                    send.at[n, k - 1],
                    recv.at[n, k - 1],
                    {"wide": to},
                )
            )
    kept = [pltpu.make_async_copy(packed.at[n, mine], out_ref.at[n, mine], local.at[n]) for n in range(own)]
    for copy in kept:
        copy.start()
    for copy in kept + copies:
        copy.wait()
    for end in line_ends:
        end()


def route(attended, weight, tokens_in, gain, hot, cots, before, after, capacity):
    across = lax.axis_size("wide")
    own = cots.shape[0]
    tokens, width = tokens_in.shape
    vmem, hbm = pl.BlockSpec(memory_space=pltpu.VMEM), pl.BlockSpec(memory_space=pl.ANY)
    one = jax.ShapeDtypeStruct(before.shape, before.dtype)
    sems = pltpu.SemaphoreType.DMA
    return pl.pallas_call(
        functools.partial(route_kernel, capacity, own),
        in_specs=[hbm] * 4 + [vmem] + [hbm] * 3,
        out_specs=[vmem, vmem] + [hbm] * 5,
        out_shape=[
            jax.ShapeDtypeStruct((tokens, width), F32),
            jax.ShapeDtypeStruct((tokens, width), BF16),
            jax.ShapeDtypeStruct(cots.shape, BF16),
            *[one] * 4,
        ],
        scratch_shapes=[
            *[pltpu.VMEM(a.shape, BF16) for a in (attended, weight, tokens_in, hot)],
            sems((4,)),
            pltpu.VMEM(cots.shape, BF16),
            sems((own, across - 1)),
            sems((own, across - 1)),
            sems((own,)),
            sems((2, 2, 2)),
        ],
        compiler_params=pltpu.CompilerParams(collective_id=4, has_side_effects=True, vmem_limit_bytes=62 << 20),
        name="route",
    )(attended, weight, tokens_in, hot, gain, cots, before, after)


def experts_kernel(
    block,
    seqs,
    rows_ref,
    cot_ref,
    router_ref,
    in_ref,
    out_ref,
    line_ref,
    before_ref,
    after_ref,
    back_ref,
    before_out,
    after_out,
    line_before,
    line_after,
    done,
    grads,
    forward,
    backward,
    in_held,
    out_held,
    back_send,
    back_recv,
    local,
    held_sems,
    line_sems,
):
    own, rows, double = back_ref.shape
    width = double // 2
    across = lax.axis_size("wide")
    me = lax.axis_index("wide")
    count = rows // across
    steps = in_ref.shape[2] // block

    def load(at):
        slot = lax.rem(at, 2)
        expert, place = lax.div(at, steps), pl.multiple_of(lax.rem(at, steps) * block, block)
        return (
            pltpu.make_async_copy(in_ref.at[expert, :, pl.ds(place, block)], in_held.at[slot], held_sems.at[0, slot]),
            pltpu.make_async_copy(out_ref.at[expert, pl.ds(place, block), :], out_held.at[slot], held_sems.at[1, slot]),
        )

    for copy in load(0):
        copy.start()
    parts = lax.axis_size("seq") // seqs
    meet([{"wide": lax.rem(me + k, across)} for k in range(1, across)] + line_peers(parts))
    line_ends = [
        pass_on(
            parts,
            (1, seqs - 2, before_ref, before_out),
            (1, seqs - 2, after_ref, after_out),
            line_sems.at[0],
        ),
        pass_on(parts, (0, seqs - 2, line_ref, line_before), (1, seqs - 1, line_ref, line_after), line_sems.at[1]),
    ]
    coming = []
    mine = pl.ds(me * count, count)
    for e in range(own):
        grads[...] = gated(rows_ref[e], cot_ref[e], router_of(router_ref, own * across), me * own + e)
        forward[...] = jnp.zeros_like(forward)
        backward[...] = jnp.zeros_like(backward)

        def step(f, carry):
            at = e * steps + f
            slot = lax.rem(at, 2)

            @pl.when(at + 1 < own * steps)
            def _():
                for copy in load(at + 1):
                    copy.start()

            for copy in load(at):
                copy.wait()
            hidden, slope = activation(contract(rows_ref[e], in_held[slot], 1, 0))
            grad_hidden = contract(grads[...], out_held[slot], 1, 1).astype(BF16).astype(F32)
            forward[...] += contract(hidden.astype(BF16), out_held[slot], 1, 0)
            backward[...] += contract((grad_hidden * slope).astype(BF16), in_held[slot], 1, 1)
            return carry

        lax.fori_loop(0, steps, step, 0)
        done[e, :, :width] = forward[...].astype(BF16)
        done[e, :, width:] = backward[...].astype(BF16)
        for k in range(1, across):
            to = lax.rem(me + k, across)
            coming.append(
                remote(
                    done.at[e, pl.ds(to * count, count)],
                    back_ref.at[e, mine],
                    back_send.at[e, k - 1],
                    back_recv.at[e, k - 1],
                    {"wide": to},
                )
            )
        kept = pltpu.make_async_copy(done.at[e, mine], back_ref.at[e, mine], local.at[e])
        kept.start()
        kept.wait()
    for copy in coming:
        copy.wait()
    for end in line_ends:
        end()


def run_experts(rows, cots, router, w_in, w_out, before, after, seqs, block):
    own, count, width = cots.shape
    units = w_in.shape[2]
    across = lax.axis_size("wide")
    vmem, hbm = pl.BlockSpec(memory_space=pltpu.VMEM), pl.BlockSpec(memory_space=pl.ANY)
    sems = pltpu.SemaphoreType.DMA
    return pl.pallas_call(
        functools.partial(experts_kernel, block, seqs),
        in_specs=[vmem, vmem, vmem, hbm, hbm, hbm, hbm, hbm],
        out_specs=[vmem, hbm, hbm, hbm, hbm],
        out_shape=[
            jax.ShapeDtypeStruct((own, count, 2 * width), BF16),
            *[jax.ShapeDtypeStruct(before.shape, BF16)] * 2,
            *[jax.ShapeDtypeStruct(rows.shape, BF16)] * 2,
        ],
        scratch_shapes=[
            pltpu.VMEM((own, count, 2 * width), BF16),
            pltpu.VMEM((count, width), BF16),
            pltpu.VMEM((count, width), F32),
            pltpu.VMEM((count, width), F32),
            pltpu.VMEM((2, width, block), BF16),
            pltpu.VMEM((2, block, width), BF16),
            sems((own, across - 1)),
            sems((own, across - 1)),
            sems((own,)),
            sems((2, 2)),
            sems((2, 2, 2)),
        ],
        compiler_params=pltpu.CompilerParams(collective_id=5, has_side_effects=True, vmem_limit_bytes=62 << 20),
        cost_estimate=pl.CostEstimate(
            flops=8 * own * count * width * units, bytes_accessed=4 * own * width * units, transcendentals=own * count * units
        ),
        name="experts",
    )(rows, cots, router, w_in, w_out, rows, before, after)


def share_kernel(expert, share_ref, rows_ref, cot_ref, router_ref, in_ref, out_ref, *refs):
    grad_in_ref, grad_out_ref, flipped, total_in = refs[-4:]
    step = pl.program_id(0)

    @pl.when(step == 0)
    def _():
        flipped[...] = in_ref[0].T
        total_in[...] = jnp.zeros_like(total_in)
        grad_out_ref[...] = jnp.zeros_like(grad_out_ref)

    rows = rows_ref[0]
    own = router_ref.shape[0] // lax.axis_size("wide")
    grads = gated(rows, cot_ref[0], router_ref[...], lax.axis_index("wide") * own + expert)
    hidden, slope = activation(contract(flipped[...], rows, 1, 1))
    grad_hidden = contract(out_ref[0], grads, 1, 1).astype(BF16).astype(F32)
    grad_out_ref[0] += contract(hidden.astype(BF16), grads, 1, 0)
    total_in[...] += contract((grad_hidden * slope).astype(BF16), rows, 1, 0)

    @pl.when(step == pl.num_programs(0) - 1)
    def _():
        grad_in_ref[0] = total_in[...].T


def run_share(me, rows, cots, router, w_in, w_out, expert, held):
    own, width, units = w_in.shape
    sources, count = rows.shape[0] // own, rows.shape[1]
    share = units // sources
    if share % LANES == 0:
        where = jnp.full((1,), me, jnp.int32)
        in_spec = pl.BlockSpec((1, width, share), lambda r, at: (expert, 0, at[0]))
        out_spec = pl.BlockSpec((1, share, width), lambda r, at: (expert, at[0], 0))
    else:
        where = jnp.zeros((1,), jnp.int32)
        w_in = lax.dynamic_slice(w_in, (0, 0, me * share), (own, width, share))
        w_out = lax.dynamic_slice(w_out, (0, me * share, 0), (own, share, width))
        in_spec = pl.BlockSpec((1, width, share), lambda r, at: (expert, 0, 0))
        out_spec = pl.BlockSpec((1, share, width), lambda r, at: (expert, 0, 0))
    held_specs = [pl.BlockSpec(memory_space=pl.ANY)] * len(held)
    return pl.pallas_call(
        functools.partial(share_kernel, expert),
        grid_spec=pltpu.PrefetchScalarGridSpec(
            num_scalar_prefetch=1,
            grid=(sources,),
            in_specs=[
                pl.BlockSpec((1, count, rows.shape[2]), lambda r, at: (own * r + expert, 0, 0)),
                pl.BlockSpec((1, count, width), lambda r, at: (own * r + expert, 0, 0)),
                pl.BlockSpec(router.shape, lambda r, at: (0, 0)),
                in_spec,
                out_spec,
                *held_specs,
            ],
            out_specs=[
                pl.BlockSpec((1, width, share), lambda r, at: (expert, 0, 0)),
                pl.BlockSpec((1, share, width), lambda r, at: (expert, 0, 0)),
            ],
            scratch_shapes=[pltpu.VMEM((share, width), BF16), pltpu.VMEM((share, width), F32)],
        ),
        out_shape=[
            jax.ShapeDtypeStruct((own, width, share), F32),
            jax.ShapeDtypeStruct((own, share, width), F32),
        ],
        input_output_aliases={6 + i: i for i in range(len(held))},
        compiler_params=pltpu.CompilerParams(vmem_limit_bytes=62 << 20),
        cost_estimate=pl.CostEstimate(
            flops=8 * sources * count * width * share, bytes_accessed=4 * sources * count * width, transcendentals=0
        ),
        name="share",
    )(where, rows, cots, router, w_in, w_out, *held)


def spread_kernel(parts, in_ref, out_ref, send, recv, pass_send, pass_recv, local):
    total = lax.axis_size("seq")
    me = lax.axis_index("seq")
    part = lax.rem(me, parts)
    meet([{"seq": lax.rem(me + k, total)} for k in range(1, total)])
    copies = []
    for k in far_first(total):
        to = lax.rem(me + k, total)
        copies.append(remote(in_ref.at[to], out_ref.at[me, lax.rem(to, parts)], send.at[k - 1], recv.at[k - 1], {"seq": to}))
    own = pltpu.make_async_copy(in_ref.at[me], out_ref.at[me, part], local)
    own.start()
    own.wait()
    passed = []

    def forward(source, k):
        for j in range(1, parts):
            to = me - part + lax.rem(part + j, parts)
            at = (j - 1) * total + k
            block = out_ref.at[source, part]
            passed.append(remote(block, block, pass_send.at[at], pass_recv.at[at], {"seq": to}))

    forward(me, 0)
    for k in far_first(total)[::-1]:
        source = lax.rem(me - k + total, total)
        block = out_ref.at[source, part]
        pltpu.make_async_remote_copy(
            block, block, send.at[k - 1], recv.at[k - 1], device_id={"seq": source}, device_id_type=MESH
        ).wait_recv()
        forward(source, k)
    for copy in copies:
        copy.wait_send()
    for copy in passed:
        copy.wait()


def spread(blocks, parts):
    total, rows, width = blocks.shape
    passes = (parts - 1) * total
    return pl.pallas_call(
        functools.partial(spread_kernel, parts),
        in_specs=[pl.BlockSpec(memory_space=pl.ANY)],
        out_specs=pl.BlockSpec(memory_space=pl.ANY),
        out_shape=jax.ShapeDtypeStruct((total, parts, rows, width), blocks.dtype),
        scratch_shapes=[
            pltpu.SemaphoreType.DMA((total - 1,)),
            pltpu.SemaphoreType.DMA((total - 1,)),
            pltpu.SemaphoreType.DMA((passes,)),
            pltpu.SemaphoreType.DMA((passes,)),
            pltpu.SemaphoreType.DMA,
        ],
        compiler_params=pltpu.CompilerParams(collective_id=0, has_side_effects=True),
        name="spread",
    )(blocks)


def begin_kernel(
    capacity,
    experts,
    in_ref,
    query_in,
    key_in,
    value_in,
    cot_in,
    table_ref,
    base_ref,
    all_out,
    qkv_out,
    flip_out,
    hot_out,
    rows_ref,
    weights_out,
    all_ref,
    qkv_ref,
    flip_ref,
    hot_ref,
    weights,
    query_ref,
    key_ref,
    value_ref,
    cot_ref,
    fetch_sems,
    packed,
    send,
    recv,
    pass_send,
    pass_recv,
    wide_send,
    wide_recv,
    local,
):
    total, parts, rows, width = all_ref.shape
    _, heads, size, length = qkv_ref.shape
    own = rows_ref.shape[0]
    cols = heads * size
    across = lax.axis_size("wide")
    me, row = lax.axis_index("seq"), lax.axis_index("wide")
    part = lax.rem(me, parts)
    other = twist(me, 1, total)
    pairs = total // 2
    held = fetch((cot_in, query_in, key_in, value_in), (cot_ref, query_ref, key_ref, value_ref), fetch_sems)
    peers = [{"seq": lax.rem(me + k, total)} for k in range(1, total)]
    peers += [{"wide": lax.rem(row + k, across)} for k in range(1, across)]
    meet(peers)
    sent = []
    for k in range(1, total):
        to = twist(me, k, total)
        sent.append(remote(in_ref.at[to], all_ref.at[me, lax.rem(to, parts)], send.at[to], recv.at[me], {"seq": to}))
    kept = pltpu.make_async_copy(in_ref.at[me], all_ref.at[me, part], local.at[0])
    kept.start()
    kept.wait()
    passed = []

    def forward(source):
        block = all_ref.at[source, part]
        passed.append(remote(block, block, pass_send.at[source], pass_recv.at[source], {"seq": other}))

    def await_recv(block, sem):
        pltpu.make_async_remote_copy(
            block, block, local.at[1], sem, device_id={"seq": other}, device_id_type=MESH
        ).wait_recv()

    forward(me)

    tokens, slots = hot_ref.shape
    routes = routes_of(table_ref, experts, tokens)
    picked = (routes == lax.broadcasted_iota(jnp.int32, (tokens, LANES), 1).astype(F32)).astype(F32)
    down = lax.broadcasted_iota(jnp.int32, (tokens, tokens), 0)
    over = lax.broadcasted_iota(jnp.int32, (tokens, tokens), 1)
    earlier = contract((over < down).astype(F32).astype(BF16), picked.astype(BF16), 1, 0)
    rank = jnp.sum(earlier * picked, axis=1, keepdims=True)
    place = jnp.sum(base_ref[...] * picked, axis=1, keepdims=True) + rank
    place = jnp.where(rank < capacity, place, float(slots)).astype(jnp.int32)
    hot = (place == lax.broadcasted_iota(jnp.int32, (tokens, slots), 1)).astype(F32).astype(BF16)
    hot_ref[...] = hot
    held[0].wait()
    stored = [pltpu.make_async_copy(hot_ref, hot_out, fetch_sems.at[4])]
    stored[0].start()
    packed[...] = contract(hot, cot_ref[...], 0, 0).astype(BF16).reshape(packed.shape)
    wide = []
    mine = pl.ds(row * capacity, capacity)
    for e in range(own):
        for k in range(1, across):
            to = lax.rem(row + k, across)
            wide.append(
                remote(
                    packed.at[e, pl.ds(to * capacity, capacity)],
                    rows_ref.at[e, mine],
                    wide_send.at[e, k - 1],
                    wide_recv.at[e, k - 1],
                    {"wide": to},
                )
            )
    stay = [pltpu.make_async_copy(packed.at[e, mine], rows_ref.at[e, mine], local.at[2 + e]) for e in range(own)]
    for copy in stay:
        copy.start()
    at = pl.ds(pl.multiple_of(part * cols, LANES), cols)
    for n, ref in enumerate((query_ref, key_ref, value_ref)):
        held[1 + n].wait()
        weights[n * cols : (n + 1) * cols, :] = ref[:, at].T
    stored.append(pltpu.make_async_copy(weights, weights_out, fetch_sems.at[5]))
    stored[1].start()

    for t in range(pairs):
        pair = twist(lax.div(me, 2), t, pairs)
        for b in range(2):
            if 2 * t + b:
                source = twist(me, 2 * t + b, total)
                await_recv(all_ref.at[source, part], recv.at[source])
                forward(source)
        for b in range(2):
            source = 2 * pair + b
            await_recv(all_ref.at[source, lax.rem(part + 1, parts)], pass_recv.at[source])
        block = all_ref[pl.ds(2 * pair, 2)].reshape(2 * parts * rows, width).astype(F32)
        normed = (block * inverse_rms(block) * table_ref[0:1, :]).astype(BF16)
        here = pl.ds(pl.multiple_of(pair * (2 * parts * rows), LANES), 2 * parts * rows)
        flip_ref[:, here] = normed.T
        projected = contract(weights[...], normed, 1, 1).astype(BF16)
        qkv_ref[:, :, :, here] = projected.reshape(3, heads, size, 2 * parts * rows)
        both = pl.ds(2 * pair, 2)
        for n, (src, dst) in enumerate(
            (
                (all_ref.at[both], all_out.at[both]),
                (flip_ref.at[:, here], flip_out.at[:, here]),
                (qkv_ref.at[:, :, :, here], qkv_out.at[:, :, :, here]),
            )
        ):
            stored.append(pltpu.make_async_copy(src, dst, fetch_sems.at[6 + 3 * t + n]))
            stored[-1].start()
    for copy in sent + passed:
        copy.wait_send()
    for copy in wide + stay + stored:
        copy.wait()


def begin(blocks, w_query, w_key, w_value, table, base, cot, heads, size, own, capacity):
    total, rows, width = blocks.shape
    tokens = cot.shape[0]
    across = lax.axis_size("wide")
    slots = own * across * capacity
    length = total * 2 * rows
    vmem, hbm = pl.BlockSpec(memory_space=pltpu.VMEM), pl.BlockSpec(memory_space=pl.ANY)
    sems = pltpu.SemaphoreType.DMA
    return pl.pallas_call(
        functools.partial(begin_kernel, capacity, own * across),
        in_specs=[hbm] * 5 + [vmem] * 2,
        out_specs=[hbm] * 4 + [vmem, hbm],
        out_shape=[
            jax.ShapeDtypeStruct((total, 2, rows, width), BF16),
            jax.ShapeDtypeStruct((3, heads, size, length), BF16),
            jax.ShapeDtypeStruct((width, length), BF16),
            jax.ShapeDtypeStruct((tokens, slots), BF16),
            jax.ShapeDtypeStruct((own, across * capacity, width), BF16),
            jax.ShapeDtypeStruct((3 * heads * size, width), BF16),
        ],
        scratch_shapes=[
            pltpu.VMEM((total, 2, rows, width), BF16),
            pltpu.VMEM((3, heads, size, length), BF16),
            pltpu.VMEM((width, length), BF16),
            pltpu.VMEM((tokens, slots), BF16),
            pltpu.VMEM((3 * heads * size, width), BF16),
            pltpu.VMEM((width, width), BF16),
            pltpu.VMEM((width, width), BF16),
            pltpu.VMEM((width, width), BF16),
            pltpu.VMEM((tokens, width), BF16),
            sems((6 + 3 * total // 2,)),
            pltpu.VMEM((own, across * capacity, width), BF16),
            sems((total,)),
            sems((total,)),
            sems((total,)),
            sems((total,)),
            sems((own, across - 1)),
            sems((own, across - 1)),
            sems((2 + own,)),
        ],
        compiler_params=pltpu.CompilerParams(collective_id=6, has_side_effects=True, vmem_limit_bytes=62 << 20),
        cost_estimate=pl.CostEstimate(flops=4 << 30, bytes_accessed=80 << 20, transcendentals=0),
        name="begin",
    )(blocks, w_query, w_key, w_value, cot, table, base)


def finish_kernel(
    seqs,
    three_ref,
    flip_ref,
    weight_ref,
    x_ref,
    early_ref,
    tiny_ref,
    table_ref,
    params_ref,
    *refs,
):
    own, steps = 2, 2 * seqs - 1
    inputs = (flip_ref, three_ref, weight_ref, x_ref)
    flip_ref, three_ref, weight_ref, x_ref, sems = refs[-5:]
    held = fetch(inputs, (flip_ref, three_ref, weight_ref, x_ref), sems)
    refs = refs[:-5]
    rows_refs = refs[: steps - 2]
    cots_refs = refs[steps - 2 : steps - 2 + 1 + own * (steps - 1)]
    finish_rest(
        seqs,
        held,
        rows_refs,
        cots_refs,
        three_ref,
        flip_ref,
        weight_ref,
        x_ref,
            early_ref,
        tiny_ref,
        table_ref,
        params_ref,
        *refs[len(rows_refs) + len(cots_refs) :],
    )


def finish_rest(
    seqs,
    held,
    rows_refs,
    cots_refs,
    three_ref,
    flip_ref,
    weight_ref,
    x_ref,
    early_ref,
    tiny_ref,
    table_ref,
    params_ref,
    in_ref,
    out_ref,
    home_ref,
    late_all,
    early_all,
    tiny,
    grad_in_ref,
    grad_out_ref,
    grads,
    near,
    summed,
    gw,
    wide_got,
    wide_sum,
    far_got,
    early_got,
    mine,
    early_mine,
    tiny_got,
    rows_held,
    cots_held,
    in_held,
    out_held,
    sums,
    total_in,
    leaving,
    share_got,
    share_sems,
    near_sems,
    home_sems,
    wide_sems,
    far_sems,
    early_sems,
    last_sems,
    last_early_sems,
    tiny_sems,
    held_sems,
    line_sems,
    local,
):
    total, across = lax.axis_size("seq"), lax.axis_size("wide")
    parts = total // seqs
    me, row = lax.axis_index("seq"), lax.axis_index("wide")
    part, seq = lax.rem(me, parts), lax.div(me, parts)
    other = twist(me, 1, total)
    width = params_ref.shape[1]
    slim = gw.shape[2]
    own = in_ref.shape[0]
    share = in_ref.shape[2] // total
    cols = three_ref.shape[1] // 3
    half = three_ref.shape[0] // 2

    def seq_at(k):
        return lax.rem(seq + k, seqs) * parts + part

    def row_at(k):
        return lax.rem(row + k, across)

    def part_at(k):
        return me - part + lax.rem(part + k, parts)

    at = pl.ds(pl.multiple_of(lax.div(me, 2) * (2 * share), LANES), 2 * share)
    weights = [
        pltpu.make_async_copy(in_ref.at[:, :, at], in_held, local.at[0]),
        pltpu.make_async_copy(out_ref.at[:, at, :], out_held, local.at[1]),
    ]
    for copy in weights:
        copy.start()

    def load_rows(e, n, k):
        return pltpu.make_async_copy(rows_refs[k].at[e], rows_held.at[e, n], held_sems.at[0, e, n])

    def load_cots(e, n, k):
        src = cots_refs[1 + own * (k - 1) + e] if k else cots_refs[0].at[e]
        return pltpu.make_async_copy(src, cots_held.at[e, n], held_sems.at[1, e, n])

    last_place = seqs - 1
    far_end = jnp.logical_or(seq == 0, seq == last_place)
    for e in range(own):
        load_rows(e, 0, 0).start()
        load_cots(e, 0, 0).start()
        for here in range(seqs):

            @pl.when(seq == here)
            def _():
                sources = [2 * k - 1 for k in range(1, here + 1)] + [2 * k for k in range(1, seqs - here)]
                for n, k in enumerate(sources):
                    load_cots(e, n + 1, k).start()
                    if k < len(rows_refs):
                        load_rows(e, n + 1, k).start()

    pairs = [(a, b) for a in range(across) for b in range(parts) if a or b]
    peers = [{"seq": lax.rem(me + k, total)} for k in range(1, total)]
    peers += [{"wide": row_at(k)} for k in range(1, across)]
    peers += [{"wide": row_at(a), "seq": part_at(b)} for a, b in pairs if a and b]
    meet(peers)

    def far_rows(e, up):
        src = rows_refs[3 if up else 4].at[e]
        to = lax.rem(me + (parts if up else total - parts), total)
        return pltpu.make_async_remote_copy(
            src, rows_held.at[e, last_place], line_sems.at[0, e], line_sems.at[1, e], device_id={"seq": to}, device_id_type=MESH
        )

    for e in range(own):

        @pl.when(seq == last_place - 1)
        def _():
            far_rows(e, True).start()

        @pl.when(seq == 1)
        def _():
            far_rows(e, False).start()

    for copy in held:
        copy.wait()
    late = contract(flip_ref[...], three_ref[...], 1, 0).astype(BF16)
    gw[...] = late.reshape(gw.shape)
    wide_copies = [
        remote(gw.at[:, row_at(k)], wide_got.at[k - 1], wide_sems.at[0, k - 1], wide_sems.at[1, k - 1], {"wide": row_at(k)})
        for k in range(1, across)
    ]

    gain = params_ref[0:1, :]
    gain_grad = jnp.zeros((1, width), F32)
    near_copies = []
    for n in range(2):
        scaled = contract(three_ref[n * half : (n + 1) * half, :], weight_ref[...], 1, 0)
        x = x_ref[n * total // 2 : (n + 1) * total // 2].reshape(half, width).astype(F32)
        inverse = inverse_rms(x)
        gain_grad = gain_grad + jnp.sum(scaled * x * inverse, axis=0, keepdims=True)
        scaled = scaled * gain
        mean_inner = jnp.mean(x * scaled, axis=-1, keepdims=True)
        value = inverse * scaled - x * (inverse * inverse * inverse) * mean_inner
        here = pl.ds(n * total // 2, total // 2)
        grads[here] = value.astype(BF16).reshape(total // 2, *grads.shape[1:])
        near_copies.append(
            remote(
                grads.at[here, lax.rem(part + 1, parts)],
                near.at[here],
                near_sems.at[0, n],
                near_sems.at[1, n],
                {"seq": other},
            )
        )
    lines = tiny_ref.shape[0]
    first = lax.broadcasted_iota(jnp.int32, tiny_ref.shape, 0) == 0
    tiny[:lines, :] = jnp.where(first, gain_grad, tiny_ref[...]).astype(BF16)
    table = table_ref[...]
    tiny[lines:, :] = jnp.concatenate([table, jnp.zeros((table.shape[0], width - table.shape[1]), F32)], axis=1).astype(BF16)

    def pass_tiny(stage, wheres):
        return [
            remote(tiny, tiny_got.at[stage, n], tiny_sems.at[0, stage, n], tiny_sems.at[1, stage, n], where)
            for n, where in enumerate(wheres)
        ]

    def take_tiny(stage, copies):
        for copy in copies:
            copy.wait()
        value = tiny[...].astype(F32)
        for n in range(len(copies)):
            value = value + tiny_got[stage, n].astype(F32)
        tiny[...] = value.astype(BF16)

    tiny_copies = pass_tiny(0, [{"wide": row_at(k)} for k in range(1, across)])
    for copy in near_copies:
        copy.wait()
    home_copies = []
    for k in range(total - 1, -1, -1):
        to = twist(me, k, total)
        summed[to] = (grads[to, part].astype(F32) + near[to].astype(F32)).astype(BF16)
        if k:
            home_copies.append(
                remote(summed.at[to], home_ref.at[me], home_sems.at[0, k - 1], home_sems.at[1, k - 1], {"seq": to})
            )
    kept = pltpu.make_async_copy(summed.at[me], home_ref.at[me], local.at[2])
    kept.start()
    for copy in weights:
        copy.wait()

    mine_rows = pl.ds(pl.multiple_of(part * share, LANES), share)
    other_rows = pl.ds(pl.multiple_of((1 - part) * share, LANES), share)

    def share_turn(e, n):
        some = rows_held.shape[1] // 2
        for m in range(n * some, (n + 1) * some):
            load_cots(e, m, 0).wait()
            if m < last_place:
                load_rows(e, m, 0).wait()
            else:

                @pl.when(far_end)
                def _():
                    far_rows(e, True).wait_recv()

                @pl.when(jnp.logical_not(far_end))
                def _():
                    load_rows(e, m, 0).wait()

        count = some * rows_held.shape[2]
        here = slice(n * some, (n + 1) * some)
        rows = rows_held[e, here].reshape(count, width)
        cots = gated(rows, cots_held[e, here].reshape(count, width), router_of(params_ref, own * across), row * own + e)
        hidden, slope = activation(contract(in_held[e].T, rows, 1, 1))
        grad_hidden = contract(out_held[e], cots, 1, 1).astype(BF16).astype(F32)
        part_out = contract(hidden.astype(BF16), cots, 1, 0)
        part_in = contract((grad_hidden * slope).astype(BF16), rows, 1, 0)
        if n == 0:
            sums[e, 0] = part_out
            sums[e, 1] = part_in
            return []
        sums[e, 0] += part_out
        sums[e, 1] += part_in
        grad_out_ref[e] = sums[e, 0, mine_rows, :]
        total_in[e] = sums[e, 1, mine_rows, :]
        copies = []
        for k in range(2):
            leaving[e, k] = sums[e, k, other_rows, :].astype(BF16)
            copies.append(
                remote(leaving.at[e, k], share_got.at[e, k], share_sems.at[0, e, k], share_sems.at[1, e, k], {"seq": other})
            )
        return copies

    def share_end(e, copies):
        for copy in copies:
            copy.wait()
        grad_out_ref[e] += share_got[e, 0].astype(F32)
        grad_in_ref[e] = (total_in[e] + share_got[e, 1].astype(F32)).T

    share_turn(0, 0)
    share_turn(1, 0)
    take_tiny(0, tiny_copies)
    for copy in wide_copies:
        copy.wait_recv()
    far_copies = []
    for k in list(range(1, seqs)) + [0]:
        place = lax.rem(seq + k, seqs)
        for p in range(parts):
            block = place * parts + p
            value = gw[block, row].astype(F32)
            for j in range(across - 1):
                value = value + wide_got[j, block].astype(F32)
            wide_sum[place, p] = value.astype(BF16)
        if k:
            where = {"seq": seq_at(k)}
            far_copies.append(
                remote(wide_sum.at[place], far_got.at[k - 1], far_sems.at[0, k - 1], far_sems.at[1, k - 1], where)
            )
            far_copies.append(
                remote(early_ref.at[place], early_got.at[k - 1], early_sems.at[0, k - 1], early_sems.at[1, k - 1], where)
            )
    tiny_copies = pass_tiny(1, [{"seq": seq_at(k)} for k in range(1, seqs)])
    first_share = share_turn(0, 1)
    take_tiny(1, tiny_copies)
    for copy in far_copies:
        copy.wait_recv()
    for p in range(parts):
        value = wide_sum[seq, p].astype(F32)
        for j in range(seqs - 1):
            value = value + far_got[j, p].astype(F32)
        mine[p] = value.astype(BF16)
    value = early_ref[seq].astype(F32)
    for j in range(seqs - 1):
        value = value + early_got[j].astype(F32)
    early_mine[...] = value.astype(BF16)
    last = pass_tiny(2, [{"seq": part_at(k)} for k in range(1, parts)])
    count = len(last)
    for a, b in pairs:
        n = a * parts + b - 1
        last.append(
            remote(
                mine.at[lax.rem(part + b, parts)],
                late_all.at[row, part],
                last_sems.at[0, n],
                last_sems.at[1, n],
                {"wide": row_at(a), "seq": part_at(b)},
            )
        )
    for k in range(1, across):
        last.append(
            remote(
                early_mine, early_all.at[row], last_early_sems.at[0, k - 1], last_early_sems.at[1, k - 1], {"wide": row_at(k)}
            )
        )
    stay = [
        pltpu.make_async_copy(mine.at[part], late_all.at[row, part], local.at[3]),
        pltpu.make_async_copy(early_mine, early_all.at[row], local.at[4]),
    ]
    for copy in stay:
        copy.start()
    second_share = share_turn(1, 1)
    share_end(0, first_share)
    take_tiny(2, last[:count])
    share_end(1, second_share)
    for e in range(own):

        @pl.when(jnp.logical_or(seq == 1, seq == last_place - 1))
        def _():
            far_rows(e, True).wait_send()

    for copy in last[count:] + stay + home_copies + [kept]:
        copy.wait()
    for copy in wide_copies + far_copies:
        copy.wait_send()


def finish(three, flipped, weights, x, early, tiny, table, params, rows, cots, w_in, w_out):
    columns = three.shape[1]
    total, parts, piece, width = x.shape
    seqs, slim, _ = early.shape
    across = lax.axis_size("wide")
    own, _, units = w_in.shape
    share = units // total
    vmem, hbm = pl.BlockSpec(memory_space=pltpu.VMEM), pl.BlockSpec(memory_space=pl.ANY)
    sems = pltpu.SemaphoreType.DMA
    most = max(across, seqs, parts) - 1
    lines = tiny.shape[0] + table.shape[0]
    return pl.pallas_call(
        functools.partial(finish_kernel, seqs),
        in_specs=[hbm] * 4 + [vmem] * 4 + [hbm] * (len(rows) + len(cots) + 2),
        out_specs=[vmem] * 6,
        out_shape=[
            jax.ShapeDtypeStruct((total, piece, width), BF16),
            jax.ShapeDtypeStruct((across, parts, slim, columns), BF16),
            jax.ShapeDtypeStruct((across, slim, width), BF16),
            jax.ShapeDtypeStruct((lines, width), BF16),
            jax.ShapeDtypeStruct((own, width, share), F32),
            jax.ShapeDtypeStruct((own, share, width), F32),
        ],
        scratch_shapes=[
            pltpu.VMEM((total, parts, piece, width), BF16),
            pltpu.VMEM((total, piece, width), BF16),
            pltpu.VMEM((total, piece, width), BF16),
            pltpu.VMEM((total, across, slim, columns), BF16),
            pltpu.VMEM((across - 1, total, slim, columns), BF16),
            pltpu.VMEM((seqs, parts, slim, columns), BF16),
            pltpu.VMEM((seqs - 1, parts, slim, columns), BF16),
            pltpu.VMEM((seqs - 1, slim, width), BF16),
            pltpu.VMEM((parts, slim, columns), BF16),
            pltpu.VMEM((slim, width), BF16),
            pltpu.VMEM((3, most, lines, width), BF16),
            pltpu.VMEM((own, seqs, *rows[0].shape[1:]), BF16),
            pltpu.VMEM((own, seqs, *cots[0].shape[1:]), BF16),
            pltpu.VMEM((own, width, 2 * share), BF16),
            pltpu.VMEM((own, 2 * share, width), BF16),
            pltpu.VMEM((own, 2, 2 * share, width), F32),
            pltpu.VMEM((own, share, width), F32),
            pltpu.VMEM((own, 2, share, width), BF16),
            pltpu.VMEM((own, 2, share, width), BF16),
            sems((2, own, 2)),
            sems((2, 2)),
            sems((2, total - 1)),
            sems((2, across - 1)),
            sems((2, seqs - 1)),
            sems((2, seqs - 1)),
            sems((2, across * parts - 1)),
            sems((2, across - 1)),
            sems((2, 3, most)),
            sems((2, own, seqs)),
            sems((2, own)),
            sems((5,)),
            *[pltpu.VMEM(a.shape, BF16) for a in (flipped, three, weights, x)],
            sems((4,)),
        ],
        compiler_params=pltpu.CompilerParams(collective_id=1, has_side_effects=True, vmem_limit_bytes=62 << 20),
        cost_estimate=pl.CostEstimate(flops=16 << 30, bytes_accessed=60 << 20, transcendentals=0),
        name="finish",
    )(three, flipped, weights, x, early, tiny, table, params, *rows, *cots, w_in, w_out)


def close_kernel(
    heads,
    home_ref,
    middle_ref,
    late_ref,
    early_ref,
    tiny_ref,
    in_ref,
    out_ref,
    result_ref,
    inputs_ref,
    query_ref,
    key_ref,
    value_ref,
    output_ref,
    gain_one_ref,
    gain_two_ref,
    router_ref,
    table_ref,
    grad_in_ref,
    grad_out_ref,
    result_out,
):
    grad_in_ref[...] = in_ref[...]
    grad_out_ref[...] = out_ref[...]
    result_out[...] = result_ref[...]
    inputs_ref[...] = middle_ref[...] + home_ref[...].reshape(middle_ref.shape).astype(F32)
    _, parts, _, columns = late_ref.shape
    cols = columns // 3
    for p in range(parts):
        for n, ref in enumerate((query_ref, key_ref, value_ref)):
            ref[:, p * cols : (p + 1) * cols] = late_ref[0, p, :, n * cols : (n + 1) * cols].astype(F32)
    output_ref[...] = early_ref[0].astype(F32)

    @pl.when(pl.program_id(0) == 0)
    def _():
        me = lax.axis_index("seq")
        width, piece = tiny_ref.shape[1], gain_one_ref.shape[1]
        chosen = lax.broadcasted_iota(jnp.int32, (width, piece), 0) == (
            lax.broadcasted_iota(jnp.int32, (width, piece), 1) + me * piece
        )
        picked = contract(tiny_ref[...], chosen.astype(F32).astype(BF16), 1, 0)
        gain_one_ref[...] = picked[0:1]
        gain_two_ref[...] = picked[1:2]
        router_ref[...] = picked[2 : 2 + router_ref.shape[0]]
        lines = table_ref.shape[0]
        chosen = lax.broadcasted_iota(jnp.int32, (lines, LANES), 1) == (
            lax.broadcasted_iota(jnp.int32, (lines, LANES), 0) + me * lines
        )
        table_ref[...] = contract(chosen.astype(F32).astype(BF16), tiny_ref[16:, :LANES], 1, 1)[:, :heads]


def close(home, middle, late, early, tiny, grad_in, grad_out, result, heads, buckets, experts):
    across, parts, slim, columns = late.shape
    width = early.shape[2]
    total, piece, _ = home.shape
    tokens = middle.shape[0]
    own, _, share = grad_in.shape
    halves = across // own
    rows = pl.BlockSpec((slim, width), lambda i: (i, 0))

    def whole(*shape):
        return pl.BlockSpec(shape, lambda i: (0,) * len(shape))

    some = pl.BlockSpec((tokens // across, width), lambda i: (i, 0))
    in_part = pl.BlockSpec((1, width // halves, share), lambda i: (i // halves, i % halves, 0))
    out_part = pl.BlockSpec((1, share // halves, width), lambda i: (i // halves, i % halves, 0))
    small = [(1, width // total), (1, width // total), (experts, width // total), (buckets // total, heads)]
    shapes = [middle.shape, *[(across * slim, width)] * 4, *small, grad_in.shape, grad_out.shape]
    return pl.pallas_call(
        functools.partial(close_kernel, heads),
        grid=(across,),
        in_specs=[
            pl.BlockSpec((total // across, piece, width), lambda i: (i, 0, 0)),
            some,
            pl.BlockSpec((1, parts, slim, columns), lambda i: (i, 0, 0, 0)),
            pl.BlockSpec((1, slim, width), lambda i: (i, 0, 0)),
            whole(*tiny.shape),
            in_part,
            out_part,
            some,
        ],
        out_specs=[some, rows, rows, rows, rows, *[whole(*shape) for shape in small], in_part, out_part, some],
        out_shape=[jax.ShapeDtypeStruct(shape, F32) for shape in shapes] + [jax.ShapeDtypeStruct(result.shape, BF16)],
        compiler_params=pltpu.CompilerParams(vmem_limit_bytes=62 << 20),
        name="close",
    )(home, middle, late, early, tiny, grad_in, grad_out, result)


def ring_pairs(total, parts, shift):
    return [(i, i - i % parts + (i % parts + shift) % parts) for i in range(total)]


def pick(pieces, index):
    out = pieces[0]
    for k in range(1, len(pieces)):
        out = jnp.where(index == k, pieces[k], out)
    return out


def swap_parts(pieces, part, parts, total):
    near = [pick(pieces, part)]
    for k in range(1, parts):
        near.append(lax.ppermute(pick(pieces, (part + k) % parts), "seq", ring_pairs(total, parts, k)))
    return [pick(near, (part - j) % parts) for j in range(parts)]


def per_device(
    inputs,
    routes,
    bucket_ids,
    gain_attn,
    w_query,
    w_key,
    w_value,
    w_output,
    rel_table,
    gain_ffn,
    w_router,
    w_in,
    w_out,
    cotangent,
):
    seqs, local_len, width = inputs.shape
    buckets, head_count = rel_table.shape
    size = width // head_count
    total = lax.axis_size("seq")
    across = lax.axis_size("wide")
    length = local_len * total
    parts = total // seqs
    heads = head_count // parts
    cols = heads * size
    me = lax.axis_index("seq")
    part = me % parts
    experts = w_router.shape[1]
    own_experts = w_in.shape[0]
    tokens = seqs * local_len
    capacity = (5 * tokens + 4 * experts - 1) // (4 * experts)
    slots = experts * capacity
    gain_one = gain_attn.astype(F32)
    gain_two = gain_ffn.astype(F32)

    fast = parts == 2 and capacity % 16 == 0 and own_experts == 2 and seqs == 4 and experts == 8 and across == 4 and cols % LANES == 0 and local_len == LANES
    flat_cot = cotangent.reshape(tokens, width)
    chosen = routes.reshape(tokens)
    blocks = inputs.reshape(total, local_len // parts, width)

    if fast:
        lines = chosen.astype(F32).reshape(tokens // LANES, LANES)
        params = jnp.concatenate(
            [
                gain_one[None],
                gain_two[None],
                w_router.T.astype(F32),
                jnp.pad(lines, ((0, 14 - experts - tokens // LANES), (0, width - LANES))),
            ],
            axis=0,
        )
        first_slot = [(e % own_experts) * (across * capacity) + (e // own_experts) * capacity for e in range(experts)]
        base = jnp.array(first_slot + [0] * (LANES - experts), F32)[None]
        seq_in, qkv, flipped, slot_hot, cot_rows, own_weights = begin(
            blocks,
            w_query,
            w_key,
            w_value,
            params,
            base,
            flat_cot,
            heads,
            size,
            own_experts,
            capacity,
        )
    else:
        own_weights = jnp.concatenate(
            [lax.dynamic_slice(w, (0, part * cols), (width, cols)) for w in (w_query, w_key, w_value)], axis=1
        )
        seq_in = spread(blocks, parts).reshape(length, width).astype(F32)
        inv_one = inverse_rms(seq_in)
        normed_one = (seq_in * inv_one * gain_one).astype(BF16)
        flipped = normed_one.T
        qkv = contract(own_weights, normed_one, 0, 1).astype(BF16).reshape(3, heads, size, length)
        picked = (chosen[:, None] == jnp.arange(experts, dtype=jnp.int32)[None, :]).astype(F32)
        order = jnp.arange(tokens, dtype=jnp.int32)
        before = (order[None, :] < order[:, None]).astype(BF16)
        earlier = jnp.dot(before, picked.astype(BF16), preferred_element_type=F32)
        rank_in = jnp.sum(earlier * picked, axis=1).astype(jnp.int32)
        place = (chosen % own_experts) * (across * capacity) + (chosen // own_experts) * capacity + rank_in
        slot_of = jnp.where(rank_in < capacity, place, slots)
        slot_hot = (slot_of[:, None] == jnp.arange(slots, dtype=jnp.int32)[None, :]).astype(BF16)
        packed = contract(slot_hot, flat_cot, 0, 0).astype(BF16).reshape(own_experts, across, capacity, width)
        cot_rows = jnp.stack([lax.all_to_all(packed[e], "wide", 0, 0, tiled=True) for e in range(own_experts)])
        cot_rows = cot_rows.reshape(own_experts, across * capacity, width)
    own_table = lax.dynamic_slice(rel_table, (0, part * heads), (buckets, heads))
    ids = jnp.concatenate([bucket_ids, jnp.full((1,), LANES, jnp.int32)])
    bucket_hot = (ids[None, :] == jnp.arange(LANES, dtype=jnp.int32)[:, None]).astype(BF16)
    reverse_hot = (ids[::-1][None, :] == jnp.arange(buckets, dtype=jnp.int32)[:, None]).astype(BF16)
    bias_line = contract(own_table, reverse_hot, 0, 0).reshape(heads, 1, 2 * length)
    outs, attended, exps, inverse, *first = attend(qkv, bias_line, total, [cot_rows] if fast else [], seqs)
    attended = attended.reshape(seqs, width, local_len)
    share = width // total
    flat_in = inputs.reshape(tokens, width)
    back = (exps, inverse, w_output.reshape(parts, cols, width), outs, qkv, bucket_hot)
    if fast:
        middle, normed_two, received, *second = route(
            attended, w_output, flat_in, params, slot_hot, cot_rows, *first, capacity
        )
        next_cots = second[2:]
        returned, *passed = run_experts(received, cot_rows, params, w_in, w_out, *next_cots, seqs, 512)
        second = [second[0], passed[0], second[1], passed[1]]
        near_rows = passed[2:]
        more = [
            returned,
            slot_hot,
            middle,
            normed_two,
            flat_cot,
            attended,
            params,
        ]
        three, table, early, output, grad_middle, tiny, *passed = attend_back(*back, None, more, near_rows, second)
        all_rows = [received, *near_rows, *passed[:2]]
        all_cots = [cot_rows, first[0], next_cots[0], first[1], next_cots[1], *second, *passed[2:]]
        home, *found = finish(
            three,
            flipped,
            own_weights,
            seq_in,
            early,
            tiny,
            table,
            params,
            all_rows,
            all_cots,
            w_in,
            w_out,
        )
        grad_inputs, *grads_qkvo, grad_gain_one, grad_gain_two, grad_router, grad_table, grad_in, grad_out, output = close(
            home, grad_middle, *found, output, head_count, buckets, experts
        )
        return (
            output.reshape(inputs.shape),
            grad_inputs.reshape(inputs.shape),
            grad_gain_one[0],
            *grads_qkvo,
            grad_table,
            grad_gain_two[0],
            grad_router.T,
            grad_in,
            grad_out,
        )

    flat_in = flat_in.astype(F32)
    middle = flat_in + jnp.einsum("sft,fe->ste", attended, w_output, preferred_element_type=F32).reshape(tokens, width)
    inv_two = inverse_rms(middle)
    normed_two = (middle * inv_two * gain_two).astype(BF16)
    router_probs = jax.nn.softmax(jnp.dot(normed_two, w_router, preferred_element_type=F32), axis=-1)
    picked = (chosen[:, None] == jnp.arange(experts, dtype=jnp.int32)[None, :]).astype(F32)
    gate_prob = jnp.sum(router_probs * picked, axis=1)
    upstream = flat_cot.astype(F32)
    packed = contract(slot_hot, normed_two, 0, 0).astype(BF16).reshape(own_experts, across, capacity, width)
    received, returned = [], []
    for e in range(own_experts):
        got = lax.all_to_all(packed[e], "wide", 0, 0, tiled=True).reshape(across * capacity, width)
        received.append(got)
        pair = run_expert(got, cot_rows[e], w_router.T, w_in, w_out, e, 512).reshape(across, capacity, 2 * width)
        returned.append(lax.all_to_all(pair, "wide", 0, 0, tiled=True).reshape(across * capacity, 2 * width))
    received, returned = jnp.stack(received), jnp.concatenate(returned, axis=0)
    token_rows = jnp.dot(slot_hot, returned, preferred_element_type=F32)
    selected, grad_token = token_rows[:, :width], token_rows[:, width:]
    output = (middle + gate_prob[:, None] * selected).astype(BF16).reshape(inputs.shape)
    grad_gate = jnp.sum(upstream * selected, axis=1)
    grad_logits = (grad_gate[:, None] * router_probs * (picked - gate_prob[:, None])).astype(BF16)
    grad_router = contract(grad_logits, normed_two, 0, 0)
    grad_normed_two = grad_token + contract(grad_logits, w_router, 1, 1)
    grad_mid_norm, grad_gain_two = norm_backward(middle, inv_two, gain_two, grad_normed_two)
    grad_middle = upstream + grad_mid_norm
    grad_branch = grad_middle.astype(BF16).reshape(seqs, local_len, width)
    grad_w_output = jnp.einsum("sft,ste->fe", attended, grad_branch, preferred_element_type=F32)
    all_cots = lax.all_gather(cot_rows, "seq", axis=0)
    all_rows = lax.all_gather(received, "seq", axis=0)
    three, table = attend_back(*back, grad_branch, [], [], [])
    grad_normed_one = contract(three, own_weights, 1, 1)
    grad_in_norm, grad_gain_one = norm_backward(seq_in, inv_one, gain_one, grad_normed_one)
    pieces = grad_in_norm.astype(BF16).reshape(total, parts, local_len // parts, width)
    swapped = swap_parts([pieces[:, p] for p in range(parts)], part, parts, total)
    home = sum(p.astype(F32) for p in swapped).astype(BF16)
    home = lax.all_to_all(home, "seq", 0, 0, tiled=True).reshape(tokens, width).astype(F32)
    grad_projections = lax.dynamic_update_slice(
        jnp.zeros((width, 3, width), F32), contract(flipped, three, 1, 0).reshape(width, 3, cols), (0, 0, part * cols)
    )
    rows = [grad_projections[:, k] for k in range(3)]
    rows += [grad_w_output, grad_gain_one[:, None], grad_gain_two[:, None], grad_router.T]
    table = table.T[:buckets]
    rows, table = lax.psum((jnp.concatenate(rows, axis=1).astype(BF16), table.astype(BF16)), "wide")
    rows = lax.psum_scatter(rows, "seq", scatter_dimension=0, tiled=True).astype(F32)
    table = lax.psum_scatter(table, "seq", scatter_dimension=0, tiled=True).astype(F32)
    held = []
    for e in range(own_experts):
        held = run_share(
            me,
            all_rows.reshape(total * own_experts, *received.shape[1:]),
            all_cots.reshape(total * own_experts, *cot_rows.shape[1:]),
            w_router.T,
            w_in,
            w_out,
            e,
            held,
        )
    last = rows[:, 4 * width :]
    return (
        output,
        (grad_middle + home).reshape(inputs.shape),
        last[:, 0],
        *[rows[:, k * width : (k + 1) * width] for k in range(4)],
        table[:, :head_count],
        last[:, 1],
        last[:, 2 : 2 + experts],
        *held,
    )


def solution(mesh):
    in_specs = (
        P("wide", "seq", None),
        P("wide", "seq", None),
        P(),
        P(),
        P(),
        P(),
        P(),
        P(),
        P(),
        P(),
        P(),
        P("wide", None, None),
        P("wide", None, None),
        P("wide", "seq", None),
    )
    out_specs = (
        P("wide", "seq", None),
        P("wide", "seq", None),
        P("seq"),
        P("seq", None),
        P("seq", None),
        P("seq", None),
        P("seq", None),
        P("seq", None),
        P("seq"),
        P("seq", None),
        P("wide", None, "seq"),
        P("wide", "seq", None),
    )
    return jax.shard_map(
        per_device, mesh=mesh, in_specs=in_specs, out_specs=out_specs, check_vma=False
    )
```

```python
import functools

import jax
import jax.numpy as jnp
from jax import lax
from jax.experimental import pallas as pl
from jax.experimental.pallas import tpu as pltpu
from jax.sharding import PartitionSpec as P

EPSILON = 1e-06
F32 = jnp.float32
BF16 = jnp.bfloat16
LANES = 128


def contract(a, b, da, db):
    return lax.dot_general(a, b, (((da,), (db,)), ((), ())), preferred_element_type=F32)


def inverse_rms(source):
    return lax.rsqrt(jnp.mean(source * source, axis=-1, keepdims=True) + EPSILON)


def norm_backward(source, inv_rms, gain_vec, upstream):
    scaled = upstream * gain_vec
    gain_grad = jnp.sum(upstream * source * inv_rms, axis=0)
    mean_inner = jnp.mean(source * scaled, axis=-1, keepdims=True)
    return (inv_rms * scaled - source * (inv_rms * inv_rms * inv_rms) * mean_inner, gain_grad)


def smooth_act(values):
    return jax.nn.gelu(values, approximate=True)


MESH = pl.DeviceIdType.MESH


def remote(src, dst, send, recv, where):
    copy = pltpu.make_async_remote_copy(src, dst, send, recv, device_id=where, device_id_type=MESH)
    copy.start()
    return copy


def router_of(table, experts):
    return table[2 : 2 + experts, :].astype(BF16)


def routes_of(table, experts, tokens):
    lines = table[2 + experts : 2 + experts + tokens // LANES, :LANES]
    lines = jnp.concatenate([lines, jnp.zeros((LANES - lines.shape[0], LANES), F32)], axis=0).T
    return jnp.concatenate([lines[:, n : n + 1] for n in range(tokens // LANES)], axis=0)


def fetch(sources, targets, sems):
    copies = [pltpu.make_async_copy(a, b, sems.at[n]) for n, (a, b) in enumerate(zip(sources, targets, strict=True))]
    for copy in copies:
        copy.start()
    return copies


def meet(peers):
    barrier = pltpu.get_barrier_semaphore()
    for where in peers:
        pl.semaphore_signal(barrier, inc=1, device_id=where, device_id_type=MESH)
    pl.semaphore_wait(barrier, len(peers))


def line_peers(parts):
    total, me = lax.axis_size("seq"), lax.axis_index("seq")
    return [{"seq": lax.rem(me + parts, total)}, {"seq": lax.rem(me - parts + total, total)}]


def line_round(parts, up, down, sems):
    me = lax.axis_index("seq")
    z = lax.div(me, parts)

    def copy(n, src, dst, step):
        return pltpu.make_async_remote_copy(
            src, dst, sems.at[0, n], sems.at[1, n], device_id={"seq": me + step}, device_id_type=MESH
        )

    legs = [(0, *up, parts), (1, *down, -parts)]

    def start():
        for n, low, high, src, dst, step in legs:

            @pl.when(jnp.logical_and(z >= low, z <= high))
            def _():
                copy(n, src, dst, step).start()

    def end():
        for n, low, high, src, dst, step in legs:
            move = 1 if step > 0 else -1

            @pl.when(jnp.logical_and(z >= low, z <= high))
            def _():
                copy(n, src, dst, step).wait_send()

            @pl.when(jnp.logical_and(z >= low + move, z <= high + move))
            def _():
                copy(n, src, dst, -step).wait_recv()

    return start, end


def pass_on(parts, up, down, sems):
    start, end = line_round(parts, up, down, sems)
    start()
    return end


def far_first(total):
    return sorted(range(1, total), key=lambda k: -min(k, total - k))


def twist(a, b, total):
    out, bit = 0, 1
    while bit < total:
        out = out + lax.rem(lax.div(a, bit) + lax.div(b, bit), 2) * bit
        bit *= 2
    return out


def attend_kernel(seqs, more_peers, next_steps, *refs):
    refs = list(refs)
    qkv_ref, bias_ref = refs[:2]
    line_ref = refs.pop(2) if seqs else None
    out_ref, home_ref, exp_ref, inv_ref = refs[2:6]
    line_outs = [refs.pop(6) for _ in range(2)] if seqs else []
    strip, keys, scores, held, send, recv, local, exp_sems, *line_sems = refs[6:]
    _, heads, size, length = qkv_ref.shape
    total = lax.axis_size("seq")
    me = lax.axis_index("seq")
    tokens = out_ref.shape[3]
    width = 2 * tokens
    pairs = total // 2
    rows = 2 * length - tokens
    chunk = 256
    meet([{"seq": lax.rem(me + k, total)} for k in range(1, total)] + more_peers)
    if seqs:
        before, after = line_outs
        line_end = pass_on(
            total // seqs, (0, seqs - 2, line_ref.at[0], before), (1, seqs - 1, line_ref.at[0], after), line_sems[0]
        )

    def prepare(h, carry):
        keys[h] = qkv_ref[1, h].T
        for b in range(rows // tokens):
            start = 2 * length - 2 * tokens - tokens * b
            base = jnp.broadcast_to(bias_ref[h, :, start : start + 2 * tokens], (tokens, 2 * tokens))
            rolled = pltpu.roll(base, 0, 1, stride=1, stride_axis=0)
            strip[h, tokens * b : tokens * (b + 1), :] = rolled[:, tokens:]
        return carry

    lax.fori_loop(0, heads, prepare, 0)

    def store(slot, pair, h):
        return pltpu.make_async_copy(held.at[slot], exp_ref.at[pair, h], exp_sems.at[slot])

    def step(t, carry):
        pair = twist(lax.div(me, 2), pairs - 1 - t, pairs)
        at = pl.ds(pl.multiple_of(pair * width, tokens), width)
        if seqs:

            @pl.when(t == pairs - 1)
            def _():
                line_end()
                for start in next_steps:
                    start()

        def head(h, carry):
            count = t * heads + h
            slot = lax.rem(count, 2)

            @pl.when(count >= 2)
            def _():
                store(slot, pair, h).wait()

            query = qkv_ref[0, h, :, at]
            tops = [jnp.full((1, tokens), -jnp.inf, F32)] * 2
            for c in range(length // chunk):
                part = contract(keys[h, c * chunk : (c + 1) * chunk, :], query, 1, 0)
                for s in range(2):
                    row = pl.multiple_of(length - tokens - (pair * width + s * tokens) + c * chunk, tokens)
                    piece = part[:, s * tokens : (s + 1) * tokens] + strip[h, pl.ds(row, chunk), :]
                    scores[c * chunk : (c + 1) * chunk, s * tokens : (s + 1) * tokens] = piece
                    tops[s] = jnp.maximum(tops[s], jnp.max(piece, axis=0, keepdims=True))
            sums = [jnp.zeros((1, tokens), F32)] * 2
            for c in range(length // chunk):
                for s in range(2):
                    piece = scores[c * chunk : (c + 1) * chunk, s * tokens : (s + 1) * tokens]
                    grown = jnp.exp(piece - tops[s])
                    sums[s] = sums[s] + jnp.sum(grown, axis=0, keepdims=True)
                    held[slot, c * chunk : (c + 1) * chunk, s * tokens : (s + 1) * tokens] = grown.astype(BF16)
            store(slot, pair, h).start()
            mixed = contract(qkv_ref[2, h], held[slot], 1, 0)
            for s in range(2):
                inverse = 1.0 / sums[s]
                inv_ref[pair, h, :, s * tokens : (s + 1) * tokens] = inverse
                out_ref[2 * pair + s, h] = (mixed[:, s * tokens : (s + 1) * tokens] * inverse).astype(BF16)
            return carry

        lax.fori_loop(0, heads, head, 0)
        for s in range(2):
            to = 2 * pair + s
            k = twist(me, to, total)

            @pl.when(to != me)
            def _():
                pltpu.make_async_remote_copy(
                    out_ref.at[to], home_ref.at[me], send.at[k], recv.at[k], device_id={"seq": to}, device_id_type=MESH
                ).start()

        return carry

    lax.fori_loop(0, pairs, step, 0)
    own = pltpu.make_async_copy(out_ref.at[me], home_ref.at[me], local)
    own.start()
    for slot in range(2):
        store(slot, 0, 0).wait()

    def settle(k, carry):
        source = twist(me, k, total)
        pltpu.make_async_remote_copy(
            out_ref.at[source], home_ref.at[source], send.at[k], recv.at[k], device_id={"seq": source}, device_id_type=MESH
        ).wait()
        return carry

    lax.fori_loop(1, total, settle, 0)
    own.wait()


def attend(qkv, bias_line, total):
    _, heads, size, length = qkv.shape
    vmem, hbm = pl.BlockSpec(memory_space=pltpu.VMEM), pl.BlockSpec(memory_space=pl.ANY)
    out_shape, scratch = attend_shapes(heads, size, length, total)
    return pl.pallas_call(
        functools.partial(attend_kernel, 0, [], None),
        in_specs=[vmem, vmem],
        out_specs=[vmem, vmem, hbm, vmem],
        out_shape=out_shape,
        scratch_shapes=scratch,
        compiler_params=pltpu.CompilerParams(collective_id=2, has_side_effects=True, vmem_limit_bytes=62 << 20),
        name="attend",
    )(qkv, bias_line)


def attend_shapes(heads, size, length, total):
    tokens = length // total
    out_shape = [
        jax.ShapeDtypeStruct((total, heads, size, tokens), BF16),
        jax.ShapeDtypeStruct((total, heads, size, tokens), BF16),
        jax.ShapeDtypeStruct((total // 2, heads, length, 2 * tokens), BF16),
        jax.ShapeDtypeStruct((total // 2, heads, 1, 2 * tokens), F32),
    ]
    scratch = [
        pltpu.VMEM((heads, 2 * length - tokens, tokens), F32),
        pltpu.VMEM((heads, length, size), BF16),
        pltpu.VMEM((length, 2 * tokens), F32),
        pltpu.VMEM((2, length, 2 * tokens), BF16),
        pltpu.SemaphoreType.DMA((total,)),
        pltpu.SemaphoreType.DMA((total,)),
        pltpu.SemaphoreType.DMA,
        pltpu.SemaphoreType.DMA((2,)),
    ]
    return out_shape, scratch


def attend_back_kernel(fast, *refs):
    refs = list(refs)
    exp_ref, inv_ref, weight_in, out_in, qkv_in, hot_ref = refs[:6]
    weight_ref, out_ref, qkv_ref, *late_sems = refs[-4:]
    refs = refs[:-4]
    late = fetch((weight_in, out_in, qkv_in), (weight_ref, out_ref, qkv_ref), late_sems[0])
    if fast:
        *soon, params_ref = refs[6:13]
        line_refs, far_refs = refs[13:15], refs[15:19]
        *held_refs, soon_sems = refs[-7:]
        soon = fetch(soon, held_refs, soon_sems)
        back_ref, slot_ref, middle_ref, normed_ref, cot_ref, att_ref = held_refs
        refs = refs[19:-7]
    else:
        branch_ref = refs[6]
        refs = refs[7:]
    three_ref, table_ref = refs[:2]
    if fast:
        early_out, output_ref, grad_middle_ref, tiny_ref = refs[2:6]
        line_outs, far_outs = refs[6:8], refs[8:12]
        refs = refs[12:]
    else:
        refs = refs[2:]
    leaving, got, strip, values, dq_all, dk_sum, dv_sum, scores, held, diagonal, send, recv, exp_sems = refs[:13]
    _, heads, size, length = qkv_ref.shape
    total = lax.axis_size("seq")
    me = lax.axis_index("seq")
    tokens = out_ref.shape[3]
    parts = weight_ref.shape[0]
    part = lax.rem(me, parts)
    width = 2 * tokens
    pairs = total // 2
    rows = 2 * length - tokens
    chunk = 256

    def pair_at(t):
        return twist(lax.div(me, 2), t, pairs)

    def load(count):
        slot = lax.rem(count, 2)
        at = exp_ref.at[pair_at(lax.div(count, heads)), lax.rem(count, heads)]
        return pltpu.make_async_copy(at, held.at[slot], exp_sems.at[slot])

    load(0).start()
    peers = [{"seq": lax.rem(me + k, total)} for k in range(1, total)]
    if fast:
        across, row = lax.axis_size("wide"), lax.axis_index("wide")
        other = twist(me, 1, total)
        peers += [{"wide": lax.rem(row + k, across)} for k in range(1, across)]
    meet(peers)
    if fast:
        branch_ref, early_ref, near, near_sum, wide_got, near_sems, wide_sems, line_sems, far_sems = refs[13:]
        seqs = early_ref.shape[0]

        def far_step(e):
            up, down = far_refs[e], far_refs[2 + e]
            return pass_on(
                parts, (seqs - 2, seqs - 2, up, far_outs[e]), (1, 1, down, far_outs[2 + e]), far_sems.at[e]
            )

        line_ends = [far_step(0)]

        def near_copy():
            return pltpu.make_async_remote_copy(
                early_ref.at[:, lax.rem(part + 1, parts)],
                near,
                near_sems.at[0],
                near_sems.at[1],
                device_id={"seq": other},
                device_id_type=MESH,
            )

        def wide_copy(k):
            to = lax.rem(row + k, across)
            return pltpu.make_async_remote_copy(
                near_sum.at[to],
                wide_got.at[k - 1],
                wide_sems.at[0, k - 1],
                wide_sems.at[1, k - 1],
                device_id={"wide": to},
                device_id_type=MESH,
            )

        for copy in soon:
            copy.wait()
        features = middle_ref.shape[1]
        found = contract(slot_ref[...], back_ref[...].reshape(slot_ref.shape[1], 2 * features), 1, 0)
        selected = found[:, :features]
        router = router_of(params_ref, 2 * across)
        logits = contract(normed_ref[...], router, 1, 1)
        grown = jnp.exp(logits - jnp.max(logits, axis=1, keepdims=True))
        probs = grown / jnp.sum(grown, axis=1, keepdims=True)
        routes = routes_of(params_ref, router.shape[0], probs.shape[0])
        picked = (routes == lax.broadcasted_iota(jnp.int32, probs.shape, 1).astype(F32)).astype(F32)
        gate = jnp.sum(probs * picked, axis=1, keepdims=True)
        upstream = cot_ref[...].astype(F32)
        middle = middle_ref[...]
        output_ref[...] = (middle + gate * selected).astype(BF16)
        grad_gate = jnp.sum(upstream * selected, axis=1, keepdims=True)
        grad_logits = (grad_gate * probs * (picked - gate)).astype(BF16)
        grad_normed = found[:, features:] + contract(grad_logits, router, 1, 0)
        inverse = inverse_rms(middle)
        gain_grad = jnp.sum(grad_normed * middle * inverse, axis=0, keepdims=True)
        grad_normed = grad_normed * params_ref[1:2, :]
        mean_inner = jnp.mean(middle * grad_normed, axis=-1, keepdims=True)
        grad_middle = upstream + inverse * grad_normed - middle * (inverse * inverse * inverse) * mean_inner
        grad_middle_ref[...] = grad_middle
        branch = grad_middle.astype(BF16)
        branch_ref[...] = branch.reshape(branch_ref.shape)

    for copy in late:
        copy.wait()

    def product(to):
        value = contract(weight_ref[lax.rem(to, parts)], branch_ref[lax.div(to, parts)], 1, 1)
        return value.astype(BF16).reshape(heads, size, tokens)

    def leave(k, carry):
        to = twist(me, k, total)
        leaving[to] = product(to)
        pltpu.make_async_remote_copy(
            leaving.at[to], got.at[me], send.at[k], recv.at[k], device_id={"seq": to}, device_id_type=MESH
        ).start()
        return carry

    lax.fori_loop(1, total, leave, 0)
    if fast:
        for e in range(line_refs[0].shape[0]):
            up, down = ((1, seqs - 2, line_refs[n].at[e], line_outs[n].at[e]) for n in range(2))
            line_ends.append(pass_on(parts, up, down, line_sems.at[e]))
        line_ends.append(far_step(1))
        attended = jnp.concatenate([att_ref[s] for s in range(seqs)], axis=1)
        early_ref[...] = contract(attended, branch, 1, 0).astype(BF16).reshape(early_ref.shape)
        near_copy().start()
        grad_router = contract(grad_logits, normed_ref[...], 0, 0)
        spare = tiny_ref.shape[0] - 2 - grad_router.shape[0]
        tiny_ref[...] = jnp.concatenate(
            [jnp.zeros((1, features), F32), gain_grad, grad_router, jnp.zeros((spare, features), F32)], axis=0
        )
    got[me] = product(me)

    def prepare(h, carry):
        values[h] = qkv_ref[2, h].T
        strip[h] = jnp.zeros(strip.shape[1:], F32)
        dk_sum[h] = jnp.zeros(dk_sum.shape[1:], F32)
        dv_sum[h] = jnp.zeros(dv_sum.shape[1:], F32)
        return carry

    lax.fori_loop(0, heads, prepare, 0)

    def arrive(k):
        source = twist(me, k, total)
        pltpu.make_async_remote_copy(
            leaving.at[source], got.at[source], send.at[k], recv.at[k], device_id={"seq": source}, device_id_type=MESH
        ).wait()

    def step(t, carry):
        pair = pair_at(t)
        at = pl.ds(pl.multiple_of(pair * width, tokens), width)

        @pl.when(t > 0)
        def _():
            arrive(2 * t)

        arrive(2 * t + 1)
        if fast:

            @pl.when(t == 1)
            def _():
                near_copy().wait()
                for n in range(seqs):
                    for a in range(across):
                        value = early_ref[n, part, a].astype(F32) + near[n, a].astype(F32)
                        near_sum[a, n] = value.astype(BF16)
                for k in range(1, across):
                    wide_copy(k).start()

            @pl.when(t == pairs - 1)
            def _():
                for k in range(1, across):
                    wide_copy(k).wait()
                for n in range(seqs):
                    value = near_sum[row, n].astype(F32)
                    for k in range(1, across):
                        value = value + wide_got[k - 1, n].astype(F32)
                    early_out[n] = value.astype(BF16)

        def head(h, carry):
            count = t * heads + h
            slot = lax.rem(count, 2)

            @pl.when(count + 1 < pairs * heads)
            def _():
                load(count + 1).start()

            grads, inner = [], []
            for s in range(2):
                inverse = inv_ref[pair, h, :, s * tokens : (s + 1) * tokens]
                scaled = got[2 * pair + s, h].astype(F32) * inverse
                inner.append(jnp.sum(scaled * out_ref[2 * pair + s, h].astype(F32), axis=0, keepdims=True))
                grads.append(scaled.astype(BF16))
            grad = jnp.concatenate(grads, axis=1)
            load(count).wait()
            for c in range(length // chunk):
                part_grad = contract(values[h, c * chunk : (c + 1) * chunk, :], grad, 1, 0)
                for s in range(2):
                    grown = held[slot, c * chunk : (c + 1) * chunk, s * tokens : (s + 1) * tokens].astype(F32)
                    slope = grown * (part_grad[:, s * tokens : (s + 1) * tokens] - inner[s])
                    line = pl.multiple_of(length - tokens - (pair * width + s * tokens) + c * chunk, tokens)
                    strip[h, pl.ds(line, chunk), :] += slope
                    scores[c * chunk : (c + 1) * chunk, s * tokens : (s + 1) * tokens] = slope.astype(BF16)
            dq_all[h, at, :] = contract(qkv_ref[1, h], scores[...], 1, 0).T.astype(BF16)
            dk_sum[h] += contract(scores[...], qkv_ref[0, h, :, at].T, 1, 0)
            dv_sum[h] += contract(held[slot], grad.T, 1, 0)
            return carry

        lax.fori_loop(0, heads, head, 0)
        return carry

    lax.fori_loop(0, pairs, step, 0)
    down = lax.broadcasted_iota(jnp.int32, (tokens, tokens), 0)
    over = lax.broadcasted_iota(jnp.int32, (tokens, tokens), 1)
    mirror = (down + over == tokens - 1).astype(F32)
    cols = heads * size
    for c in range(length // chunk):
        here = slice(c * chunk, (c + 1) * chunk)
        for n, ref in enumerate((dq_all, dk_sum, dv_sum)):
            joined = jnp.concatenate([ref[h, here, :].astype(F32) for h in range(heads)], axis=1)
            three_ref[here, n * cols : (n + 1) * cols] = joined.astype(BF16)

    def close(h, carry):
        diagonal[h] = jnp.zeros(diagonal.shape[1:], F32)
        for b in range(rows // tokens):
            flipped = lax.dot_general(
                strip[h, tokens * b : tokens * (b + 1), :],
                mirror,
                (((1,), (0,)), ((), ())),
                precision=lax.Precision.HIGHEST,
                preferred_element_type=F32,
            )
            spread_out = jnp.concatenate([flipped, jnp.zeros_like(flipped)], axis=1)
            rolled = pltpu.roll(spread_out, 0, 1, stride=1, stride_axis=0)
            diagonal[h, :, tokens * b : tokens * (b + 2)] += jnp.sum(rolled, axis=0, keepdims=True)
        return carry

    lax.fori_loop(0, heads, close, 0)
    sums = jnp.concatenate([diagonal[h] for h in range(heads)], axis=0)
    table = lax.dot_general(
        sums,
        hot_ref[...].astype(F32),
        (((1,), (1,)), ((), ())),
        precision=lax.Precision.HIGHEST,
        preferred_element_type=F32,
    )
    line = lax.broadcasted_iota(jnp.int32, (table_ref.shape[0], heads), 0)
    head_line = lax.broadcasted_iota(jnp.int32, (table_ref.shape[0], heads), 1) + part * heads
    table_ref[...] = lax.dot_general(
        (line == head_line).astype(F32),
        table,
        (((1,), (0,)), ((), ())),
        precision=lax.Precision.HIGHEST,
        preferred_element_type=F32,
    )
    if fast:
        for end in line_ends:
            end()


def attend_back(exps, inverse, weight, outs, qkv, hot, branch, more, line, far):
    _, heads, size, length = qkv.shape
    total, tokens = outs.shape[0], outs.shape[3]
    parts, cols, width = weight.shape
    vmem, hbm = pl.BlockSpec(memory_space=pltpu.VMEM), pl.BlockSpec(memory_space=pl.ANY)
    sems = pltpu.SemaphoreType.DMA
    out_shape = [
        jax.ShapeDtypeStruct((length, 3 * heads * size), BF16),
        jax.ShapeDtypeStruct((16, hot.shape[0]), F32),
    ]
    given, scratch = [branch], []
    if branch is None:
        given = more
        across = lax.axis_size("wide")
        slim = width // total // across
        seqs = total // parts
        count = seqs * tokens
        out_shape += [
            jax.ShapeDtypeStruct((seqs, slim, width), BF16),
            jax.ShapeDtypeStruct((count, width), BF16),
            jax.ShapeDtypeStruct((count, width), F32),
            jax.ShapeDtypeStruct((16, width), F32),
        ]
        scratch = [
            pltpu.VMEM((seqs, tokens, width), BF16),
            pltpu.VMEM((seqs, parts, across, slim, width), BF16),
            pltpu.VMEM((seqs, across, slim, width), BF16),
            pltpu.VMEM((across, seqs, slim, width), BF16),
            pltpu.VMEM((across - 1, seqs, slim, width), BF16),
            sems((2,)),
            sems((2, across - 1)),
            sems((line[0].shape[0], 2, 2)),
            sems((len(far) // 2, 2, 2)),
        ]
    passed = [*line, *far]
    held = [pltpu.VMEM(a.shape, a.dtype) for a in more[:6]] + [sems((6,))] if branch is None else []
    spaces = [hbm] * 6 + [vmem] if branch is None else [vmem]
    in_place = len(out_shape)
    out_shape += [jax.ShapeDtypeStruct(rows.shape, BF16) for rows in passed]
    return pl.pallas_call(
        functools.partial(attend_back_kernel, branch is None),
        in_specs=[hbm, vmem, hbm, hbm, hbm, vmem] + spaces + [hbm] * len(passed),
        out_specs=[vmem] * in_place + [hbm] * len(passed),
        out_shape=out_shape,
        scratch_shapes=[
            pltpu.VMEM((total, heads, size, tokens), BF16),
            pltpu.VMEM((total, heads, size, tokens), BF16),
            pltpu.VMEM((heads, 2 * length - tokens, tokens), F32),
            pltpu.VMEM((heads, length, size), BF16),
            pltpu.VMEM((heads, length, size), BF16),
            pltpu.VMEM((heads, length, size), F32),
            pltpu.VMEM((heads, length, size), F32),
            pltpu.VMEM((length, 2 * tokens), BF16),
            pltpu.VMEM((2, length, 2 * tokens), BF16),
            pltpu.VMEM((heads, 1, 2 * length), F32),
            sems((total,)),
            sems((total,)),
            sems((2,)),
            *scratch,
            *held,
            *[pltpu.VMEM(a.shape, a.dtype) for a in (weight, outs, qkv)],
            sems((3,)),
        ],
        compiler_params=pltpu.CompilerParams(collective_id=3, has_side_effects=True, vmem_limit_bytes=62 << 20),
        cost_estimate=pl.CostEstimate(
            flops=8 * heads * length * length * size, bytes_accessed=2 * heads * length * length, transcendentals=0
        ),
        name="attend_back",
    )(exps, inverse, weight, outs, qkv, hot, *given, *passed)


def activation(v):
    square = v * v
    bent = jnp.tanh(0.7978845608 * v * (1.0 + 0.044715 * square))
    half = 0.5 * (1.0 + bent)
    slope = half + 0.5 * v * (1.0 - bent * bent) * (0.7978845608 * (1.0 + 3.0 * 0.044715 * square))
    return v * half, slope


def gated(rows, cots, router, expert):
    logits = contract(rows, router, 1, 1)
    grown = jnp.exp(logits - jnp.max(logits, axis=1, keepdims=True))
    named = lax.broadcasted_iota(jnp.int32, grown.shape, 1) == expert
    gate = jnp.sum(jnp.where(named, grown, 0.0), axis=1, keepdims=True) / jnp.sum(grown, axis=1, keepdims=True)
    return (gate * cots.astype(F32)).astype(BF16)


def expert_kernel(expert, rows_ref, cot_ref, router_ref, in_ref, out_ref, both_ref, forward, backward):
    step = pl.program_id(0)
    width = cot_ref.shape[1]

    @pl.when(step == 0)
    def _():
        forward[...] = jnp.zeros_like(forward)
        backward[...] = jnp.zeros_like(backward)

    rows = rows_ref[...]
    own = router_ref.shape[0] // lax.axis_size("wide")
    grads = gated(rows, cot_ref[...], router_ref[...], lax.axis_index("wide") * own + expert)
    hidden, slope = activation(contract(rows, in_ref[0], 1, 0))
    grad_hidden = contract(grads, out_ref[0], 1, 1).astype(BF16).astype(F32)
    forward[...] += contract(hidden.astype(BF16), out_ref[0], 1, 0)
    backward[...] += contract((grad_hidden * slope).astype(BF16), in_ref[0], 1, 1)

    @pl.when(step == pl.num_programs(0) - 1)
    def _():
        both_ref[:, :width] = forward[...].astype(BF16)
        both_ref[:, width:] = backward[...].astype(BF16)


def run_expert(rows, cots, router, w_in, w_out, expert, block):
    count, width = cots.shape
    units = w_in.shape[2]
    return pl.pallas_call(
        functools.partial(expert_kernel, expert),
        grid=(units // block,),
        in_specs=[
            pl.BlockSpec(rows.shape, lambda f: (0, 0)),
            pl.BlockSpec(cots.shape, lambda f: (0, 0)),
            pl.BlockSpec(router.shape, lambda f: (0, 0)),
            pl.BlockSpec((1, width, block), lambda f: (expert, 0, f)),
            pl.BlockSpec((1, block, width), lambda f: (expert, f, 0)),
        ],
        out_specs=pl.BlockSpec((count, 2 * width), lambda f: (0, 0)),
        out_shape=jax.ShapeDtypeStruct((count, 2 * width), BF16),
        scratch_shapes=[pltpu.VMEM((count, width), F32), pltpu.VMEM((count, width), F32)],
        compiler_params=pltpu.CompilerParams(vmem_limit_bytes=40 << 20),
        name="expert",
    )(rows, cots, router, w_in, w_out)


def forward_kernel(
    capacity,
    block,
    qkv_ref,
    bias_ref,
    weight_in,
    tokens_in,
    hot_in,
    cot_in,
    table_ref,
    in_ref,
    out_ref,
    outs_ref,
    att_ref,
    exp_ref,
    inv_ref,
    before_ref,
    after_ref,
    middle_ref,
    normed_ref,
    rows_ref,
    back_ref,
    second_before,
    second_after,
    next_before,
    next_after,
    last_before,
    last_after,
    line_before,
    line_after,
    weight_ref,
    home_ref,
    hot_ref,
    cot_ref,
    fetch_sems,
    packed,
    done,
    grads,
    forward,
    backward,
    in_held,
    out_held,
    send,
    recv,
    back_send,
    back_recv,
    local,
    held_sems,
    line_sems,
    *attend_scratch,
):
    own, count, width = rows_ref.shape
    across = lax.axis_size("wide")
    total, heads, size, tokens = att_ref.shape
    parts = width // (heads * size)
    seqs = total // parts
    me = lax.axis_index("wide")
    steps = in_ref.shape[2] // block

    def load(at):
        slot = lax.rem(at, 2)
        expert, place = lax.div(at, steps), pl.multiple_of(lax.rem(at, steps) * block, block)
        return (
            pltpu.make_async_copy(in_ref.at[expert, :, pl.ds(place, block)], in_held.at[slot], held_sems.at[0, slot]),
            pltpu.make_async_copy(out_ref.at[expert, pl.ds(place, block), :], out_held.at[slot], held_sems.at[1, slot]),
        )

    held = fetch((weight_in, tokens_in, hot_in, cot_in), (weight_ref, home_ref, hot_ref, cot_ref), fetch_sems)
    for copy in load(0):
        copy.start()
    next_start, first_end = line_round(
        parts, (0, seqs - 2, cot_in.at[1], next_before), (1, seqs - 1, cot_in.at[1], next_after), line_sems.at[0]
    )
    second_start, second_end = line_round(
        parts, (1, seqs - 2, before_ref, second_before), (1, seqs - 2, after_ref, second_after), line_sems.at[1]
    )
    attend_kernel(
        seqs,
        [{"wide": lax.rem(me + k, across)} for k in range(1, across)],
        [next_start, second_start],
        qkv_ref,
        bias_ref,
        cot_in,
        outs_ref,
        att_ref,
        exp_ref,
        inv_ref,
        before_ref,
        after_ref,
        *attend_scratch,
    )
    line_ends = [second_end]
    for copy in held:
        copy.wait()
    attended = [att_ref[parts * s : parts * (s + 1)].reshape(width, tokens) for s in range(seqs)]
    attended = jnp.concatenate(attended, axis=1)
    middle = home_ref[...].astype(F32) + contract(attended, weight_ref[...], 0, 0)
    middle_ref[...] = middle
    normed = (middle * inverse_rms(middle) * table_ref[1:2, :]).astype(BF16)
    normed_ref[...] = normed
    packed[...] = contract(hot_ref[...], normed, 0, 0).astype(BF16).reshape(packed.shape)
    going, kept = [], []
    mine = pl.ds(me * capacity, capacity)
    for n in range(own):
        for k in range(1, across):
            to = lax.rem(me + k, across)
            going.append(
                remote(
                    packed.at[n, pl.ds(to * capacity, capacity)],
                    rows_ref.at[n, mine],
                    send.at[n, k - 1],
                    recv.at[n, k - 1],
                    {"wide": to},
                )
            )
        kept.append(pltpu.make_async_copy(packed.at[n, mine], rows_ref.at[n, mine], local.at[n]))
        kept[n].start()
    first_end()
    line_ends.append(
        pass_on(parts, (1, seqs - 2, next_before, last_before), (1, seqs - 2, next_after, last_after), line_sems.at[2])
    )
    coming = []
    for e in range(own):
        for copy in going[e * (across - 1) : (e + 1) * (across - 1)] + [kept[e]]:
            copy.wait()
        line_ends.append(
            pass_on(
                parts,
                (0, seqs - 2, rows_ref.at[e], line_before.at[e]),
                (1, seqs - 1, rows_ref.at[e], line_after.at[e]),
                line_sems.at[3 + e],
            )
        )
        grads[...] = gated(rows_ref[e], cot_ref[e], router_of(table_ref, own * across), me * own + e)
        forward[...] = jnp.zeros_like(forward)
        backward[...] = jnp.zeros_like(backward)

        def step(f, carry):
            at = e * steps + f
            slot = lax.rem(at, 2)

            @pl.when(at + 1 < own * steps)
            def _():
                for copy in load(at + 1):
                    copy.start()

            for copy in load(at):
                copy.wait()
            hidden, slope = activation(contract(rows_ref[e], in_held[slot], 1, 0))
            grad_hidden = contract(grads[...], out_held[slot], 1, 1).astype(BF16).astype(F32)
            forward[...] += contract(hidden.astype(BF16), out_held[slot], 1, 0)
            backward[...] += contract((grad_hidden * slope).astype(BF16), in_held[slot], 1, 1)
            return carry

        lax.fori_loop(0, steps, step, 0)
        done[e, :, :width] = forward[...].astype(BF16)
        done[e, :, width:] = backward[...].astype(BF16)
        for k in range(1, across):
            to = lax.rem(me + k, across)
            coming.append(
                remote(
                    done.at[e, pl.ds(to * capacity, capacity)],
                    back_ref.at[e, mine],
                    back_send.at[e, k - 1],
                    back_recv.at[e, k - 1],
                    {"wide": to},
                )
            )
        coming.append(pltpu.make_async_copy(done.at[e, mine], back_ref.at[e, mine], local.at[own + e]))
        coming[-1].start()
    for copy in coming:
        copy.wait()
    for end in line_ends:
        end()


def run_forward(qkv, bias_line, weight, tokens_in, table, hot, cots, w_in, w_out, capacity, block):
    own, count, width = cots.shape
    tokens = tokens_in.shape[0]
    units = w_in.shape[2]
    across, total = lax.axis_size("wide"), lax.axis_size("seq")
    _, heads, size, length = qkv.shape
    vmem, hbm = pl.BlockSpec(memory_space=pltpu.VMEM), pl.BlockSpec(memory_space=pl.ANY)
    sems = pltpu.SemaphoreType.DMA
    fetched = (weight, tokens_in, hot, cots)
    attend_out, attend_scratch = attend_shapes(heads, size, length, total)
    block_rows = jax.ShapeDtypeStruct(cots.shape[1:], BF16)
    return pl.pallas_call(
        functools.partial(forward_kernel, capacity, block),
        in_specs=[vmem] * 2 + [hbm] * 4 + [vmem] + [hbm] * 2,
        out_specs=[vmem, vmem, hbm, vmem, hbm, hbm] + [vmem] * 4 + [hbm] * 8,
        out_shape=[
            *attend_out,
            *[block_rows] * 2,
            jax.ShapeDtypeStruct((tokens, width), F32),
            jax.ShapeDtypeStruct((tokens, width), BF16),
            jax.ShapeDtypeStruct(cots.shape, BF16),
            jax.ShapeDtypeStruct((own, count, 2 * width), BF16),
            *[block_rows] * 6,
            *[jax.ShapeDtypeStruct(cots.shape, BF16)] * 2,
        ],
        scratch_shapes=[
            *[pltpu.VMEM(a.shape, BF16) for a in fetched],
            sems((len(fetched),)),
            pltpu.VMEM(cots.shape, BF16),
            pltpu.VMEM((own, count, 2 * width), BF16),
            pltpu.VMEM((count, width), BF16),
            pltpu.VMEM((count, width), F32),
            pltpu.VMEM((count, width), F32),
            pltpu.VMEM((2, width, block), BF16),
            pltpu.VMEM((2, block, width), BF16),
            sems((own, across - 1)),
            sems((own, across - 1)),
            sems((own, across - 1)),
            sems((own, across - 1)),
            sems((2 * own,)),
            sems((2, 2)),
            sems((3 + own, 2, 2)),
            *attend_scratch,
            sems((2, 2)),
        ],
        compiler_params=pltpu.CompilerParams(collective_id=5, has_side_effects=True, vmem_limit_bytes=62 << 20),
        cost_estimate=pl.CostEstimate(
            flops=8 * own * count * width * units, bytes_accessed=4 * own * width * units, transcendentals=own * count * units
        ),
        name="forward",
    )(qkv, bias_line, *fetched, table, w_in, w_out)


def share_kernel(expert, share_ref, rows_ref, cot_ref, router_ref, in_ref, out_ref, *refs):
    grad_in_ref, grad_out_ref, flipped, total_in = refs[-4:]
    step = pl.program_id(0)

    @pl.when(step == 0)
    def _():
        flipped[...] = in_ref[0].T
        total_in[...] = jnp.zeros_like(total_in)
        grad_out_ref[...] = jnp.zeros_like(grad_out_ref)

    rows = rows_ref[0]
    own = router_ref.shape[0] // lax.axis_size("wide")
    grads = gated(rows, cot_ref[0], router_ref[...], lax.axis_index("wide") * own + expert)
    hidden, slope = activation(contract(flipped[...], rows, 1, 1))
    grad_hidden = contract(out_ref[0], grads, 1, 1).astype(BF16).astype(F32)
    grad_out_ref[0] += contract(hidden.astype(BF16), grads, 1, 0)
    total_in[...] += contract((grad_hidden * slope).astype(BF16), rows, 1, 0)

    @pl.when(step == pl.num_programs(0) - 1)
    def _():
        grad_in_ref[0] = total_in[...].T


def run_share(me, rows, cots, router, w_in, w_out, expert, held):
    own, width, units = w_in.shape
    sources, count = rows.shape[0] // own, rows.shape[1]
    share = units // sources
    if share % LANES == 0:
        where = jnp.full((1,), me, jnp.int32)
        in_spec = pl.BlockSpec((1, width, share), lambda r, at: (expert, 0, at[0]))
        out_spec = pl.BlockSpec((1, share, width), lambda r, at: (expert, at[0], 0))
    else:
        where = jnp.zeros((1,), jnp.int32)
        w_in = lax.dynamic_slice(w_in, (0, 0, me * share), (own, width, share))
        w_out = lax.dynamic_slice(w_out, (0, me * share, 0), (own, share, width))
        in_spec = pl.BlockSpec((1, width, share), lambda r, at: (expert, 0, 0))
        out_spec = pl.BlockSpec((1, share, width), lambda r, at: (expert, 0, 0))
    held_specs = [pl.BlockSpec(memory_space=pl.ANY)] * len(held)
    return pl.pallas_call(
        functools.partial(share_kernel, expert),
        grid_spec=pltpu.PrefetchScalarGridSpec(
            num_scalar_prefetch=1,
            grid=(sources,),
            in_specs=[
                pl.BlockSpec((1, count, rows.shape[2]), lambda r, at: (own * r + expert, 0, 0)),
                pl.BlockSpec((1, count, width), lambda r, at: (own * r + expert, 0, 0)),
                pl.BlockSpec(router.shape, lambda r, at: (0, 0)),
                in_spec,
                out_spec,
                *held_specs,
            ],
            out_specs=[
                pl.BlockSpec((1, width, share), lambda r, at: (expert, 0, 0)),
                pl.BlockSpec((1, share, width), lambda r, at: (expert, 0, 0)),
            ],
            scratch_shapes=[pltpu.VMEM((share, width), BF16), pltpu.VMEM((share, width), F32)],
        ),
        out_shape=[
            jax.ShapeDtypeStruct((own, width, share), F32),
            jax.ShapeDtypeStruct((own, share, width), F32),
        ],
        input_output_aliases={6 + i: i for i in range(len(held))},
        compiler_params=pltpu.CompilerParams(vmem_limit_bytes=62 << 20),
        cost_estimate=pl.CostEstimate(
            flops=8 * sources * count * width * share, bytes_accessed=4 * sources * count * width, transcendentals=0
        ),
        name="share",
    )(where, rows, cots, router, w_in, w_out, *held)


def spread_kernel(parts, in_ref, out_ref, send, recv, pass_send, pass_recv, local):
    total = lax.axis_size("seq")
    me = lax.axis_index("seq")
    part = lax.rem(me, parts)
    meet([{"seq": lax.rem(me + k, total)} for k in range(1, total)])
    copies = []
    for k in far_first(total):
        to = lax.rem(me + k, total)
        copies.append(remote(in_ref.at[to], out_ref.at[me, lax.rem(to, parts)], send.at[k - 1], recv.at[k - 1], {"seq": to}))
    own = pltpu.make_async_copy(in_ref.at[me], out_ref.at[me, part], local)
    own.start()
    own.wait()
    passed = []

    def forward(source, k):
        for j in range(1, parts):
            to = me - part + lax.rem(part + j, parts)
            at = (j - 1) * total + k
            block = out_ref.at[source, part]
            passed.append(remote(block, block, pass_send.at[at], pass_recv.at[at], {"seq": to}))

    forward(me, 0)
    for k in far_first(total)[::-1]:
        source = lax.rem(me - k + total, total)
        block = out_ref.at[source, part]
        pltpu.make_async_remote_copy(
            block, block, send.at[k - 1], recv.at[k - 1], device_id={"seq": source}, device_id_type=MESH
        ).wait_recv()
        forward(source, k)
    for copy in copies:
        copy.wait_send()
    for copy in passed:
        copy.wait()


def spread(blocks, parts):
    total, rows, width = blocks.shape
    passes = (parts - 1) * total
    return pl.pallas_call(
        functools.partial(spread_kernel, parts),
        in_specs=[pl.BlockSpec(memory_space=pl.ANY)],
        out_specs=pl.BlockSpec(memory_space=pl.ANY),
        out_shape=jax.ShapeDtypeStruct((total, parts, rows, width), blocks.dtype),
        scratch_shapes=[
            pltpu.SemaphoreType.DMA((total - 1,)),
            pltpu.SemaphoreType.DMA((total - 1,)),
            pltpu.SemaphoreType.DMA((passes,)),
            pltpu.SemaphoreType.DMA((passes,)),
            pltpu.SemaphoreType.DMA,
        ],
        compiler_params=pltpu.CompilerParams(collective_id=0, has_side_effects=True),
        name="spread",
    )(blocks)


def begin_kernel(
    capacity,
    experts,
    in_ref,
    query_in,
    key_in,
    value_in,
    cot_in,
    table_ref,
    base_ref,
    all_out,
    qkv_out,
    flip_out,
    hot_out,
    rows_ref,
    weights_out,
    all_ref,
    qkv_ref,
    flip_ref,
    hot_ref,
    weights,
    query_ref,
    key_ref,
    value_ref,
    cot_ref,
    fetch_sems,
    packed,
    send,
    recv,
    pass_send,
    pass_recv,
    wide_send,
    wide_recv,
    local,
):
    total, parts, rows, width = all_ref.shape
    _, heads, size, length = qkv_ref.shape
    own = rows_ref.shape[0]
    cols = heads * size
    across = lax.axis_size("wide")
    me, row = lax.axis_index("seq"), lax.axis_index("wide")
    part = lax.rem(me, parts)
    other = twist(me, 1, total)
    pairs = total // 2
    held = fetch((cot_in, query_in, key_in, value_in), (cot_ref, query_ref, key_ref, value_ref), fetch_sems)
    peers = [{"seq": lax.rem(me + k, total)} for k in range(1, total)]
    peers += [{"wide": lax.rem(row + k, across)} for k in range(1, across)]
    meet(peers)
    sent = []
    for k in range(1, total):
        to = twist(me, k, total)
        sent.append(remote(in_ref.at[to], all_ref.at[me, lax.rem(to, parts)], send.at[to], recv.at[me], {"seq": to}))
    kept = pltpu.make_async_copy(in_ref.at[me], all_ref.at[me, part], local.at[0])
    kept.start()
    kept.wait()
    passed = []

    def forward(source):
        block = all_ref.at[source, part]
        passed.append(remote(block, block, pass_send.at[source], pass_recv.at[source], {"seq": other}))

    def await_recv(block, sem):
        pltpu.make_async_remote_copy(
            block, block, local.at[1], sem, device_id={"seq": other}, device_id_type=MESH
        ).wait_recv()

    forward(me)

    tokens, slots = hot_ref.shape
    routes = routes_of(table_ref, experts, tokens)
    picked = (routes == lax.broadcasted_iota(jnp.int32, (tokens, LANES), 1).astype(F32)).astype(F32)
    down = lax.broadcasted_iota(jnp.int32, (tokens, tokens), 0)
    over = lax.broadcasted_iota(jnp.int32, (tokens, tokens), 1)
    earlier = contract((over < down).astype(F32).astype(BF16), picked.astype(BF16), 1, 0)
    rank = jnp.sum(earlier * picked, axis=1, keepdims=True)
    place = jnp.sum(base_ref[...] * picked, axis=1, keepdims=True) + rank
    place = jnp.where(rank < capacity, place, float(slots)).astype(jnp.int32)
    hot = (place == lax.broadcasted_iota(jnp.int32, (tokens, slots), 1)).astype(F32).astype(BF16)
    hot_ref[...] = hot
    held[0].wait()
    stored = [pltpu.make_async_copy(hot_ref, hot_out, fetch_sems.at[4])]
    stored[0].start()
    packed[...] = contract(hot, cot_ref[...], 0, 0).astype(BF16).reshape(packed.shape)
    wide = []
    mine = pl.ds(row * capacity, capacity)
    for e in range(own):
        for k in range(1, across):
            to = lax.rem(row + k, across)
            wide.append(
                remote(
                    packed.at[e, pl.ds(to * capacity, capacity)],
                    rows_ref.at[e, mine],
                    wide_send.at[e, k - 1],
                    wide_recv.at[e, k - 1],
                    {"wide": to},
                )
            )
    stay = [pltpu.make_async_copy(packed.at[e, mine], rows_ref.at[e, mine], local.at[2 + e]) for e in range(own)]
    for copy in stay:
        copy.start()
    at = pl.ds(pl.multiple_of(part * cols, LANES), cols)
    for n, ref in enumerate((query_ref, key_ref, value_ref)):
        held[1 + n].wait()
        weights[n * cols : (n + 1) * cols, :] = ref[:, at].T
    stored.append(pltpu.make_async_copy(weights, weights_out, fetch_sems.at[5]))
    stored[1].start()

    for t in range(pairs):
        pair = twist(lax.div(me, 2), t, pairs)
        for b in range(2):
            if 2 * t + b:
                source = twist(me, 2 * t + b, total)
                await_recv(all_ref.at[source, part], recv.at[source])
                forward(source)
        for b in range(2):
            source = 2 * pair + b
            await_recv(all_ref.at[source, lax.rem(part + 1, parts)], pass_recv.at[source])
        block = all_ref[pl.ds(2 * pair, 2)].reshape(2 * parts * rows, width).astype(F32)
        normed = (block * inverse_rms(block) * table_ref[0:1, :]).astype(BF16)
        here = pl.ds(pl.multiple_of(pair * (2 * parts * rows), LANES), 2 * parts * rows)
        flip_ref[:, here] = normed.T
        projected = contract(weights[...], normed, 1, 1).astype(BF16)
        qkv_ref[:, :, :, here] = projected.reshape(3, heads, size, 2 * parts * rows)
        both = pl.ds(2 * pair, 2)
        for n, (src, dst) in enumerate(
            (
                (all_ref.at[both], all_out.at[both]),
                (flip_ref.at[:, here], flip_out.at[:, here]),
                (qkv_ref.at[:, :, :, here], qkv_out.at[:, :, :, here]),
            )
        ):
            stored.append(pltpu.make_async_copy(src, dst, fetch_sems.at[6 + 3 * t + n]))
            stored[-1].start()
    for copy in sent + passed:
        copy.wait_send()
    for copy in wide + stay + stored:
        copy.wait()


def begin(blocks, w_query, w_key, w_value, table, base, cot, heads, size, own, capacity):
    total, rows, width = blocks.shape
    tokens = cot.shape[0]
    across = lax.axis_size("wide")
    slots = own * across * capacity
    length = total * 2 * rows
    vmem, hbm = pl.BlockSpec(memory_space=pltpu.VMEM), pl.BlockSpec(memory_space=pl.ANY)
    sems = pltpu.SemaphoreType.DMA
    return pl.pallas_call(
        functools.partial(begin_kernel, capacity, own * across),
        in_specs=[hbm] * 5 + [vmem] * 2,
        out_specs=[hbm] * 4 + [vmem, hbm],
        out_shape=[
            jax.ShapeDtypeStruct((total, 2, rows, width), BF16),
            jax.ShapeDtypeStruct((3, heads, size, length), BF16),
            jax.ShapeDtypeStruct((width, length), BF16),
            jax.ShapeDtypeStruct((tokens, slots), BF16),
            jax.ShapeDtypeStruct((own, across * capacity, width), BF16),
            jax.ShapeDtypeStruct((3 * heads * size, width), BF16),
        ],
        scratch_shapes=[
            pltpu.VMEM((total, 2, rows, width), BF16),
            pltpu.VMEM((3, heads, size, length), BF16),
            pltpu.VMEM((width, length), BF16),
            pltpu.VMEM((tokens, slots), BF16),
            pltpu.VMEM((3 * heads * size, width), BF16),
            pltpu.VMEM((width, width), BF16),
            pltpu.VMEM((width, width), BF16),
            pltpu.VMEM((width, width), BF16),
            pltpu.VMEM((tokens, width), BF16),
            sems((6 + 3 * total // 2,)),
            pltpu.VMEM((own, across * capacity, width), BF16),
            sems((total,)),
            sems((total,)),
            sems((total,)),
            sems((total,)),
            sems((own, across - 1)),
            sems((own, across - 1)),
            sems((2 + own,)),
        ],
        compiler_params=pltpu.CompilerParams(collective_id=6, has_side_effects=True, vmem_limit_bytes=62 << 20),
        cost_estimate=pl.CostEstimate(flops=4 << 30, bytes_accessed=80 << 20, transcendentals=0),
        name="begin",
    )(blocks, w_query, w_key, w_value, cot, table, base)


def finish_kernel(
    seqs,
    three_ref,
    flip_ref,
    weight_ref,
    x_ref,
    early_ref,
    tiny_ref,
    table_ref,
    params_ref,
    *refs,
):
    own, steps = 2, 2 * seqs - 1
    inputs = (flip_ref, three_ref, weight_ref, x_ref)
    flip_ref, three_ref, weight_ref, x_ref, sems = refs[-5:]
    held = fetch(inputs, (flip_ref, three_ref, weight_ref, x_ref), sems)
    refs = refs[:-5]
    rows_refs = refs[: steps - 2]
    cots_refs = refs[steps - 2 : steps - 2 + 1 + own * (steps - 1)]
    finish_rest(
        seqs,
        held,
        rows_refs,
        cots_refs,
        three_ref,
        flip_ref,
        weight_ref,
        x_ref,
            early_ref,
        tiny_ref,
        table_ref,
        params_ref,
        *refs[len(rows_refs) + len(cots_refs) :],
    )


def finish_rest(
    seqs,
    held,
    rows_refs,
    cots_refs,
    three_ref,
    flip_ref,
    weight_ref,
    x_ref,
    early_ref,
    tiny_ref,
    table_ref,
    params_ref,
    in_ref,
    out_ref,
    home_ref,
    late_all,
    early_all,
    tiny,
    grad_in_ref,
    grad_out_ref,
    grads,
    near,
    summed,
    gw,
    wide_got,
    wide_sum,
    far_got,
    early_got,
    mine,
    early_mine,
    tiny_got,
    rows_held,
    cots_held,
    in_held,
    out_held,
    sums,
    total_in,
    leaving,
    share_got,
    share_sems,
    near_sems,
    home_sems,
    wide_sems,
    far_sems,
    early_sems,
    last_sems,
    last_early_sems,
    tiny_sems,
    held_sems,
    line_sems,
    local,
):
    total, across = lax.axis_size("seq"), lax.axis_size("wide")
    parts = total // seqs
    me, row = lax.axis_index("seq"), lax.axis_index("wide")
    part, seq = lax.rem(me, parts), lax.div(me, parts)
    other = twist(me, 1, total)
    width = params_ref.shape[1]
    slim = gw.shape[2]
    own = in_ref.shape[0]
    share = in_ref.shape[2] // total
    cols = three_ref.shape[1] // 3
    half = three_ref.shape[0] // 2

    def seq_at(k):
        return lax.rem(seq + k, seqs) * parts + part

    def row_at(k):
        return lax.rem(row + k, across)

    def part_at(k):
        return me - part + lax.rem(part + k, parts)

    at = pl.ds(pl.multiple_of(lax.div(me, 2) * (2 * share), LANES), 2 * share)
    weights = [
        pltpu.make_async_copy(in_ref.at[:, :, at], in_held, local.at[0]),
        pltpu.make_async_copy(out_ref.at[:, at, :], out_held, local.at[1]),
    ]
    for copy in weights:
        copy.start()

    def load_rows(e, n, k):
        return pltpu.make_async_copy(rows_refs[k].at[e], rows_held.at[e, n], held_sems.at[0, e, n])

    def load_cots(e, n, k):
        src = cots_refs[1 + own * (k - 1) + e] if k else cots_refs[0].at[e]
        return pltpu.make_async_copy(src, cots_held.at[e, n], held_sems.at[1, e, n])

    last_place = seqs - 1
    far_end = jnp.logical_or(seq == 0, seq == last_place)
    for e in range(own):
        load_rows(e, 0, 0).start()
        load_cots(e, 0, 0).start()
        for here in range(seqs):

            @pl.when(seq == here)
            def _():
                sources = [2 * k - 1 for k in range(1, here + 1)] + [2 * k for k in range(1, seqs - here)]
                for n, k in enumerate(sources):
                    load_cots(e, n + 1, k).start()
                    if k < len(rows_refs):
                        load_rows(e, n + 1, k).start()

    pairs = [(a, b) for a in range(across) for b in range(parts) if a or b]
    peers = [{"seq": lax.rem(me + k, total)} for k in range(1, total)]
    peers += [{"wide": row_at(k)} for k in range(1, across)]
    peers += [{"wide": row_at(a), "seq": part_at(b)} for a, b in pairs if a and b]
    meet(peers)

    def far_rows(e, up):
        src = rows_refs[3 if up else 4].at[e]
        to = lax.rem(me + (parts if up else total - parts), total)
        return pltpu.make_async_remote_copy(
            src, rows_held.at[e, last_place], line_sems.at[0, e], line_sems.at[1, e], device_id={"seq": to}, device_id_type=MESH
        )

    for e in range(own):

        @pl.when(seq == last_place - 1)
        def _():
            far_rows(e, True).start()

        @pl.when(seq == 1)
        def _():
            far_rows(e, False).start()

    for copy in held:
        copy.wait()
    late = contract(flip_ref[...], three_ref[...], 1, 0).astype(BF16)
    gw[...] = late.reshape(gw.shape)
    wide_copies = [
        remote(gw.at[:, row_at(k)], wide_got.at[k - 1], wide_sems.at[0, k - 1], wide_sems.at[1, k - 1], {"wide": row_at(k)})
        for k in range(1, across)
    ]

    gain = params_ref[0:1, :]
    gain_grad = jnp.zeros((1, width), F32)
    near_copies = []
    for n in range(2):
        scaled = contract(three_ref[n * half : (n + 1) * half, :], weight_ref[...], 1, 0)
        x = x_ref[n * total // 2 : (n + 1) * total // 2].reshape(half, width).astype(F32)
        inverse = inverse_rms(x)
        gain_grad = gain_grad + jnp.sum(scaled * x * inverse, axis=0, keepdims=True)
        scaled = scaled * gain
        mean_inner = jnp.mean(x * scaled, axis=-1, keepdims=True)
        value = inverse * scaled - x * (inverse * inverse * inverse) * mean_inner
        here = pl.ds(n * total // 2, total // 2)
        grads[here] = value.astype(BF16).reshape(total // 2, *grads.shape[1:])
        near_copies.append(
            remote(
                grads.at[here, lax.rem(part + 1, parts)],
                near.at[here],
                near_sems.at[0, n],
                near_sems.at[1, n],
                {"seq": other},
            )
        )
    lines = tiny_ref.shape[0]
    first = lax.broadcasted_iota(jnp.int32, tiny_ref.shape, 0) == 0
    tiny[:lines, :] = jnp.where(first, gain_grad, tiny_ref[...]).astype(BF16)
    table = table_ref[...]
    tiny[lines:, :] = jnp.concatenate([table, jnp.zeros((table.shape[0], width - table.shape[1]), F32)], axis=1).astype(BF16)

    def pass_tiny(stage, wheres):
        return [
            remote(tiny, tiny_got.at[stage, n], tiny_sems.at[0, stage, n], tiny_sems.at[1, stage, n], where)
            for n, where in enumerate(wheres)
        ]

    def take_tiny(stage, copies):
        for copy in copies:
            copy.wait()
        value = tiny[...].astype(F32)
        for n in range(len(copies)):
            value = value + tiny_got[stage, n].astype(F32)
        tiny[...] = value.astype(BF16)

    tiny_copies = pass_tiny(0, [{"wide": row_at(k)} for k in range(1, across)])
    for copy in near_copies:
        copy.wait()
    home_copies = []
    for k in range(total - 1, -1, -1):
        to = twist(me, k, total)
        summed[to] = (grads[to, part].astype(F32) + near[to].astype(F32)).astype(BF16)
        if k:
            home_copies.append(
                remote(summed.at[to], home_ref.at[me], home_sems.at[0, k - 1], home_sems.at[1, k - 1], {"seq": to})
            )
    kept = pltpu.make_async_copy(summed.at[me], home_ref.at[me], local.at[2])
    kept.start()
    for copy in weights:
        copy.wait()

    mine_rows = pl.ds(pl.multiple_of(part * share, LANES), share)
    other_rows = pl.ds(pl.multiple_of((1 - part) * share, LANES), share)

    def share_turn(e, n):
        some = rows_held.shape[1] // 2
        for m in range(n * some, (n + 1) * some):
            load_cots(e, m, 0).wait()
            if m < last_place:
                load_rows(e, m, 0).wait()
            else:

                @pl.when(far_end)
                def _():
                    far_rows(e, True).wait_recv()

                @pl.when(jnp.logical_not(far_end))
                def _():
                    load_rows(e, m, 0).wait()

        count = some * rows_held.shape[2]
        here = slice(n * some, (n + 1) * some)
        rows = rows_held[e, here].reshape(count, width)
        cots = gated(rows, cots_held[e, here].reshape(count, width), router_of(params_ref, own * across), row * own + e)
        hidden, slope = activation(contract(in_held[e].T, rows, 1, 1))
        grad_hidden = contract(out_held[e], cots, 1, 1).astype(BF16).astype(F32)
        part_out = contract(hidden.astype(BF16), cots, 1, 0)
        part_in = contract((grad_hidden * slope).astype(BF16), rows, 1, 0)
        if n == 0:
            sums[e, 0] = part_out
            sums[e, 1] = part_in
            return []
        sums[e, 0] += part_out
        sums[e, 1] += part_in
        grad_out_ref[e] = sums[e, 0, mine_rows, :]
        total_in[e] = sums[e, 1, mine_rows, :]
        copies = []
        for k in range(2):
            leaving[e, k] = sums[e, k, other_rows, :].astype(BF16)
            copies.append(
                remote(leaving.at[e, k], share_got.at[e, k], share_sems.at[0, e, k], share_sems.at[1, e, k], {"seq": other})
            )
        return copies

    def share_end(e, copies):
        for copy in copies:
            copy.wait()
        grad_out_ref[e] += share_got[e, 0].astype(F32)
        grad_in_ref[e] = (total_in[e] + share_got[e, 1].astype(F32)).T

    share_turn(0, 0)
    share_turn(1, 0)
    take_tiny(0, tiny_copies)
    for copy in wide_copies:
        copy.wait_recv()
    far_copies = []
    for k in list(range(1, seqs)) + [0]:
        place = lax.rem(seq + k, seqs)
        for p in range(parts):
            block = place * parts + p
            value = gw[block, row].astype(F32)
            for j in range(across - 1):
                value = value + wide_got[j, block].astype(F32)
            wide_sum[place, p] = value.astype(BF16)
        if k:
            where = {"seq": seq_at(k)}
            far_copies.append(
                remote(wide_sum.at[place], far_got.at[k - 1], far_sems.at[0, k - 1], far_sems.at[1, k - 1], where)
            )
            far_copies.append(
                remote(early_ref.at[place], early_got.at[k - 1], early_sems.at[0, k - 1], early_sems.at[1, k - 1], where)
            )
    tiny_copies = pass_tiny(1, [{"seq": seq_at(k)} for k in range(1, seqs)])
    first_share = share_turn(0, 1)
    take_tiny(1, tiny_copies)
    for copy in far_copies:
        copy.wait_recv()
    for p in range(parts):
        value = wide_sum[seq, p].astype(F32)
        for j in range(seqs - 1):
            value = value + far_got[j, p].astype(F32)
        mine[p] = value.astype(BF16)
    value = early_ref[seq].astype(F32)
    for j in range(seqs - 1):
        value = value + early_got[j].astype(F32)
    early_mine[...] = value.astype(BF16)
    last = pass_tiny(2, [{"seq": part_at(k)} for k in range(1, parts)])
    count = len(last)
    for a, b in pairs:
        n = a * parts + b - 1
        last.append(
            remote(
                mine.at[lax.rem(part + b, parts)],
                late_all.at[row, part],
                last_sems.at[0, n],
                last_sems.at[1, n],
                {"wide": row_at(a), "seq": part_at(b)},
            )
        )
    for k in range(1, across):
        last.append(
            remote(
                early_mine, early_all.at[row], last_early_sems.at[0, k - 1], last_early_sems.at[1, k - 1], {"wide": row_at(k)}
            )
        )
    stay = [
        pltpu.make_async_copy(mine.at[part], late_all.at[row, part], local.at[3]),
        pltpu.make_async_copy(early_mine, early_all.at[row], local.at[4]),
    ]
    for copy in stay:
        copy.start()
    second_share = share_turn(1, 1)
    share_end(0, first_share)
    take_tiny(2, last[:count])
    share_end(1, second_share)
    for e in range(own):

        @pl.when(jnp.logical_or(seq == 1, seq == last_place - 1))
        def _():
            far_rows(e, True).wait_send()

    for copy in last[count:] + stay + home_copies + [kept]:
        copy.wait()
    for copy in wide_copies + far_copies:
        copy.wait_send()


def finish(three, flipped, weights, x, early, tiny, table, params, rows, cots, w_in, w_out):
    columns = three.shape[1]
    total, parts, piece, width = x.shape
    seqs, slim, _ = early.shape
    across = lax.axis_size("wide")
    own, _, units = w_in.shape
    share = units // total
    vmem, hbm = pl.BlockSpec(memory_space=pltpu.VMEM), pl.BlockSpec(memory_space=pl.ANY)
    sems = pltpu.SemaphoreType.DMA
    most = max(across, seqs, parts) - 1
    lines = tiny.shape[0] + table.shape[0]
    return pl.pallas_call(
        functools.partial(finish_kernel, seqs),
        in_specs=[hbm] * 4 + [vmem] * 4 + [hbm] * (len(rows) + len(cots) + 2),
        out_specs=[vmem] * 6,
        out_shape=[
            jax.ShapeDtypeStruct((total, piece, width), BF16),
            jax.ShapeDtypeStruct((across, parts, slim, columns), BF16),
            jax.ShapeDtypeStruct((across, slim, width), BF16),
            jax.ShapeDtypeStruct((lines, width), BF16),
            jax.ShapeDtypeStruct((own, width, share), F32),
            jax.ShapeDtypeStruct((own, share, width), F32),
        ],
        scratch_shapes=[
            pltpu.VMEM((total, parts, piece, width), BF16),
            pltpu.VMEM((total, piece, width), BF16),
            pltpu.VMEM((total, piece, width), BF16),
            pltpu.VMEM((total, across, slim, columns), BF16),
            pltpu.VMEM((across - 1, total, slim, columns), BF16),
            pltpu.VMEM((seqs, parts, slim, columns), BF16),
            pltpu.VMEM((seqs - 1, parts, slim, columns), BF16),
            pltpu.VMEM((seqs - 1, slim, width), BF16),
            pltpu.VMEM((parts, slim, columns), BF16),
            pltpu.VMEM((slim, width), BF16),
            pltpu.VMEM((3, most, lines, width), BF16),
            pltpu.VMEM((own, seqs, *rows[0].shape[1:]), BF16),
            pltpu.VMEM((own, seqs, *cots[0].shape[1:]), BF16),
            pltpu.VMEM((own, width, 2 * share), BF16),
            pltpu.VMEM((own, 2 * share, width), BF16),
            pltpu.VMEM((own, 2, 2 * share, width), F32),
            pltpu.VMEM((own, share, width), F32),
            pltpu.VMEM((own, 2, share, width), BF16),
            pltpu.VMEM((own, 2, share, width), BF16),
            sems((2, own, 2)),
            sems((2, 2)),
            sems((2, total - 1)),
            sems((2, across - 1)),
            sems((2, seqs - 1)),
            sems((2, seqs - 1)),
            sems((2, across * parts - 1)),
            sems((2, across - 1)),
            sems((2, 3, most)),
            sems((2, own, seqs)),
            sems((2, own)),
            sems((5,)),
            *[pltpu.VMEM(a.shape, BF16) for a in (flipped, three, weights, x)],
            sems((4,)),
        ],
        compiler_params=pltpu.CompilerParams(collective_id=1, has_side_effects=True, vmem_limit_bytes=62 << 20),
        cost_estimate=pl.CostEstimate(flops=16 << 30, bytes_accessed=60 << 20, transcendentals=0),
        name="finish",
    )(three, flipped, weights, x, early, tiny, table, params, *rows, *cots, w_in, w_out)


def close_kernel(
    heads,
    home_ref,
    middle_ref,
    late_ref,
    early_ref,
    tiny_ref,
    in_ref,
    out_ref,
    result_ref,
    inputs_ref,
    query_ref,
    key_ref,
    value_ref,
    output_ref,
    gain_one_ref,
    gain_two_ref,
    router_ref,
    table_ref,
    grad_in_ref,
    grad_out_ref,
    result_out,
):
    grad_in_ref[...] = in_ref[...]
    grad_out_ref[...] = out_ref[...]
    result_out[...] = result_ref[...]
    inputs_ref[...] = middle_ref[...] + home_ref[...].reshape(middle_ref.shape).astype(F32)
    _, parts, _, columns = late_ref.shape
    cols = columns // 3
    for p in range(parts):
        for n, ref in enumerate((query_ref, key_ref, value_ref)):
            ref[:, p * cols : (p + 1) * cols] = late_ref[0, p, :, n * cols : (n + 1) * cols].astype(F32)
    output_ref[...] = early_ref[0].astype(F32)

    @pl.when(pl.program_id(0) == 0)
    def _():
        me = lax.axis_index("seq")
        width, piece = tiny_ref.shape[1], gain_one_ref.shape[1]
        chosen = lax.broadcasted_iota(jnp.int32, (width, piece), 0) == (
            lax.broadcasted_iota(jnp.int32, (width, piece), 1) + me * piece
        )
        picked = contract(tiny_ref[...], chosen.astype(F32).astype(BF16), 1, 0)
        gain_one_ref[...] = picked[0:1]
        gain_two_ref[...] = picked[1:2]
        router_ref[...] = picked[2 : 2 + router_ref.shape[0]]
        lines = table_ref.shape[0]
        chosen = lax.broadcasted_iota(jnp.int32, (lines, LANES), 1) == (
            lax.broadcasted_iota(jnp.int32, (lines, LANES), 0) + me * lines
        )
        table_ref[...] = contract(chosen.astype(F32).astype(BF16), tiny_ref[16:, :LANES], 1, 1)[:, :heads]


def close(home, middle, late, early, tiny, grad_in, grad_out, result, heads, buckets, experts):
    across, parts, slim, columns = late.shape
    width = early.shape[2]
    total, piece, _ = home.shape
    tokens = middle.shape[0]
    own, _, share = grad_in.shape
    halves = across // own
    rows = pl.BlockSpec((slim, width), lambda i: (i, 0))

    def whole(*shape):
        return pl.BlockSpec(shape, lambda i: (0,) * len(shape))

    some = pl.BlockSpec((tokens // across, width), lambda i: (i, 0))
    in_part = pl.BlockSpec((1, width // halves, share), lambda i: (i // halves, i % halves, 0))
    out_part = pl.BlockSpec((1, share // halves, width), lambda i: (i // halves, i % halves, 0))
    small = [(1, width // total), (1, width // total), (experts, width // total), (buckets // total, heads)]
    shapes = [middle.shape, *[(across * slim, width)] * 4, *small, grad_in.shape, grad_out.shape]
    return pl.pallas_call(
        functools.partial(close_kernel, heads),
        grid=(across,),
        in_specs=[
            pl.BlockSpec((total // across, piece, width), lambda i: (i, 0, 0)),
            some,
            pl.BlockSpec((1, parts, slim, columns), lambda i: (i, 0, 0, 0)),
            pl.BlockSpec((1, slim, width), lambda i: (i, 0, 0)),
            whole(*tiny.shape),
            in_part,
            out_part,
            some,
        ],
        out_specs=[some, rows, rows, rows, rows, *[whole(*shape) for shape in small], in_part, out_part, some],
        out_shape=[jax.ShapeDtypeStruct(shape, F32) for shape in shapes] + [jax.ShapeDtypeStruct(result.shape, BF16)],
        compiler_params=pltpu.CompilerParams(vmem_limit_bytes=62 << 20),
        name="close",
    )(home, middle, late, early, tiny, grad_in, grad_out, result)


def ring_pairs(total, parts, shift):
    return [(i, i - i % parts + (i % parts + shift) % parts) for i in range(total)]


def pick(pieces, index):
    out = pieces[0]
    for k in range(1, len(pieces)):
        out = jnp.where(index == k, pieces[k], out)
    return out


def swap_parts(pieces, part, parts, total):
    near = [pick(pieces, part)]
    for k in range(1, parts):
        near.append(lax.ppermute(pick(pieces, (part + k) % parts), "seq", ring_pairs(total, parts, k)))
    return [pick(near, (part - j) % parts) for j in range(parts)]


def per_device(
    inputs,
    routes,
    bucket_ids,
    gain_attn,
    w_query,
    w_key,
    w_value,
    w_output,
    rel_table,
    gain_ffn,
    w_router,
    w_in,
    w_out,
    cotangent,
):
    seqs, local_len, width = inputs.shape
    buckets, head_count = rel_table.shape
    size = width // head_count
    total = lax.axis_size("seq")
    across = lax.axis_size("wide")
    length = local_len * total
    parts = total // seqs
    heads = head_count // parts
    cols = heads * size
    me = lax.axis_index("seq")
    part = me % parts
    experts = w_router.shape[1]
    own_experts = w_in.shape[0]
    tokens = seqs * local_len
    capacity = (5 * tokens + 4 * experts - 1) // (4 * experts)
    slots = experts * capacity
    gain_one = gain_attn.astype(F32)
    gain_two = gain_ffn.astype(F32)

    fast = parts == 2 and capacity % 16 == 0 and own_experts == 2 and seqs == 4 and experts == 8 and across == 4 and cols % LANES == 0 and local_len == LANES
    flat_cot = cotangent.reshape(tokens, width)
    chosen = routes.reshape(tokens)
    blocks = inputs.reshape(total, local_len // parts, width)

    if fast:
        lines = chosen.astype(F32).reshape(tokens // LANES, LANES)
        params = jnp.concatenate(
            [
                gain_one[None],
                gain_two[None],
                w_router.T.astype(F32),
                jnp.pad(lines, ((0, 14 - experts - tokens // LANES), (0, width - LANES))),
            ],
            axis=0,
        )
        first_slot = [(e % own_experts) * (across * capacity) + (e // own_experts) * capacity for e in range(experts)]
        base = jnp.array(first_slot + [0] * (LANES - experts), F32)[None]
        seq_in, qkv, flipped, slot_hot, cot_rows, own_weights = begin(
            blocks,
            w_query,
            w_key,
            w_value,
            params,
            base,
            flat_cot,
            heads,
            size,
            own_experts,
            capacity,
        )
    else:
        own_weights = jnp.concatenate(
            [lax.dynamic_slice(w, (0, part * cols), (width, cols)) for w in (w_query, w_key, w_value)], axis=1
        )
        seq_in = spread(blocks, parts).reshape(length, width).astype(F32)
        inv_one = inverse_rms(seq_in)
        normed_one = (seq_in * inv_one * gain_one).astype(BF16)
        flipped = normed_one.T
        qkv = contract(own_weights, normed_one, 0, 1).astype(BF16).reshape(3, heads, size, length)
        picked = (chosen[:, None] == jnp.arange(experts, dtype=jnp.int32)[None, :]).astype(F32)
        order = jnp.arange(tokens, dtype=jnp.int32)
        before = (order[None, :] < order[:, None]).astype(BF16)
        earlier = jnp.dot(before, picked.astype(BF16), preferred_element_type=F32)
        rank_in = jnp.sum(earlier * picked, axis=1).astype(jnp.int32)
        place = (chosen % own_experts) * (across * capacity) + (chosen // own_experts) * capacity + rank_in
        slot_of = jnp.where(rank_in < capacity, place, slots)
        slot_hot = (slot_of[:, None] == jnp.arange(slots, dtype=jnp.int32)[None, :]).astype(BF16)
        packed = contract(slot_hot, flat_cot, 0, 0).astype(BF16).reshape(own_experts, across, capacity, width)
        cot_rows = jnp.stack([lax.all_to_all(packed[e], "wide", 0, 0, tiled=True) for e in range(own_experts)])
        cot_rows = cot_rows.reshape(own_experts, across * capacity, width)
    own_table = lax.dynamic_slice(rel_table, (0, part * heads), (buckets, heads))
    ids = jnp.concatenate([bucket_ids, jnp.full((1,), LANES, jnp.int32)])
    bucket_hot = (ids[None, :] == jnp.arange(LANES, dtype=jnp.int32)[:, None]).astype(BF16)
    reverse_hot = (ids[::-1][None, :] == jnp.arange(buckets, dtype=jnp.int32)[:, None]).astype(BF16)
    bias_line = contract(own_table, reverse_hot, 0, 0).reshape(heads, 1, 2 * length)
    share = width // total
    flat_in = inputs.reshape(tokens, width)
    split_output = w_output.reshape(parts, cols, width)
    if fast:
        outs, attended, exps, inverse, *passed = run_forward(
            qkv, bias_line, w_output, flat_in, params, slot_hot, cot_rows, w_in, w_out, capacity, 512
        )
        attended = attended.reshape(seqs, width, local_len)
        first, (middle, normed_two, received, returned, *passed) = passed[:2], passed[2:]
        second = [passed[0], passed[4], passed[1], passed[5]]
        next_cots, near_rows = passed[2:4], passed[6:]
        back = (exps, inverse, split_output, outs, qkv, bucket_hot)
        more = [
            returned,
            slot_hot,
            middle,
            normed_two,
            flat_cot,
            attended,
            params,
        ]
        three, table, early, output, grad_middle, tiny, *passed = attend_back(*back, None, more, near_rows, second)
        all_rows = [received, *near_rows, *passed[:2]]
        all_cots = [cot_rows, first[0], next_cots[0], first[1], next_cots[1], *second, *passed[2:]]
        home, *found = finish(
            three,
            flipped,
            own_weights,
            seq_in,
            early,
            tiny,
            table,
            params,
            all_rows,
            all_cots,
            w_in,
            w_out,
        )
        grad_inputs, *grads_qkvo, grad_gain_one, grad_gain_two, grad_router, grad_table, grad_in, grad_out, output = close(
            home, grad_middle, *found, output, head_count, buckets, experts
        )
        return (
            output.reshape(inputs.shape),
            grad_inputs.reshape(inputs.shape),
            grad_gain_one[0],
            *grads_qkvo,
            grad_table,
            grad_gain_two[0],
            grad_router.T,
            grad_in,
            grad_out,
        )

    outs, attended, exps, inverse = attend(qkv, bias_line, total)
    attended = attended.reshape(seqs, width, local_len)
    back = (exps, inverse, split_output, outs, qkv, bucket_hot)

    flat_in = flat_in.astype(F32)
    middle = flat_in + jnp.einsum("sft,fe->ste", attended, w_output, preferred_element_type=F32).reshape(tokens, width)
    inv_two = inverse_rms(middle)
    normed_two = (middle * inv_two * gain_two).astype(BF16)
    router_probs = jax.nn.softmax(jnp.dot(normed_two, w_router, preferred_element_type=F32), axis=-1)
    picked = (chosen[:, None] == jnp.arange(experts, dtype=jnp.int32)[None, :]).astype(F32)
    gate_prob = jnp.sum(router_probs * picked, axis=1)
    upstream = flat_cot.astype(F32)
    packed = contract(slot_hot, normed_two, 0, 0).astype(BF16).reshape(own_experts, across, capacity, width)
    received, returned = [], []
    for e in range(own_experts):
        got = lax.all_to_all(packed[e], "wide", 0, 0, tiled=True).reshape(across * capacity, width)
        received.append(got)
        pair = run_expert(got, cot_rows[e], w_router.T, w_in, w_out, e, 512).reshape(across, capacity, 2 * width)
        returned.append(lax.all_to_all(pair, "wide", 0, 0, tiled=True).reshape(across * capacity, 2 * width))
    received, returned = jnp.stack(received), jnp.concatenate(returned, axis=0)
    token_rows = jnp.dot(slot_hot, returned, preferred_element_type=F32)
    selected, grad_token = token_rows[:, :width], token_rows[:, width:]
    output = (middle + gate_prob[:, None] * selected).astype(BF16).reshape(inputs.shape)
    grad_gate = jnp.sum(upstream * selected, axis=1)
    grad_logits = (grad_gate[:, None] * router_probs * (picked - gate_prob[:, None])).astype(BF16)
    grad_router = contract(grad_logits, normed_two, 0, 0)
    grad_normed_two = grad_token + contract(grad_logits, w_router, 1, 1)
    grad_mid_norm, grad_gain_two = norm_backward(middle, inv_two, gain_two, grad_normed_two)
    grad_middle = upstream + grad_mid_norm
    grad_branch = grad_middle.astype(BF16).reshape(seqs, local_len, width)
    grad_w_output = jnp.einsum("sft,ste->fe", attended, grad_branch, preferred_element_type=F32)
    all_cots = lax.all_gather(cot_rows, "seq", axis=0)
    all_rows = lax.all_gather(received, "seq", axis=0)
    three, table = attend_back(*back, grad_branch, [], [], [])
    grad_normed_one = contract(three, own_weights, 1, 1)
    grad_in_norm, grad_gain_one = norm_backward(seq_in, inv_one, gain_one, grad_normed_one)
    pieces = grad_in_norm.astype(BF16).reshape(total, parts, local_len // parts, width)
    swapped = swap_parts([pieces[:, p] for p in range(parts)], part, parts, total)
    home = sum(p.astype(F32) for p in swapped).astype(BF16)
    home = lax.all_to_all(home, "seq", 0, 0, tiled=True).reshape(tokens, width).astype(F32)
    grad_projections = lax.dynamic_update_slice(
        jnp.zeros((width, 3, width), F32), contract(flipped, three, 1, 0).reshape(width, 3, cols), (0, 0, part * cols)
    )
    rows = [grad_projections[:, k] for k in range(3)]
    rows += [grad_w_output, grad_gain_one[:, None], grad_gain_two[:, None], grad_router.T]
    table = table.T[:buckets]
    rows, table = lax.psum((jnp.concatenate(rows, axis=1).astype(BF16), table.astype(BF16)), "wide")
    rows = lax.psum_scatter(rows, "seq", scatter_dimension=0, tiled=True).astype(F32)
    table = lax.psum_scatter(table, "seq", scatter_dimension=0, tiled=True).astype(F32)
    held = []
    for e in range(own_experts):
        held = run_share(
            me,
            all_rows.reshape(total * own_experts, *received.shape[1:]),
            all_cots.reshape(total * own_experts, *cot_rows.shape[1:]),
            w_router.T,
            w_in,
            w_out,
            e,
            held,
        )
    last = rows[:, 4 * width :]
    return (
        output,
        (grad_middle + home).reshape(inputs.shape),
        last[:, 0],
        *[rows[:, k * width : (k + 1) * width] for k in range(4)],
        table[:, :head_count],
        last[:, 1],
        last[:, 2 : 2 + experts],
        *held,
    )


def solution(mesh):
    in_specs = (
        P("wide", "seq", None),
        P("wide", "seq", None),
        P(),
        P(),
        P(),
        P(),
        P(),
        P(),
        P(),
        P(),
        P(),
        P("wide", None, None),
        P("wide", None, None),
        P("wide", "seq", None),
    )
    out_specs = (
        P("wide", "seq", None),
        P("wide", "seq", None),
        P("seq"),
        P("seq", None),
        P("seq", None),
        P("seq", None),
        P("seq", None),
        P("seq", None),
        P("seq"),
        P("seq", None),
        P("wide", None, "seq"),
        P("wide", "seq", None),
    )
    return jax.shard_map(
        per_device, mesh=mesh, in_specs=in_specs, out_specs=out_specs, check_vma=False
    )
```

```python
import functools

import jax
import jax.numpy as jnp
from jax import lax
from jax.experimental import pallas as pl
from jax.experimental.pallas import tpu as pltpu
from jax.sharding import PartitionSpec as P

EPSILON = 1e-06
F32 = jnp.float32
BF16 = jnp.bfloat16
LANES = 128


def contract(a, b, da, db):
    return lax.dot_general(a, b, (((da,), (db,)), ((), ())), preferred_element_type=F32)


def inverse_rms(source):
    return lax.rsqrt(jnp.mean(source * source, axis=-1, keepdims=True) + EPSILON)


def norm_backward(source, inv_rms, gain_vec, upstream):
    scaled = upstream * gain_vec
    gain_grad = jnp.sum(upstream * source * inv_rms, axis=0)
    mean_inner = jnp.mean(source * scaled, axis=-1, keepdims=True)
    return (inv_rms * scaled - source * (inv_rms * inv_rms * inv_rms) * mean_inner, gain_grad)


def smooth_act(values):
    return jax.nn.gelu(values, approximate=True)


MESH = pl.DeviceIdType.MESH


def remote(src, dst, send, recv, where):
    copy = pltpu.make_async_remote_copy(src, dst, send, recv, device_id=where, device_id_type=MESH)
    copy.start()
    return copy


def router_of(table, experts):
    return table[2 : 2 + experts, :].astype(BF16)


def routes_of(table, experts, tokens):
    lines = table[2 + experts : 2 + experts + tokens // LANES, :LANES]
    lines = jnp.concatenate([lines, jnp.zeros((LANES - lines.shape[0], LANES), F32)], axis=0).T
    return jnp.concatenate([lines[:, n : n + 1] for n in range(tokens // LANES)], axis=0)


def fetch(sources, targets, sems):
    copies = [pltpu.make_async_copy(a, b, sems.at[n]) for n, (a, b) in enumerate(zip(sources, targets, strict=True))]
    for copy in copies:
        copy.start()
    return copies


def meet(peers):
    barrier = pltpu.get_barrier_semaphore()
    for where in peers:
        pl.semaphore_signal(barrier, inc=1, device_id=where, device_id_type=MESH)
    pl.semaphore_wait(barrier, len(peers))


def line_peers(parts):
    total, me = lax.axis_size("seq"), lax.axis_index("seq")
    return [{"seq": lax.rem(me + parts, total)}, {"seq": lax.rem(me - parts + total, total)}]


def line_round(parts, up, down, sems):
    me = lax.axis_index("seq")
    z = lax.div(me, parts)

    def copy(n, src, dst, step):
        return pltpu.make_async_remote_copy(
            src, dst, sems.at[0, n], sems.at[1, n], device_id={"seq": me + step}, device_id_type=MESH
        )

    legs = [(0, *up, parts), (1, *down, -parts)]

    def start():
        for n, low, high, src, dst, step in legs:

            @pl.when(jnp.logical_and(z >= low, z <= high))
            def _():
                copy(n, src, dst, step).start()

    def end():
        for n, low, high, src, dst, step in legs:
            move = 1 if step > 0 else -1

            @pl.when(jnp.logical_and(z >= low, z <= high))
            def _():
                copy(n, src, dst, step).wait_send()

            @pl.when(jnp.logical_and(z >= low + move, z <= high + move))
            def _():
                copy(n, src, dst, -step).wait_recv()

    return start, end


def pass_on(parts, up, down, sems):
    start, end = line_round(parts, up, down, sems)
    start()
    return end


def far_first(total):
    return sorted(range(1, total), key=lambda k: -min(k, total - k))


def twist(a, b, total):
    out, bit = 0, 1
    while bit < total:
        out = out + lax.rem(lax.div(a, bit) + lax.div(b, bit), 2) * bit
        bit *= 2
    return out


def attend_kernel(seqs, meets, next_steps, *refs):
    refs = list(refs)
    qkv_ref, bias_ref = refs[:2]
    line_ref = refs.pop(2) if seqs else None
    out_ref, home_ref, exp_ref, inv_ref = refs[2:6]
    line_outs = [refs.pop(6) for _ in range(2)] if seqs else []
    strip, keys, scores, held, send, recv, local, exp_sems, *line_sems = refs[6:]
    _, heads, size, length = qkv_ref.shape
    total = lax.axis_size("seq")
    me = lax.axis_index("seq")
    tokens = out_ref.shape[3]
    width = 2 * tokens
    pairs = total // 2
    rows = 2 * length - tokens
    chunk = 256
    if meets:
        meet([{"seq": lax.rem(me + k, total)} for k in range(1, total)])
    if seqs:
        before, after = line_outs
        line_end = pass_on(
            total // seqs, (0, seqs - 2, line_ref.at[0], before), (1, seqs - 1, line_ref.at[0], after), line_sems[0]
        )

    def prepare(h, carry):
        keys[h] = qkv_ref[1, h].T
        for b in range(rows // tokens):
            start = 2 * length - 2 * tokens - tokens * b
            base = jnp.broadcast_to(bias_ref[h, :, start : start + 2 * tokens], (tokens, 2 * tokens))
            rolled = pltpu.roll(base, 0, 1, stride=1, stride_axis=0)
            strip[h, tokens * b : tokens * (b + 1), :] = rolled[:, tokens:]
        return carry

    lax.fori_loop(0, heads, prepare, 0)

    def store(slot, pair, h):
        return pltpu.make_async_copy(held.at[slot], exp_ref.at[pair, h], exp_sems.at[slot])

    def step(t, carry):
        pair = twist(lax.div(me, 2), pairs - 1 - t, pairs)
        at = pl.ds(pl.multiple_of(pair * width, tokens), width)
        if seqs:

            @pl.when(t == pairs - 1)
            def _():
                line_end()
                for start in next_steps:
                    start()

        def head(h, carry):
            count = t * heads + h
            slot = lax.rem(count, 2)

            @pl.when(count >= 2)
            def _():
                store(slot, pair, h).wait()

            query = qkv_ref[0, h, :, at]
            tops = [jnp.full((1, tokens), -jnp.inf, F32)] * 2
            for c in range(length // chunk):
                part = contract(keys[h, c * chunk : (c + 1) * chunk, :], query, 1, 0)
                for s in range(2):
                    row = pl.multiple_of(length - tokens - (pair * width + s * tokens) + c * chunk, tokens)
                    piece = part[:, s * tokens : (s + 1) * tokens] + strip[h, pl.ds(row, chunk), :]
                    scores[c * chunk : (c + 1) * chunk, s * tokens : (s + 1) * tokens] = piece
                    tops[s] = jnp.maximum(tops[s], jnp.max(piece, axis=0, keepdims=True))
            sums = [jnp.zeros((1, tokens), F32)] * 2
            for c in range(length // chunk):
                for s in range(2):
                    piece = scores[c * chunk : (c + 1) * chunk, s * tokens : (s + 1) * tokens]
                    grown = jnp.exp(piece - tops[s])
                    sums[s] = sums[s] + jnp.sum(grown, axis=0, keepdims=True)
                    held[slot, c * chunk : (c + 1) * chunk, s * tokens : (s + 1) * tokens] = grown.astype(BF16)
            store(slot, pair, h).start()
            mixed = contract(qkv_ref[2, h], held[slot], 1, 0)
            for s in range(2):
                inverse = 1.0 / sums[s]
                inv_ref[pair, h, :, s * tokens : (s + 1) * tokens] = inverse
                out_ref[2 * pair + s, h] = (mixed[:, s * tokens : (s + 1) * tokens] * inverse).astype(BF16)
            return carry

        lax.fori_loop(0, heads, head, 0)
        for s in range(2):
            to = 2 * pair + s
            k = twist(me, to, total)

            @pl.when(to != me)
            def _():
                pltpu.make_async_remote_copy(
                    out_ref.at[to], home_ref.at[me], send.at[k], recv.at[k], device_id={"seq": to}, device_id_type=MESH
                ).start()

        return carry

    lax.fori_loop(0, pairs, step, 0)
    own = pltpu.make_async_copy(out_ref.at[me], home_ref.at[me], local)
    own.start()
    for slot in range(2):
        store(slot, 0, 0).wait()

    def settle(k, carry):
        source = twist(me, k, total)
        pltpu.make_async_remote_copy(
            out_ref.at[source], home_ref.at[source], send.at[k], recv.at[k], device_id={"seq": source}, device_id_type=MESH
        ).wait()
        return carry

    lax.fori_loop(1, total, settle, 0)
    own.wait()


def attend(qkv, bias_line, total):
    _, heads, size, length = qkv.shape
    vmem, hbm = pl.BlockSpec(memory_space=pltpu.VMEM), pl.BlockSpec(memory_space=pl.ANY)
    out_shape, scratch = attend_shapes(heads, size, length, total)
    return pl.pallas_call(
        functools.partial(attend_kernel, 0, True, None),
        in_specs=[vmem, vmem],
        out_specs=[vmem, vmem, hbm, vmem],
        out_shape=out_shape,
        scratch_shapes=scratch,
        compiler_params=pltpu.CompilerParams(collective_id=2, has_side_effects=True, vmem_limit_bytes=62 << 20),
        name="attend",
    )(qkv, bias_line)


def attend_shapes(heads, size, length, total):
    tokens = length // total
    out_shape = [
        jax.ShapeDtypeStruct((total, heads, size, tokens), BF16),
        jax.ShapeDtypeStruct((total, heads, size, tokens), BF16),
        jax.ShapeDtypeStruct((total // 2, heads, length, 2 * tokens), BF16),
        jax.ShapeDtypeStruct((total // 2, heads, 1, 2 * tokens), F32),
    ]
    scratch = [
        pltpu.VMEM((heads, 2 * length - tokens, tokens), F32),
        pltpu.VMEM((heads, length, size), BF16),
        pltpu.VMEM((length, 2 * tokens), F32),
        pltpu.VMEM((2, length, 2 * tokens), BF16),
        pltpu.SemaphoreType.DMA((total,)),
        pltpu.SemaphoreType.DMA((total,)),
        pltpu.SemaphoreType.DMA,
        pltpu.SemaphoreType.DMA((2,)),
    ]
    return out_shape, scratch


def attend_back_kernel(fast, *refs):
    refs = list(refs)
    exp_ref, inv_ref, weight_in, out_in, qkv_in, hot_ref = refs[:6]
    weight_ref, out_ref, qkv_ref, *late_sems = refs[-4:]
    refs = refs[:-4]
    late = fetch((weight_in, out_in, qkv_in), (weight_ref, out_ref, qkv_ref), late_sems[0])
    if fast:
        *soon, params_ref = refs[6:13]
        line_refs, far_refs = refs[13:15], refs[15:19]
        *held_refs, soon_sems = refs[-7:]
        soon = fetch(soon, held_refs, soon_sems)
        back_ref, slot_ref, middle_ref, normed_ref, cot_ref, att_ref = held_refs
        refs = refs[19:-7]
    else:
        branch_ref = refs[6]
        refs = refs[7:]
    three_ref, table_ref = refs[:2]
    if fast:
        early_out, output_ref, grad_middle_ref, tiny_ref = refs[2:6]
        line_outs, far_outs = refs[6:8], refs[8:12]
        refs = refs[12:]
    else:
        refs = refs[2:]
    leaving, got, strip, values, dq_all, dk_sum, dv_sum, scores, held, diagonal, send, recv, exp_sems = refs[:13]
    _, heads, size, length = qkv_ref.shape
    total = lax.axis_size("seq")
    me = lax.axis_index("seq")
    tokens = out_ref.shape[3]
    parts = weight_ref.shape[0]
    part = lax.rem(me, parts)
    width = 2 * tokens
    pairs = total // 2
    rows = 2 * length - tokens
    chunk = 256

    def pair_at(t):
        return twist(lax.div(me, 2), t, pairs)

    def load(count):
        slot = lax.rem(count, 2)
        at = exp_ref.at[pair_at(lax.div(count, heads)), lax.rem(count, heads)]
        return pltpu.make_async_copy(at, held.at[slot], exp_sems.at[slot])

    load(0).start()
    peers = [{"seq": lax.rem(me + k, total)} for k in range(1, total)]
    if fast:
        across, row = lax.axis_size("wide"), lax.axis_index("wide")
        other = twist(me, 1, total)
        peers += [{"wide": lax.rem(row + k, across)} for k in range(1, across)]
    meet(peers)
    if fast:
        branch_ref, early_ref, near, near_sum, wide_got, near_sems, wide_sems, line_sems, far_sems = refs[13:]
        seqs = early_ref.shape[0]

        def far_step(e):
            up, down = far_refs[e], far_refs[2 + e]
            return pass_on(
                parts, (seqs - 2, seqs - 2, up, far_outs[e]), (1, 1, down, far_outs[2 + e]), far_sems.at[e]
            )

        line_ends = [far_step(0)]

        def near_copy():
            return pltpu.make_async_remote_copy(
                early_ref.at[:, lax.rem(part + 1, parts)],
                near,
                near_sems.at[0],
                near_sems.at[1],
                device_id={"seq": other},
                device_id_type=MESH,
            )

        def wide_copy(k):
            to = lax.rem(row + k, across)
            return pltpu.make_async_remote_copy(
                near_sum.at[to],
                wide_got.at[k - 1],
                wide_sems.at[0, k - 1],
                wide_sems.at[1, k - 1],
                device_id={"wide": to},
                device_id_type=MESH,
            )

        for copy in soon:
            copy.wait()
        features = middle_ref.shape[1]
        found = contract(slot_ref[...], back_ref[...].reshape(slot_ref.shape[1], 2 * features), 1, 0)
        selected = found[:, :features]
        router = router_of(params_ref, 2 * across)
        logits = contract(normed_ref[...], router, 1, 1)
        grown = jnp.exp(logits - jnp.max(logits, axis=1, keepdims=True))
        probs = grown / jnp.sum(grown, axis=1, keepdims=True)
        routes = routes_of(params_ref, router.shape[0], probs.shape[0])
        picked = (routes == lax.broadcasted_iota(jnp.int32, probs.shape, 1).astype(F32)).astype(F32)
        gate = jnp.sum(probs * picked, axis=1, keepdims=True)
        upstream = cot_ref[...].astype(F32)
        middle = middle_ref[...]
        output_ref[...] = (middle + gate * selected).astype(BF16)
        grad_gate = jnp.sum(upstream * selected, axis=1, keepdims=True)
        grad_logits = (grad_gate * probs * (picked - gate)).astype(BF16)
        grad_normed = found[:, features:] + contract(grad_logits, router, 1, 0)
        inverse = inverse_rms(middle)
        gain_grad = jnp.sum(grad_normed * middle * inverse, axis=0, keepdims=True)
        grad_normed = grad_normed * params_ref[1:2, :]
        mean_inner = jnp.mean(middle * grad_normed, axis=-1, keepdims=True)
        grad_middle = upstream + inverse * grad_normed - middle * (inverse * inverse * inverse) * mean_inner
        grad_middle_ref[...] = grad_middle
        branch = grad_middle.astype(BF16)
        branch_ref[...] = branch.reshape(branch_ref.shape)

    for copy in late:
        copy.wait()

    def product(to):
        value = contract(weight_ref[lax.rem(to, parts)], branch_ref[lax.div(to, parts)], 1, 1)
        return value.astype(BF16).reshape(heads, size, tokens)

    def leave(k, carry):
        to = twist(me, k, total)
        leaving[to] = product(to)
        pltpu.make_async_remote_copy(
            leaving.at[to], got.at[me], send.at[k], recv.at[k], device_id={"seq": to}, device_id_type=MESH
        ).start()
        return carry

    lax.fori_loop(1, total, leave, 0)
    if fast:
        for e in range(line_refs[0].shape[0]):
            up, down = ((1, seqs - 2, line_refs[n].at[e], line_outs[n].at[e]) for n in range(2))
            line_ends.append(pass_on(parts, up, down, line_sems.at[e]))
        line_ends.append(far_step(1))
        attended = jnp.concatenate([att_ref[s] for s in range(seqs)], axis=1)
        early_ref[...] = contract(attended, branch, 1, 0).astype(BF16).reshape(early_ref.shape)
        near_copy().start()
        grad_router = contract(grad_logits, normed_ref[...], 0, 0)
        spare = tiny_ref.shape[0] - 2 - grad_router.shape[0]
        tiny_ref[...] = jnp.concatenate(
            [jnp.zeros((1, features), F32), gain_grad, grad_router, jnp.zeros((spare, features), F32)], axis=0
        )
    got[me] = product(me)

    def prepare(h, carry):
        values[h] = qkv_ref[2, h].T
        strip[h] = jnp.zeros(strip.shape[1:], F32)
        dk_sum[h] = jnp.zeros(dk_sum.shape[1:], F32)
        dv_sum[h] = jnp.zeros(dv_sum.shape[1:], F32)
        return carry

    lax.fori_loop(0, heads, prepare, 0)

    def arrive(k):
        source = twist(me, k, total)
        pltpu.make_async_remote_copy(
            leaving.at[source], got.at[source], send.at[k], recv.at[k], device_id={"seq": source}, device_id_type=MESH
        ).wait()

    def step(t, carry):
        pair = pair_at(t)
        at = pl.ds(pl.multiple_of(pair * width, tokens), width)

        @pl.when(t > 0)
        def _():
            arrive(2 * t)

        arrive(2 * t + 1)
        if fast:

            @pl.when(t == 1)
            def _():
                near_copy().wait()
                for n in range(seqs):
                    for a in range(across):
                        value = early_ref[n, part, a].astype(F32) + near[n, a].astype(F32)
                        near_sum[a, n] = value.astype(BF16)
                for k in range(1, across):
                    wide_copy(k).start()

            @pl.when(t == pairs - 1)
            def _():
                for k in range(1, across):
                    wide_copy(k).wait()
                for n in range(seqs):
                    value = near_sum[row, n].astype(F32)
                    for k in range(1, across):
                        value = value + wide_got[k - 1, n].astype(F32)
                    early_out[n] = value.astype(BF16)

        def head(h, carry):
            count = t * heads + h
            slot = lax.rem(count, 2)

            @pl.when(count + 1 < pairs * heads)
            def _():
                load(count + 1).start()

            grads, inner = [], []
            for s in range(2):
                inverse = inv_ref[pair, h, :, s * tokens : (s + 1) * tokens]
                scaled = got[2 * pair + s, h].astype(F32) * inverse
                inner.append(jnp.sum(scaled * out_ref[2 * pair + s, h].astype(F32), axis=0, keepdims=True))
                grads.append(scaled.astype(BF16))
            grad = jnp.concatenate(grads, axis=1)
            load(count).wait()
            for c in range(length // chunk):
                part_grad = contract(values[h, c * chunk : (c + 1) * chunk, :], grad, 1, 0)
                for s in range(2):
                    grown = held[slot, c * chunk : (c + 1) * chunk, s * tokens : (s + 1) * tokens].astype(F32)
                    slope = grown * (part_grad[:, s * tokens : (s + 1) * tokens] - inner[s])
                    line = pl.multiple_of(length - tokens - (pair * width + s * tokens) + c * chunk, tokens)
                    strip[h, pl.ds(line, chunk), :] += slope
                    scores[c * chunk : (c + 1) * chunk, s * tokens : (s + 1) * tokens] = slope.astype(BF16)
            dq_all[h, at, :] = contract(qkv_ref[1, h], scores[...], 1, 0).T.astype(BF16)
            dk_sum[h] += contract(scores[...], qkv_ref[0, h, :, at].T, 1, 0)
            dv_sum[h] += contract(held[slot], grad.T, 1, 0)
            return carry

        lax.fori_loop(0, heads, head, 0)
        return carry

    lax.fori_loop(0, pairs, step, 0)
    down = lax.broadcasted_iota(jnp.int32, (tokens, tokens), 0)
    over = lax.broadcasted_iota(jnp.int32, (tokens, tokens), 1)
    mirror = (down + over == tokens - 1).astype(F32)
    cols = heads * size
    for c in range(length // chunk):
        here = slice(c * chunk, (c + 1) * chunk)
        for n, ref in enumerate((dq_all, dk_sum, dv_sum)):
            joined = jnp.concatenate([ref[h, here, :].astype(F32) for h in range(heads)], axis=1)
            three_ref[here, n * cols : (n + 1) * cols] = joined.astype(BF16)

    def close(h, carry):
        diagonal[h] = jnp.zeros(diagonal.shape[1:], F32)
        for b in range(rows // tokens):
            flipped = lax.dot_general(
                strip[h, tokens * b : tokens * (b + 1), :],
                mirror,
                (((1,), (0,)), ((), ())),
                precision=lax.Precision.HIGHEST,
                preferred_element_type=F32,
            )
            spread_out = jnp.concatenate([flipped, jnp.zeros_like(flipped)], axis=1)
            rolled = pltpu.roll(spread_out, 0, 1, stride=1, stride_axis=0)
            diagonal[h, :, tokens * b : tokens * (b + 2)] += jnp.sum(rolled, axis=0, keepdims=True)
        return carry

    lax.fori_loop(0, heads, close, 0)
    sums = jnp.concatenate([diagonal[h] for h in range(heads)], axis=0)
    table = lax.dot_general(
        sums,
        hot_ref[...].astype(F32),
        (((1,), (1,)), ((), ())),
        precision=lax.Precision.HIGHEST,
        preferred_element_type=F32,
    )
    line = lax.broadcasted_iota(jnp.int32, (table_ref.shape[0], heads), 0)
    head_line = lax.broadcasted_iota(jnp.int32, (table_ref.shape[0], heads), 1) + part * heads
    table_ref[...] = lax.dot_general(
        (line == head_line).astype(F32),
        table,
        (((1,), (0,)), ((), ())),
        precision=lax.Precision.HIGHEST,
        preferred_element_type=F32,
    )
    if fast:
        for end in line_ends:
            end()


def attend_back(exps, inverse, weight, outs, qkv, hot, branch, more, line, far):
    _, heads, size, length = qkv.shape
    total, tokens = outs.shape[0], outs.shape[3]
    parts, cols, width = weight.shape
    vmem, hbm = pl.BlockSpec(memory_space=pltpu.VMEM), pl.BlockSpec(memory_space=pl.ANY)
    sems = pltpu.SemaphoreType.DMA
    out_shape = [
        jax.ShapeDtypeStruct((length, 3 * heads * size), BF16),
        jax.ShapeDtypeStruct((16, hot.shape[0]), F32),
    ]
    given, scratch = [branch], []
    if branch is None:
        given = more
        across = lax.axis_size("wide")
        slim = width // total // across
        seqs = total // parts
        count = seqs * tokens
        out_shape += [
            jax.ShapeDtypeStruct((seqs, slim, width), BF16),
            jax.ShapeDtypeStruct((count, width), BF16),
            jax.ShapeDtypeStruct((count, width), F32),
            jax.ShapeDtypeStruct((16, width), F32),
        ]
        scratch = [
            pltpu.VMEM((seqs, tokens, width), BF16),
            pltpu.VMEM((seqs, parts, across, slim, width), BF16),
            pltpu.VMEM((seqs, across, slim, width), BF16),
            pltpu.VMEM((across, seqs, slim, width), BF16),
            pltpu.VMEM((across - 1, seqs, slim, width), BF16),
            sems((2,)),
            sems((2, across - 1)),
            sems((line[0].shape[0], 2, 2)),
            sems((len(far) // 2, 2, 2)),
        ]
    passed = [*line, *far]
    held = [pltpu.VMEM(a.shape, a.dtype) for a in more[:6]] + [sems((6,))] if branch is None else []
    spaces = [hbm] * 6 + [vmem] if branch is None else [vmem]
    in_place = len(out_shape)
    out_shape += [jax.ShapeDtypeStruct(rows.shape, BF16) for rows in passed]
    return pl.pallas_call(
        functools.partial(attend_back_kernel, branch is None),
        in_specs=[hbm, vmem, hbm, hbm, hbm, vmem] + spaces + [hbm] * len(passed),
        out_specs=[vmem] * in_place + [hbm] * len(passed),
        out_shape=out_shape,
        scratch_shapes=[
            pltpu.VMEM((total, heads, size, tokens), BF16),
            pltpu.VMEM((total, heads, size, tokens), BF16),
            pltpu.VMEM((heads, 2 * length - tokens, tokens), F32),
            pltpu.VMEM((heads, length, size), BF16),
            pltpu.VMEM((heads, length, size), BF16),
            pltpu.VMEM((heads, length, size), F32),
            pltpu.VMEM((heads, length, size), F32),
            pltpu.VMEM((length, 2 * tokens), BF16),
            pltpu.VMEM((2, length, 2 * tokens), BF16),
            pltpu.VMEM((heads, 1, 2 * length), F32),
            sems((total,)),
            sems((total,)),
            sems((2,)),
            *scratch,
            *held,
            *[pltpu.VMEM(a.shape, a.dtype) for a in (weight, outs, qkv)],
            sems((3,)),
        ],
        compiler_params=pltpu.CompilerParams(collective_id=3, has_side_effects=True, vmem_limit_bytes=62 << 20),
        cost_estimate=pl.CostEstimate(
            flops=8 * heads * length * length * size, bytes_accessed=2 * heads * length * length, transcendentals=0
        ),
        name="attend_back",
    )(exps, inverse, weight, outs, qkv, hot, *given, *passed)


def activation(v):
    square = v * v
    bent = jnp.tanh(0.7978845608 * v * (1.0 + 0.044715 * square))
    half = 0.5 * (1.0 + bent)
    slope = half + 0.5 * v * (1.0 - bent * bent) * (0.7978845608 * (1.0 + 3.0 * 0.044715 * square))
    return v * half, slope


def gated(rows, cots, router, expert):
    logits = contract(rows, router, 1, 1)
    grown = jnp.exp(logits - jnp.max(logits, axis=1, keepdims=True))
    named = lax.broadcasted_iota(jnp.int32, grown.shape, 1) == expert
    gate = jnp.sum(jnp.where(named, grown, 0.0), axis=1, keepdims=True) / jnp.sum(grown, axis=1, keepdims=True)
    return (gate * cots.astype(F32)).astype(BF16)


def expert_kernel(expert, rows_ref, cot_ref, router_ref, in_ref, out_ref, both_ref, forward, backward):
    step = pl.program_id(0)
    width = cot_ref.shape[1]

    @pl.when(step == 0)
    def _():
        forward[...] = jnp.zeros_like(forward)
        backward[...] = jnp.zeros_like(backward)

    rows = rows_ref[...]
    own = router_ref.shape[0] // lax.axis_size("wide")
    grads = gated(rows, cot_ref[...], router_ref[...], lax.axis_index("wide") * own + expert)
    hidden, slope = activation(contract(rows, in_ref[0], 1, 0))
    grad_hidden = contract(grads, out_ref[0], 1, 1).astype(BF16).astype(F32)
    forward[...] += contract(hidden.astype(BF16), out_ref[0], 1, 0)
    backward[...] += contract((grad_hidden * slope).astype(BF16), in_ref[0], 1, 1)

    @pl.when(step == pl.num_programs(0) - 1)
    def _():
        both_ref[:, :width] = forward[...].astype(BF16)
        both_ref[:, width:] = backward[...].astype(BF16)


def run_expert(rows, cots, router, w_in, w_out, expert, block):
    count, width = cots.shape
    units = w_in.shape[2]
    return pl.pallas_call(
        functools.partial(expert_kernel, expert),
        grid=(units // block,),
        in_specs=[
            pl.BlockSpec(rows.shape, lambda f: (0, 0)),
            pl.BlockSpec(cots.shape, lambda f: (0, 0)),
            pl.BlockSpec(router.shape, lambda f: (0, 0)),
            pl.BlockSpec((1, width, block), lambda f: (expert, 0, f)),
            pl.BlockSpec((1, block, width), lambda f: (expert, f, 0)),
        ],
        out_specs=pl.BlockSpec((count, 2 * width), lambda f: (0, 0)),
        out_shape=jax.ShapeDtypeStruct((count, 2 * width), BF16),
        scratch_shapes=[pltpu.VMEM((count, width), F32), pltpu.VMEM((count, width), F32)],
        compiler_params=pltpu.CompilerParams(vmem_limit_bytes=40 << 20),
        name="expert",
    )(rows, cots, router, w_in, w_out)


def forward_kernel(
    capacity,
    block,
    qkv_ref,
    bias_ref,
    weight_in,
    tokens_in,
    hot_ref,
    cot_ref,
    table_ref,
    in_ref,
    out_ref,
    outs_ref,
    att_ref,
    exp_ref,
    inv_ref,
    before_ref,
    after_ref,
    middle_ref,
    normed_ref,
    rows_ref,
    back_ref,
    second_before,
    second_after,
    next_before,
    next_after,
    last_before,
    last_after,
    line_before,
    line_after,
    weight_ref,
    home_ref,
    fetch_sems,
    packed,
    done,
    grads,
    forward,
    backward,
    in_held,
    out_held,
    send,
    recv,
    back_send,
    back_recv,
    local,
    held_sems,
    line_sems,
    *attend_scratch,
):
    own, count, width = rows_ref.shape
    across = lax.axis_size("wide")
    total, heads, size, tokens = att_ref.shape
    parts = width // (heads * size)
    seqs = total // parts
    me = lax.axis_index("wide")
    steps = in_ref.shape[2] // block

    def load(at):
        slot = lax.rem(at, 2)
        expert, place = lax.div(at, steps), pl.multiple_of(lax.rem(at, steps) * block, block)
        return (
            pltpu.make_async_copy(in_ref.at[expert, :, pl.ds(place, block)], in_held.at[slot], held_sems.at[0, slot]),
            pltpu.make_async_copy(out_ref.at[expert, pl.ds(place, block), :], out_held.at[slot], held_sems.at[1, slot]),
        )

    held = fetch((weight_in, tokens_in), (weight_ref, home_ref), fetch_sems)
    for copy in load(0):
        copy.start()
    next_start, first_end = line_round(
        parts, (0, seqs - 2, cot_ref.at[1], next_before), (1, seqs - 1, cot_ref.at[1], next_after), line_sems.at[0]
    )
    second_start, second_end = line_round(
        parts, (1, seqs - 2, before_ref, second_before), (1, seqs - 2, after_ref, second_after), line_sems.at[1]
    )
    attend_kernel(
        seqs,
        False,
        [next_start, second_start],
        qkv_ref,
        bias_ref,
        cot_ref,
        outs_ref,
        att_ref,
        exp_ref,
        inv_ref,
        before_ref,
        after_ref,
        *attend_scratch,
    )
    line_ends = [second_end]
    for copy in held:
        copy.wait()
    attended = [att_ref[parts * s : parts * (s + 1)].reshape(width, tokens) for s in range(seqs)]
    attended = jnp.concatenate(attended, axis=1)
    middle = home_ref[...].astype(F32) + contract(attended, weight_ref[...], 0, 0)
    middle_ref[...] = middle
    normed = (middle * inverse_rms(middle) * table_ref[1:2, :]).astype(BF16)
    normed_ref[...] = normed
    packed[...] = contract(hot_ref[...], normed, 0, 0).astype(BF16).reshape(packed.shape)
    going, kept = [], []
    mine = pl.ds(me * capacity, capacity)
    for n in range(own):
        for k in range(1, across):
            to = lax.rem(me + k, across)
            going.append(
                remote(
                    packed.at[n, pl.ds(to * capacity, capacity)],
                    rows_ref.at[n, mine],
                    send.at[n, k - 1],
                    recv.at[n, k - 1],
                    {"wide": to},
                )
            )
        kept.append(pltpu.make_async_copy(packed.at[n, mine], rows_ref.at[n, mine], local.at[n]))
        kept[n].start()
    first_end()
    line_ends.append(
        pass_on(parts, (1, seqs - 2, next_before, last_before), (1, seqs - 2, next_after, last_after), line_sems.at[2])
    )
    coming = []
    for e in range(own):
        for copy in going[e * (across - 1) : (e + 1) * (across - 1)] + [kept[e]]:
            copy.wait()
        line_ends.append(
            pass_on(
                parts,
                (0, seqs - 2, rows_ref.at[e], line_before.at[e]),
                (1, seqs - 1, rows_ref.at[e], line_after.at[e]),
                line_sems.at[3 + e],
            )
        )
        grads[...] = gated(rows_ref[e], cot_ref[e], router_of(table_ref, own * across), me * own + e)
        forward[...] = jnp.zeros_like(forward)
        backward[...] = jnp.zeros_like(backward)

        def step(f, carry):
            at = e * steps + f
            slot = lax.rem(at, 2)

            @pl.when(at + 1 < own * steps)
            def _():
                for copy in load(at + 1):
                    copy.start()

            for copy in load(at):
                copy.wait()
            hidden, slope = activation(contract(rows_ref[e], in_held[slot], 1, 0))
            grad_hidden = contract(grads[...], out_held[slot], 1, 1).astype(BF16).astype(F32)
            forward[...] += contract(hidden.astype(BF16), out_held[slot], 1, 0)
            backward[...] += contract((grad_hidden * slope).astype(BF16), in_held[slot], 1, 1)
            return carry

        lax.fori_loop(0, steps, step, 0)
        done[e, :, :width] = forward[...].astype(BF16)
        done[e, :, width:] = backward[...].astype(BF16)
        for k in range(1, across):
            to = lax.rem(me + k, across)
            coming.append(
                remote(
                    done.at[e, pl.ds(to * capacity, capacity)],
                    back_ref.at[e, mine],
                    back_send.at[e, k - 1],
                    back_recv.at[e, k - 1],
                    {"wide": to},
                )
            )
        coming.append(pltpu.make_async_copy(done.at[e, mine], back_ref.at[e, mine], local.at[own + e]))
        coming[-1].start()
    for copy in coming:
        copy.wait()
    for end in line_ends:
        end()


def both_kernel(capacity, block, experts, *refs):
    given, (bias, weight, tokens, w_in, w_out) = refs[:7], refs[7:12]
    made, found = refs[12:18], refs[18:36]
    kept, rest = refs[36:54], refs[54:]
    begin_kernel(capacity, experts, *given, *made, *kept)
    forward_kernel(
        capacity, block, kept[1], bias, weight, tokens, kept[3], made[4], given[5], w_in, w_out, *found, *rest
    )


def run_forward(
    blocks, w_query, w_key, w_value, cot, table, base, bias_line, weight, tokens_in, w_in, w_out, heads, size, capacity, block
):
    tokens, width = tokens_in.shape
    own, _, units = w_in.shape
    across, total = lax.axis_size("wide"), lax.axis_size("seq")
    count = across * capacity
    rows = blocks.shape[1]
    length = total * 2 * rows
    slots = own * count
    vmem, hbm = pl.BlockSpec(memory_space=pltpu.VMEM), pl.BlockSpec(memory_space=pl.ANY)
    sems = pltpu.SemaphoreType.DMA
    attend_out, attend_scratch = attend_shapes(heads, size, length, total)
    one = jax.ShapeDtypeStruct((count, width), BF16)
    every = jax.ShapeDtypeStruct((own, count, width), BF16)
    first_out = [
        jax.ShapeDtypeStruct((total, 2, rows, width), BF16),
        jax.ShapeDtypeStruct((3, heads, size, length), BF16),
        jax.ShapeDtypeStruct((width, length), BF16),
        jax.ShapeDtypeStruct((tokens, slots), BF16),
        every,
        jax.ShapeDtypeStruct((3 * heads * size, width), BF16),
    ]
    first_scratch = [
        *[pltpu.VMEM(first_out[n].shape, BF16) for n in (0, 1, 2, 3, 5)],
        *[pltpu.VMEM((width, width), BF16)] * 3,
        pltpu.VMEM((tokens, width), BF16),
        sems((6 + 3 * total // 2,)),
        pltpu.VMEM(every.shape, BF16),
        *[sems((total,))] * 4,
        *[sems((own, across - 1))] * 2,
        sems((2 + own,)),
    ]
    return pl.pallas_call(
        functools.partial(both_kernel, capacity, block, own * across),
        in_specs=[hbm] * 5 + [vmem] * 3 + [hbm] * 4,
        out_specs=[hbm] * 4 + [vmem, hbm] + [vmem, vmem, hbm, vmem, hbm, hbm] + [vmem] * 4 + [hbm] * 8,
        out_shape=[
            *first_out,
            *attend_out,
            *[one] * 2,
            jax.ShapeDtypeStruct((tokens, width), F32),
            jax.ShapeDtypeStruct((tokens, width), BF16),
            every,
            jax.ShapeDtypeStruct((own, count, 2 * width), BF16),
            *[one] * 6,
            *[every] * 2,
        ],
        scratch_shapes=[
            *first_scratch,
            pltpu.VMEM(weight.shape, BF16),
            pltpu.VMEM(tokens_in.shape, BF16),
            sems((2,)),
            pltpu.VMEM(every.shape, BF16),
            pltpu.VMEM((own, count, 2 * width), BF16),
            pltpu.VMEM((count, width), BF16),
            pltpu.VMEM((count, width), F32),
            pltpu.VMEM((count, width), F32),
            pltpu.VMEM((2, width, block), BF16),
            pltpu.VMEM((2, block, width), BF16),
            sems((own, across - 1)),
            sems((own, across - 1)),
            sems((own, across - 1)),
            sems((own, across - 1)),
            sems((2 * own,)),
            sems((2, 2)),
            sems((3 + own, 2, 2)),
            *attend_scratch,
            sems((2, 2)),
        ],
        compiler_params=pltpu.CompilerParams(collective_id=5, has_side_effects=True, vmem_limit_bytes=62 << 20),
        cost_estimate=pl.CostEstimate(
            flops=8 * own * count * width * units, bytes_accessed=4 * own * width * units, transcendentals=own * count * units
        ),
        name="forward",
    )(blocks, w_query, w_key, w_value, cot, table, base, bias_line, weight, tokens_in, w_in, w_out)


def share_kernel(expert, share_ref, rows_ref, cot_ref, router_ref, in_ref, out_ref, *refs):
    grad_in_ref, grad_out_ref, flipped, total_in = refs[-4:]
    step = pl.program_id(0)

    @pl.when(step == 0)
    def _():
        flipped[...] = in_ref[0].T
        total_in[...] = jnp.zeros_like(total_in)
        grad_out_ref[...] = jnp.zeros_like(grad_out_ref)

    rows = rows_ref[0]
    own = router_ref.shape[0] // lax.axis_size("wide")
    grads = gated(rows, cot_ref[0], router_ref[...], lax.axis_index("wide") * own + expert)
    hidden, slope = activation(contract(flipped[...], rows, 1, 1))
    grad_hidden = contract(out_ref[0], grads, 1, 1).astype(BF16).astype(F32)
    grad_out_ref[0] += contract(hidden.astype(BF16), grads, 1, 0)
    total_in[...] += contract((grad_hidden * slope).astype(BF16), rows, 1, 0)

    @pl.when(step == pl.num_programs(0) - 1)
    def _():
        grad_in_ref[0] = total_in[...].T


def run_share(me, rows, cots, router, w_in, w_out, expert, held):
    own, width, units = w_in.shape
    sources, count = rows.shape[0] // own, rows.shape[1]
    share = units // sources
    if share % LANES == 0:
        where = jnp.full((1,), me, jnp.int32)
        in_spec = pl.BlockSpec((1, width, share), lambda r, at: (expert, 0, at[0]))
        out_spec = pl.BlockSpec((1, share, width), lambda r, at: (expert, at[0], 0))
    else:
        where = jnp.zeros((1,), jnp.int32)
        w_in = lax.dynamic_slice(w_in, (0, 0, me * share), (own, width, share))
        w_out = lax.dynamic_slice(w_out, (0, me * share, 0), (own, share, width))
        in_spec = pl.BlockSpec((1, width, share), lambda r, at: (expert, 0, 0))
        out_spec = pl.BlockSpec((1, share, width), lambda r, at: (expert, 0, 0))
    held_specs = [pl.BlockSpec(memory_space=pl.ANY)] * len(held)
    return pl.pallas_call(
        functools.partial(share_kernel, expert),
        grid_spec=pltpu.PrefetchScalarGridSpec(
            num_scalar_prefetch=1,
            grid=(sources,),
            in_specs=[
                pl.BlockSpec((1, count, rows.shape[2]), lambda r, at: (own * r + expert, 0, 0)),
                pl.BlockSpec((1, count, width), lambda r, at: (own * r + expert, 0, 0)),
                pl.BlockSpec(router.shape, lambda r, at: (0, 0)),
                in_spec,
                out_spec,
                *held_specs,
            ],
            out_specs=[
                pl.BlockSpec((1, width, share), lambda r, at: (expert, 0, 0)),
                pl.BlockSpec((1, share, width), lambda r, at: (expert, 0, 0)),
            ],
            scratch_shapes=[pltpu.VMEM((share, width), BF16), pltpu.VMEM((share, width), F32)],
        ),
        out_shape=[
            jax.ShapeDtypeStruct((own, width, share), F32),
            jax.ShapeDtypeStruct((own, share, width), F32),
        ],
        input_output_aliases={6 + i: i for i in range(len(held))},
        compiler_params=pltpu.CompilerParams(vmem_limit_bytes=62 << 20),
        cost_estimate=pl.CostEstimate(
            flops=8 * sources * count * width * share, bytes_accessed=4 * sources * count * width, transcendentals=0
        ),
        name="share",
    )(where, rows, cots, router, w_in, w_out, *held)


def spread_kernel(parts, in_ref, out_ref, send, recv, pass_send, pass_recv, local):
    total = lax.axis_size("seq")
    me = lax.axis_index("seq")
    part = lax.rem(me, parts)
    meet([{"seq": lax.rem(me + k, total)} for k in range(1, total)])
    copies = []
    for k in far_first(total):
        to = lax.rem(me + k, total)
        copies.append(remote(in_ref.at[to], out_ref.at[me, lax.rem(to, parts)], send.at[k - 1], recv.at[k - 1], {"seq": to}))
    own = pltpu.make_async_copy(in_ref.at[me], out_ref.at[me, part], local)
    own.start()
    own.wait()
    passed = []

    def forward(source, k):
        for j in range(1, parts):
            to = me - part + lax.rem(part + j, parts)
            at = (j - 1) * total + k
            block = out_ref.at[source, part]
            passed.append(remote(block, block, pass_send.at[at], pass_recv.at[at], {"seq": to}))

    forward(me, 0)
    for k in far_first(total)[::-1]:
        source = lax.rem(me - k + total, total)
        block = out_ref.at[source, part]
        pltpu.make_async_remote_copy(
            block, block, send.at[k - 1], recv.at[k - 1], device_id={"seq": source}, device_id_type=MESH
        ).wait_recv()
        forward(source, k)
    for copy in copies:
        copy.wait_send()
    for copy in passed:
        copy.wait()


def spread(blocks, parts):
    total, rows, width = blocks.shape
    passes = (parts - 1) * total
    return pl.pallas_call(
        functools.partial(spread_kernel, parts),
        in_specs=[pl.BlockSpec(memory_space=pl.ANY)],
        out_specs=pl.BlockSpec(memory_space=pl.ANY),
        out_shape=jax.ShapeDtypeStruct((total, parts, rows, width), blocks.dtype),
        scratch_shapes=[
            pltpu.SemaphoreType.DMA((total - 1,)),
            pltpu.SemaphoreType.DMA((total - 1,)),
            pltpu.SemaphoreType.DMA((passes,)),
            pltpu.SemaphoreType.DMA((passes,)),
            pltpu.SemaphoreType.DMA,
        ],
        compiler_params=pltpu.CompilerParams(collective_id=0, has_side_effects=True),
        name="spread",
    )(blocks)


def begin_kernel(
    capacity,
    experts,
    in_ref,
    query_in,
    key_in,
    value_in,
    cot_in,
    table_ref,
    base_ref,
    all_out,
    qkv_out,
    flip_out,
    hot_out,
    rows_ref,
    weights_out,
    all_ref,
    qkv_ref,
    flip_ref,
    hot_ref,
    weights,
    query_ref,
    key_ref,
    value_ref,
    cot_ref,
    fetch_sems,
    packed,
    send,
    recv,
    pass_send,
    pass_recv,
    wide_send,
    wide_recv,
    local,
):
    total, parts, rows, width = all_ref.shape
    _, heads, size, length = qkv_ref.shape
    own = rows_ref.shape[0]
    cols = heads * size
    across = lax.axis_size("wide")
    me, row = lax.axis_index("seq"), lax.axis_index("wide")
    part = lax.rem(me, parts)
    other = twist(me, 1, total)
    pairs = total // 2
    held = fetch((cot_in, query_in, key_in, value_in), (cot_ref, query_ref, key_ref, value_ref), fetch_sems)
    peers = [{"seq": lax.rem(me + k, total)} for k in range(1, total)]
    peers += [{"wide": lax.rem(row + k, across)} for k in range(1, across)]
    meet(peers)
    sent = []
    for k in range(1, total):
        to = twist(me, k, total)
        sent.append(remote(in_ref.at[to], all_ref.at[me, lax.rem(to, parts)], send.at[to], recv.at[me], {"seq": to}))
    kept = pltpu.make_async_copy(in_ref.at[me], all_ref.at[me, part], local.at[0])
    kept.start()
    kept.wait()
    passed = []

    def forward(source):
        block = all_ref.at[source, part]
        passed.append(remote(block, block, pass_send.at[source], pass_recv.at[source], {"seq": other}))

    def await_recv(block, sem):
        pltpu.make_async_remote_copy(
            block, block, local.at[1], sem, device_id={"seq": other}, device_id_type=MESH
        ).wait_recv()

    forward(me)

    tokens, slots = hot_ref.shape
    routes = routes_of(table_ref, experts, tokens)
    picked = (routes == lax.broadcasted_iota(jnp.int32, (tokens, LANES), 1).astype(F32)).astype(F32)
    down = lax.broadcasted_iota(jnp.int32, (tokens, tokens), 0)
    over = lax.broadcasted_iota(jnp.int32, (tokens, tokens), 1)
    earlier = contract((over < down).astype(F32).astype(BF16), picked.astype(BF16), 1, 0)
    rank = jnp.sum(earlier * picked, axis=1, keepdims=True)
    place = jnp.sum(base_ref[...] * picked, axis=1, keepdims=True) + rank
    place = jnp.where(rank < capacity, place, float(slots)).astype(jnp.int32)
    hot = (place == lax.broadcasted_iota(jnp.int32, (tokens, slots), 1)).astype(F32).astype(BF16)
    hot_ref[...] = hot
    held[0].wait()
    stored = [pltpu.make_async_copy(hot_ref, hot_out, fetch_sems.at[4])]
    stored[0].start()
    packed[...] = contract(hot, cot_ref[...], 0, 0).astype(BF16).reshape(packed.shape)
    wide = []
    mine = pl.ds(row * capacity, capacity)
    for e in range(own):
        for k in range(1, across):
            to = lax.rem(row + k, across)
            wide.append(
                remote(
                    packed.at[e, pl.ds(to * capacity, capacity)],
                    rows_ref.at[e, mine],
                    wide_send.at[e, k - 1],
                    wide_recv.at[e, k - 1],
                    {"wide": to},
                )
            )
    stay = [pltpu.make_async_copy(packed.at[e, mine], rows_ref.at[e, mine], local.at[2 + e]) for e in range(own)]
    for copy in stay:
        copy.start()
    at = pl.ds(pl.multiple_of(part * cols, LANES), cols)
    for n, ref in enumerate((query_ref, key_ref, value_ref)):
        held[1 + n].wait()
        weights[n * cols : (n + 1) * cols, :] = ref[:, at].T
    stored.append(pltpu.make_async_copy(weights, weights_out, fetch_sems.at[5]))
    stored[1].start()

    for t in range(pairs):
        pair = twist(lax.div(me, 2), t, pairs)
        for b in range(2):
            if 2 * t + b:
                source = twist(me, 2 * t + b, total)
                await_recv(all_ref.at[source, part], recv.at[source])
                forward(source)
        for b in range(2):
            source = 2 * pair + b
            await_recv(all_ref.at[source, lax.rem(part + 1, parts)], pass_recv.at[source])
        block = all_ref[pl.ds(2 * pair, 2)].reshape(2 * parts * rows, width).astype(F32)
        normed = (block * inverse_rms(block) * table_ref[0:1, :]).astype(BF16)
        here = pl.ds(pl.multiple_of(pair * (2 * parts * rows), LANES), 2 * parts * rows)
        flip_ref[:, here] = normed.T
        projected = contract(weights[...], normed, 1, 1).astype(BF16)
        qkv_ref[:, :, :, here] = projected.reshape(3, heads, size, 2 * parts * rows)
        both = pl.ds(2 * pair, 2)
        for n, (src, dst) in enumerate(
            (
                (all_ref.at[both], all_out.at[both]),
                (flip_ref.at[:, here], flip_out.at[:, here]),
                (qkv_ref.at[:, :, :, here], qkv_out.at[:, :, :, here]),
            )
        ):
            stored.append(pltpu.make_async_copy(src, dst, fetch_sems.at[6 + 3 * t + n]))
            stored[-1].start()
    for copy in sent + passed:
        copy.wait_send()
    for copy in wide + stay + stored:
        copy.wait()


def finish_kernel(
    seqs,
    three_ref,
    flip_ref,
    weight_ref,
    x_ref,
    early_ref,
    tiny_ref,
    table_ref,
    params_ref,
    *refs,
):
    own, steps = 2, 2 * seqs - 1
    inputs = (flip_ref, three_ref, weight_ref, x_ref)
    flip_ref, three_ref, weight_ref, x_ref, sems = refs[-5:]
    held = fetch(inputs, (flip_ref, three_ref, weight_ref, x_ref), sems)
    refs = refs[:-5]
    rows_refs = refs[: steps - 2]
    cots_refs = refs[steps - 2 : steps - 2 + 1 + own * (steps - 1)]
    finish_rest(
        seqs,
        held,
        rows_refs,
        cots_refs,
        three_ref,
        flip_ref,
        weight_ref,
        x_ref,
            early_ref,
        tiny_ref,
        table_ref,
        params_ref,
        *refs[len(rows_refs) + len(cots_refs) :],
    )


def finish_rest(
    seqs,
    held,
    rows_refs,
    cots_refs,
    three_ref,
    flip_ref,
    weight_ref,
    x_ref,
    early_ref,
    tiny_ref,
    table_ref,
    params_ref,
    in_ref,
    out_ref,
    home_ref,
    late_all,
    early_all,
    tiny,
    grad_in_ref,
    grad_out_ref,
    grads,
    near,
    summed,
    gw,
    wide_got,
    wide_sum,
    far_got,
    early_got,
    mine,
    early_mine,
    tiny_got,
    rows_held,
    cots_held,
    in_held,
    out_held,
    sums,
    total_in,
    leaving,
    share_got,
    share_sems,
    near_sems,
    home_sems,
    wide_sems,
    far_sems,
    early_sems,
    last_sems,
    last_early_sems,
    tiny_sems,
    held_sems,
    line_sems,
    local,
):
    total, across = lax.axis_size("seq"), lax.axis_size("wide")
    parts = total // seqs
    me, row = lax.axis_index("seq"), lax.axis_index("wide")
    part, seq = lax.rem(me, parts), lax.div(me, parts)
    other = twist(me, 1, total)
    width = params_ref.shape[1]
    slim = gw.shape[2]
    own = in_ref.shape[0]
    share = in_ref.shape[2] // total
    cols = three_ref.shape[1] // 3
    half = three_ref.shape[0] // 2

    def seq_at(k):
        return lax.rem(seq + k, seqs) * parts + part

    def row_at(k):
        return lax.rem(row + k, across)

    def part_at(k):
        return me - part + lax.rem(part + k, parts)

    at = pl.ds(pl.multiple_of(lax.div(me, 2) * (2 * share), LANES), 2 * share)
    weights = [
        pltpu.make_async_copy(in_ref.at[:, :, at], in_held, local.at[0]),
        pltpu.make_async_copy(out_ref.at[:, at, :], out_held, local.at[1]),
    ]
    for copy in weights:
        copy.start()

    def load_rows(e, n, k):
        return pltpu.make_async_copy(rows_refs[k].at[e], rows_held.at[e, n], held_sems.at[0, e, n])

    def load_cots(e, n, k):
        src = cots_refs[1 + own * (k - 1) + e] if k else cots_refs[0].at[e]
        return pltpu.make_async_copy(src, cots_held.at[e, n], held_sems.at[1, e, n])

    last_place = seqs - 1
    far_end = jnp.logical_or(seq == 0, seq == last_place)
    for e in range(own):
        load_rows(e, 0, 0).start()
        load_cots(e, 0, 0).start()
        for here in range(seqs):

            @pl.when(seq == here)
            def _():
                sources = [2 * k - 1 for k in range(1, here + 1)] + [2 * k for k in range(1, seqs - here)]
                for n, k in enumerate(sources):
                    load_cots(e, n + 1, k).start()
                    if k < len(rows_refs):
                        load_rows(e, n + 1, k).start()

    pairs = [(a, b) for a in range(across) for b in range(parts) if a or b]
    peers = [{"seq": lax.rem(me + k, total)} for k in range(1, total)]
    peers += [{"wide": row_at(k)} for k in range(1, across)]
    peers += [{"wide": row_at(a), "seq": part_at(b)} for a, b in pairs if a and b]
    meet(peers)

    def far_rows(e, up):
        src = rows_refs[3 if up else 4].at[e]
        to = lax.rem(me + (parts if up else total - parts), total)
        return pltpu.make_async_remote_copy(
            src, rows_held.at[e, last_place], line_sems.at[0, e], line_sems.at[1, e], device_id={"seq": to}, device_id_type=MESH
        )

    for e in range(own):

        @pl.when(seq == last_place - 1)
        def _():
            far_rows(e, True).start()

        @pl.when(seq == 1)
        def _():
            far_rows(e, False).start()

    for copy in held:
        copy.wait()
    late = contract(flip_ref[...], three_ref[...], 1, 0).astype(BF16)
    gw[...] = late.reshape(gw.shape)
    wide_copies = [
        remote(gw.at[:, row_at(k)], wide_got.at[k - 1], wide_sems.at[0, k - 1], wide_sems.at[1, k - 1], {"wide": row_at(k)})
        for k in range(1, across)
    ]

    gain = params_ref[0:1, :]
    gain_grad = jnp.zeros((1, width), F32)
    near_copies = []
    for n in range(2):
        scaled = contract(three_ref[n * half : (n + 1) * half, :], weight_ref[...], 1, 0)
        x = x_ref[n * total // 2 : (n + 1) * total // 2].reshape(half, width).astype(F32)
        inverse = inverse_rms(x)
        gain_grad = gain_grad + jnp.sum(scaled * x * inverse, axis=0, keepdims=True)
        scaled = scaled * gain
        mean_inner = jnp.mean(x * scaled, axis=-1, keepdims=True)
        value = inverse * scaled - x * (inverse * inverse * inverse) * mean_inner
        here = pl.ds(n * total // 2, total // 2)
        grads[here] = value.astype(BF16).reshape(total // 2, *grads.shape[1:])
        near_copies.append(
            remote(
                grads.at[here, lax.rem(part + 1, parts)],
                near.at[here],
                near_sems.at[0, n],
                near_sems.at[1, n],
                {"seq": other},
            )
        )
    lines = tiny_ref.shape[0]
    first = lax.broadcasted_iota(jnp.int32, tiny_ref.shape, 0) == 0
    tiny[:lines, :] = jnp.where(first, gain_grad, tiny_ref[...]).astype(BF16)
    table = table_ref[...]
    tiny[lines:, :] = jnp.concatenate([table, jnp.zeros((table.shape[0], width - table.shape[1]), F32)], axis=1).astype(BF16)

    def pass_tiny(stage, wheres):
        return [
            remote(tiny, tiny_got.at[stage, n], tiny_sems.at[0, stage, n], tiny_sems.at[1, stage, n], where)
            for n, where in enumerate(wheres)
        ]

    def take_tiny(stage, copies):
        for copy in copies:
            copy.wait()
        value = tiny[...].astype(F32)
        for n in range(len(copies)):
            value = value + tiny_got[stage, n].astype(F32)
        tiny[...] = value.astype(BF16)

    tiny_copies = pass_tiny(0, [{"wide": row_at(k)} for k in range(1, across)])
    for copy in near_copies:
        copy.wait()
    home_copies = []
    for k in range(total - 1, -1, -1):
        to = twist(me, k, total)
        summed[to] = (grads[to, part].astype(F32) + near[to].astype(F32)).astype(BF16)
        if k:
            home_copies.append(
                remote(summed.at[to], home_ref.at[me], home_sems.at[0, k - 1], home_sems.at[1, k - 1], {"seq": to})
            )
    kept = pltpu.make_async_copy(summed.at[me], home_ref.at[me], local.at[2])
    kept.start()
    for copy in weights:
        copy.wait()

    mine_rows = pl.ds(pl.multiple_of(part * share, LANES), share)
    other_rows = pl.ds(pl.multiple_of((1 - part) * share, LANES), share)

    def share_turn(e, n):
        some = rows_held.shape[1] // 2
        for m in range(n * some, (n + 1) * some):
            load_cots(e, m, 0).wait()
            if m < last_place:
                load_rows(e, m, 0).wait()
            else:

                @pl.when(far_end)
                def _():
                    far_rows(e, True).wait_recv()

                @pl.when(jnp.logical_not(far_end))
                def _():
                    load_rows(e, m, 0).wait()

        count = some * rows_held.shape[2]
        here = slice(n * some, (n + 1) * some)
        rows = rows_held[e, here].reshape(count, width)
        cots = gated(rows, cots_held[e, here].reshape(count, width), router_of(params_ref, own * across), row * own + e)
        hidden, slope = activation(contract(in_held[e].T, rows, 1, 1))
        grad_hidden = contract(out_held[e], cots, 1, 1).astype(BF16).astype(F32)
        part_out = contract(hidden.astype(BF16), cots, 1, 0)
        part_in = contract((grad_hidden * slope).astype(BF16), rows, 1, 0)
        if n == 0:
            sums[e, 0] = part_out
            sums[e, 1] = part_in
            return []
        sums[e, 0] += part_out
        sums[e, 1] += part_in
        grad_out_ref[e] = sums[e, 0, mine_rows, :]
        total_in[e] = sums[e, 1, mine_rows, :]
        copies = []
        for k in range(2):
            leaving[e, k] = sums[e, k, other_rows, :].astype(BF16)
            copies.append(
                remote(leaving.at[e, k], share_got.at[e, k], share_sems.at[0, e, k], share_sems.at[1, e, k], {"seq": other})
            )
        return copies

    def share_end(e, copies):
        for copy in copies:
            copy.wait()
        grad_out_ref[e] += share_got[e, 0].astype(F32)
        grad_in_ref[e] = (total_in[e] + share_got[e, 1].astype(F32)).T

    share_turn(0, 0)
    share_turn(1, 0)
    take_tiny(0, tiny_copies)
    for copy in wide_copies:
        copy.wait_recv()
    far_copies = []
    for k in list(range(1, seqs)) + [0]:
        place = lax.rem(seq + k, seqs)
        for p in range(parts):
            block = place * parts + p
            value = gw[block, row].astype(F32)
            for j in range(across - 1):
                value = value + wide_got[j, block].astype(F32)
            wide_sum[place, p] = value.astype(BF16)
        if k:
            where = {"seq": seq_at(k)}
            far_copies.append(
                remote(wide_sum.at[place], far_got.at[k - 1], far_sems.at[0, k - 1], far_sems.at[1, k - 1], where)
            )
            far_copies.append(
                remote(early_ref.at[place], early_got.at[k - 1], early_sems.at[0, k - 1], early_sems.at[1, k - 1], where)
            )
    tiny_copies = pass_tiny(1, [{"seq": seq_at(k)} for k in range(1, seqs)])
    first_share = share_turn(0, 1)
    take_tiny(1, tiny_copies)
    for copy in far_copies:
        copy.wait_recv()
    for p in range(parts):
        value = wide_sum[seq, p].astype(F32)
        for j in range(seqs - 1):
            value = value + far_got[j, p].astype(F32)
        mine[p] = value.astype(BF16)
    value = early_ref[seq].astype(F32)
    for j in range(seqs - 1):
        value = value + early_got[j].astype(F32)
    early_mine[...] = value.astype(BF16)
    last = pass_tiny(2, [{"seq": part_at(k)} for k in range(1, parts)])
    count = len(last)
    for a, b in pairs:
        n = a * parts + b - 1
        last.append(
            remote(
                mine.at[lax.rem(part + b, parts)],
                late_all.at[row, part],
                last_sems.at[0, n],
                last_sems.at[1, n],
                {"wide": row_at(a), "seq": part_at(b)},
            )
        )
    for k in range(1, across):
        last.append(
            remote(
                early_mine, early_all.at[row], last_early_sems.at[0, k - 1], last_early_sems.at[1, k - 1], {"wide": row_at(k)}
            )
        )
    stay = [
        pltpu.make_async_copy(mine.at[part], late_all.at[row, part], local.at[3]),
        pltpu.make_async_copy(early_mine, early_all.at[row], local.at[4]),
    ]
    for copy in stay:
        copy.start()
    second_share = share_turn(1, 1)
    share_end(0, first_share)
    take_tiny(2, last[:count])
    share_end(1, second_share)
    for e in range(own):

        @pl.when(jnp.logical_or(seq == 1, seq == last_place - 1))
        def _():
            far_rows(e, True).wait_send()

    for copy in last[count:] + stay + home_copies + [kept]:
        copy.wait()
    for copy in wide_copies + far_copies:
        copy.wait_send()


def finish(three, flipped, weights, x, early, tiny, table, params, rows, cots, w_in, w_out):
    columns = three.shape[1]
    total, parts, piece, width = x.shape
    seqs, slim, _ = early.shape
    across = lax.axis_size("wide")
    own, _, units = w_in.shape
    share = units // total
    vmem, hbm = pl.BlockSpec(memory_space=pltpu.VMEM), pl.BlockSpec(memory_space=pl.ANY)
    sems = pltpu.SemaphoreType.DMA
    most = max(across, seqs, parts) - 1
    lines = tiny.shape[0] + table.shape[0]
    return pl.pallas_call(
        functools.partial(finish_kernel, seqs),
        in_specs=[hbm] * 4 + [vmem] * 4 + [hbm] * (len(rows) + len(cots) + 2),
        out_specs=[vmem] * 6,
        out_shape=[
            jax.ShapeDtypeStruct((total, piece, width), BF16),
            jax.ShapeDtypeStruct((across, parts, slim, columns), BF16),
            jax.ShapeDtypeStruct((across, slim, width), BF16),
            jax.ShapeDtypeStruct((lines, width), BF16),
            jax.ShapeDtypeStruct((own, width, share), F32),
            jax.ShapeDtypeStruct((own, share, width), F32),
        ],
        scratch_shapes=[
            pltpu.VMEM((total, parts, piece, width), BF16),
            pltpu.VMEM((total, piece, width), BF16),
            pltpu.VMEM((total, piece, width), BF16),
            pltpu.VMEM((total, across, slim, columns), BF16),
            pltpu.VMEM((across - 1, total, slim, columns), BF16),
            pltpu.VMEM((seqs, parts, slim, columns), BF16),
            pltpu.VMEM((seqs - 1, parts, slim, columns), BF16),
            pltpu.VMEM((seqs - 1, slim, width), BF16),
            pltpu.VMEM((parts, slim, columns), BF16),
            pltpu.VMEM((slim, width), BF16),
            pltpu.VMEM((3, most, lines, width), BF16),
            pltpu.VMEM((own, seqs, *rows[0].shape[1:]), BF16),
            pltpu.VMEM((own, seqs, *cots[0].shape[1:]), BF16),
            pltpu.VMEM((own, width, 2 * share), BF16),
            pltpu.VMEM((own, 2 * share, width), BF16),
            pltpu.VMEM((own, 2, 2 * share, width), F32),
            pltpu.VMEM((own, share, width), F32),
            pltpu.VMEM((own, 2, share, width), BF16),
            pltpu.VMEM((own, 2, share, width), BF16),
            sems((2, own, 2)),
            sems((2, 2)),
            sems((2, total - 1)),
            sems((2, across - 1)),
            sems((2, seqs - 1)),
            sems((2, seqs - 1)),
            sems((2, across * parts - 1)),
            sems((2, across - 1)),
            sems((2, 3, most)),
            sems((2, own, seqs)),
            sems((2, own)),
            sems((5,)),
            *[pltpu.VMEM(a.shape, BF16) for a in (flipped, three, weights, x)],
            sems((4,)),
        ],
        compiler_params=pltpu.CompilerParams(collective_id=1, has_side_effects=True, vmem_limit_bytes=62 << 20),
        cost_estimate=pl.CostEstimate(flops=16 << 30, bytes_accessed=60 << 20, transcendentals=0),
        name="finish",
    )(three, flipped, weights, x, early, tiny, table, params, *rows, *cots, w_in, w_out)


def close_kernel(
    heads,
    home_ref,
    middle_ref,
    late_ref,
    early_ref,
    tiny_ref,
    in_ref,
    out_ref,
    result_ref,
    inputs_ref,
    query_ref,
    key_ref,
    value_ref,
    output_ref,
    gain_one_ref,
    gain_two_ref,
    router_ref,
    table_ref,
    grad_in_ref,
    grad_out_ref,
    result_out,
):
    grad_in_ref[...] = in_ref[...]
    grad_out_ref[...] = out_ref[...]
    result_out[...] = result_ref[...]
    inputs_ref[...] = middle_ref[...] + home_ref[...].reshape(middle_ref.shape).astype(F32)
    _, parts, _, columns = late_ref.shape
    cols = columns // 3
    for p in range(parts):
        for n, ref in enumerate((query_ref, key_ref, value_ref)):
            ref[:, p * cols : (p + 1) * cols] = late_ref[0, p, :, n * cols : (n + 1) * cols].astype(F32)
    output_ref[...] = early_ref[0].astype(F32)

    @pl.when(pl.program_id(0) == 0)
    def _():
        me = lax.axis_index("seq")
        width, piece = tiny_ref.shape[1], gain_one_ref.shape[1]
        chosen = lax.broadcasted_iota(jnp.int32, (width, piece), 0) == (
            lax.broadcasted_iota(jnp.int32, (width, piece), 1) + me * piece
        )
        picked = contract(tiny_ref[...], chosen.astype(F32).astype(BF16), 1, 0)
        gain_one_ref[...] = picked[0:1]
        gain_two_ref[...] = picked[1:2]
        router_ref[...] = picked[2 : 2 + router_ref.shape[0]]
        lines = table_ref.shape[0]
        chosen = lax.broadcasted_iota(jnp.int32, (lines, LANES), 1) == (
            lax.broadcasted_iota(jnp.int32, (lines, LANES), 0) + me * lines
        )
        table_ref[...] = contract(chosen.astype(F32).astype(BF16), tiny_ref[16:, :LANES], 1, 1)[:, :heads]


def close(home, middle, late, early, tiny, grad_in, grad_out, result, heads, buckets, experts):
    across, parts, slim, columns = late.shape
    width = early.shape[2]
    total, piece, _ = home.shape
    tokens = middle.shape[0]
    own, _, share = grad_in.shape
    halves = across // own
    rows = pl.BlockSpec((slim, width), lambda i: (i, 0))

    def whole(*shape):
        return pl.BlockSpec(shape, lambda i: (0,) * len(shape))

    some = pl.BlockSpec((tokens // across, width), lambda i: (i, 0))
    in_part = pl.BlockSpec((1, width // halves, share), lambda i: (i // halves, i % halves, 0))
    out_part = pl.BlockSpec((1, share // halves, width), lambda i: (i // halves, i % halves, 0))
    small = [(1, width // total), (1, width // total), (experts, width // total), (buckets // total, heads)]
    shapes = [middle.shape, *[(across * slim, width)] * 4, *small, grad_in.shape, grad_out.shape]
    return pl.pallas_call(
        functools.partial(close_kernel, heads),
        grid=(across,),
        in_specs=[
            pl.BlockSpec((total // across, piece, width), lambda i: (i, 0, 0)),
            some,
            pl.BlockSpec((1, parts, slim, columns), lambda i: (i, 0, 0, 0)),
            pl.BlockSpec((1, slim, width), lambda i: (i, 0, 0)),
            whole(*tiny.shape),
            in_part,
            out_part,
            some,
        ],
        out_specs=[some, rows, rows, rows, rows, *[whole(*shape) for shape in small], in_part, out_part, some],
        out_shape=[jax.ShapeDtypeStruct(shape, F32) for shape in shapes] + [jax.ShapeDtypeStruct(result.shape, BF16)],
        compiler_params=pltpu.CompilerParams(vmem_limit_bytes=62 << 20),
        name="close",
    )(home, middle, late, early, tiny, grad_in, grad_out, result)


def ring_pairs(total, parts, shift):
    return [(i, i - i % parts + (i % parts + shift) % parts) for i in range(total)]


def pick(pieces, index):
    out = pieces[0]
    for k in range(1, len(pieces)):
        out = jnp.where(index == k, pieces[k], out)
    return out


def swap_parts(pieces, part, parts, total):
    near = [pick(pieces, part)]
    for k in range(1, parts):
        near.append(lax.ppermute(pick(pieces, (part + k) % parts), "seq", ring_pairs(total, parts, k)))
    return [pick(near, (part - j) % parts) for j in range(parts)]


def per_device(
    inputs,
    routes,
    bucket_ids,
    gain_attn,
    w_query,
    w_key,
    w_value,
    w_output,
    rel_table,
    gain_ffn,
    w_router,
    w_in,
    w_out,
    cotangent,
):
    seqs, local_len, width = inputs.shape
    buckets, head_count = rel_table.shape
    size = width // head_count
    total = lax.axis_size("seq")
    across = lax.axis_size("wide")
    length = local_len * total
    parts = total // seqs
    heads = head_count // parts
    cols = heads * size
    me = lax.axis_index("seq")
    part = me % parts
    experts = w_router.shape[1]
    own_experts = w_in.shape[0]
    tokens = seqs * local_len
    capacity = (5 * tokens + 4 * experts - 1) // (4 * experts)
    slots = experts * capacity
    gain_one = gain_attn.astype(F32)
    gain_two = gain_ffn.astype(F32)

    fast = parts == 2 and capacity % 16 == 0 and own_experts == 2 and seqs == 4 and experts == 8 and across == 4 and cols % LANES == 0 and local_len == LANES
    flat_cot = cotangent.reshape(tokens, width)
    chosen = routes.reshape(tokens)
    blocks = inputs.reshape(total, local_len // parts, width)

    if fast:
        lines = chosen.astype(F32).reshape(tokens // LANES, LANES)
        params = jnp.concatenate(
            [
                gain_one[None],
                gain_two[None],
                w_router.T.astype(F32),
                jnp.pad(lines, ((0, 14 - experts - tokens // LANES), (0, width - LANES))),
            ],
            axis=0,
        )
        first_slot = [(e % own_experts) * (across * capacity) + (e // own_experts) * capacity for e in range(experts)]
        base = jnp.array(first_slot + [0] * (LANES - experts), F32)[None]
    else:
        own_weights = jnp.concatenate(
            [lax.dynamic_slice(w, (0, part * cols), (width, cols)) for w in (w_query, w_key, w_value)], axis=1
        )
        seq_in = spread(blocks, parts).reshape(length, width).astype(F32)
        inv_one = inverse_rms(seq_in)
        normed_one = (seq_in * inv_one * gain_one).astype(BF16)
        flipped = normed_one.T
        qkv = contract(own_weights, normed_one, 0, 1).astype(BF16).reshape(3, heads, size, length)
        picked = (chosen[:, None] == jnp.arange(experts, dtype=jnp.int32)[None, :]).astype(F32)
        order = jnp.arange(tokens, dtype=jnp.int32)
        before = (order[None, :] < order[:, None]).astype(BF16)
        earlier = jnp.dot(before, picked.astype(BF16), preferred_element_type=F32)
        rank_in = jnp.sum(earlier * picked, axis=1).astype(jnp.int32)
        place = (chosen % own_experts) * (across * capacity) + (chosen // own_experts) * capacity + rank_in
        slot_of = jnp.where(rank_in < capacity, place, slots)
        slot_hot = (slot_of[:, None] == jnp.arange(slots, dtype=jnp.int32)[None, :]).astype(BF16)
        packed = contract(slot_hot, flat_cot, 0, 0).astype(BF16).reshape(own_experts, across, capacity, width)
        cot_rows = jnp.stack([lax.all_to_all(packed[e], "wide", 0, 0, tiled=True) for e in range(own_experts)])
        cot_rows = cot_rows.reshape(own_experts, across * capacity, width)
    own_table = lax.dynamic_slice(rel_table, (0, part * heads), (buckets, heads))
    ids = jnp.concatenate([bucket_ids, jnp.full((1,), LANES, jnp.int32)])
    bucket_hot = (ids[None, :] == jnp.arange(LANES, dtype=jnp.int32)[:, None]).astype(BF16)
    reverse_hot = (ids[::-1][None, :] == jnp.arange(buckets, dtype=jnp.int32)[:, None]).astype(BF16)
    bias_line = contract(own_table, reverse_hot, 0, 0).reshape(heads, 1, 2 * length)
    share = width // total
    flat_in = inputs.reshape(tokens, width)
    split_output = w_output.reshape(parts, cols, width)
    if fast:
        seq_in, qkv, flipped, slot_hot, cot_rows, own_weights, outs, attended, exps, inverse, *passed = run_forward(
            blocks,
            w_query,
            w_key,
            w_value,
            flat_cot,
            params,
            base,
            bias_line,
            w_output,
            flat_in,
            w_in,
            w_out,
            heads,
            size,
            capacity,
            512,
        )
        attended = attended.reshape(seqs, width, local_len)
        first, (middle, normed_two, received, returned, *passed) = passed[:2], passed[2:]
        second = [passed[0], passed[4], passed[1], passed[5]]
        next_cots, near_rows = passed[2:4], passed[6:]
        back = (exps, inverse, split_output, outs, qkv, bucket_hot)
        more = [
            returned,
            slot_hot,
            middle,
            normed_two,
            flat_cot,
            attended,
            params,
        ]
        three, table, early, output, grad_middle, tiny, *passed = attend_back(*back, None, more, near_rows, second)
        all_rows = [received, *near_rows, *passed[:2]]
        all_cots = [cot_rows, first[0], next_cots[0], first[1], next_cots[1], *second, *passed[2:]]
        home, *found = finish(
            three,
            flipped,
            own_weights,
            seq_in,
            early,
            tiny,
            table,
            params,
            all_rows,
            all_cots,
            w_in,
            w_out,
        )
        grad_inputs, *grads_qkvo, grad_gain_one, grad_gain_two, grad_router, grad_table, grad_in, grad_out, output = close(
            home, grad_middle, *found, output, head_count, buckets, experts
        )
        return (
            output.reshape(inputs.shape),
            grad_inputs.reshape(inputs.shape),
            grad_gain_one[0],
            *grads_qkvo,
            grad_table,
            grad_gain_two[0],
            grad_router.T,
            grad_in,
            grad_out,
        )

    outs, attended, exps, inverse = attend(qkv, bias_line, total)
    attended = attended.reshape(seqs, width, local_len)
    back = (exps, inverse, split_output, outs, qkv, bucket_hot)

    flat_in = flat_in.astype(F32)
    middle = flat_in + jnp.einsum("sft,fe->ste", attended, w_output, preferred_element_type=F32).reshape(tokens, width)
    inv_two = inverse_rms(middle)
    normed_two = (middle * inv_two * gain_two).astype(BF16)
    router_probs = jax.nn.softmax(jnp.dot(normed_two, w_router, preferred_element_type=F32), axis=-1)
    picked = (chosen[:, None] == jnp.arange(experts, dtype=jnp.int32)[None, :]).astype(F32)
    gate_prob = jnp.sum(router_probs * picked, axis=1)
    upstream = flat_cot.astype(F32)
    packed = contract(slot_hot, normed_two, 0, 0).astype(BF16).reshape(own_experts, across, capacity, width)
    received, returned = [], []
    for e in range(own_experts):
        got = lax.all_to_all(packed[e], "wide", 0, 0, tiled=True).reshape(across * capacity, width)
        received.append(got)
        pair = run_expert(got, cot_rows[e], w_router.T, w_in, w_out, e, 512).reshape(across, capacity, 2 * width)
        returned.append(lax.all_to_all(pair, "wide", 0, 0, tiled=True).reshape(across * capacity, 2 * width))
    received, returned = jnp.stack(received), jnp.concatenate(returned, axis=0)
    token_rows = jnp.dot(slot_hot, returned, preferred_element_type=F32)
    selected, grad_token = token_rows[:, :width], token_rows[:, width:]
    output = (middle + gate_prob[:, None] * selected).astype(BF16).reshape(inputs.shape)
    grad_gate = jnp.sum(upstream * selected, axis=1)
    grad_logits = (grad_gate[:, None] * router_probs * (picked - gate_prob[:, None])).astype(BF16)
    grad_router = contract(grad_logits, normed_two, 0, 0)
    grad_normed_two = grad_token + contract(grad_logits, w_router, 1, 1)
    grad_mid_norm, grad_gain_two = norm_backward(middle, inv_two, gain_two, grad_normed_two)
    grad_middle = upstream + grad_mid_norm
    grad_branch = grad_middle.astype(BF16).reshape(seqs, local_len, width)
    grad_w_output = jnp.einsum("sft,ste->fe", attended, grad_branch, preferred_element_type=F32)
    all_cots = lax.all_gather(cot_rows, "seq", axis=0)
    all_rows = lax.all_gather(received, "seq", axis=0)
    three, table = attend_back(*back, grad_branch, [], [], [])
    grad_normed_one = contract(three, own_weights, 1, 1)
    grad_in_norm, grad_gain_one = norm_backward(seq_in, inv_one, gain_one, grad_normed_one)
    pieces = grad_in_norm.astype(BF16).reshape(total, parts, local_len // parts, width)
    swapped = swap_parts([pieces[:, p] for p in range(parts)], part, parts, total)
    home = sum(p.astype(F32) for p in swapped).astype(BF16)
    home = lax.all_to_all(home, "seq", 0, 0, tiled=True).reshape(tokens, width).astype(F32)
    grad_projections = lax.dynamic_update_slice(
        jnp.zeros((width, 3, width), F32), contract(flipped, three, 1, 0).reshape(width, 3, cols), (0, 0, part * cols)
    )
    rows = [grad_projections[:, k] for k in range(3)]
    rows += [grad_w_output, grad_gain_one[:, None], grad_gain_two[:, None], grad_router.T]
    table = table.T[:buckets]
    rows, table = lax.psum((jnp.concatenate(rows, axis=1).astype(BF16), table.astype(BF16)), "wide")
    rows = lax.psum_scatter(rows, "seq", scatter_dimension=0, tiled=True).astype(F32)
    table = lax.psum_scatter(table, "seq", scatter_dimension=0, tiled=True).astype(F32)
    held = []
    for e in range(own_experts):
        held = run_share(
            me,
            all_rows.reshape(total * own_experts, *received.shape[1:]),
            all_cots.reshape(total * own_experts, *cot_rows.shape[1:]),
            w_router.T,
            w_in,
            w_out,
            e,
            held,
        )
    last = rows[:, 4 * width :]
    return (
        output,
        (grad_middle + home).reshape(inputs.shape),
        last[:, 0],
        *[rows[:, k * width : (k + 1) * width] for k in range(4)],
        table[:, :head_count],
        last[:, 1],
        last[:, 2 : 2 + experts],
        *held,
    )


def solution(mesh):
    in_specs = (
        P("wide", "seq", None),
        P("wide", "seq", None),
        P(),
        P(),
        P(),
        P(),
        P(),
        P(),
        P(),
        P(),
        P(),
        P("wide", None, None),
        P("wide", None, None),
        P("wide", "seq", None),
    )
    out_specs = (
        P("wide", "seq", None),
        P("wide", "seq", None),
        P("seq"),
        P("seq", None),
        P("seq", None),
        P("seq", None),
        P("seq", None),
        P("seq", None),
        P("seq"),
        P("seq", None),
        P("wide", None, "seq"),
        P("wide", "seq", None),
    )
    return jax.shard_map(
        per_device, mesh=mesh, in_specs=in_specs, out_specs=out_specs, check_vma=False
    )
```

```python
import functools

import jax
import jax.numpy as jnp
from jax import lax
from jax.experimental import pallas as pl
from jax.experimental.pallas import tpu as pltpu
from jax.sharding import PartitionSpec as P

EPSILON = 1e-06
F32 = jnp.float32
BF16 = jnp.bfloat16
LANES = 128


def contract(a, b, da, db):
    return lax.dot_general(a, b, (((da,), (db,)), ((), ())), preferred_element_type=F32)


def inverse_rms(source):
    return lax.rsqrt(jnp.mean(source * source, axis=-1, keepdims=True) + EPSILON)


def norm_backward(source, inv_rms, gain_vec, upstream):
    scaled = upstream * gain_vec
    gain_grad = jnp.sum(upstream * source * inv_rms, axis=0)
    mean_inner = jnp.mean(source * scaled, axis=-1, keepdims=True)
    return (inv_rms * scaled - source * (inv_rms * inv_rms * inv_rms) * mean_inner, gain_grad)


def smooth_act(values):
    return jax.nn.gelu(values, approximate=True)


MESH = pl.DeviceIdType.MESH


def remote(src, dst, send, recv, where):
    copy = pltpu.make_async_remote_copy(src, dst, send, recv, device_id=where, device_id_type=MESH)
    copy.start()
    return copy


def router_of(table, experts):
    return table[2 : 2 + experts, :].astype(BF16)


def routes_of(table, experts, tokens):
    lines = table[2 + experts : 2 + experts + tokens // LANES, :LANES]
    lines = jnp.concatenate([lines, jnp.zeros((LANES - lines.shape[0], LANES), F32)], axis=0).T
    return jnp.concatenate([lines[:, n : n + 1] for n in range(tokens // LANES)], axis=0)


def fetch(sources, targets, sems):
    copies = [pltpu.make_async_copy(a, b, sems.at[n]) for n, (a, b) in enumerate(zip(sources, targets, strict=True))]
    for copy in copies:
        copy.start()
    return copies


def meet(peers):
    barrier = pltpu.get_barrier_semaphore()
    for where in peers:
        pl.semaphore_signal(barrier, inc=1, device_id=where, device_id_type=MESH)
    pl.semaphore_wait(barrier, len(peers))


def line_peers(parts):
    total, me = lax.axis_size("seq"), lax.axis_index("seq")
    return [{"seq": lax.rem(me + parts, total)}, {"seq": lax.rem(me - parts + total, total)}]


def line_round(parts, up, down, sems):
    me = lax.axis_index("seq")
    z = lax.div(me, parts)

    def copy(n, src, dst, step):
        return pltpu.make_async_remote_copy(
            src, dst, sems.at[0, n], sems.at[1, n], device_id={"seq": me + step}, device_id_type=MESH
        )

    legs = [(0, *up, parts), (1, *down, -parts)]

    def start():
        for n, low, high, src, dst, step in legs:

            @pl.when(jnp.logical_and(z >= low, z <= high))
            def _():
                copy(n, src, dst, step).start()

    def end():
        for n, low, high, src, dst, step in legs:
            move = 1 if step > 0 else -1

            @pl.when(jnp.logical_and(z >= low, z <= high))
            def _():
                copy(n, src, dst, step).wait_send()

            @pl.when(jnp.logical_and(z >= low + move, z <= high + move))
            def _():
                copy(n, src, dst, -step).wait_recv()

    return start, end


def pass_on(parts, up, down, sems):
    start, end = line_round(parts, up, down, sems)
    start()
    return end


def far_first(total):
    return sorted(range(1, total), key=lambda k: -min(k, total - k))


def twist(a, b, total):
    out, bit = 0, 1
    while bit < total:
        out = out + lax.rem(lax.div(a, bit) + lax.div(b, bit), 2) * bit
        bit *= 2
    return out


def first_round(seqs, rows, targets, sems):
    before, after = targets
    parts = lax.axis_size("seq") // seqs
    return line_round(parts, (0, seqs - 2, rows.at[0], before), (1, seqs - 1, rows.at[0], after), sems)


def attend_kernel(seqs, meets, next_steps, *refs):
    refs = list(refs)
    qkv_ref, bias_ref = refs[:2]
    line_ref = refs.pop(2) if seqs else None
    out_ref, home_ref, exp_ref, inv_ref = refs[2:6]
    line_outs = [refs.pop(6) for _ in range(2)] if seqs else []
    strip, keys, scores, held, send, recv, local, exp_sems, *line_sems = refs[6:]
    _, heads, size, length = qkv_ref.shape
    total = lax.axis_size("seq")
    me = lax.axis_index("seq")
    tokens = out_ref.shape[3]
    width = 2 * tokens
    pairs = total // 2
    rows = 2 * length - tokens
    chunk = 256
    if meets:
        meet([{"seq": lax.rem(me + k, total)} for k in range(1, total)])
    if seqs:
        line_end = first_round(seqs, line_ref, line_outs, line_sems[0])[1]

    def prepare(h, carry):
        keys[h] = qkv_ref[1, h].T
        for b in range(rows // tokens):
            start = 2 * length - 2 * tokens - tokens * b
            base = jnp.broadcast_to(bias_ref[h, :, start : start + 2 * tokens], (tokens, 2 * tokens))
            rolled = pltpu.roll(base, 0, 1, stride=1, stride_axis=0)
            strip[h, tokens * b : tokens * (b + 1), :] = rolled[:, tokens:]
        return carry

    lax.fori_loop(0, heads, prepare, 0)

    def store(slot, pair, h):
        return pltpu.make_async_copy(held.at[slot], exp_ref.at[pair, h], exp_sems.at[slot])

    def step(t, carry):
        pair = twist(lax.div(me, 2), pairs - 1 - t, pairs)
        at = pl.ds(pl.multiple_of(pair * width, tokens), width)
        if seqs:

            @pl.when(t == pairs - 1)
            def _():
                line_end()
                for start in next_steps:
                    start()

        def head(h, carry):
            count = t * heads + h
            slot = lax.rem(count, 2)

            @pl.when(count >= 2)
            def _():
                store(slot, pair, h).wait()

            query = qkv_ref[0, h, :, at]
            tops = [jnp.full((1, tokens), -jnp.inf, F32)] * 2
            for c in range(length // chunk):
                part = contract(keys[h, c * chunk : (c + 1) * chunk, :], query, 1, 0)
                for s in range(2):
                    row = pl.multiple_of(length - tokens - (pair * width + s * tokens) + c * chunk, tokens)
                    piece = part[:, s * tokens : (s + 1) * tokens] + strip[h, pl.ds(row, chunk), :]
                    scores[c * chunk : (c + 1) * chunk, s * tokens : (s + 1) * tokens] = piece
                    tops[s] = jnp.maximum(tops[s], jnp.max(piece, axis=0, keepdims=True))
            sums = [jnp.zeros((1, tokens), F32)] * 2
            for c in range(length // chunk):
                for s in range(2):
                    piece = scores[c * chunk : (c + 1) * chunk, s * tokens : (s + 1) * tokens]
                    grown = jnp.exp(piece - tops[s])
                    sums[s] = sums[s] + jnp.sum(grown, axis=0, keepdims=True)
                    held[slot, c * chunk : (c + 1) * chunk, s * tokens : (s + 1) * tokens] = grown.astype(BF16)
            store(slot, pair, h).start()
            mixed = contract(qkv_ref[2, h], held[slot], 1, 0)
            for s in range(2):
                inverse = 1.0 / sums[s]
                inv_ref[pair, h, :, s * tokens : (s + 1) * tokens] = inverse
                out_ref[2 * pair + s, h] = (mixed[:, s * tokens : (s + 1) * tokens] * inverse).astype(BF16)
            return carry

        lax.fori_loop(0, heads, head, 0)
        for s in range(2):
            to = 2 * pair + s
            k = twist(me, to, total)

            @pl.when(to != me)
            def _():
                pltpu.make_async_remote_copy(
                    out_ref.at[to], home_ref.at[me], send.at[k], recv.at[k], device_id={"seq": to}, device_id_type=MESH
                ).start()

        return carry

    lax.fori_loop(0, pairs, step, 0)
    own = pltpu.make_async_copy(out_ref.at[me], home_ref.at[me], local)
    own.start()
    for slot in range(2):
        store(slot, 0, 0).wait()

    def settle(k, carry):
        source = twist(me, k, total)
        pltpu.make_async_remote_copy(
            out_ref.at[source], home_ref.at[source], send.at[k], recv.at[k], device_id={"seq": source}, device_id_type=MESH
        ).wait()
        return carry

    lax.fori_loop(1, total, settle, 0)
    own.wait()


def attend(qkv, bias_line, total):
    _, heads, size, length = qkv.shape
    vmem, hbm = pl.BlockSpec(memory_space=pltpu.VMEM), pl.BlockSpec(memory_space=pl.ANY)
    out_shape, scratch = attend_shapes(heads, size, length, total)
    return pl.pallas_call(
        functools.partial(attend_kernel, 0, True, None),
        in_specs=[vmem, vmem],
        out_specs=[vmem, vmem, hbm, vmem],
        out_shape=out_shape,
        scratch_shapes=scratch,
        compiler_params=pltpu.CompilerParams(collective_id=2, has_side_effects=True, vmem_limit_bytes=62 << 20),
        name="attend",
    )(qkv, bias_line)


def attend_shapes(heads, size, length, total):
    tokens = length // total
    out_shape = [
        jax.ShapeDtypeStruct((total, heads, size, tokens), BF16),
        jax.ShapeDtypeStruct((total, heads, size, tokens), BF16),
        jax.ShapeDtypeStruct((total // 2, heads, length, 2 * tokens), BF16),
        jax.ShapeDtypeStruct((total // 2, heads, 1, 2 * tokens), F32),
    ]
    scratch = [
        pltpu.VMEM((heads, 2 * length - tokens, tokens), F32),
        pltpu.VMEM((heads, length, size), BF16),
        pltpu.VMEM((length, 2 * tokens), F32),
        pltpu.VMEM((2, length, 2 * tokens), BF16),
        pltpu.SemaphoreType.DMA((total,)),
        pltpu.SemaphoreType.DMA((total,)),
        pltpu.SemaphoreType.DMA,
        pltpu.SemaphoreType.DMA((2,)),
    ]
    return out_shape, scratch


def attend_back_kernel(fast, *refs):
    refs = list(refs)
    exp_ref, inv_ref, weight_in, out_in, qkv_in, hot_ref = refs[:6]
    weight_ref, out_ref, qkv_ref, *late_sems = refs[-4:]
    refs = refs[:-4]
    late = fetch((weight_in, out_in, qkv_in), (weight_ref, out_ref, qkv_ref), late_sems[0])
    if fast:
        *soon, params_ref = refs[6:13]
        line_refs, far_refs = refs[13:15], refs[15:19]
        *held_refs, soon_sems = refs[-7:]
        soon = fetch(soon, held_refs, soon_sems)
        back_ref, slot_ref, middle_ref, normed_ref, cot_ref, att_ref = held_refs
        refs = refs[19:-7]
    else:
        branch_ref = refs[6]
        refs = refs[7:]
    three_ref, table_ref = refs[:2]
    if fast:
        early_out, output_ref, grad_middle_ref, tiny_ref = refs[2:6]
        line_outs, far_outs = refs[6:8], refs[8:12]
        refs = refs[12:]
    else:
        refs = refs[2:]
    leaving, got, strip, values, dq_all, dk_sum, dv_sum, scores, held, diagonal, send, recv, exp_sems = refs[:13]
    _, heads, size, length = qkv_ref.shape
    total = lax.axis_size("seq")
    me = lax.axis_index("seq")
    tokens = out_ref.shape[3]
    parts = weight_ref.shape[0]
    part = lax.rem(me, parts)
    width = 2 * tokens
    pairs = total // 2
    rows = 2 * length - tokens
    chunk = 256

    def pair_at(t):
        return twist(lax.div(me, 2), t, pairs)

    def load(count):
        slot = lax.rem(count, 2)
        at = exp_ref.at[pair_at(lax.div(count, heads)), lax.rem(count, heads)]
        return pltpu.make_async_copy(at, held.at[slot], exp_sems.at[slot])

    load(0).start()
    peers = [{"seq": lax.rem(me + k, total)} for k in range(1, total)]
    if fast:
        across, row = lax.axis_size("wide"), lax.axis_index("wide")
        other = twist(me, 1, total)
        peers += [{"wide": lax.rem(row + k, across)} for k in range(1, across)]
    meet(peers)
    if fast:
        branch_ref, early_ref, near, near_sum, wide_got, near_sems, wide_sems, line_sems, far_sems = refs[13:]
        seqs = early_ref.shape[0]

        def far_step(e):
            up, down = far_refs[e], far_refs[2 + e]
            return pass_on(
                parts, (seqs - 2, seqs - 2, up, far_outs[e]), (1, 1, down, far_outs[2 + e]), far_sems.at[e]
            )

        line_ends = [far_step(0)]

        def near_copy():
            return pltpu.make_async_remote_copy(
                early_ref.at[:, lax.rem(part + 1, parts)],
                near,
                near_sems.at[0],
                near_sems.at[1],
                device_id={"seq": other},
                device_id_type=MESH,
            )

        def wide_copy(k):
            to = lax.rem(row + k, across)
            return pltpu.make_async_remote_copy(
                near_sum.at[to],
                wide_got.at[k - 1],
                wide_sems.at[0, k - 1],
                wide_sems.at[1, k - 1],
                device_id={"wide": to},
                device_id_type=MESH,
            )

        for copy in soon:
            copy.wait()
        features = middle_ref.shape[1]
        found = contract(slot_ref[...], back_ref[...].reshape(slot_ref.shape[1], 2 * features), 1, 0)
        selected = found[:, :features]
        router = router_of(params_ref, 2 * across)
        logits = contract(normed_ref[...], router, 1, 1)
        grown = jnp.exp(logits - jnp.max(logits, axis=1, keepdims=True))
        probs = grown / jnp.sum(grown, axis=1, keepdims=True)
        routes = routes_of(params_ref, router.shape[0], probs.shape[0])
        picked = (routes == lax.broadcasted_iota(jnp.int32, probs.shape, 1).astype(F32)).astype(F32)
        gate = jnp.sum(probs * picked, axis=1, keepdims=True)
        upstream = cot_ref[...].astype(F32)
        middle = middle_ref[...]
        output_ref[...] = (middle + gate * selected).astype(BF16)
        grad_gate = jnp.sum(upstream * selected, axis=1, keepdims=True)
        grad_logits = (grad_gate * probs * (picked - gate)).astype(BF16)
        grad_normed = found[:, features:] + contract(grad_logits, router, 1, 0)
        inverse = inverse_rms(middle)
        gain_grad = jnp.sum(grad_normed * middle * inverse, axis=0, keepdims=True)
        grad_normed = grad_normed * params_ref[1:2, :]
        mean_inner = jnp.mean(middle * grad_normed, axis=-1, keepdims=True)
        grad_middle = upstream + inverse * grad_normed - middle * (inverse * inverse * inverse) * mean_inner
        grad_middle_ref[...] = grad_middle
        branch = grad_middle.astype(BF16)
        branch_ref[...] = branch.reshape(branch_ref.shape)

    for copy in late:
        copy.wait()

    def product(to):
        value = contract(weight_ref[lax.rem(to, parts)], branch_ref[lax.div(to, parts)], 1, 1)
        return value.astype(BF16).reshape(heads, size, tokens)

    def leave(k, carry):
        to = twist(me, k, total)
        leaving[to] = product(to)
        pltpu.make_async_remote_copy(
            leaving.at[to], got.at[me], send.at[k], recv.at[k], device_id={"seq": to}, device_id_type=MESH
        ).start()
        return carry

    lax.fori_loop(1, total, leave, 0)
    if fast:
        for e in range(line_refs[0].shape[0]):
            up, down = ((1, seqs - 2, line_refs[n].at[e], line_outs[n].at[e]) for n in range(2))
            line_ends.append(pass_on(parts, up, down, line_sems.at[e]))
        line_ends.append(far_step(1))
        attended = jnp.concatenate([att_ref[s] for s in range(seqs)], axis=1)
        early_ref[...] = contract(attended, branch, 1, 0).astype(BF16).reshape(early_ref.shape)
        near_copy().start()
        grad_router = contract(grad_logits, normed_ref[...], 0, 0)
        spare = tiny_ref.shape[0] - 2 - grad_router.shape[0]
        tiny_ref[...] = jnp.concatenate(
            [jnp.zeros((1, features), F32), gain_grad, grad_router, jnp.zeros((spare, features), F32)], axis=0
        )
    got[me] = product(me)

    def prepare(h, carry):
        values[h] = qkv_ref[2, h].T
        strip[h] = jnp.zeros(strip.shape[1:], F32)
        dk_sum[h] = jnp.zeros(dk_sum.shape[1:], F32)
        dv_sum[h] = jnp.zeros(dv_sum.shape[1:], F32)
        return carry

    lax.fori_loop(0, heads, prepare, 0)

    def arrive(k):
        source = twist(me, k, total)
        pltpu.make_async_remote_copy(
            leaving.at[source], got.at[source], send.at[k], recv.at[k], device_id={"seq": source}, device_id_type=MESH
        ).wait()

    def step(t, carry):
        pair = pair_at(t)
        at = pl.ds(pl.multiple_of(pair * width, tokens), width)

        @pl.when(t > 0)
        def _():
            arrive(2 * t)

        arrive(2 * t + 1)
        if fast:

            @pl.when(t == 1)
            def _():
                near_copy().wait()
                for n in range(seqs):
                    for a in range(across):
                        value = early_ref[n, part, a].astype(F32) + near[n, a].astype(F32)
                        near_sum[a, n] = value.astype(BF16)
                for k in range(1, across):
                    wide_copy(k).start()

            @pl.when(t == pairs - 1)
            def _():
                for k in range(1, across):
                    wide_copy(k).wait()
                for n in range(seqs):
                    value = near_sum[row, n].astype(F32)
                    for k in range(1, across):
                        value = value + wide_got[k - 1, n].astype(F32)
                    early_out[n] = value.astype(BF16)

        def head(h, carry):
            count = t * heads + h
            slot = lax.rem(count, 2)

            @pl.when(count + 1 < pairs * heads)
            def _():
                load(count + 1).start()

            grads, inner = [], []
            for s in range(2):
                inverse = inv_ref[pair, h, :, s * tokens : (s + 1) * tokens]
                scaled = got[2 * pair + s, h].astype(F32) * inverse
                inner.append(jnp.sum(scaled * out_ref[2 * pair + s, h].astype(F32), axis=0, keepdims=True))
                grads.append(scaled.astype(BF16))
            grad = jnp.concatenate(grads, axis=1)
            load(count).wait()
            for c in range(length // chunk):
                part_grad = contract(values[h, c * chunk : (c + 1) * chunk, :], grad, 1, 0)
                for s in range(2):
                    grown = held[slot, c * chunk : (c + 1) * chunk, s * tokens : (s + 1) * tokens].astype(F32)
                    slope = grown * (part_grad[:, s * tokens : (s + 1) * tokens] - inner[s])
                    line = pl.multiple_of(length - tokens - (pair * width + s * tokens) + c * chunk, tokens)
                    strip[h, pl.ds(line, chunk), :] += slope
                    scores[c * chunk : (c + 1) * chunk, s * tokens : (s + 1) * tokens] = slope.astype(BF16)
            dq_all[h, at, :] = contract(qkv_ref[1, h], scores[...], 1, 0).T.astype(BF16)
            dk_sum[h] += contract(scores[...], qkv_ref[0, h, :, at].T, 1, 0)
            dv_sum[h] += contract(held[slot], grad.T, 1, 0)
            return carry

        lax.fori_loop(0, heads, head, 0)
        return carry

    lax.fori_loop(0, pairs, step, 0)
    down = lax.broadcasted_iota(jnp.int32, (tokens, tokens), 0)
    over = lax.broadcasted_iota(jnp.int32, (tokens, tokens), 1)
    mirror = (down + over == tokens - 1).astype(F32)
    cols = heads * size
    for c in range(length // chunk):
        here = slice(c * chunk, (c + 1) * chunk)
        for n, ref in enumerate((dq_all, dk_sum, dv_sum)):
            joined = jnp.concatenate([ref[h, here, :].astype(F32) for h in range(heads)], axis=1)
            three_ref[here, n * cols : (n + 1) * cols] = joined.astype(BF16)

    def close(h, carry):
        diagonal[h] = jnp.zeros(diagonal.shape[1:], F32)
        for b in range(rows // tokens):
            flipped = lax.dot_general(
                strip[h, tokens * b : tokens * (b + 1), :],
                mirror,
                (((1,), (0,)), ((), ())),
                precision=lax.Precision.HIGHEST,
                preferred_element_type=F32,
            )
            spread_out = jnp.concatenate([flipped, jnp.zeros_like(flipped)], axis=1)
            rolled = pltpu.roll(spread_out, 0, 1, stride=1, stride_axis=0)
            diagonal[h, :, tokens * b : tokens * (b + 2)] += jnp.sum(rolled, axis=0, keepdims=True)
        return carry

    lax.fori_loop(0, heads, close, 0)
    sums = jnp.concatenate([diagonal[h] for h in range(heads)], axis=0)
    table = lax.dot_general(
        sums,
        hot_ref[...].astype(F32),
        (((1,), (1,)), ((), ())),
        precision=lax.Precision.HIGHEST,
        preferred_element_type=F32,
    )
    line = lax.broadcasted_iota(jnp.int32, (table_ref.shape[0], heads), 0)
    head_line = lax.broadcasted_iota(jnp.int32, (table_ref.shape[0], heads), 1) + part * heads
    table_ref[...] = lax.dot_general(
        (line == head_line).astype(F32),
        table,
        (((1,), (0,)), ((), ())),
        precision=lax.Precision.HIGHEST,
        preferred_element_type=F32,
    )
    if fast:
        for end in line_ends:
            end()


def attend_back(exps, inverse, weight, outs, qkv, hot, branch, more, line, far):
    _, heads, size, length = qkv.shape
    total, tokens = outs.shape[0], outs.shape[3]
    parts, cols, width = weight.shape
    vmem, hbm = pl.BlockSpec(memory_space=pltpu.VMEM), pl.BlockSpec(memory_space=pl.ANY)
    sems = pltpu.SemaphoreType.DMA
    out_shape = [
        jax.ShapeDtypeStruct((length, 3 * heads * size), BF16),
        jax.ShapeDtypeStruct((16, hot.shape[0]), F32),
    ]
    given, scratch = [branch], []
    if branch is None:
        given = more
        across = lax.axis_size("wide")
        slim = width // total // across
        seqs = total // parts
        count = seqs * tokens
        out_shape += [
            jax.ShapeDtypeStruct((seqs, slim, width), BF16),
            jax.ShapeDtypeStruct((count, width), BF16),
            jax.ShapeDtypeStruct((count, width), F32),
            jax.ShapeDtypeStruct((16, width), F32),
        ]
        scratch = [
            pltpu.VMEM((seqs, tokens, width), BF16),
            pltpu.VMEM((seqs, parts, across, slim, width), BF16),
            pltpu.VMEM((seqs, across, slim, width), BF16),
            pltpu.VMEM((across, seqs, slim, width), BF16),
            pltpu.VMEM((across - 1, seqs, slim, width), BF16),
            sems((2,)),
            sems((2, across - 1)),
            sems((line[0].shape[0], 2, 2)),
            sems((len(far) // 2, 2, 2)),
        ]
    passed = [*line, *far]
    held = [pltpu.VMEM(a.shape, a.dtype) for a in more[:6]] + [sems((6,))] if branch is None else []
    spaces = [hbm] * 6 + [vmem] if branch is None else [vmem]
    in_place = len(out_shape)
    out_shape += [jax.ShapeDtypeStruct(rows.shape, BF16) for rows in passed]
    return pl.pallas_call(
        functools.partial(attend_back_kernel, branch is None),
        in_specs=[hbm, vmem, hbm, hbm, hbm, vmem] + spaces + [hbm] * len(passed),
        out_specs=[vmem] * in_place + [hbm] * len(passed),
        out_shape=out_shape,
        scratch_shapes=[
            pltpu.VMEM((total, heads, size, tokens), BF16),
            pltpu.VMEM((total, heads, size, tokens), BF16),
            pltpu.VMEM((heads, 2 * length - tokens, tokens), F32),
            pltpu.VMEM((heads, length, size), BF16),
            pltpu.VMEM((heads, length, size), BF16),
            pltpu.VMEM((heads, length, size), F32),
            pltpu.VMEM((heads, length, size), F32),
            pltpu.VMEM((length, 2 * tokens), BF16),
            pltpu.VMEM((2, length, 2 * tokens), BF16),
            pltpu.VMEM((heads, 1, 2 * length), F32),
            sems((total,)),
            sems((total,)),
            sems((2,)),
            *scratch,
            *held,
            *[pltpu.VMEM(a.shape, a.dtype) for a in (weight, outs, qkv)],
            sems((3,)),
        ],
        compiler_params=pltpu.CompilerParams(collective_id=3, has_side_effects=True, vmem_limit_bytes=62 << 20),
        cost_estimate=pl.CostEstimate(
            flops=8 * heads * length * length * size, bytes_accessed=2 * heads * length * length, transcendentals=0
        ),
        name="attend_back",
    )(exps, inverse, weight, outs, qkv, hot, *given, *passed)


def activation(v):
    square = v * v
    bent = jnp.tanh(0.7978845608 * v * (1.0 + 0.044715 * square))
    half = 0.5 * (1.0 + bent)
    slope = half + 0.5 * v * (1.0 - bent * bent) * (0.7978845608 * (1.0 + 3.0 * 0.044715 * square))
    return v * half, slope


def gated(rows, cots, router, expert):
    logits = contract(rows, router, 1, 1)
    grown = jnp.exp(logits - jnp.max(logits, axis=1, keepdims=True))
    named = lax.broadcasted_iota(jnp.int32, grown.shape, 1) == expert
    gate = jnp.sum(jnp.where(named, grown, 0.0), axis=1, keepdims=True) / jnp.sum(grown, axis=1, keepdims=True)
    return (gate * cots.astype(F32)).astype(BF16)


def expert_kernel(expert, rows_ref, cot_ref, router_ref, in_ref, out_ref, both_ref, forward, backward):
    step = pl.program_id(0)
    width = cot_ref.shape[1]

    @pl.when(step == 0)
    def _():
        forward[...] = jnp.zeros_like(forward)
        backward[...] = jnp.zeros_like(backward)

    rows = rows_ref[...]
    own = router_ref.shape[0] // lax.axis_size("wide")
    grads = gated(rows, cot_ref[...], router_ref[...], lax.axis_index("wide") * own + expert)
    hidden, slope = activation(contract(rows, in_ref[0], 1, 0))
    grad_hidden = contract(grads, out_ref[0], 1, 1).astype(BF16).astype(F32)
    forward[...] += contract(hidden.astype(BF16), out_ref[0], 1, 0)
    backward[...] += contract((grad_hidden * slope).astype(BF16), in_ref[0], 1, 1)

    @pl.when(step == pl.num_programs(0) - 1)
    def _():
        both_ref[:, :width] = forward[...].astype(BF16)
        both_ref[:, width:] = backward[...].astype(BF16)


def run_expert(rows, cots, router, w_in, w_out, expert, block):
    count, width = cots.shape
    units = w_in.shape[2]
    return pl.pallas_call(
        functools.partial(expert_kernel, expert),
        grid=(units // block,),
        in_specs=[
            pl.BlockSpec(rows.shape, lambda f: (0, 0)),
            pl.BlockSpec(cots.shape, lambda f: (0, 0)),
            pl.BlockSpec(router.shape, lambda f: (0, 0)),
            pl.BlockSpec((1, width, block), lambda f: (expert, 0, f)),
            pl.BlockSpec((1, block, width), lambda f: (expert, f, 0)),
        ],
        out_specs=pl.BlockSpec((count, 2 * width), lambda f: (0, 0)),
        out_shape=jax.ShapeDtypeStruct((count, 2 * width), BF16),
        scratch_shapes=[pltpu.VMEM((count, width), F32), pltpu.VMEM((count, width), F32)],
        compiler_params=pltpu.CompilerParams(vmem_limit_bytes=40 << 20),
        name="expert",
    )(rows, cots, router, w_in, w_out)


def forward_kernel(
    capacity,
    block,
    qkv_ref,
    bias_ref,
    weight_in,
    tokens_in,
    hot_ref,
    cot_ref,
    table_ref,
    in_ref,
    out_ref,
    outs_ref,
    att_ref,
    exp_ref,
    inv_ref,
    before_ref,
    after_ref,
    middle_ref,
    normed_ref,
    rows_ref,
    back_ref,
    second_before,
    second_after,
    next_before,
    next_after,
    last_before,
    last_after,
    line_before,
    line_after,
    weight_ref,
    home_ref,
    fetch_sems,
    packed,
    done,
    grads,
    forward,
    backward,
    in_held,
    out_held,
    send,
    recv,
    back_send,
    back_recv,
    local,
    held_sems,
    line_sems,
    *attend_scratch,
):
    own, count, width = rows_ref.shape
    across = lax.axis_size("wide")
    total, heads, size, tokens = att_ref.shape
    parts = width // (heads * size)
    seqs = total // parts
    me = lax.axis_index("wide")
    steps = in_ref.shape[2] // block

    def load(at):
        slot = lax.rem(at, 2)
        expert, place = lax.div(at, steps), pl.multiple_of(lax.rem(at, steps) * block, block)
        return (
            pltpu.make_async_copy(in_ref.at[expert, :, pl.ds(place, block)], in_held.at[slot], held_sems.at[0, slot]),
            pltpu.make_async_copy(out_ref.at[expert, pl.ds(place, block), :], out_held.at[slot], held_sems.at[1, slot]),
        )

    held = fetch((weight_in, tokens_in), (weight_ref, home_ref), fetch_sems)
    for copy in load(0):
        copy.start()
    next_start, first_end = line_round(
        parts, (0, seqs - 2, cot_ref.at[1], next_before), (1, seqs - 1, cot_ref.at[1], next_after), line_sems.at[0]
    )
    second_start, second_end = line_round(
        parts, (1, seqs - 2, before_ref, second_before), (1, seqs - 2, after_ref, second_after), line_sems.at[1]
    )
    attend_kernel(
        seqs,
        False,
        [next_start, second_start],
        qkv_ref,
        bias_ref,
        cot_ref,
        outs_ref,
        att_ref,
        exp_ref,
        inv_ref,
        before_ref,
        after_ref,
        *attend_scratch,
    )
    line_ends = [second_end]
    for copy in held:
        copy.wait()
    attended = [att_ref[parts * s : parts * (s + 1)].reshape(width, tokens) for s in range(seqs)]
    attended = jnp.concatenate(attended, axis=1)
    middle = home_ref[...].astype(F32) + contract(attended, weight_ref[...], 0, 0)
    middle_ref[...] = middle
    normed = (middle * inverse_rms(middle) * table_ref[1:2, :]).astype(BF16)
    normed_ref[...] = normed
    packed[...] = contract(hot_ref[...], normed, 0, 0).astype(BF16).reshape(packed.shape)
    going, kept = [], []
    mine = pl.ds(me * capacity, capacity)
    for n in range(own):
        for k in range(1, across):
            to = lax.rem(me + k, across)
            going.append(
                remote(
                    packed.at[n, pl.ds(to * capacity, capacity)],
                    rows_ref.at[n, mine],
                    send.at[n, k - 1],
                    recv.at[n, k - 1],
                    {"wide": to},
                )
            )
        kept.append(pltpu.make_async_copy(packed.at[n, mine], rows_ref.at[n, mine], local.at[n]))
        kept[n].start()
    first_end()
    line_ends.append(
        pass_on(parts, (1, seqs - 2, next_before, last_before), (1, seqs - 2, next_after, last_after), line_sems.at[2])
    )
    coming = []
    for e in range(own):
        for copy in going[e * (across - 1) : (e + 1) * (across - 1)] + [kept[e]]:
            copy.wait()
        line_ends.append(
            pass_on(
                parts,
                (0, seqs - 2, rows_ref.at[e], line_before.at[e]),
                (1, seqs - 1, rows_ref.at[e], line_after.at[e]),
                line_sems.at[3 + e],
            )
        )
        grads[...] = gated(rows_ref[e], cot_ref[e], router_of(table_ref, own * across), me * own + e)
        forward[...] = jnp.zeros_like(forward)
        backward[...] = jnp.zeros_like(backward)

        def step(f, carry):
            at = e * steps + f
            slot = lax.rem(at, 2)

            @pl.when(at + 1 < own * steps)
            def _():
                for copy in load(at + 1):
                    copy.start()

            for copy in load(at):
                copy.wait()
            hidden, slope = activation(contract(rows_ref[e], in_held[slot], 1, 0))
            grad_hidden = contract(grads[...], out_held[slot], 1, 1).astype(BF16).astype(F32)
            forward[...] += contract(hidden.astype(BF16), out_held[slot], 1, 0)
            backward[...] += contract((grad_hidden * slope).astype(BF16), in_held[slot], 1, 1)
            return carry

        lax.fori_loop(0, steps, step, 0)
        done[e, :, :width] = forward[...].astype(BF16)
        done[e, :, width:] = backward[...].astype(BF16)
        for k in range(1, across):
            to = lax.rem(me + k, across)
            coming.append(
                remote(
                    done.at[e, pl.ds(to * capacity, capacity)],
                    back_ref.at[e, mine],
                    back_send.at[e, k - 1],
                    back_recv.at[e, k - 1],
                    {"wide": to},
                )
            )
        coming.append(pltpu.make_async_copy(done.at[e, mine], back_ref.at[e, mine], local.at[own + e]))
        coming[-1].start()
    for copy in coming:
        copy.wait()
    for end in line_ends:
        end()


def both_kernel(capacity, block, experts, *refs):
    given, (bias, weight, tokens, w_in, w_out) = refs[:7], refs[7:12]
    made, found = refs[12:18], refs[18:36]
    kept, rest = refs[36:54], refs[54:]
    seqs = lax.axis_size("seq") // kept[0].shape[1]
    first_start = first_round(seqs, made[4], found[4:6], rest[-1])[0]
    begin_kernel(capacity, experts, first_start, *given, *made, *kept)
    forward_kernel(
        capacity, block, kept[1], bias, weight, tokens, kept[3], made[4], given[5], w_in, w_out, *found, *rest
    )


def run_forward(
    blocks, w_query, w_key, w_value, cot, table, base, bias_line, weight, tokens_in, w_in, w_out, heads, size, capacity, block
):
    tokens, width = tokens_in.shape
    own, _, units = w_in.shape
    across, total = lax.axis_size("wide"), lax.axis_size("seq")
    count = across * capacity
    rows = blocks.shape[1]
    length = total * 2 * rows
    slots = own * count
    vmem, hbm = pl.BlockSpec(memory_space=pltpu.VMEM), pl.BlockSpec(memory_space=pl.ANY)
    sems = pltpu.SemaphoreType.DMA
    attend_out, attend_scratch = attend_shapes(heads, size, length, total)
    one = jax.ShapeDtypeStruct((count, width), BF16)
    every = jax.ShapeDtypeStruct((own, count, width), BF16)
    first_out = [
        jax.ShapeDtypeStruct((total, 2, rows, width), BF16),
        jax.ShapeDtypeStruct((3, heads, size, length), BF16),
        jax.ShapeDtypeStruct((width, length), BF16),
        jax.ShapeDtypeStruct((tokens, slots), BF16),
        every,
        jax.ShapeDtypeStruct((3 * heads * size, width), BF16),
    ]
    first_scratch = [
        *[pltpu.VMEM(first_out[n].shape, BF16) for n in (0, 1, 2, 3, 5)],
        *[pltpu.VMEM((width, width), BF16)] * 3,
        pltpu.VMEM((tokens, width), BF16),
        sems((6 + 3 * total // 2,)),
        pltpu.VMEM(every.shape, BF16),
        *[sems((total,))] * 4,
        *[sems((own, across - 1))] * 2,
        sems((2 + own,)),
    ]
    return pl.pallas_call(
        functools.partial(both_kernel, capacity, block, own * across),
        in_specs=[hbm] * 5 + [vmem] * 3 + [hbm] * 4,
        out_specs=[hbm] * 4 + [vmem, hbm] + [vmem, vmem, hbm, vmem, hbm, hbm] + [vmem] * 4 + [hbm] * 8,
        out_shape=[
            *first_out,
            *attend_out,
            *[one] * 2,
            jax.ShapeDtypeStruct((tokens, width), F32),
            jax.ShapeDtypeStruct((tokens, width), BF16),
            every,
            jax.ShapeDtypeStruct((own, count, 2 * width), BF16),
            *[one] * 6,
            *[every] * 2,
        ],
        scratch_shapes=[
            *first_scratch,
            pltpu.VMEM(weight.shape, BF16),
            pltpu.VMEM(tokens_in.shape, BF16),
            sems((2,)),
            pltpu.VMEM(every.shape, BF16),
            pltpu.VMEM((own, count, 2 * width), BF16),
            pltpu.VMEM((count, width), BF16),
            pltpu.VMEM((count, width), F32),
            pltpu.VMEM((count, width), F32),
            pltpu.VMEM((2, width, block), BF16),
            pltpu.VMEM((2, block, width), BF16),
            sems((own, across - 1)),
            sems((own, across - 1)),
            sems((own, across - 1)),
            sems((own, across - 1)),
            sems((2 * own,)),
            sems((2, 2)),
            sems((3 + own, 2, 2)),
            *attend_scratch,
            sems((2, 2)),
        ],
        compiler_params=pltpu.CompilerParams(collective_id=5, has_side_effects=True, vmem_limit_bytes=62 << 20),
        cost_estimate=pl.CostEstimate(
            flops=8 * own * count * width * units, bytes_accessed=4 * own * width * units, transcendentals=own * count * units
        ),
        name="forward",
    )(blocks, w_query, w_key, w_value, cot, table, base, bias_line, weight, tokens_in, w_in, w_out)


def share_kernel(expert, share_ref, rows_ref, cot_ref, router_ref, in_ref, out_ref, *refs):
    grad_in_ref, grad_out_ref, flipped, total_in = refs[-4:]
    step = pl.program_id(0)

    @pl.when(step == 0)
    def _():
        flipped[...] = in_ref[0].T
        total_in[...] = jnp.zeros_like(total_in)
        grad_out_ref[...] = jnp.zeros_like(grad_out_ref)

    rows = rows_ref[0]
    own = router_ref.shape[0] // lax.axis_size("wide")
    grads = gated(rows, cot_ref[0], router_ref[...], lax.axis_index("wide") * own + expert)
    hidden, slope = activation(contract(flipped[...], rows, 1, 1))
    grad_hidden = contract(out_ref[0], grads, 1, 1).astype(BF16).astype(F32)
    grad_out_ref[0] += contract(hidden.astype(BF16), grads, 1, 0)
    total_in[...] += contract((grad_hidden * slope).astype(BF16), rows, 1, 0)

    @pl.when(step == pl.num_programs(0) - 1)
    def _():
        grad_in_ref[0] = total_in[...].T


def run_share(me, rows, cots, router, w_in, w_out, expert, held):
    own, width, units = w_in.shape
    sources, count = rows.shape[0] // own, rows.shape[1]
    share = units // sources
    if share % LANES == 0:
        where = jnp.full((1,), me, jnp.int32)
        in_spec = pl.BlockSpec((1, width, share), lambda r, at: (expert, 0, at[0]))
        out_spec = pl.BlockSpec((1, share, width), lambda r, at: (expert, at[0], 0))
    else:
        where = jnp.zeros((1,), jnp.int32)
        w_in = lax.dynamic_slice(w_in, (0, 0, me * share), (own, width, share))
        w_out = lax.dynamic_slice(w_out, (0, me * share, 0), (own, share, width))
        in_spec = pl.BlockSpec((1, width, share), lambda r, at: (expert, 0, 0))
        out_spec = pl.BlockSpec((1, share, width), lambda r, at: (expert, 0, 0))
    held_specs = [pl.BlockSpec(memory_space=pl.ANY)] * len(held)
    return pl.pallas_call(
        functools.partial(share_kernel, expert),
        grid_spec=pltpu.PrefetchScalarGridSpec(
            num_scalar_prefetch=1,
            grid=(sources,),
            in_specs=[
                pl.BlockSpec((1, count, rows.shape[2]), lambda r, at: (own * r + expert, 0, 0)),
                pl.BlockSpec((1, count, width), lambda r, at: (own * r + expert, 0, 0)),
                pl.BlockSpec(router.shape, lambda r, at: (0, 0)),
                in_spec,
                out_spec,
                *held_specs,
            ],
            out_specs=[
                pl.BlockSpec((1, width, share), lambda r, at: (expert, 0, 0)),
                pl.BlockSpec((1, share, width), lambda r, at: (expert, 0, 0)),
            ],
            scratch_shapes=[pltpu.VMEM((share, width), BF16), pltpu.VMEM((share, width), F32)],
        ),
        out_shape=[
            jax.ShapeDtypeStruct((own, width, share), F32),
            jax.ShapeDtypeStruct((own, share, width), F32),
        ],
        input_output_aliases={6 + i: i for i in range(len(held))},
        compiler_params=pltpu.CompilerParams(vmem_limit_bytes=62 << 20),
        cost_estimate=pl.CostEstimate(
            flops=8 * sources * count * width * share, bytes_accessed=4 * sources * count * width, transcendentals=0
        ),
        name="share",
    )(where, rows, cots, router, w_in, w_out, *held)


def spread_kernel(parts, in_ref, out_ref, send, recv, pass_send, pass_recv, local):
    total = lax.axis_size("seq")
    me = lax.axis_index("seq")
    part = lax.rem(me, parts)
    meet([{"seq": lax.rem(me + k, total)} for k in range(1, total)])
    copies = []
    for k in far_first(total):
        to = lax.rem(me + k, total)
        copies.append(remote(in_ref.at[to], out_ref.at[me, lax.rem(to, parts)], send.at[k - 1], recv.at[k - 1], {"seq": to}))
    own = pltpu.make_async_copy(in_ref.at[me], out_ref.at[me, part], local)
    own.start()
    own.wait()
    passed = []

    def forward(source, k):
        for j in range(1, parts):
            to = me - part + lax.rem(part + j, parts)
            at = (j - 1) * total + k
            block = out_ref.at[source, part]
            passed.append(remote(block, block, pass_send.at[at], pass_recv.at[at], {"seq": to}))

    forward(me, 0)
    for k in far_first(total)[::-1]:
        source = lax.rem(me - k + total, total)
        block = out_ref.at[source, part]
        pltpu.make_async_remote_copy(
            block, block, send.at[k - 1], recv.at[k - 1], device_id={"seq": source}, device_id_type=MESH
        ).wait_recv()
        forward(source, k)
    for copy in copies:
        copy.wait_send()
    for copy in passed:
        copy.wait()


def spread(blocks, parts):
    total, rows, width = blocks.shape
    passes = (parts - 1) * total
    return pl.pallas_call(
        functools.partial(spread_kernel, parts),
        in_specs=[pl.BlockSpec(memory_space=pl.ANY)],
        out_specs=pl.BlockSpec(memory_space=pl.ANY),
        out_shape=jax.ShapeDtypeStruct((total, parts, rows, width), blocks.dtype),
        scratch_shapes=[
            pltpu.SemaphoreType.DMA((total - 1,)),
            pltpu.SemaphoreType.DMA((total - 1,)),
            pltpu.SemaphoreType.DMA((passes,)),
            pltpu.SemaphoreType.DMA((passes,)),
            pltpu.SemaphoreType.DMA,
        ],
        compiler_params=pltpu.CompilerParams(collective_id=0, has_side_effects=True),
        name="spread",
    )(blocks)


def begin_kernel(
    capacity,
    experts,
    next_step,
    in_ref,
    query_in,
    key_in,
    value_in,
    cot_in,
    table_ref,
    base_ref,
    all_out,
    qkv_out,
    flip_out,
    hot_out,
    rows_ref,
    weights_out,
    all_ref,
    qkv_ref,
    flip_ref,
    hot_ref,
    weights,
    query_ref,
    key_ref,
    value_ref,
    cot_ref,
    fetch_sems,
    packed,
    send,
    recv,
    pass_send,
    pass_recv,
    wide_send,
    wide_recv,
    local,
):
    total, parts, rows, width = all_ref.shape
    _, heads, size, length = qkv_ref.shape
    own = rows_ref.shape[0]
    cols = heads * size
    across = lax.axis_size("wide")
    me, row = lax.axis_index("seq"), lax.axis_index("wide")
    part = lax.rem(me, parts)
    other = twist(me, 1, total)
    pairs = total // 2
    held = fetch((cot_in, query_in, key_in, value_in), (cot_ref, query_ref, key_ref, value_ref), fetch_sems)
    peers = [{"seq": lax.rem(me + k, total)} for k in range(1, total)]
    peers += [{"wide": lax.rem(row + k, across)} for k in range(1, across)]
    meet(peers)
    sent = []
    for k in range(1, total):
        to = twist(me, k, total)
        sent.append(remote(in_ref.at[to], all_ref.at[me, lax.rem(to, parts)], send.at[to], recv.at[me], {"seq": to}))
    kept = pltpu.make_async_copy(in_ref.at[me], all_ref.at[me, part], local.at[0])
    kept.start()
    kept.wait()
    passed = []

    def forward(source):
        block = all_ref.at[source, part]
        passed.append(remote(block, block, pass_send.at[source], pass_recv.at[source], {"seq": other}))

    def await_recv(block, sem):
        pltpu.make_async_remote_copy(
            block, block, local.at[1], sem, device_id={"seq": other}, device_id_type=MESH
        ).wait_recv()

    forward(me)

    tokens, slots = hot_ref.shape
    routes = routes_of(table_ref, experts, tokens)
    picked = (routes == lax.broadcasted_iota(jnp.int32, (tokens, LANES), 1).astype(F32)).astype(F32)
    down = lax.broadcasted_iota(jnp.int32, (tokens, tokens), 0)
    over = lax.broadcasted_iota(jnp.int32, (tokens, tokens), 1)
    earlier = contract((over < down).astype(F32).astype(BF16), picked.astype(BF16), 1, 0)
    rank = jnp.sum(earlier * picked, axis=1, keepdims=True)
    place = jnp.sum(base_ref[...] * picked, axis=1, keepdims=True) + rank
    place = jnp.where(rank < capacity, place, float(slots)).astype(jnp.int32)
    hot = (place == lax.broadcasted_iota(jnp.int32, (tokens, slots), 1)).astype(F32).astype(BF16)
    hot_ref[...] = hot
    held[0].wait()
    stored = [pltpu.make_async_copy(hot_ref, hot_out, fetch_sems.at[4])]
    stored[0].start()
    packed[...] = contract(hot, cot_ref[...], 0, 0).astype(BF16).reshape(packed.shape)
    wide = []
    mine = pl.ds(row * capacity, capacity)
    for e in range(own):
        for k in range(1, across):
            to = lax.rem(row + k, across)
            wide.append(
                remote(
                    packed.at[e, pl.ds(to * capacity, capacity)],
                    rows_ref.at[e, mine],
                    wide_send.at[e, k - 1],
                    wide_recv.at[e, k - 1],
                    {"wide": to},
                )
            )
    stay = [pltpu.make_async_copy(packed.at[e, mine], rows_ref.at[e, mine], local.at[2 + e]) for e in range(own)]
    for copy in stay:
        copy.start()
    at = pl.ds(pl.multiple_of(part * cols, LANES), cols)
    for n, ref in enumerate((query_ref, key_ref, value_ref)):
        held[1 + n].wait()
        weights[n * cols : (n + 1) * cols, :] = ref[:, at].T
    stored.append(pltpu.make_async_copy(weights, weights_out, fetch_sems.at[5]))
    stored[1].start()

    for t in range(pairs):
        pair = twist(lax.div(me, 2), t, pairs)
        if t == pairs - 1:
            for copy in wide + stay:
                copy.wait()
            next_step()
        for b in range(2):
            if 2 * t + b:
                source = twist(me, 2 * t + b, total)
                await_recv(all_ref.at[source, part], recv.at[source])
                forward(source)
        for b in range(2):
            source = 2 * pair + b
            await_recv(all_ref.at[source, lax.rem(part + 1, parts)], pass_recv.at[source])
        block = all_ref[pl.ds(2 * pair, 2)].reshape(2 * parts * rows, width).astype(F32)
        normed = (block * inverse_rms(block) * table_ref[0:1, :]).astype(BF16)
        here = pl.ds(pl.multiple_of(pair * (2 * parts * rows), LANES), 2 * parts * rows)
        flip_ref[:, here] = normed.T
        projected = contract(weights[...], normed, 1, 1).astype(BF16)
        qkv_ref[:, :, :, here] = projected.reshape(3, heads, size, 2 * parts * rows)
        both = pl.ds(2 * pair, 2)
        for n, (src, dst) in enumerate(
            (
                (all_ref.at[both], all_out.at[both]),
                (flip_ref.at[:, here], flip_out.at[:, here]),
                (qkv_ref.at[:, :, :, here], qkv_out.at[:, :, :, here]),
            )
        ):
            stored.append(pltpu.make_async_copy(src, dst, fetch_sems.at[6 + 3 * t + n]))
            stored[-1].start()
    for copy in sent + passed:
        copy.wait_send()
    for copy in stored:
        copy.wait()


def finish_kernel(
    seqs,
    three_ref,
    flip_ref,
    weight_ref,
    x_ref,
    early_ref,
    tiny_ref,
    table_ref,
    params_ref,
    *refs,
):
    own, steps = 2, 2 * seqs - 1
    inputs = (flip_ref, three_ref, weight_ref, x_ref)
    flip_ref, three_ref, weight_ref, x_ref, sems = refs[-5:]
    held = fetch(inputs, (flip_ref, three_ref, weight_ref, x_ref), sems)
    refs = refs[:-5]
    rows_refs = refs[: steps - 2]
    cots_refs = refs[steps - 2 : steps - 2 + 1 + own * (steps - 1)]
    finish_rest(
        seqs,
        held,
        rows_refs,
        cots_refs,
        three_ref,
        flip_ref,
        weight_ref,
        x_ref,
            early_ref,
        tiny_ref,
        table_ref,
        params_ref,
        *refs[len(rows_refs) + len(cots_refs) :],
    )


def finish_rest(
    seqs,
    held,
    rows_refs,
    cots_refs,
    three_ref,
    flip_ref,
    weight_ref,
    x_ref,
    early_ref,
    tiny_ref,
    table_ref,
    params_ref,
    in_ref,
    out_ref,
    home_ref,
    late_all,
    early_all,
    tiny,
    grad_in_ref,
    grad_out_ref,
    grads,
    near,
    summed,
    gw,
    wide_got,
    wide_sum,
    far_got,
    early_got,
    mine,
    early_mine,
    tiny_got,
    rows_held,
    cots_held,
    in_held,
    out_held,
    sums,
    total_in,
    leaving,
    share_got,
    share_sems,
    near_sems,
    home_sems,
    wide_sems,
    far_sems,
    early_sems,
    last_sems,
    last_early_sems,
    tiny_sems,
    held_sems,
    line_sems,
    local,
):
    total, across = lax.axis_size("seq"), lax.axis_size("wide")
    parts = total // seqs
    me, row = lax.axis_index("seq"), lax.axis_index("wide")
    part, seq = lax.rem(me, parts), lax.div(me, parts)
    other = twist(me, 1, total)
    width = params_ref.shape[1]
    slim = gw.shape[2]
    own = in_ref.shape[0]
    share = in_ref.shape[2] // total
    cols = three_ref.shape[1] // 3
    half = three_ref.shape[0] // 2

    def seq_at(k):
        return lax.rem(seq + k, seqs) * parts + part

    def row_at(k):
        return lax.rem(row + k, across)

    def part_at(k):
        return me - part + lax.rem(part + k, parts)

    at = pl.ds(pl.multiple_of(lax.div(me, 2) * (2 * share), LANES), 2 * share)
    weights = [
        pltpu.make_async_copy(in_ref.at[:, :, at], in_held, local.at[0]),
        pltpu.make_async_copy(out_ref.at[:, at, :], out_held, local.at[1]),
    ]
    for copy in weights:
        copy.start()

    def load_rows(e, n, k):
        return pltpu.make_async_copy(rows_refs[k].at[e], rows_held.at[e, n], held_sems.at[0, e, n])

    def load_cots(e, n, k):
        src = cots_refs[1 + own * (k - 1) + e] if k else cots_refs[0].at[e]
        return pltpu.make_async_copy(src, cots_held.at[e, n], held_sems.at[1, e, n])

    last_place = seqs - 1
    far_end = jnp.logical_or(seq == 0, seq == last_place)
    for e in range(own):
        load_rows(e, 0, 0).start()
        load_cots(e, 0, 0).start()
        for here in range(seqs):

            @pl.when(seq == here)
            def _():
                sources = [2 * k - 1 for k in range(1, here + 1)] + [2 * k for k in range(1, seqs - here)]
                for n, k in enumerate(sources):
                    load_cots(e, n + 1, k).start()
                    if k < len(rows_refs):
                        load_rows(e, n + 1, k).start()

    pairs = [(a, b) for a in range(across) for b in range(parts) if a or b]
    peers = [{"seq": lax.rem(me + k, total)} for k in range(1, total)]
    peers += [{"wide": row_at(k)} for k in range(1, across)]
    peers += [{"wide": row_at(a), "seq": part_at(b)} for a, b in pairs if a and b]
    meet(peers)

    def far_rows(e, up):
        src = rows_refs[3 if up else 4].at[e]
        to = lax.rem(me + (parts if up else total - parts), total)
        return pltpu.make_async_remote_copy(
            src, rows_held.at[e, last_place], line_sems.at[0, e], line_sems.at[1, e], device_id={"seq": to}, device_id_type=MESH
        )

    for e in range(own):

        @pl.when(seq == last_place - 1)
        def _():
            far_rows(e, True).start()

        @pl.when(seq == 1)
        def _():
            far_rows(e, False).start()

    for copy in held:
        copy.wait()
    late = contract(flip_ref[...], three_ref[...], 1, 0).astype(BF16)
    gw[...] = late.reshape(gw.shape)
    wide_copies = [
        remote(gw.at[:, row_at(k)], wide_got.at[k - 1], wide_sems.at[0, k - 1], wide_sems.at[1, k - 1], {"wide": row_at(k)})
        for k in range(1, across)
    ]

    gain = params_ref[0:1, :]
    gain_grad = jnp.zeros((1, width), F32)
    near_copies = []
    for n in range(2):
        scaled = contract(three_ref[n * half : (n + 1) * half, :], weight_ref[...], 1, 0)
        x = x_ref[n * total // 2 : (n + 1) * total // 2].reshape(half, width).astype(F32)
        inverse = inverse_rms(x)
        gain_grad = gain_grad + jnp.sum(scaled * x * inverse, axis=0, keepdims=True)
        scaled = scaled * gain
        mean_inner = jnp.mean(x * scaled, axis=-1, keepdims=True)
        value = inverse * scaled - x * (inverse * inverse * inverse) * mean_inner
        here = pl.ds(n * total // 2, total // 2)
        grads[here] = value.astype(BF16).reshape(total // 2, *grads.shape[1:])
        near_copies.append(
            remote(
                grads.at[here, lax.rem(part + 1, parts)],
                near.at[here],
                near_sems.at[0, n],
                near_sems.at[1, n],
                {"seq": other},
            )
        )
    lines = tiny_ref.shape[0]
    first = lax.broadcasted_iota(jnp.int32, tiny_ref.shape, 0) == 0
    tiny[:lines, :] = jnp.where(first, gain_grad, tiny_ref[...]).astype(BF16)
    table = table_ref[...]
    tiny[lines:, :] = jnp.concatenate([table, jnp.zeros((table.shape[0], width - table.shape[1]), F32)], axis=1).astype(BF16)

    def pass_tiny(stage, wheres):
        return [
            remote(tiny, tiny_got.at[stage, n], tiny_sems.at[0, stage, n], tiny_sems.at[1, stage, n], where)
            for n, where in enumerate(wheres)
        ]

    def take_tiny(stage, copies):
        for copy in copies:
            copy.wait()
        value = tiny[...].astype(F32)
        for n in range(len(copies)):
            value = value + tiny_got[stage, n].astype(F32)
        tiny[...] = value.astype(BF16)

    tiny_copies = pass_tiny(0, [{"wide": row_at(k)} for k in range(1, across)])
    for copy in near_copies:
        copy.wait()
    home_copies = []
    for k in range(total - 1, -1, -1):
        to = twist(me, k, total)
        summed[to] = (grads[to, part].astype(F32) + near[to].astype(F32)).astype(BF16)
        if k:
            home_copies.append(
                remote(summed.at[to], home_ref.at[me], home_sems.at[0, k - 1], home_sems.at[1, k - 1], {"seq": to})
            )
    kept = pltpu.make_async_copy(summed.at[me], home_ref.at[me], local.at[2])
    kept.start()
    for copy in weights:
        copy.wait()

    mine_rows = pl.ds(pl.multiple_of(part * share, LANES), share)
    other_rows = pl.ds(pl.multiple_of((1 - part) * share, LANES), share)

    def share_turn(e, n):
        some = rows_held.shape[1] // 2
        for m in range(n * some, (n + 1) * some):
            load_cots(e, m, 0).wait()
            if m < last_place:
                load_rows(e, m, 0).wait()
            else:

                @pl.when(far_end)
                def _():
                    far_rows(e, True).wait_recv()

                @pl.when(jnp.logical_not(far_end))
                def _():
                    load_rows(e, m, 0).wait()

        count = some * rows_held.shape[2]
        here = slice(n * some, (n + 1) * some)
        rows = rows_held[e, here].reshape(count, width)
        cots = gated(rows, cots_held[e, here].reshape(count, width), router_of(params_ref, own * across), row * own + e)
        hidden, slope = activation(contract(in_held[e].T, rows, 1, 1))
        grad_hidden = contract(out_held[e], cots, 1, 1).astype(BF16).astype(F32)
        part_out = contract(hidden.astype(BF16), cots, 1, 0)
        part_in = contract((grad_hidden * slope).astype(BF16), rows, 1, 0)
        if n == 0:
            sums[e, 0] = part_out
            sums[e, 1] = part_in
            return []
        sums[e, 0] += part_out
        sums[e, 1] += part_in
        grad_out_ref[e] = sums[e, 0, mine_rows, :]
        total_in[e] = sums[e, 1, mine_rows, :]
        copies = []
        for k in range(2):
            leaving[e, k] = sums[e, k, other_rows, :].astype(BF16)
            copies.append(
                remote(leaving.at[e, k], share_got.at[e, k], share_sems.at[0, e, k], share_sems.at[1, e, k], {"seq": other})
            )
        return copies

    def share_end(e, copies):
        for copy in copies:
            copy.wait()
        grad_out_ref[e] += share_got[e, 0].astype(F32)
        grad_in_ref[e] = (total_in[e] + share_got[e, 1].astype(F32)).T

    share_turn(0, 0)
    share_turn(1, 0)
    take_tiny(0, tiny_copies)
    for copy in wide_copies:
        copy.wait_recv()
    far_copies = []
    for k in list(range(1, seqs)) + [0]:
        place = lax.rem(seq + k, seqs)
        for p in range(parts):
            block = place * parts + p
            value = gw[block, row].astype(F32)
            for j in range(across - 1):
                value = value + wide_got[j, block].astype(F32)
            wide_sum[place, p] = value.astype(BF16)
        if k:
            where = {"seq": seq_at(k)}
            far_copies.append(
                remote(wide_sum.at[place], far_got.at[k - 1], far_sems.at[0, k - 1], far_sems.at[1, k - 1], where)
            )
            far_copies.append(
                remote(early_ref.at[place], early_got.at[k - 1], early_sems.at[0, k - 1], early_sems.at[1, k - 1], where)
            )
    tiny_copies = pass_tiny(1, [{"seq": seq_at(k)} for k in range(1, seqs)])
    first_share = share_turn(0, 1)
    take_tiny(1, tiny_copies)
    for copy in far_copies:
        copy.wait_recv()
    for p in range(parts):
        value = wide_sum[seq, p].astype(F32)
        for j in range(seqs - 1):
            value = value + far_got[j, p].astype(F32)
        mine[p] = value.astype(BF16)
    value = early_ref[seq].astype(F32)
    for j in range(seqs - 1):
        value = value + early_got[j].astype(F32)
    early_mine[...] = value.astype(BF16)
    last = pass_tiny(2, [{"seq": part_at(k)} for k in range(1, parts)])
    count = len(last)
    for a, b in pairs:
        n = a * parts + b - 1
        last.append(
            remote(
                mine.at[lax.rem(part + b, parts)],
                late_all.at[row, part],
                last_sems.at[0, n],
                last_sems.at[1, n],
                {"wide": row_at(a), "seq": part_at(b)},
            )
        )
    for k in range(1, across):
        last.append(
            remote(
                early_mine, early_all.at[row], last_early_sems.at[0, k - 1], last_early_sems.at[1, k - 1], {"wide": row_at(k)}
            )
        )
    stay = [
        pltpu.make_async_copy(mine.at[part], late_all.at[row, part], local.at[3]),
        pltpu.make_async_copy(early_mine, early_all.at[row], local.at[4]),
    ]
    for copy in stay:
        copy.start()
    second_share = share_turn(1, 1)
    share_end(0, first_share)
    take_tiny(2, last[:count])
    share_end(1, second_share)
    for e in range(own):

        @pl.when(jnp.logical_or(seq == 1, seq == last_place - 1))
        def _():
            far_rows(e, True).wait_send()

    for copy in last[count:] + stay + home_copies + [kept]:
        copy.wait()
    for copy in wide_copies + far_copies:
        copy.wait_send()


def finish(three, flipped, weights, x, early, tiny, table, params, rows, cots, w_in, w_out):
    columns = three.shape[1]
    total, parts, piece, width = x.shape
    seqs, slim, _ = early.shape
    across = lax.axis_size("wide")
    own, _, units = w_in.shape
    share = units // total
    vmem, hbm = pl.BlockSpec(memory_space=pltpu.VMEM), pl.BlockSpec(memory_space=pl.ANY)
    sems = pltpu.SemaphoreType.DMA
    most = max(across, seqs, parts) - 1
    lines = tiny.shape[0] + table.shape[0]
    return pl.pallas_call(
        functools.partial(finish_kernel, seqs),
        in_specs=[hbm] * 4 + [vmem] * 4 + [hbm] * (len(rows) + len(cots) + 2),
        out_specs=[vmem] * 6,
        out_shape=[
            jax.ShapeDtypeStruct((total, piece, width), BF16),
            jax.ShapeDtypeStruct((across, parts, slim, columns), BF16),
            jax.ShapeDtypeStruct((across, slim, width), BF16),
            jax.ShapeDtypeStruct((lines, width), BF16),
            jax.ShapeDtypeStruct((own, width, share), F32),
            jax.ShapeDtypeStruct((own, share, width), F32),
        ],
        scratch_shapes=[
            pltpu.VMEM((total, parts, piece, width), BF16),
            pltpu.VMEM((total, piece, width), BF16),
            pltpu.VMEM((total, piece, width), BF16),
            pltpu.VMEM((total, across, slim, columns), BF16),
            pltpu.VMEM((across - 1, total, slim, columns), BF16),
            pltpu.VMEM((seqs, parts, slim, columns), BF16),
            pltpu.VMEM((seqs - 1, parts, slim, columns), BF16),
            pltpu.VMEM((seqs - 1, slim, width), BF16),
            pltpu.VMEM((parts, slim, columns), BF16),
            pltpu.VMEM((slim, width), BF16),
            pltpu.VMEM((3, most, lines, width), BF16),
            pltpu.VMEM((own, seqs, *rows[0].shape[1:]), BF16),
            pltpu.VMEM((own, seqs, *cots[0].shape[1:]), BF16),
            pltpu.VMEM((own, width, 2 * share), BF16),
            pltpu.VMEM((own, 2 * share, width), BF16),
            pltpu.VMEM((own, 2, 2 * share, width), F32),
            pltpu.VMEM((own, share, width), F32),
            pltpu.VMEM((own, 2, share, width), BF16),
            pltpu.VMEM((own, 2, share, width), BF16),
            sems((2, own, 2)),
            sems((2, 2)),
            sems((2, total - 1)),
            sems((2, across - 1)),
            sems((2, seqs - 1)),
            sems((2, seqs - 1)),
            sems((2, across * parts - 1)),
            sems((2, across - 1)),
            sems((2, 3, most)),
            sems((2, own, seqs)),
            sems((2, own)),
            sems((5,)),
            *[pltpu.VMEM(a.shape, BF16) for a in (flipped, three, weights, x)],
            sems((4,)),
        ],
        compiler_params=pltpu.CompilerParams(collective_id=1, has_side_effects=True, vmem_limit_bytes=62 << 20),
        cost_estimate=pl.CostEstimate(flops=16 << 30, bytes_accessed=60 << 20, transcendentals=0),
        name="finish",
    )(three, flipped, weights, x, early, tiny, table, params, *rows, *cots, w_in, w_out)


def close_kernel(
    heads,
    home_ref,
    middle_ref,
    late_ref,
    early_ref,
    tiny_ref,
    in_ref,
    out_ref,
    result_ref,
    inputs_ref,
    query_ref,
    key_ref,
    value_ref,
    output_ref,
    gain_one_ref,
    gain_two_ref,
    router_ref,
    table_ref,
    grad_in_ref,
    grad_out_ref,
    result_out,
):
    grad_in_ref[...] = in_ref[...]
    grad_out_ref[...] = out_ref[...]
    result_out[...] = result_ref[...]
    inputs_ref[...] = middle_ref[...] + home_ref[...].reshape(middle_ref.shape).astype(F32)
    _, parts, _, columns = late_ref.shape
    cols = columns // 3
    for p in range(parts):
        for n, ref in enumerate((query_ref, key_ref, value_ref)):
            ref[:, p * cols : (p + 1) * cols] = late_ref[0, p, :, n * cols : (n + 1) * cols].astype(F32)
    output_ref[...] = early_ref[0].astype(F32)

    @pl.when(pl.program_id(0) == 0)
    def _():
        me = lax.axis_index("seq")
        width, piece = tiny_ref.shape[1], gain_one_ref.shape[1]
        chosen = lax.broadcasted_iota(jnp.int32, (width, piece), 0) == (
            lax.broadcasted_iota(jnp.int32, (width, piece), 1) + me * piece
        )
        picked = contract(tiny_ref[...], chosen.astype(F32).astype(BF16), 1, 0)
        gain_one_ref[...] = picked[0:1]
        gain_two_ref[...] = picked[1:2]
        router_ref[...] = picked[2 : 2 + router_ref.shape[0]]
        lines = table_ref.shape[0]
        chosen = lax.broadcasted_iota(jnp.int32, (lines, LANES), 1) == (
            lax.broadcasted_iota(jnp.int32, (lines, LANES), 0) + me * lines
        )
        table_ref[...] = contract(chosen.astype(F32).astype(BF16), tiny_ref[16:, :LANES], 1, 1)[:, :heads]


def close(home, middle, late, early, tiny, grad_in, grad_out, result, heads, buckets, experts):
    across, parts, slim, columns = late.shape
    width = early.shape[2]
    total, piece, _ = home.shape
    tokens = middle.shape[0]
    own, _, share = grad_in.shape
    halves = across // own
    rows = pl.BlockSpec((slim, width), lambda i: (i, 0))

    def whole(*shape):
        return pl.BlockSpec(shape, lambda i: (0,) * len(shape))

    some = pl.BlockSpec((tokens // across, width), lambda i: (i, 0))
    in_part = pl.BlockSpec((1, width // halves, share), lambda i: (i // halves, i % halves, 0))
    out_part = pl.BlockSpec((1, share // halves, width), lambda i: (i // halves, i % halves, 0))
    small = [(1, width // total), (1, width // total), (experts, width // total), (buckets // total, heads)]
    shapes = [middle.shape, *[(across * slim, width)] * 4, *small, grad_in.shape, grad_out.shape]
    return pl.pallas_call(
        functools.partial(close_kernel, heads),
        grid=(across,),
        in_specs=[
            pl.BlockSpec((total // across, piece, width), lambda i: (i, 0, 0)),
            some,
            pl.BlockSpec((1, parts, slim, columns), lambda i: (i, 0, 0, 0)),
            pl.BlockSpec((1, slim, width), lambda i: (i, 0, 0)),
            whole(*tiny.shape),
            in_part,
            out_part,
            some,
        ],
        out_specs=[some, rows, rows, rows, rows, *[whole(*shape) for shape in small], in_part, out_part, some],
        out_shape=[jax.ShapeDtypeStruct(shape, F32) for shape in shapes] + [jax.ShapeDtypeStruct(result.shape, BF16)],
        compiler_params=pltpu.CompilerParams(vmem_limit_bytes=62 << 20),
        name="close",
    )(home, middle, late, early, tiny, grad_in, grad_out, result)


def ring_pairs(total, parts, shift):
    return [(i, i - i % parts + (i % parts + shift) % parts) for i in range(total)]


def pick(pieces, index):
    out = pieces[0]
    for k in range(1, len(pieces)):
        out = jnp.where(index == k, pieces[k], out)
    return out


def swap_parts(pieces, part, parts, total):
    near = [pick(pieces, part)]
    for k in range(1, parts):
        near.append(lax.ppermute(pick(pieces, (part + k) % parts), "seq", ring_pairs(total, parts, k)))
    return [pick(near, (part - j) % parts) for j in range(parts)]


def per_device(
    inputs,
    routes,
    bucket_ids,
    gain_attn,
    w_query,
    w_key,
    w_value,
    w_output,
    rel_table,
    gain_ffn,
    w_router,
    w_in,
    w_out,
    cotangent,
):
    seqs, local_len, width = inputs.shape
    buckets, head_count = rel_table.shape
    size = width // head_count
    total = lax.axis_size("seq")
    across = lax.axis_size("wide")
    length = local_len * total
    parts = total // seqs
    heads = head_count // parts
    cols = heads * size
    me = lax.axis_index("seq")
    part = me % parts
    experts = w_router.shape[1]
    own_experts = w_in.shape[0]
    tokens = seqs * local_len
    capacity = (5 * tokens + 4 * experts - 1) // (4 * experts)
    slots = experts * capacity
    gain_one = gain_attn.astype(F32)
    gain_two = gain_ffn.astype(F32)

    fast = parts == 2 and capacity % 16 == 0 and own_experts == 2 and seqs == 4 and experts == 8 and across == 4 and cols % LANES == 0 and local_len == LANES
    flat_cot = cotangent.reshape(tokens, width)
    chosen = routes.reshape(tokens)
    blocks = inputs.reshape(total, local_len // parts, width)

    if fast:
        lines = chosen.astype(F32).reshape(tokens // LANES, LANES)
        params = jnp.concatenate(
            [
                gain_one[None],
                gain_two[None],
                w_router.T.astype(F32),
                jnp.pad(lines, ((0, 14 - experts - tokens // LANES), (0, width - LANES))),
            ],
            axis=0,
        )
        first_slot = [(e % own_experts) * (across * capacity) + (e // own_experts) * capacity for e in range(experts)]
        base = jnp.array(first_slot + [0] * (LANES - experts), F32)[None]
    else:
        own_weights = jnp.concatenate(
            [lax.dynamic_slice(w, (0, part * cols), (width, cols)) for w in (w_query, w_key, w_value)], axis=1
        )
        seq_in = spread(blocks, parts).reshape(length, width).astype(F32)
        inv_one = inverse_rms(seq_in)
        normed_one = (seq_in * inv_one * gain_one).astype(BF16)
        flipped = normed_one.T
        qkv = contract(own_weights, normed_one, 0, 1).astype(BF16).reshape(3, heads, size, length)
        picked = (chosen[:, None] == jnp.arange(experts, dtype=jnp.int32)[None, :]).astype(F32)
        order = jnp.arange(tokens, dtype=jnp.int32)
        before = (order[None, :] < order[:, None]).astype(BF16)
        earlier = jnp.dot(before, picked.astype(BF16), preferred_element_type=F32)
        rank_in = jnp.sum(earlier * picked, axis=1).astype(jnp.int32)
        place = (chosen % own_experts) * (across * capacity) + (chosen // own_experts) * capacity + rank_in
        slot_of = jnp.where(rank_in < capacity, place, slots)
        slot_hot = (slot_of[:, None] == jnp.arange(slots, dtype=jnp.int32)[None, :]).astype(BF16)
        packed = contract(slot_hot, flat_cot, 0, 0).astype(BF16).reshape(own_experts, across, capacity, width)
        cot_rows = jnp.stack([lax.all_to_all(packed[e], "wide", 0, 0, tiled=True) for e in range(own_experts)])
        cot_rows = cot_rows.reshape(own_experts, across * capacity, width)
    own_table = lax.dynamic_slice(rel_table, (0, part * heads), (buckets, heads))
    ids = jnp.concatenate([bucket_ids, jnp.full((1,), LANES, jnp.int32)])
    bucket_hot = (ids[None, :] == jnp.arange(LANES, dtype=jnp.int32)[:, None]).astype(BF16)
    reverse_hot = (ids[::-1][None, :] == jnp.arange(buckets, dtype=jnp.int32)[:, None]).astype(BF16)
    bias_line = contract(own_table, reverse_hot, 0, 0).reshape(heads, 1, 2 * length)
    share = width // total
    flat_in = inputs.reshape(tokens, width)
    split_output = w_output.reshape(parts, cols, width)
    if fast:
        seq_in, qkv, flipped, slot_hot, cot_rows, own_weights, outs, attended, exps, inverse, *passed = run_forward(
            blocks,
            w_query,
            w_key,
            w_value,
            flat_cot,
            params,
            base,
            bias_line,
            w_output,
            flat_in,
            w_in,
            w_out,
            heads,
            size,
            capacity,
            1024,
        )
        attended = attended.reshape(seqs, width, local_len)
        first, (middle, normed_two, received, returned, *passed) = passed[:2], passed[2:]
        second = [passed[0], passed[4], passed[1], passed[5]]
        next_cots, near_rows = passed[2:4], passed[6:]
        back = (exps, inverse, split_output, outs, qkv, bucket_hot)
        more = [
            returned,
            slot_hot,
            middle,
            normed_two,
            flat_cot,
            attended,
            params,
        ]
        three, table, early, output, grad_middle, tiny, *passed = attend_back(*back, None, more, near_rows, second)
        all_rows = [received, *near_rows, *passed[:2]]
        all_cots = [cot_rows, first[0], next_cots[0], first[1], next_cots[1], *second, *passed[2:]]
        home, *found = finish(
            three,
            flipped,
            own_weights,
            seq_in,
            early,
            tiny,
            table,
            params,
            all_rows,
            all_cots,
            w_in,
            w_out,
        )
        grad_inputs, *grads_qkvo, grad_gain_one, grad_gain_two, grad_router, grad_table, grad_in, grad_out, output = close(
            home, grad_middle, *found, output, head_count, buckets, experts
        )
        return (
            output.reshape(inputs.shape),
            grad_inputs.reshape(inputs.shape),
            grad_gain_one[0],
            *grads_qkvo,
            grad_table,
            grad_gain_two[0],
            grad_router.T,
            grad_in,
            grad_out,
        )

    outs, attended, exps, inverse = attend(qkv, bias_line, total)
    attended = attended.reshape(seqs, width, local_len)
    back = (exps, inverse, split_output, outs, qkv, bucket_hot)

    flat_in = flat_in.astype(F32)
    middle = flat_in + jnp.einsum("sft,fe->ste", attended, w_output, preferred_element_type=F32).reshape(tokens, width)
    inv_two = inverse_rms(middle)
    normed_two = (middle * inv_two * gain_two).astype(BF16)
    router_probs = jax.nn.softmax(jnp.dot(normed_two, w_router, preferred_element_type=F32), axis=-1)
    picked = (chosen[:, None] == jnp.arange(experts, dtype=jnp.int32)[None, :]).astype(F32)
    gate_prob = jnp.sum(router_probs * picked, axis=1)
    upstream = flat_cot.astype(F32)
    packed = contract(slot_hot, normed_two, 0, 0).astype(BF16).reshape(own_experts, across, capacity, width)
    received, returned = [], []
    for e in range(own_experts):
        got = lax.all_to_all(packed[e], "wide", 0, 0, tiled=True).reshape(across * capacity, width)
        received.append(got)
        pair = run_expert(got, cot_rows[e], w_router.T, w_in, w_out, e, 512).reshape(across, capacity, 2 * width)
        returned.append(lax.all_to_all(pair, "wide", 0, 0, tiled=True).reshape(across * capacity, 2 * width))
    received, returned = jnp.stack(received), jnp.concatenate(returned, axis=0)
    token_rows = jnp.dot(slot_hot, returned, preferred_element_type=F32)
    selected, grad_token = token_rows[:, :width], token_rows[:, width:]
    output = (middle + gate_prob[:, None] * selected).astype(BF16).reshape(inputs.shape)
    grad_gate = jnp.sum(upstream * selected, axis=1)
    grad_logits = (grad_gate[:, None] * router_probs * (picked - gate_prob[:, None])).astype(BF16)
    grad_router = contract(grad_logits, normed_two, 0, 0)
    grad_normed_two = grad_token + contract(grad_logits, w_router, 1, 1)
    grad_mid_norm, grad_gain_two = norm_backward(middle, inv_two, gain_two, grad_normed_two)
    grad_middle = upstream + grad_mid_norm
    grad_branch = grad_middle.astype(BF16).reshape(seqs, local_len, width)
    grad_w_output = jnp.einsum("sft,ste->fe", attended, grad_branch, preferred_element_type=F32)
    all_cots = lax.all_gather(cot_rows, "seq", axis=0)
    all_rows = lax.all_gather(received, "seq", axis=0)
    three, table = attend_back(*back, grad_branch, [], [], [])
    grad_normed_one = contract(three, own_weights, 1, 1)
    grad_in_norm, grad_gain_one = norm_backward(seq_in, inv_one, gain_one, grad_normed_one)
    pieces = grad_in_norm.astype(BF16).reshape(total, parts, local_len // parts, width)
    swapped = swap_parts([pieces[:, p] for p in range(parts)], part, parts, total)
    home = sum(p.astype(F32) for p in swapped).astype(BF16)
    home = lax.all_to_all(home, "seq", 0, 0, tiled=True).reshape(tokens, width).astype(F32)
    grad_projections = lax.dynamic_update_slice(
        jnp.zeros((width, 3, width), F32), contract(flipped, three, 1, 0).reshape(width, 3, cols), (0, 0, part * cols)
    )
    rows = [grad_projections[:, k] for k in range(3)]
    rows += [grad_w_output, grad_gain_one[:, None], grad_gain_two[:, None], grad_router.T]
    table = table.T[:buckets]
    rows, table = lax.psum((jnp.concatenate(rows, axis=1).astype(BF16), table.astype(BF16)), "wide")
    rows = lax.psum_scatter(rows, "seq", scatter_dimension=0, tiled=True).astype(F32)
    table = lax.psum_scatter(table, "seq", scatter_dimension=0, tiled=True).astype(F32)
    held = []
    for e in range(own_experts):
        held = run_share(
            me,
            all_rows.reshape(total * own_experts, *received.shape[1:]),
            all_cots.reshape(total * own_experts, *cot_rows.shape[1:]),
            w_router.T,
            w_in,
            w_out,
            e,
            held,
        )
    last = rows[:, 4 * width :]
    return (
        output,
        (grad_middle + home).reshape(inputs.shape),
        last[:, 0],
        *[rows[:, k * width : (k + 1) * width] for k in range(4)],
        table[:, :head_count],
        last[:, 1],
        last[:, 2 : 2 + experts],
        *held,
    )


def solution(mesh):
    in_specs = (
        P("wide", "seq", None),
        P("wide", "seq", None),
        P(),
        P(),
        P(),
        P(),
        P(),
        P(),
        P(),
        P(),
        P(),
        P("wide", None, None),
        P("wide", None, None),
        P("wide", "seq", None),
    )
    out_specs = (
        P("wide", "seq", None),
        P("wide", "seq", None),
        P("seq"),
        P("seq", None),
        P("seq", None),
        P("seq", None),
        P("seq", None),
        P("seq", None),
        P("seq"),
        P("seq", None),
        P("wide", None, "seq"),
        P("wide", "seq", None),
    )
    return jax.shard_map(
        per_device, mesh=mesh, in_specs=in_specs, out_specs=out_specs, check_vma=False
    )
```
